128 devices in a mesh: plane: 8 (over x, core), elem: 16 (over z, y).
Axes of the slice: x: 4, y: 4, z: 4, core: 2. Of those that a mesh axis runs over, the one named last changes fastest.
Arguments:
- scalar_modes: float32 [256, 6, 6, 2048], P('plane', None, None, 'elem'), may hold values from -6 to 6
- velocity: float32 [2, 256, 6, 6, 2048], P(None, None, None, None, ('elem', 'plane')), may hold values from -0.5 to 0.5
- viscosity: float32 [2048], P('elem'), may hold values from 0.05 to 0.5
- mortar_links: int32 [8, 2048], P(None, 'elem'), may hold values from 0 to 2047, as said below
- mortar_sides: int32 [2, 8, 2048], P(None, None, 'elem'), may hold values from 0 to 3, as said below
- layout: int32 [2048], P('elem'), may hold values from 0 to 1, as said below
Outputs:
- advanced: float32 [256, 6, 6, 2048], P('plane', None, None, 'elem')
The draws below stay inside these ranges and needn't reach their ends.
Inputs may be any that keep to these rules, and one draw needn't show every extreme that they name: `mortar_links`: slots 0 and 1 lie on the west face, 2 and 3 on the east, 4 and 5 on the south, 6 and 7 on the north; an unused slot names the element itself. The relation is symmetric (the neighbour's slot on the opposite face names the element back, with the two rows of mortar_sides swapped). A west neighbour lies on the same index of elem or on the index before, an east neighbour on the same or the one after, cyclically; south and north neighbours on the same. At most 16 elements of one index of elem have a west neighbour on another index (likewise east), and some index has exactly that many. `mortar_sides`: 0 the whole face, 1 its lower half, 2 its upper half, 3 an unused slot (both rows 3). The second slot of a face is used only where the first has own code 1 and the second own code 2. `layout`: 0: the element is 1 wide and 2 tall; 1: 2 wide and 1 tall. All elements of one index of elem share it.
All inputs are finite; a program needn't handle non-finite values.
Results may differ from the reference program's by a relative error of at most 0.0003.
Values sent between devices are 32-bit elements; how exact they have to be, the bound alone decides.
No kernel may reach another device: no remote copies, remote signals or barrier semaphores. Data moves between devices by JAX's collectives and lax.ppermute only.
A program may use at most 128 MiB of HBM per device.

```python
import math
import jax
import jax.numpy as jnp
import numpy as np
from jax import lax

NZ = 256
NP = 6
COLS = 8
ROWS = 8
ITERS = 4
E_DEV = 128
NEL = 2048
N_PLANE = 8
N_ELEM = 16


def mesh_tables(key):
    base_key = jax.random.fold_in(key, 11)
    type_key, order_key = jax.random.split(base_key)
    strips = N_ELEM
    per_dev = E_DEV
    kinds = jax.random.randint(type_key, (strips,), 0, 2, dtype=jnp.int32)
    kinds = kinds.at[0].set(0).at[1].set(1)
    scores = jax.random.randint(order_key, (strips, per_dev), 0, per_dev, dtype=jnp.int32) * per_dev + jnp.arange(per_dev, dtype=jnp.int32)[None, :]
    order_of = jnp.argsort(scores, axis=1).astype(jnp.int32)
    place_of = jnp.argsort(order_of, axis=1).astype(jnp.int32).reshape(-1)

    def where_is(device, column, row_at):
        row_count = ROWS * (1 + kinds[device])
        geometric = jnp.clip(column * row_count + row_at, 0, per_dev - 1)
        return device * per_dev + place_of[device * per_dev + geometric]
    device = jnp.broadcast_to(jnp.arange(strips, dtype=jnp.int32)[:, None], (strips, per_dev))
    geo_k = jnp.broadcast_to(jnp.arange(per_dev, dtype=jnp.int32)[None, :], (strips, per_dev))
    kind = kinds[device]
    row_count = ROWS * (1 + kind)
    col_count = 2 * COLS - COLS * kind
    column = geo_k // row_count
    row_at = geo_k % row_count
    self_id = where_is(device, column, row_at)
    dev_west = (device + strips - 1) % strips
    dev_east = (device + 1) % strips
    south = where_is(device, column, (row_at + row_count - 1) % row_count)
    north = where_is(device, column, (row_at + 1) % row_count)

    def side_links(neighbour_dev, inner, inner_col, same_col, big_col, small_col):
        neighbour_kind = kinds[neighbour_dev]
        same_kind = neighbour_kind == kind
        big_face = jnp.logical_not(inner) & (kind == 0) & (neighbour_kind == 1)
        small_face = jnp.logical_not(inner) & (kind == 1) & (neighbour_kind == 0)
        first_link = jnp.where(inner, where_is(device, inner_col, row_at), jnp.where(same_kind, where_is(neighbour_dev, same_col, row_at), jnp.where(big_face, where_is(neighbour_dev, big_col, 2 * row_at), where_is(neighbour_dev, small_col, row_at // 2))))
        second_link = jnp.where(big_face, where_is(neighbour_dev, big_col, 2 * row_at + 1), self_id)
        own_first = jnp.where(big_face, 1, 0)
        far_first = jnp.where(small_face, 1 + row_at % 2, 0)
        own_second = jnp.where(big_face, 2, 3)
        far_second = jnp.where(big_face, 0, 3)
        return ([first_link, second_link], [own_first, own_second], [far_first, far_second])
    west_side = side_links(dev_west, column > 0, column - 1, col_count - 1, COLS - 1, 2 * COLS - 1)
    east_side = side_links(dev_east, column < col_count - 1, column + 1, 0 * column, 0 * column, 0 * column)
    zero_code = jnp.zeros_like(geo_k)
    empty_code = zero_code + 3
    links_geo = jnp.stack(west_side[0] + east_side[0] + [south, self_id, north, self_id]).astype(jnp.int32)
    own_geo = jnp.stack(west_side[1] + east_side[1] + [zero_code, empty_code, zero_code, empty_code]).astype(jnp.int32)
    far_geo = jnp.stack(west_side[2] + east_side[2] + [zero_code, empty_code, zero_code, empty_code]).astype(jnp.int32)
    links_out = jnp.take_along_axis(links_geo, order_of[None], axis=2).reshape(8, strips * per_dev)
    own_out = jnp.take_along_axis(own_geo, order_of[None], axis=2).reshape(8, strips * per_dev)
    far_out = jnp.take_along_axis(far_geo, order_of[None], axis=2).reshape(8, strips * per_dev)
    sides_out = jnp.stack([own_out, far_out]).astype(jnp.int32)
    layout_out = kind.reshape(-1).astype(jnp.int32)
    return (links_out.astype(jnp.int32), sides_out, layout_out)


def draw_mortar_links(key, part):
    return mesh_tables(key)[0]


def draw_mortar_sides(key, part):
    return mesh_tables(key)[1]


def draw_layout(key, part):
    return mesh_tables(key)[2]


def block_scale(own_key, dims, pieces, smallest, high):
    factor_of, own = 1.0, jax.random.fold_in(own_key, 6)
    for axis_at, parts in pieces:
        draws = jnp.exp(jax.random.uniform(jax.random.fold_in(own, axis_at), (parts,), jnp.float32, smallest / len(pieces), high / len(pieces)))
        factor_of = factor_of * jnp.repeat(draws, dims[axis_at] // parts).reshape([-1 if axis == axis_at else 1 for axis in range(len(dims))])
    return factor_of


def centred(stream_key, shape, width, bound, shards=(), kind=jnp.bfloat16):
    factor_of = block_scale(stream_key, shape, shards, -0.22, 0.18) if shards else 1.0
    values = jax.random.normal(stream_key, shape, jnp.float32) * width * factor_of
    return jnp.minimum(jnp.maximum(values, -bound), bound).astype(kind)


def setup_inputs(seed: int = 0) -> dict:
    seeds = jax.random.split(jax.random.key(seed), 7)
    scalar_modes = centred(seeds[0], (NZ, NP, NP, NEL), 1.0, 6.0, ((0, 8), (3, 16)), jnp.float32)
    velocity = jnp.clip(jax.random.uniform(seeds[1], (2, NZ, NP, NP, NEL), jnp.float32, -0.5, 0.5) * block_scale(seeds[1], (2, NZ, NP, NP, NEL), ((4, 128),), -0.4, 0.0), -0.5, 0.5)
    viscosity = jnp.clip(jnp.exp(math.log(0.5) - 2.3025851 * jax.random.uniform(seeds[2], (NEL,), jnp.float32) ** block_scale(seeds[2], (NEL,), ((0, 16),), -0.2, 0.2)), 0.05, 0.5)
    mortar_links = draw_mortar_links(jax.random.fold_in(seeds[6], 71), 0)
    mortar_sides = draw_mortar_sides(jax.random.fold_in(seeds[6], 71), 0)
    layout = draw_layout(jax.random.fold_in(seeds[6], 71), 0)
    return {"scalar_modes": scalar_modes, "velocity": velocity, "viscosity": viscosity, "mortar_links": mortar_links, "mortar_sides": mortar_sides, "layout": layout}


highest = lax.Precision.HIGHEST
inv_step = 2.0
penalty = 10.0
spanwise = 0.0625

def lagrange_at(points, targets):
    matrix_out = np.ones((6, 6))
    for row_a in range(6):
        for col_b in range(6):
            for other_k in range(6):
                if other_k != col_b:
                    matrix_out[row_a, col_b] *= (targets[row_a] - points[other_k]) / (points[col_b] - points[other_k])
    return matrix_out

def node_tables():
    root_seven = math.sqrt(7.0)
    outer_point = math.sqrt(1.0 / 3.0 + 2.0 * root_seven / 21.0)
    inner_point = math.sqrt(1.0 / 3.0 - 2.0 * root_seven / 21.0)
    points = np.array([-1.0, -outer_point, -inner_point, inner_point, outer_point, 1.0])
    weights = np.array([1.0 / 15.0, (14.0 - root_seven) / 30.0, (14.0 + root_seven) / 30.0, (14.0 + root_seven) / 30.0, (14.0 - root_seven) / 30.0, 1.0 / 15.0])
    barycentric = np.array([1.0 / np.prod([points[col_j] - points[other_k] for other_k in range(6) if other_k != col_j]) for col_j in range(6)])
    derivative = np.zeros((6, 6))
    for row_i in range(6):
        for col_j in range(6):
            if row_i != col_j:
                derivative[row_i, col_j] = barycentric[col_j] / barycentric[row_i] / (points[row_i] - points[col_j])
        derivative[row_i, row_i] = -np.sum(derivative[row_i])
    lower_half = lagrange_at(points, (points - 1.0) / 2.0)
    upper_half = lagrange_at(points, (points + 1.0) / 2.0)
    stiffness = derivative.T @ (weights[:, None] * derivative)
    return (jnp.asarray(weights, jnp.float32), jnp.asarray(derivative, jnp.float32), jnp.asarray(lower_half, jnp.float32), jnp.asarray(upper_half, jnp.float32), jnp.asarray(stiffness, jnp.float32))

def plane_tables(plane_count):
    planes = np.arange(plane_count)[:, None]
    coeffs = np.arange(plane_count)[None, :]
    harmonic = (coeffs + 1) // 2
    phase_angle = 2.0 * np.pi * (harmonic * planes % plane_count) / plane_count
    synthesis = np.where(coeffs == 0, 1.0, np.where(coeffs % 2 == 1, np.cos(phase_angle), np.sin(phase_angle)))
    normalizer = np.where((coeffs == 0) | (coeffs == plane_count - 1), float(plane_count), plane_count / 2.0)
    analysis = (synthesis / normalizer).T
    return (jnp.asarray(synthesis, jnp.float32), jnp.asarray(analysis, jnp.float32))

def transform(matrix, volume):
    flat = jnp.dot(matrix, volume.reshape(volume.shape[0], -1), precision=highest)
    return flat.reshape(volume.shape)

def along_first(matrix, volume):
    return jnp.einsum('ia,zaje->zije', matrix, volume, precision=highest)

def along_second(matrix, volume):
    return jnp.einsum('jb,zibe->zije', matrix, volume, precision=highest)

def on_face(matrix, trace_in):
    return jnp.einsum('ab,zbe->zae', matrix, trace_in, precision=highest)

def cut_face(trace_in, code_hot, lower_half, upper_half):
    return trace_in * code_hot[0] + on_face(lower_half, trace_in) * code_hot[1] + on_face(upper_half, trace_in) * code_hot[2]

def spread_face(jump_in, code_hot, lower_half, upper_half):
    return jump_in * code_hot[0] + on_face(lower_half.T, jump_in) * code_hot[1] + on_face(upper_half.T, jump_in) * code_hot[2]

def face_traces(volume):
    return [volume[:, 0, :, :], volume[:, 5, :, :], volume[:, :, 0, :], volume[:, :, 5, :]]

def code_table(codes):
    return jnp.stack([(codes == level_id).astype(jnp.float32) for level_id in range(3)], axis=1)

def add_faces(result, extras):
    result = result.at[:, 0, :, :].add(extras[0])
    result = result.at[:, 5, :, :].add(extras[1])
    result = result.at[:, :, 0, :].add(extras[2])
    return result.at[:, :, 5, :].add(extras[3])

def mortar_sum(faces, neighbours, own_hot, far_hot, weights, lower_half, upper_half):
    extras = []
    for face_id in range(4):
        total_face = jnp.zeros_like(faces[face_id])
        for half_id in range(2):
            slot_id = 2 * face_id + half_id
            jump_in = cut_face(faces[face_id], own_hot[slot_id], lower_half, upper_half) - cut_face(neighbours[slot_id], far_hot[slot_id], lower_half, upper_half)
            total_face = total_face + spread_face(weights[None, :, None] * jump_in, own_hot[slot_id], lower_half, upper_half)
        extras.append(penalty * total_face)
    return extras

def local_part(volume, shift_mode, viscosity, ratio_x, ratio_y, weights, stiffness):
    grad_x = along_first(stiffness, volume) * weights[None, None, :, None]
    grad_y = along_second(stiffness, volume) * weights[None, :, None, None]
    mass_w = 0.5 * weights[:, None] * weights[None, :]
    return viscosity * (ratio_x * grad_x + ratio_y * grad_y) + shift_mode * mass_w[None, :, :, None] * volume

def mode_sum(left_in, right_in):
    return lax.optimization_barrier(jnp.sum(left_in * right_in, axis=(1, 2, 3)))

def per_mode(values):
    return values[:, None, None, None]

def reference(scalar_modes, velocity, viscosity, mortar_links, mortar_sides, layout):
    weights, derivative, lower_half, upper_half, stiffness = node_tables()
    synthesis, analysis = plane_tables(NZ)
    width_x = jnp.where(layout == 0, 1.0, 2.0).astype(jnp.float32)
    width_y = (3.0 - width_x).astype(jnp.float32)
    ratio_x = width_y / width_x
    ratio_y = width_x / width_y
    own_hot = code_table(mortar_sides[0])
    far_hot = code_table(mortar_sides[1])

    def advect_block(block_id):
        first_elem = block_id * E_DEV
        block_modes = lax.dynamic_slice_in_dim(scalar_modes, first_elem, E_DEV, 3)
        block_speed = lax.dynamic_slice_in_dim(velocity, first_elem, E_DEV, 4)
        scale_x = 2.0 / lax.dynamic_slice_in_dim(width_x, first_elem, E_DEV, 0)
        scale_y = 2.0 / lax.dynamic_slice_in_dim(width_y, first_elem, E_DEV, 0)
        phys_x = transform(synthesis, along_first(derivative, block_modes) * scale_x)
        phys_y = transform(synthesis, along_second(derivative, block_modes) * scale_y)
        product = -(block_speed[0] * phys_x + block_speed[1] * phys_y)
        return transform(analysis, product)
    blocks = lax.map(advect_block, jnp.arange(N_ELEM, dtype=jnp.int32))
    advection = jnp.moveaxis(blocks, 0, 3).reshape(NZ, NP, NP, NEL)
    mass_w = 0.5 * weights[:, None] * weights[None, :]
    rhs_all = mass_w[None, :, :, None] * (inv_step * scalar_modes + advection)
    opposite = [1, 0, 3, 2]

    def operate(volume, shift_mode):
        faces = face_traces(volume)
        neighbours = [jnp.take(faces[opposite[slot_id // 2]], mortar_links[slot_id], axis=2) for slot_id in range(8)]
        result = local_part(volume, shift_mode, viscosity, ratio_x, ratio_y, weights, stiffness)
        return add_faces(result, mortar_sum(faces, neighbours, own_hot, far_hot, weights, lower_half, upper_half))
    mode_count = NZ // N_PLANE

    def solve_block(block_id):
        first_mode = block_id * mode_count
        start_guess = lax.dynamic_slice_in_dim(scalar_modes, first_mode, mode_count, 0)
        rhs_block = lax.dynamic_slice_in_dim(rhs_all, first_mode, mode_count, 0)
        coeff_id = first_mode + jnp.arange(mode_count, dtype=jnp.int32)
        harmonic = ((coeff_id + 1) // 2).astype(jnp.float32)
        shift_mode = inv_step + viscosity[None, None, None, :] * per_mode((spanwise * harmonic) ** 2)
        solution = start_guess
        residual = rhs_block - operate(start_guess, shift_mode)
        direction = residual
        norm_now = mode_sum(residual, residual)
        for turn_id in range(ITERS):
            image_dir = operate(direction, shift_mode)
            step_size = norm_now / mode_sum(direction, image_dir)
            solution = solution + per_mode(step_size) * direction
            if turn_id + 1 < ITERS:
                residual = residual - per_mode(step_size) * image_dir
                norm_next = mode_sum(residual, residual)
                direction = residual + per_mode(norm_next / norm_now) * direction
                norm_now = norm_next
        return solution
    solved = lax.map(solve_block, jnp.arange(N_PLANE, dtype=jnp.int32))
    return solved.reshape(NZ, NP, NP, NEL)
```

```python
import math

import jax
import jax.numpy as jnp
import ml_dtypes
import numpy as np
from jax import lax
from jax.experimental import pallas as pl
from jax.experimental.pallas import tpu as pltpu
from jax.sharding import PartitionSpec as P

F32 = jnp.float32
BF16 = jnp.bfloat16
PENALTY = 10.0
SPANWISE = 0.0625
VMEM = pltpu.VMEM
SMEM = pltpu.SMEM
LIST_W, LIST_E, RANK, REMOTE, LOCAL = 0, 1, 2, 6, 10


def lagrange_at(points, targets):
    out = np.ones((6, 6))
    for row in range(6):
        for col in range(6):
            for other in range(6):
                if other != col:
                    out[row, col] *= (targets[row] - points[other]) / (points[col] - points[other])
    return out


def node_tables():
    root = math.sqrt(7.0)
    outer = math.sqrt(1.0 / 3.0 + 2.0 * root / 21.0)
    inner = math.sqrt(1.0 / 3.0 - 2.0 * root / 21.0)
    points = np.array([-1.0, -outer, -inner, inner, outer, 1.0])
    half = [1.0 / 15.0, (14.0 - root) / 30.0, (14.0 + root) / 30.0]
    weights = np.array(half + half[::-1])
    bary = np.array(
        [1.0 / np.prod([points[c] - points[k] for k in range(6) if k != c]) for c in range(6)]
    )
    deriv = np.zeros((6, 6))
    for i in range(6):
        for j in range(6):
            if i != j:
                deriv[i, j] = bary[j] / bary[i] / (points[i] - points[j])
        deriv[i, i] = -np.sum(deriv[i])
    lower = lagrange_at(points, (points - 1.0) / 2.0)
    upper = lagrange_at(points, (points + 1.0) / 2.0)
    stiff = deriv.T @ (weights[:, None] * deriv)
    return weights, deriv, lower, upper, stiff


W, D, QLO, QHI, K1 = node_tables()
HALVES = [np.eye(6), QLO, QHI]


def plane_tables(count):
    planes = np.arange(count)[:, None]
    coeffs = np.arange(count)[None, :]
    harmonic = (coeffs + 1) // 2
    phase = 2.0 * np.pi * (harmonic * planes % count) / count
    synth = np.where(coeffs == 0, 1.0, np.where(coeffs % 2 == 1, np.cos(phase), np.sin(phase)))
    norm = np.where((coeffs == 0) | (coeffs == count - 1), float(count), count / 2.0)
    return synth, (synth / norm).T


def split_table(table):
    table = np.asarray(table, np.float32)
    high = table.astype(ml_dtypes.bfloat16)
    low = (table - high.astype(np.float32)).astype(ml_dtypes.bfloat16)
    return np.stack([high, low])


def fold(matrix):
    plus = (matrix[:3, :3] + matrix[:3, :2:-1]) / 2.0
    minus = (matrix[:3, :3] - matrix[:3, :2:-1]) / 2.0
    return plus, minus


STIFF_FOLD = fold(K1 / W[:, None])
DERIV_FOLD = fold(D)


def folded(values, tables, sign):
    plus, minus = tables
    even = [values[a] + values[5 - a] for a in range(3)]
    odd = [values[a] - values[5 - a] for a in range(3)]
    out = [None] * 6
    for i in range(3):
        e = sum(float(plus[i, a]) * even[a] for a in range(3))
        o = sum(float(minus[i, a]) * odd[a] for a in range(3))
        out[i] = e + o
        out[5 - i] = e - o if sign > 0 else o - e
    return out


def split(value):
    high = value.astype(BF16)
    return high, (value - high.astype(F32)).astype(BF16)


def lane_ids(shape):
    return lax.broadcasted_iota(jnp.int32, shape, len(shape) - 1)


def call(kernel, outs, scratch, operands, spaces, flops=4_000_000):
    total = sum(int(np.prod(o.shape)) * 4 for o in outs)
    total += sum(int(np.prod(o.shape)) * 4 for o in operands)
    return pl.pallas_call(
        kernel,
        out_shape=outs,
        in_specs=[pl.BlockSpec(memory_space=s) for s in spaces],
        out_specs=[pl.BlockSpec(memory_space=VMEM) for _ in outs],
        scratch_shapes=scratch,
        compiler_params=pltpu.CompilerParams(vmem_limit_bytes=40 * 2**20),
        cost_estimate=pl.CostEstimate(flops=flops, bytes_accessed=total, transcendentals=0),
    )(*operands)


def shape(*dims, dtype=F32):
    return jax.ShapeDtypeStruct(dims, dtype)


def prep_kernel(meta, links, sides, visc, layout, idx, tab, own_c, far_c):
    me = meta[1]
    dev = lax.shift_right_logical(links[...], 7)
    loc = jnp.bitwise_and(links[...], 127)
    remote = (dev != me).astype(jnp.int32)
    idx[LOCAL : LOCAL + 8, :] = loc
    idx[REMOTE : REMOTE + 4, :] = remote[0:4]
    idx[18:24, :] = jnp.zeros((6, 128), jnp.int32)
    row = lax.broadcasted_iota(jnp.int32, (128, 128), 0)
    col = lane_ids((128, 128))
    for side in range(2):
        rem = [remote[2 * side + t : 2 * side + t + 1] for t in range(2)]
        far = [loc[2 * side + t : 2 * side + t + 1] for t in range(2)]
        any_rem = jnp.maximum(rem[0], rem[1])
        before = jnp.sum(jnp.where(col < row, any_rem, 0).astype(F32), axis=1, keepdims=True)
        mine = jnp.sum(jnp.where(col == row, any_rem, 0).astype(F32), axis=1, keepdims=True)
        slot = jnp.bitwise_and(col, 15).astype(F32)
        chosen = jnp.where((before == slot) & (mine > 0.0), row.astype(F32), 0.0)
        listed = jnp.sum(chosen, axis=0, keepdims=True).astype(jnp.int32)
        idx[side : side + 1, :] = listed
        named = jnp.where(
            ((far[0] == row) & (rem[0] > 0)) | ((far[1] == row) & (rem[1] > 0)), 1.0, 0.0
        )
        named = jnp.max(named, axis=1, keepdims=True)
        for t in range(2):
            rank = jnp.sum(jnp.where(row < far[t], named, 0.0), axis=0, keepdims=True)
            rank = jnp.where(rem[t] > 0, rank.astype(jnp.int32), 0)
            idx[RANK + 2 * side + t : RANK + 2 * side + t + 1, :] = rank
    nu = visc[...]
    wide = layout[...] == 0
    own, other = sides[0], sides[1]
    tab[0:1, :] = nu * jnp.where(wide, 2.0, 0.5)
    tab[1:2, :] = nu * jnp.where(wide, 0.5, 2.0)
    tab[2:3, :] = nu
    tab[3:4, :] = (own[4:5] == 0).astype(F32)
    tab[4:5, :] = (own[6:7] == 0).astype(F32)
    tab[5:8, :] = jnp.zeros((3, 128), F32)
    own_hot = [(own == o).astype(F32) for o in range(3)]
    pair_hot = [[own_hot[o] * (other == c).astype(F32) for c in range(3)] for o in range(3)]
    own_m = [PENALTY * HALVES[o].T @ np.diag(W) @ HALVES[o] for o in range(3)]
    far_m = [
        [-PENALTY * HALVES[o].T @ np.diag(W) @ HALVES[c] for c in range(3)] for o in range(3)
    ]
    for a in range(6):
        for b in range(6):
            mine = sum(float(own_m[o][a, b]) * own_hot[o] for o in range(3))
            own_c[6 * a + b] = mine + pltpu.roll(mine, 7, 0)
            far_c[6 * a + b] = sum(
                float(far_m[o][c][a, b]) * pair_hot[o][c] for o in range(3) for c in range(3)
            )


def take(value, index):
    return jnp.take_along_axis(value, index, axis=1)


def compact(faces, group, idx, send_w, send_e):
    part = lax.shift_right_logical(lane_ids((8, 128)), 4)
    for face, row, ref in ((faces[0], LIST_W, send_w), (faces[1], LIST_E, send_e)):
        index = jnp.broadcast_to(idx[row : row + 1, :], (8, 128))
        for c in range(3):
            low, high = take(face[2 * c], index), take(face[2 * c + 1], index)
            old = ref[8 * c : 8 * c + 8, :]
            new = jnp.where(part == group, low, jnp.where(part == group + 4, high, old))
            ref[8 * c : 8 * c + 8, :] = new


def operator(group, meta, idx, tab, own_c, far_c, v_ref, from_w, from_e, out):
    rows = pl.ds(pl.multiple_of(group * 8, 8), 8)
    v = [[v_ref[6 * i + j, rows, :] for j in range(6)] for i in range(6)]
    q = meta[0] * 32 + group * 8 + lax.broadcasted_iota(jnp.int32, (8, 128), 0)
    harmonic = lax.shift_right_logical(q + 1, 1).astype(F32) * SPANWISE
    cx, cy, nu = tab[0:1, :], tab[1:2, :], tab[2:3, :]
    shift = 1.0 + 0.5 * nu * (harmonic * harmonic)
    res = [[shift * v[i][j] for j in range(6)] for i in range(6)]
    for j in range(6):
        g = folded([v[i][j] for i in range(6)], STIFF_FOLD, 1)
        for i in range(6):
            res[i][j] = res[i][j] + cx * g[i]
    for i in range(6):
        g = folded(v[i], STIFF_FOLD, 1)
        for j in range(6):
            out[6 * i + j, rows, :] = float(W[i] * W[j]) * (res[i][j] + cy * g[j])

    def nodes(face):
        return [(0, b) if face == 0 else (5, b) if face == 1 else (b, 0) if face == 2 else (b, 5)
                for b in range(6)]

    def row_of(ref, r):
        return jnp.broadcast_to(ref[r : r + 1, :], (8, 128))

    def general(face):
        own = [v[i][j] for i, j in nodes(face)]
        far = [v[i][j] for i, j in nodes(face ^ 1)]
        near = []
        for s in (2 * face, 2 * face + 1):
            local = row_of(idx, LOCAL + s)
            got = [take(far[b], local) for b in range(6)]
            if face < 2:
                pool = from_w if face == 0 else from_e
                rank = row_of(idx, RANK + s) + 16 * group
                rem = row_of(idx, REMOTE + s) > 0
                for b in range(6):
                    c = b // 2
                    sent = take(pool[8 * c : 8 * c + 8, :], rank + 64 * (b % 2))
                    got[b] = jnp.where(rem, sent, got[b])
            near.append(got)
        for a in range(6):
            i, j = nodes(face)[a]
            extra = out[6 * i + j, rows, :]
            for b in range(6):
                extra = extra + own_c[6 * a + b, 2 * face : 2 * face + 1, :] * own[b]
                for t in range(2):
                    s = 2 * face + t
                    extra = extra + far_c[6 * a + b, s : s + 1, :] * near[t][b]
            out[6 * i + j, rows, :] = extra

    general(0)
    general(1)

    @pl.when(meta[2] == 0)
    def _():
        for face in (2, 3):
            active = tab[face + 1 : face + 2, :]
            local = row_of(idx, LOCAL + 2 * face)
            for a in range(6):
                i, j = nodes(face)[a]
                fi, fj = nodes(face ^ 1)[a]
                jump = active * (v[i][j] - take(v[fi][fj], local))
                out[6 * i + j, rows, :] += float(PENALTY * W[a]) * jump

    @pl.when(meta[2] != 0)
    def _():
        general(2)
        general(3)

    return rows, v


def faces_of(ref, rows):
    return [ref[b, rows, :] for b in range(6)], [ref[30 + b, rows, :] for b in range(6)]


def store_sums(acc, pad, count):
    width = count * 128
    lhs = (
        lax.broadcasted_iota(jnp.int32, (8, width), 0)
        == lax.shift_right_logical(lane_ids((8, width)), 7)
    ).astype(F32)
    sums = lax.dot_general(
        lhs, acc[...], (((1,), (1,)), ((), ())),
        precision=lax.Precision.HIGHEST, preferred_element_type=F32,
    )
    pad[...] = jnp.ones((8, 128), F32)
    pad[:, 0:32] = sums


def start_kernel(meta, idx, tab, own_c, far_c, v, from_w, from_e, out):
    def body(group, carry):
        rows, _ = operator(group, meta, idx, tab, own_c, far_c, v, from_w, from_e, out)
        for i in range(6):
            for j in range(6):
                n = 6 * i + j
                out[n, rows, :] = float(W[i] * W[j]) * v[n, rows, :] - out[n, rows, :]
        return carry

    lax.fori_loop(0, 4, body, 0)


def apply_kernel(meta, idx, tab, own_c, far_c, v, from_w, from_e, out, send_w, send_e):
    def body(group, carry):
        rows, _ = operator(group, meta, idx, tab, own_c, far_c, v, from_w, from_e, out)
        compact(faces_of(out, rows), group, idx, send_w, send_e)
        return carry

    lax.fori_loop(0, 4, body, 0)


def apply_last_kernel(meta, idx, tab, own_c, far_c, v, from_w, from_e, out):
    def body(group, carry):
        operator(group, meta, idx, tab, own_c, far_c, v, from_w, from_e, out)
        return carry

    lax.fori_loop(0, 4, body, 0)


def apply_sum_kernel(
    meta, idx, tab, own_c, far_c, v, from_w, from_e, v0, out, send_w, send_e, red, acc, pad
):
    def body(group, carry):
        rows, _ = operator(group, meta, idx, tab, own_c, far_c, v, from_w, from_e, out)
        compact(faces_of(out, rows), group, idx, send_w, send_e)
        sums = [jnp.zeros((8, 128), F32)] * 5
        for n in range(36):
            a, b, c = v0[n, rows, :], v[n, rows, :], out[n, rows, :]
            for k, term in enumerate((a * a, a * b, b * b, b * c, c * c)):
                sums[k] = sums[k] + term
        for k in range(5):
            acc[rows, 128 * k : 128 * k + 128] = sums[k]
        return carry

    lax.fori_loop(0, 4, body, 0)
    store_sums(acc, pad, 5)
    for k in range(16):
        red[k] = pad[...]


def energy_kernel(
    meta, idx, tab, own_c, far_c, v, from_w, from_e, part, red, out, acc, pad
):
    def body(group, carry):
        rows, _ = operator(group, meta, idx, tab, own_c, far_c, v, from_w, from_e, out)
        total = jnp.zeros((8, 128), F32)
        for n in range(36):
            total = total + v[n, rows, :] * out[n, rows, :]
        acc[rows, :] = total
        return carry

    lax.fori_loop(0, 4, body, 0)
    store_sums(acc, pad, 1)
    row = lax.broadcasted_iota(jnp.int32, (8, 128), 0)
    last = jnp.broadcast_to(pad[0:1, :], (8, 128))
    mixed = jnp.where(row == 7, last, part[...])
    for k in range(16):
        red[k] = mixed


def send_kernel(idx, v, send_w, send_e):
    def body(group, carry):
        rows = pl.ds(pl.multiple_of(group * 8, 8), 8)
        compact(faces_of(v, rows), group, idx, send_w, send_e)
        return carry

    lax.fori_loop(0, 4, body, 0)


def residual_kernel(idx, back, base, out, send_w, send_e):
    for g in range(9):
        turned = back[:, 16 * g : 16 * g + 16, :].reshape(128, 128).T
        for m in range(4):
            n = 4 * g + m
            out[n] = base[n] + turned[32 * m : 32 * m + 32]

    def body(group, carry):
        rows = pl.ds(pl.multiple_of(group * 8, 8), 8)
        compact(faces_of(out, rows), group, idx, send_w, send_e)
        return carry

    lax.fori_loop(0, 4, body, 0)


def spread(rows, coef):
    rows = rows + [jnp.zeros((1, 128), F32)] * (8 - len(rows))
    turned = jnp.concatenate(rows, axis=0).T
    for k in range(coef.shape[0]):
        coef[k] = jnp.broadcast_to(turned[0:32, k : k + 1], (32, 128))


def total_rows(red):
    total = red[0]
    for k in range(1, 16):
        total = total + red[k]
    return [total[k : k + 1] for k in range(8)]


def half_kernel(
    idx, red, v0, v1, v2, v3, x0, r2, p2, y, x2, send_w, send_e, part, coef, acc, pad
):
    m00, m01, m11, m12, m22 = total_rows(red)[:5]
    a0 = m00 / m01
    g1 = m00 - 2.0 * a0 * m01 + a0 * a0 * m11
    b0 = 1.0 + g1 / m00
    a1 = g1 / (b0 * b0 * m01 - 2.0 * b0 * a0 * m11 + a0 * a0 * m12)
    c1 = -(a0 + a1 * b0)
    c2 = a0 * a1
    g2 = m00 + 2.0 * c1 * m01 + (c1 * c1 + 2.0 * c2) * m11 + 2.0 * c1 * c2 * m12 + c2 * c2 * m22
    b1 = g2 / g1
    spread([c1, c2, 1.0 + b1 * b0, c1 - b1 * a0], coef)

    def body(group, carry):
        rows = pl.ds(pl.multiple_of(group * 8, 8), 8)
        k1, k2, d0, d1 = [coef[k, rows, :] for k in range(4)]
        sums = [jnp.zeros((8, 128), F32)] * 7
        for n in range(36):
            w0, w1, w2, w3 = v0[n, rows, :], v1[n, rows, :], v2[n, rows, :], v3[n, rows, :]
            rr = w0 + k1 * w1 + k2 * w2
            ar = w1 + k1 * w2 + k2 * w3
            pp = d0 * w0 + d1 * w1 + k2 * w2
            yy = d0 * w1 + d1 * w2 + k2 * w3
            r2[n, rows, :] = rr
            p2[n, rows, :] = pp
            y[n, rows, :] = yy
            x2[n, rows, :] = x0[n, rows, :] - k1 * w0 - k2 * w1
            for k, term in enumerate((rr * rr, rr * pp, rr * ar, rr * yy, yy * ar, pp * yy, yy * yy)):
                sums[k] = sums[k] + term
        for k in range(7):
            acc[rows, 128 * k : 128 * k + 128] = sums[k]
        compact(faces_of(y, rows), group, idx, send_w, send_e)
        return carry

    lax.fori_loop(0, 4, body, 0)
    store_sums(acc, pad, 7)
    part[...] = pad[...]


def finish_kernel(red, r2, p2, y, x2, out, coef):
    rr, rp, rar, ry, yar, py, yy, yz = total_rows(red)
    a2 = rp / py
    g3 = rr - 2.0 * a2 * ry + a2 * a2 * yy
    b2 = g3 / rr
    d3 = rar + 2.0 * b2 * ry - 2.0 * a2 * yar + b2 * b2 * py - 2.0 * a2 * b2 * yy + a2 * a2 * yz
    a3 = g3 / d3
    spread([a3, a2 + a3 * b2, -a2 * a3], coef)
    for n in range(36):
        out[n] = x2[n] + coef[0] * r2[n] + coef[1] * p2[n] + coef[2] * y[n]


def pack_kernel(u, out):
    for g in range(9):
        turned = u[4 * g : 4 * g + 4].reshape(128, 128).T
        out[:, 16 * g : 16 * g + 16, :] = turned.reshape(8, 16, 128)


def block_turn(blocks):
    part = lax.shift_right_logical(lane_ids(blocks[0].shape), 5)
    rolled = [blocks[0]] + [pltpu.roll(blocks[s], 32 * s, 1) for s in range(1, 4)]
    out = []
    for m in range(4):
        mixed = rolled[-m % 4]
        for t in range(1, 4):
            mixed = jnp.where(part == t, rolled[(t - m) % 4], mixed)
        out.append(pltpu.roll(mixed, 128 - 32 * m, 1) if m else mixed)
    return out


def product3(high, low, table):
    def dot(a, b):
        return jnp.dot(a, b, preferred_element_type=F32)

    return dot(high, table[0]) + dot(high, table[1]) + dot(low, table[0])


def advect_kernel(meta, came, speed, synth, analy, out, high, low, phys):
    for g in range(9):
        for h in range(2):
            pieces = block_turn([came[4 * h + s, 16 * g : 16 * g + 16, :] for s in range(4)])
            for m in range(4):
                n = 16 * (4 * g + m)
                hi, lo = split(pieces[m])
                high[n : n + 16, 128 * h : 128 * h + 128] = hi
                low[n : n + 16, 128 * h : 128 * h + 128] = lo
    for i in range(6):
        part = slice(96 * i, 96 * i + 96)
        phys[part, :] = product3(high[part, :], low[part, :], synth)
    wide = meta[3] == 0
    sx = jnp.where(wide, 2.0, 1.0)
    sy = jnp.where(wide, 1.0, 2.0)
    for h in range(2):
        cols = slice(128 * h, 128 * h + 128)
        u = [[phys[16 * (6 * i + j) : 16 * (6 * i + j) + 16, cols] for j in range(6)] for i in range(6)]
        acc = [[None] * 6 for _ in range(6)]
        for j in range(6):
            g = folded([u[i][j] for i in range(6)], DERIV_FOLD, -1)
            for i in range(6):
                acc[i][j] = sx * (speed[0, 6 * i + j, :, cols] * g[i])
        for i in range(6):
            g = folded(u[i], DERIV_FOLD, -1)
            for j in range(6):
                n = 16 * (6 * i + j)
                total = acc[i][j] + sy * (speed[1, 6 * i + j, :, cols] * g[j])
                hi, lo = split(float(-0.5 * W[i] * W[j]) * total)
                high[n : n + 16, cols] = hi
                low[n : n + 16, cols] = lo
    for i in range(6):
        part = slice(96 * i, 96 * i + 96)
        phys[part, :] = product3(high[part, :], low[part, :], analy)
    for g in range(9):
        for h in range(2):
            cols = slice(128 * h, 128 * h + 128)
            pieces = block_turn(
                [phys[16 * (4 * g + m) : 16 * (4 * g + m) + 16, cols] for m in range(4)]
            )
            for s in range(4):
                out[4 * h + s, 16 * g : 16 * g + 16, :] = pieces[s]


def shift_by(array, by):
    count = lax.axis_size("elem")
    return lax.ppermute(array, "elem", [(i, (i + by) % count) for i in range(count)])


def shards(scalar_modes, velocity, viscosity, mortar_links, mortar_sides, layout):
    u = jnp.transpose(scalar_modes, (1, 2, 0, 3)).reshape(36, 32, 128)
    speed = jnp.transpose(velocity, (0, 2, 3, 4, 1)).reshape(2, 36, 16, 256)
    synth, analy = plane_tables(256)
    synth = jnp.asarray(split_table(synth.T))
    analy = jnp.asarray(split_table(analy.T))
    cross = mortar_sides[:, 4:8]
    mixed = jnp.any((cross == 1) | (cross == 2)) | jnp.any(cross[:, 1::2] != 3)
    meta = jnp.stack(
        [lax.axis_index("plane"), lax.axis_index("elem"), mixed.astype(jnp.int32), layout[0]]
    ).astype(jnp.int32)

    vol, edge = shape(36, 32, 128), shape(24, 128)
    blocks = shape(8, 144, 128)
    packed = call(pack_kernel, [blocks], [], [u], [VMEM])[0]
    came = lax.all_to_all(packed, "plane", 0, 0, tiled=True)

    tables = call(
        prep_kernel,
        [shape(24, 128, dtype=jnp.int32), shape(8, 128), shape(36, 8, 128), shape(36, 8, 128)],
        [],
        [meta, mortar_links, mortar_sides, viscosity[None], layout[None]],
        [SMEM] + [VMEM] * 4,
    )
    idx = tables[0]
    head = [meta, *tables]

    def trade(send_w, send_e):
        return shift_by(send_e, 1), shift_by(send_w, -1)

    def run(kernel, outs, scratch, operands):
        args = head + operands
        return call(kernel, outs, scratch, args, [SMEM] + [VMEM] * (len(args) - 1))

    sums = [VMEM((32, 640), F32), VMEM((8, 128), F32)]
    edges = call(send_kernel, [edge, edge], [], [idx, u], [VMEM] * 2)
    base = run(start_kernel, [vol], [], [u, *trade(*edges)])[0]

    back = call(
        advect_kernel,
        [blocks],
        [VMEM((576, 256), BF16), VMEM((576, 256), BF16), VMEM((576, 256), F32)],
        [meta, came, speed, synth, analy],
        [SMEM] + [VMEM] * 4,
    )[0]
    back = lax.all_to_all(back, "plane", 0, 0, tiled=True)

    v0, *edges = call(
        residual_kernel, [vol, edge, edge], [], [idx, back, base], [VMEM] * 3
    )
    v1, *edges = run(apply_kernel, [vol, edge, edge], [], [v0, *trade(*edges)])
    v2, send_w, send_e, red = run(
        apply_sum_kernel,
        [vol, edge, edge, shape(16, 8, 128)],
        sums,
        [v1, *trade(*edges), v0],
    )
    red = lax.all_to_all(red, "elem", 0, 0, tiled=True)
    v3 = run(apply_last_kernel, [vol], [], [v2, *trade(send_w, send_e)])[0]
    r2, p2, y, x2, send_w, send_e, part = call(
        half_kernel,
        [vol, vol, vol, vol, edge, edge, shape(8, 128)],
        [VMEM((4, 32, 128), F32), VMEM((32, 896), F32), VMEM((8, 128), F32)],
        [idx, red, v0, v1, v2, v3, u],
        [VMEM] * 7,
    )
    red = run(
        energy_kernel,
        [shape(16, 8, 128)],
        [VMEM((36, 32, 128), F32), VMEM((32, 128), F32), VMEM((8, 128), F32)],
        [y, *trade(send_w, send_e), part],
    )[0]
    red = lax.all_to_all(red, "elem", 0, 0, tiled=True)
    out = call(
        finish_kernel, [vol], [VMEM((3, 32, 128), F32)], [red, r2, p2, y, x2], [VMEM] * 5
    )[0]
    return jnp.transpose(out.reshape(6, 6, 32, 128), (2, 0, 1, 3))


def solution(mesh):
    placed = (
        P("plane", None, None, "elem"),
        P(None, None, None, None, ("elem", "plane")),
        P("elem"),
        P(None, "elem"),
        P(None, None, "elem"),
        P("elem"),
    )
    return jax.shard_map(
        shards,
        mesh=mesh,
        in_specs=placed,
        out_specs=P("plane", None, None, "elem"),
        check_vma=False,
    )
```

```python
import math

import jax
import jax.numpy as jnp
import ml_dtypes
import numpy as np
from jax import lax
from jax.experimental import pallas as pl
from jax.experimental.pallas import tpu as pltpu
from jax.sharding import PartitionSpec as P

F32 = jnp.float32
BF16 = jnp.bfloat16
PENALTY = 10.0
SPANWISE = 0.0625
VMEM = pltpu.VMEM
SMEM = pltpu.SMEM
SELF, ANY, LOCAL = 2, 4, 10


def lagrange_at(points, targets):
    out = np.ones((6, 6))
    for row in range(6):
        for col in range(6):
            for other in range(6):
                if other != col:
                    out[row, col] *= (targets[row] - points[other]) / (points[col] - points[other])
    return out


def node_tables():
    root = math.sqrt(7.0)
    outer = math.sqrt(1.0 / 3.0 + 2.0 * root / 21.0)
    inner = math.sqrt(1.0 / 3.0 - 2.0 * root / 21.0)
    points = np.array([-1.0, -outer, -inner, inner, outer, 1.0])
    half = [1.0 / 15.0, (14.0 - root) / 30.0, (14.0 + root) / 30.0]
    weights = np.array(half + half[::-1])
    bary = np.array(
        [1.0 / np.prod([points[c] - points[k] for k in range(6) if k != c]) for c in range(6)]
    )
    deriv = np.zeros((6, 6))
    for i in range(6):
        for j in range(6):
            if i != j:
                deriv[i, j] = bary[j] / bary[i] / (points[i] - points[j])
        deriv[i, i] = -np.sum(deriv[i])
    lower = lagrange_at(points, (points - 1.0) / 2.0)
    upper = lagrange_at(points, (points + 1.0) / 2.0)
    stiff = deriv.T @ (weights[:, None] * deriv)
    return weights, deriv, lower, upper, stiff


W, D, QLO, QHI, K1 = node_tables()
HALVES = [np.eye(6), QLO, QHI]


def plane_tables(count):
    planes = np.arange(count)[:, None]
    coeffs = np.arange(count)[None, :]
    harmonic = (coeffs + 1) // 2
    phase = 2.0 * np.pi * (harmonic * planes % count) / count
    synth = np.where(coeffs == 0, 1.0, np.where(coeffs % 2 == 1, np.cos(phase), np.sin(phase)))
    norm = np.where((coeffs == 0) | (coeffs == count - 1), float(count), count / 2.0)
    return synth, (synth / norm).T


def split_table(table):
    table = np.asarray(table, np.float32)
    high = table.astype(ml_dtypes.bfloat16)
    low = (table - high.astype(np.float32)).astype(ml_dtypes.bfloat16)
    return np.stack([high, low])


def fold(matrix):
    plus = (matrix[:3, :3] + matrix[:3, :2:-1]) / 2.0
    minus = (matrix[:3, :3] - matrix[:3, :2:-1]) / 2.0
    return plus, minus


STIFF_FOLD = fold(K1 / W[:, None])
DERIV_FOLD = fold(D)


def folded(values, tables, sign):
    plus, minus = tables
    even = [values[a] + values[5 - a] for a in range(3)]
    odd = [values[a] - values[5 - a] for a in range(3)]
    out = [None] * 6
    for i in range(3):
        e = sum(float(plus[i, a]) * even[a] for a in range(3))
        o = sum(float(minus[i, a]) * odd[a] for a in range(3))
        out[i] = e + o
        out[5 - i] = e - o if sign > 0 else o - e
    return out


def split(value):
    high = value.astype(BF16)
    return high, (value - high.astype(F32)).astype(BF16)


def lane_ids(shape):
    return lax.broadcasted_iota(jnp.int32, shape, len(shape) - 1)


def call(kernel, outs, scratch, operands, spaces, flops=4_000_000):
    total = sum(int(np.prod(o.shape)) * 4 for o in outs)
    total += sum(int(np.prod(o.shape)) * 4 for o in operands)
    return pl.pallas_call(
        kernel,
        out_shape=outs,
        in_specs=[pl.BlockSpec(memory_space=s) for s in spaces],
        out_specs=[pl.BlockSpec(memory_space=VMEM) for _ in outs],
        scratch_shapes=scratch,
        compiler_params=pltpu.CompilerParams(vmem_limit_bytes=40 * 2**20),
        cost_estimate=pl.CostEstimate(flops=flops, bytes_accessed=total, transcendentals=0),
    )(*operands)


def shape(*dims, dtype=F32):
    return jax.ShapeDtypeStruct(dims, dtype)


def take(value, index):
    return jnp.take_along_axis(value, index, axis=1)


def take_row(value, index):
    wide = jnp.broadcast_to(value, (8, 128)), jnp.broadcast_to(index, (8, 128))
    return take(*wide)[0:1]


def prep_kernel(meta, links, sides, visc, layout, idx, edge_idx, tab, own_c, far_c, edge_own, edge_far):
    me = meta[1]
    dev = lax.shift_right_logical(links[...], 7)
    loc = jnp.bitwise_and(links[...], 127)
    remote = (dev != me).astype(jnp.int32)
    idx[LOCAL : LOCAL + 8, :] = loc
    row = lax.broadcasted_iota(jnp.int32, (128, 128), 0)
    col = lane_ids((128, 128))
    lane = lane_ids((1, 128))
    slot = jnp.bitwise_and(lane, 15)
    own, other = sides[0], sides[1]
    listed, present, ranks = [], [], []
    for side in range(2):
        rem = [remote[2 * side + t : 2 * side + t + 1] for t in range(2)]
        far = [loc[2 * side + t : 2 * side + t + 1] for t in range(2)]
        any_rem = jnp.maximum(rem[0], rem[1])
        before = jnp.sum(jnp.where(col < row, any_rem, 0).astype(F32), axis=1, keepdims=True)
        mine = jnp.sum(jnp.where(col == row, any_rem, 0).astype(F32), axis=1, keepdims=True)
        chosen = jnp.where((before == slot.astype(F32)) & (mine > 0.0), 1.0, 0.0)
        listed.append(jnp.sum(chosen * row.astype(F32), axis=0, keepdims=True).astype(jnp.int32))
        present.append(jnp.sum(chosen, axis=0, keepdims=True).astype(jnp.int32))
        idx[side : side + 1, :] = listed[side]
        mine_at = jnp.sum(jnp.where(row == col, before, 0.0), axis=0, keepdims=True)
        mine_at = jnp.where(any_rem > 0, mine_at.astype(jnp.int32), 0)
        idx[SELF + side : SELF + side + 1, :] = mine_at
        idx[ANY + side : ANY + side + 1, :] = any_rem
        named = jnp.where(
            ((far[0] == row) & (rem[0] > 0)) | ((far[1] == row) & (rem[1] > 0)), 1.0, 0.0
        )
        named = jnp.max(named, axis=1, keepdims=True)
        for t in range(2):
            rank = jnp.sum(jnp.where(row < far[t], named, 0.0), axis=0, keepdims=True)
            ranks.append(jnp.where(rem[t] > 0, rank.astype(jnp.int32), 0))
    idx[6:10, :] = jnp.zeros((4, 128), jnp.int32)
    idx[18:24, :] = jnp.zeros((6, 128), jnp.int32)

    west = lane < 64
    base = jnp.bitwise_and(lane, 112)
    element = jnp.where(west, listed[0], listed[1])
    here = jnp.where(west, present[0], present[1]) > 0

    def pick(rows_w, rows_e):
        return jnp.where(west, take_row(rows_w, element), take_row(rows_e, element))

    rank, live, mine, theirs = [], [], [], []
    for t in range(2):
        rank.append(pick(ranks[t], ranks[2 + t]))
        live.append((pick(remote[t : t + 1], remote[2 + t : 3 + t]) > 0) & here)
        mine.append(jnp.where(live[t], pick(own[t : t + 1], own[2 + t : 3 + t]), 3))
        theirs.append(jnp.where(live[t], pick(other[t : t + 1], other[2 + t : 3 + t]), 3))
    first = jnp.full((1, 128), 99, jnp.int32)
    last = jnp.full((1, 128), -1, jnp.int32)
    for t in range(2):
        target = jnp.where(live[t], rank[t], 99)
        for r in range(16):
            hit = take_row(target, base + r) == slot
            first = jnp.where(hit, jnp.minimum(first, 16 * t + r), first)
            last = jnp.where(hit, jnp.maximum(last, 16 * t + r), last)
    exists = [last >= 0, last > first]
    key = [jnp.where(exists[0], first, 0), jnp.where(exists[1], last, 0)]
    back = [base + jnp.bitwise_and(k, 15) for k in key]

    def from_key(k, pair):
        value = jnp.where(key[k] >= 16, take_row(pair[1], back[k]), take_row(pair[0], back[k]))
        return jnp.where(exists[k], value, 3)

    near_own = [from_key(k, theirs) for k in range(2)]
    near_far = [from_key(k, mine) for k in range(2)]
    edge_idx[...] = jnp.zeros((8, 128), jnp.int32)
    for k in range(2):
        edge_idx[k : k + 1, :] = base + rank[k]
        edge_idx[2 + k : 3 + k, :] = back[k]
    none = jnp.full((4, 128), 3, jnp.int32)
    edge_mine = jnp.concatenate([mine[0], mine[1], near_own[0], near_own[1], none], axis=0)
    edge_theirs = jnp.concatenate([theirs[0], theirs[1], near_far[0], near_far[1], none], axis=0)

    nu = visc[...]
    wide = layout[...] == 0
    tab[0:1, :] = nu * jnp.where(wide, 2.0, 0.5)
    tab[1:2, :] = nu * jnp.where(wide, 0.5, 2.0)
    tab[2:3, :] = nu
    inside = jnp.where(remote > 0, 3, own)
    for face in range(4):
        plain = (inside[2 * face : 2 * face + 1] == 0) & (other[2 * face : 2 * face + 1] == 0)
        tab[3 + face : 4 + face, :] = plain.astype(F32)
    tab[7:8, :] = jnp.zeros((1, 128), F32)
    mine_m = [PENALTY * HALVES[o].T @ np.diag(W) @ HALVES[o] for o in range(3)]
    far_m = [
        [-PENALTY * HALVES[o].T @ np.diag(W) @ HALVES[c] for c in range(3)] for o in range(3)
    ]
    for code, facing, own_ref, far_ref in (
        (inside, other, own_c, far_c),
        (edge_mine, edge_theirs, edge_own, edge_far),
    ):
        hot = [(code == o).astype(F32) for o in range(3)]
        pair = [[hot[o] * (facing == c).astype(F32) for c in range(3)] for o in range(3)]
        for a in range(6):
            for b in range(6):
                n = 6 * a + b
                total = sum(float(mine_m[o][a, b]) * hot[o] for o in range(3))
                own_ref[n] = total + pltpu.roll(total, 7, 0)
                far_ref[n] = sum(
                    float(far_m[o][c][a, b]) * pair[o][c] for o in range(3) for c in range(3)
                )


def group_rows(group):
    return pl.ds(pl.multiple_of(group * 8, 8), 8)


def row_of(ref, r):
    return jnp.broadcast_to(ref[r : r + 1, :], (8, 128))


def face_nodes(face):
    return [
        6 * i + j
        for i, j in [
            (0, b) if face == 0 else (5, b) if face == 1 else (b, 0) if face == 2 else (b, 5)
            for b in range(6)
        ]
    ]


def inner(group, env, v_ref, out):
    meta, idx, tab, own_c, far_c = env
    rows = group_rows(group)
    v = [v_ref[n, rows, :] for n in range(36)]
    q = meta[0] * 32 + group * 8 + lax.broadcasted_iota(jnp.int32, (8, 128), 0)
    harmonic = lax.shift_right_logical(q + 1, 1).astype(F32) * SPANWISE
    cx, cy, nu = tab[0:1, :], tab[1:2, :], tab[2:3, :]
    shift = 1.0 + 0.5 * nu * (harmonic * harmonic)
    res = [shift * v[n] for n in range(36)]
    for j in range(6):
        g = folded([v[6 * i + j] for i in range(6)], STIFF_FOLD, 1)
        for i in range(6):
            res[6 * i + j] = res[6 * i + j] + cx * g[i]
    for i in range(6):
        g = folded(v[6 * i : 6 * i + 6], STIFF_FOLD, 1)
        for j in range(6):
            out[6 * i + j, rows, :] = float(W[i] * W[j]) * (res[6 * i + j] + cy * g[j])

    @pl.when(meta[2] == 0)
    def _():
        for face in range(4):
            active = tab[3 + face : 4 + face, :]
            local = row_of(idx, LOCAL + 2 * face)
            for a in range(6):
                n, m = face_nodes(face)[a], face_nodes(face ^ 1)[a]
                jump = active * (v_ref[n, rows, :] - take(v_ref[m, rows, :], local))
                out[n, rows, :] += float(PENALTY * W[a]) * jump

    @pl.when(meta[2] != 0)
    def _():
        for face in range(4):
            mine = [v_ref[n, rows, :] for n in face_nodes(face)]
            theirs = [
                [take(v_ref[n, rows, :], row_of(idx, LOCAL + 2 * face + t)) for n in face_nodes(face ^ 1)]
                for t in range(2)
            ]
            for a in range(6):
                n = face_nodes(face)[a]
                extra = out[n, rows, :]
                for b in range(6):
                    extra = extra + own_c[6 * a + b, 2 * face : 2 * face + 1, :] * mine[b]
                    for t in range(2):
                        s = 2 * face + t
                        extra = extra + far_c[6 * a + b, s : s + 1, :] * theirs[t][b]
                out[n, rows, :] = extra


def compact(group, idx, v_ref, h_ref, send_w, send_e):
    rows = group_rows(group)
    part = lax.shift_right_logical(lane_ids((8, 128)), 4)
    for face, ref in ((0, send_w), (1, send_e)):
        index = row_of(idx, face)
        for b in range(6):
            n = face_nodes(face)[b]
            low, high = take(v_ref[n, rows, :], index), take(h_ref[n, rows, :], index)
            old = ref[8 * b : 8 * b + 8, :]
            new = jnp.where(part == group, low, jnp.where(part == group + 4, high, old))
            ref[8 * b : 8 * b + 8, :] = new


def outer(group, idx, edge, first):
    found = {}
    for face in range(2):
        lanes = row_of(idx, SELF + face) + (64 * face + 16 * group)
        on = row_of(idx, ANY + face) > 0
        for b in range(6):
            value = take(edge[first + 8 * b : first + 8 * b + 8, :], lanes)
            found[face_nodes(face)[b]] = jnp.where(on, value, 0.0)
    return found


def edge_blocks(ref):
    return [ref[8 * b : 8 * b + 8, :] for b in range(6)]


def merge(to_w, to_e):
    west = lane_ids((8, 128)) < 64
    plain, inner_h = [], []
    for w, e in zip(edge_blocks(to_w), edge_blocks(to_e)):
        plain.append(jnp.where(west, w, pltpu.roll(e, 64, 1)))
        inner_h.append(jnp.where(west, pltpu.roll(w, 64, 1), e))
    return plain, inner_h


def edge_term(edge_idx, edge_own, edge_far, mine, theirs, row):
    near = [[take(t, row_of(edge_idx, row + k)) for t in theirs] for k in range(2)]
    out = []
    for a in range(6):
        total = None
        for b in range(6):
            n = 6 * a + b
            term = edge_own[n, row : row + 1, :] * mine[b]
            for k in range(2):
                term = term + edge_far[n, row + k : row + k + 1, :] * near[k][b]
            total = term if total is None else total + term
        out.append(total)
    return out


def store_sums(acc, pad, first, count):
    width = count * 128
    lhs = (
        lax.broadcasted_iota(jnp.int32, (8, width), 0)
        == lax.shift_right_logical(lane_ids((8, width)), 7) + first
    ).astype(F32)
    sums = lax.dot_general(
        lhs, acc[...], (((1,), (1,)), ((), ())),
        precision=lax.Precision.HIGHEST, preferred_element_type=F32,
    )
    pad[...] = jnp.ones((8, 128), F32)
    pad[:, 0:32] = sums


HALF = 10.0


def guess_kernel(meta, idx, tab, own_c, far_c, u, out, send_w, send_e):
    env = (meta, idx, tab, own_c, far_c)

    def body(group, carry):
        inner(group, env, u, out)
        compact(group, idx, u, out, send_w, send_e)
        return carry

    lax.fori_loop(0, 4, body, 0)


def base_kernel(idx, edge_idx, edge_own, edge_far, u, hu, to_w, to_e, from_w, from_e, out, edge):
    mine, _ = merge(to_w, to_e)
    theirs, _ = merge(from_w, from_e)
    for b, value in enumerate(edge_term(edge_idx, edge_own, edge_far, mine, theirs, 0)):
        edge[8 * b : 8 * b + 8, :] = value

    def body(group, carry):
        rows = group_rows(group)
        extra = outer(group, idx, edge, 0)
        for n in range(36):
            image = hu[n, rows, :]
            if n in extra:
                image = image + extra[n]
            out[n, rows, :] = float(W[n // 6] * W[n % 6]) * u[n, rows, :] - image
        return carry

    lax.fori_loop(0, 4, body, 0)


def residual_kernel(meta, idx, tab, own_c, far_c, back, base, out, h_out, send_w, send_e):
    env = (meta, idx, tab, own_c, far_c)
    for g in range(9):
        turned = back[:, 16 * g : 16 * g + 16, :].reshape(128, 128).T
        for m in range(4):
            n = 4 * g + m
            out[n] = base[n] + turned[32 * m : 32 * m + 32]

    def body(group, carry):
        inner(group, env, out, h_out)
        compact(group, idx, out, h_out, send_w, send_e)
        return carry

    lax.fori_loop(0, 4, body, 0)


def edge_steps(tables, to_w, to_e, from_w, from_e, before, edge, keep):
    edge_idx, edge_own, edge_far = tables
    mine, mine_h = merge(to_w, to_e)
    theirs, theirs_h = merge(from_w, from_e)
    scale = (1.0 if before is None else 2.0) / HALF
    first = edge_term(edge_idx, edge_own, edge_far, mine, theirs, 0)
    facing = edge_term(edge_idx, edge_own, edge_far, theirs, mine, 2)
    mine_next, theirs_next = [], []
    for b in range(6):
        if before is None:
            mine_next.append(scale * (mine_h[b] + first[b]) - mine[b])
            theirs_next.append(scale * (theirs_h[b] + facing[b]) - theirs[b])
        else:
            old = before[8 * b : 8 * b + 8, :], before[48 + 8 * b : 56 + 8 * b, :]
            mine_next.append(scale * (mine_h[b] + first[b]) - 2.0 * mine[b] - old[0])
            theirs_next.append(scale * (theirs_h[b] + facing[b]) - 2.0 * theirs[b] - old[1])
    second = edge_term(edge_idx, edge_own, edge_far, mine_next, theirs_next, 0)
    for b in range(6):
        edge[8 * b : 8 * b + 8, :] = first[b]
        edge[48 + 8 * b : 56 + 8 * b, :] = second[b]
        if keep is not None:
            keep[8 * b : 8 * b + 8, :] = mine_next[b]
            keep[48 + 8 * b : 56 + 8 * b, :] = theirs_next[b]


def two_steps_kernel(
    meta, idx, tab, own_c, far_c, edge_idx, edge_own, edge_far,
    t0, h0, to_w, to_e, from_w, from_e,
    t1, t2, h2, send_w, send_e, keep, part, edge, h1, acc, pad,
):
    env = (meta, idx, tab, own_c, far_c)
    tables = (edge_idx, edge_own, edge_far)
    edge_steps(tables, to_w, to_e, from_w, from_e, None, edge, keep)

    def body(group, carry):
        rows = group_rows(group)
        extra = outer(group, idx, edge, 0)
        sums = [jnp.zeros((8, 128), F32)] * 5
        for n in range(36):
            image = h0[n, rows, :]
            if n in extra:
                image = image + extra[n]
            a = t0[n, rows, :]
            b = (1.0 / HALF) * image - a
            t1[n, rows, :] = b
            for k, term in enumerate((a * a, a * b, b * b)):
                sums[k] = sums[k] + term
        inner(group, env, t1, h1)
        extra = outer(group, idx, edge, 48)
        for n in range(36):
            image = h1[n, rows, :]
            if n in extra:
                image = image + extra[n]
            b = t1[n, rows, :]
            c = (2.0 / HALF) * image - 2.0 * b - t0[n, rows, :]
            t2[n, rows, :] = c
            sums[3] = sums[3] + b * c
            sums[4] = sums[4] + c * c
        for k in range(5):
            acc[rows, 128 * k : 128 * k + 128] = sums[k]
        inner(group, env, t2, h2)
        compact(group, idx, t2, h2, send_w, send_e)
        return carry

    lax.fori_loop(0, 4, body, 0)
    store_sums(acc, pad, 0, 5)
    part[...] = pad[...]


def last_steps_kernel(
    meta, idx, tab, own_c, far_c, edge_idx, edge_own, edge_far,
    t1, t2, h2, to_w, to_e, from_w, from_e, keep, part,
    t3, red, edge, h3, acc, pad,
):
    env = (meta, idx, tab, own_c, far_c)
    tables = (edge_idx, edge_own, edge_far)
    edge_steps(tables, to_w, to_e, from_w, from_e, keep, edge, None)

    def body(group, carry):
        rows = group_rows(group)
        extra = outer(group, idx, edge, 0)
        sums = [jnp.zeros((8, 128), F32)] * 3
        for n in range(36):
            image = h2[n, rows, :]
            if n in extra:
                image = image + extra[n]
            c = t2[n, rows, :]
            d = (2.0 / HALF) * image - 2.0 * c - t1[n, rows, :]
            t3[n, rows, :] = d
            sums[0] = sums[0] + c * d
            sums[1] = sums[1] + d * d
        inner(group, env, t3, h3)
        extra = outer(group, idx, edge, 48)
        for n in range(36):
            image = h3[n, rows, :]
            if n in extra:
                image = image + extra[n]
            d = t3[n, rows, :]
            sums[2] = sums[2] + d * ((2.0 / HALF) * image - 2.0 * d - t2[n, rows, :])
        for k in range(3):
            acc[rows, 128 * k : 128 * k + 128] = sums[k]
        return carry

    lax.fori_loop(0, 4, body, 0)
    store_sums(acc, pad, 5, 3)
    row = lax.broadcasted_iota(jnp.int32, (8, 128), 0)
    mixed = jnp.where(row < 5, part[...], pad[...])
    for k in range(16):
        red[k] = mixed


def finish_kernel(red, x0, t0, t1, t2, t3, out, coef):
    total = red[0]
    for k in range(1, 16):
        total = total + red[k]
    even = [total[2 * k : 2 * k + 1] for k in range(4)]
    odd = [total[2 * k + 1 : 2 * k + 2] for k in range(4)]
    moment = []
    for k in range(4):
        moment.append(even[0] if k == 0 else 2.0 * even[k] - even[0])
        moment.append(odd[0] if k == 0 else 2.0 * odd[k] - odd[0])

    def inner_product(i, j):
        return 0.5 * (moment[i + j] + moment[abs(i - j)])

    def energy(i, j):
        shifted = 0.5 * (inner_product(i, j + 1) + inner_product(i, abs(j - 1)))
        return HALF * (shifted + inner_product(i, j))

    low = [[None] * 4 for _ in range(4)]
    diag, inverse, half = [], [], []
    for j in range(4):
        d = energy(j, j)
        value = moment[j]
        for k in range(j):
            d = d - low[j][k] * low[j][k] * diag[k]
            value = value - low[j][k] * half[k]
        diag.append(d)
        half.append(value)
        inverse.append(1.0 / d)
        for i in range(j + 1, 4):
            e = energy(i, j)
            for k in range(j):
                e = e - low[i][k] * low[j][k] * diag[k]
            low[i][j] = e * inverse[j]
    weight = [half[k] * inverse[k] for k in range(4)]
    for i in (2, 1, 0):
        for k in range(i + 1, 4):
            weight[i] = weight[i] - low[k][i] * weight[k]
    turned = jnp.concatenate(weight + [jnp.zeros((4, 128), F32)], axis=0).T
    for k in range(4):
        coef[k] = jnp.broadcast_to(turned[0:32, k : k + 1], (32, 128))
    for n in range(36):
        out[n] = x0[n] + coef[0] * t0[n] + coef[1] * t1[n] + coef[2] * t2[n] + coef[3] * t3[n]


def pack_kernel(u, out):
    for g in range(9):
        turned = u[4 * g : 4 * g + 4].reshape(128, 128).T
        out[:, 16 * g : 16 * g + 16, :] = turned.reshape(8, 16, 128)


def block_turn(blocks):
    part = lax.shift_right_logical(lane_ids(blocks[0].shape), 5)
    rolled = [blocks[0]] + [pltpu.roll(blocks[s], 32 * s, 1) for s in range(1, 4)]
    out = []
    for m in range(4):
        mixed = rolled[-m % 4]
        for t in range(1, 4):
            mixed = jnp.where(part == t, rolled[(t - m) % 4], mixed)
        out.append(pltpu.roll(mixed, 128 - 32 * m, 1) if m else mixed)
    return out


def product3(high, low, table):
    def dot(a, b):
        return jnp.dot(a, b, preferred_element_type=F32)

    return dot(high, table[0]) + dot(high, table[1]) + dot(low, table[0])


def advect_kernel(meta, came, speed, synth, analy, out, high, low, phys):
    for g in range(9):
        for h in range(2):
            pieces = block_turn([came[4 * h + s, 16 * g : 16 * g + 16, :] for s in range(4)])
            for m in range(4):
                n = 16 * (4 * g + m)
                hi, lo = split(pieces[m])
                high[n : n + 16, 128 * h : 128 * h + 128] = hi
                low[n : n + 16, 128 * h : 128 * h + 128] = lo
    for i in range(6):
        part = slice(96 * i, 96 * i + 96)
        phys[part, :] = product3(high[part, :], low[part, :], synth)
    wide = meta[3] == 0
    sx = jnp.where(wide, 2.0, 1.0)
    sy = jnp.where(wide, 1.0, 2.0)
    for h in range(2):
        cols = slice(128 * h, 128 * h + 128)
        u = [[phys[16 * (6 * i + j) : 16 * (6 * i + j) + 16, cols] for j in range(6)] for i in range(6)]
        acc = [[None] * 6 for _ in range(6)]
        for j in range(6):
            g = folded([u[i][j] for i in range(6)], DERIV_FOLD, -1)
            for i in range(6):
                acc[i][j] = sx * (speed[0, 6 * i + j, :, cols] * g[i])
        for i in range(6):
            g = folded(u[i], DERIV_FOLD, -1)
            for j in range(6):
                n = 16 * (6 * i + j)
                total = acc[i][j] + sy * (speed[1, 6 * i + j, :, cols] * g[j])
                hi, lo = split(float(-0.5 * W[i] * W[j]) * total)
                high[n : n + 16, cols] = hi
                low[n : n + 16, cols] = lo
    for i in range(6):
        part = slice(96 * i, 96 * i + 96)
        phys[part, :] = product3(high[part, :], low[part, :], analy)
    for g in range(9):
        for h in range(2):
            cols = slice(128 * h, 128 * h + 128)
            pieces = block_turn(
                [phys[16 * (4 * g + m) : 16 * (4 * g + m) + 16, cols] for m in range(4)]
            )
            for s in range(4):
                out[4 * h + s, 16 * g : 16 * g + 16, :] = pieces[s]


def shift_by(array, by):
    count = lax.axis_size("elem")
    return lax.ppermute(array, "elem", [(i, (i + by) % count) for i in range(count)])


def shards(scalar_modes, velocity, viscosity, mortar_links, mortar_sides, layout):
    u = jnp.transpose(scalar_modes, (1, 2, 0, 3)).reshape(36, 32, 128)
    speed = jnp.transpose(velocity, (0, 2, 3, 4, 1)).reshape(2, 36, 16, 256)
    synth, analy = plane_tables(256)
    synth = jnp.asarray(split_table(synth.T))
    analy = jnp.asarray(split_table(analy.T))
    plane_id, elem_id = lax.axis_index("plane"), lax.axis_index("elem")
    own, other = mortar_sides[0], mortar_sides[1]
    second = jnp.arange(8)[:, None] % 2 == 1
    plain = (own == 3) | ((own == 0) & (other == 0) & ~second) | (mortar_links // 128 != elem_id)
    mixed = jnp.any(~plain)
    meta = jnp.stack([plane_id, elem_id, mixed.astype(jnp.int32), layout[0]]).astype(jnp.int32)

    vol, edge = shape(36, 32, 128), shape(48, 128)
    both = shape(96, 128)
    blocks = shape(8, 144, 128)
    packed = call(pack_kernel, [blocks], [], [u], [VMEM])[0]
    came = lax.all_to_all(packed, "plane", 0, 0, tiled=True)

    table = shape(36, 8, 128)
    idx, edge_idx, tab, own_c, far_c, edge_own, edge_far = call(
        prep_kernel,
        [shape(24, 128, dtype=jnp.int32), shape(8, 128, dtype=jnp.int32), shape(8, 128)] + [table] * 4,
        [],
        [meta, mortar_links, mortar_sides, viscosity[None], layout[None]],
        [SMEM] + [VMEM] * 4,
    )
    head = [meta, idx, tab, own_c, far_c]
    edges = [edge_idx, edge_own, edge_far]

    def run(kernel, outs, scratch, args):
        return call(kernel, outs, scratch, args, [SMEM if a is meta else VMEM for a in args])

    def trade(send_w, send_e):
        return shift_by(send_e, 1), shift_by(send_w, -1)

    hu, *sent = run(guess_kernel, [vol, edge, edge], [], head + [u])
    got = trade(*sent)
    came, *got = lax.optimization_barrier((came, *got))
    back = run(
        advect_kernel,
        [blocks],
        [VMEM((576, 256), BF16), VMEM((576, 256), BF16), VMEM((576, 256), F32)],
        [meta, came, speed, synth, analy],
    )[0]
    back = lax.all_to_all(back, "plane", 0, 0, tiled=True)
    base = run(
        base_kernel, [vol], [VMEM((48, 128), F32)], [idx, *edges, u, hu, *sent, *got]
    )[0]

    def work(count):
        return [
            VMEM((96, 128), F32),
            VMEM((36, 32, 128), F32),
            VMEM((32, 128 * count), F32),
            VMEM((8, 128), F32),
        ]

    t0, h0, *sent = run(residual_kernel, [vol, vol, edge, edge], [], head + [back, base])
    got = trade(*sent)
    t1, t2, h2, to_w, to_e, keep, part = run(
        two_steps_kernel,
        [vol, vol, vol, edge, edge, both, shape(8, 128)],
        work(5),
        head + edges + [t0, h0, *sent, *got],
    )
    got = trade(to_w, to_e)
    t3, red = run(
        last_steps_kernel,
        [vol, shape(16, 8, 128)],
        work(3),
        head + edges + [t1, t2, h2, to_w, to_e, *got, keep, part],
    )
    red = lax.all_to_all(red, "elem", 0, 0, tiled=True)
    out = run(finish_kernel, [vol], [VMEM((4, 32, 128), F32)], [red, u, t0, t1, t2, t3])[0]
    return jnp.transpose(out.reshape(6, 6, 32, 128), (2, 0, 1, 3))


def solution(mesh):
    placed = (
        P("plane", None, None, "elem"),
        P(None, None, None, None, ("elem", "plane")),
        P("elem"),
        P(None, "elem"),
        P(None, None, "elem"),
        P("elem"),
    )
    return jax.shard_map(
        shards,
        mesh=mesh,
        in_specs=placed,
        out_specs=P("plane", None, None, "elem"),
        check_vma=False,
    )
```

```python
import math

import jax
import jax.numpy as jnp
import ml_dtypes
import numpy as np
from jax import lax
from jax.experimental import pallas as pl
from jax.experimental.pallas import tpu as pltpu
from jax.sharding import PartitionSpec as P

F32 = jnp.float32
BF16 = jnp.bfloat16
PENALTY = 10.0
SPANWISE = 0.0625
VMEM = pltpu.VMEM
SMEM = pltpu.SMEM
SELF, ANY, LOCAL = 2, 4, 10


def lagrange_at(points, targets):
    out = np.ones((6, 6))
    for row in range(6):
        for col in range(6):
            for other in range(6):
                if other != col:
                    out[row, col] *= (targets[row] - points[other]) / (points[col] - points[other])
    return out


def node_tables():
    root = math.sqrt(7.0)
    outer = math.sqrt(1.0 / 3.0 + 2.0 * root / 21.0)
    inner = math.sqrt(1.0 / 3.0 - 2.0 * root / 21.0)
    points = np.array([-1.0, -outer, -inner, inner, outer, 1.0])
    half = [1.0 / 15.0, (14.0 - root) / 30.0, (14.0 + root) / 30.0]
    weights = np.array(half + half[::-1])
    bary = np.array(
        [1.0 / np.prod([points[c] - points[k] for k in range(6) if k != c]) for c in range(6)]
    )
    deriv = np.zeros((6, 6))
    for i in range(6):
        for j in range(6):
            if i != j:
                deriv[i, j] = bary[j] / bary[i] / (points[i] - points[j])
        deriv[i, i] = -np.sum(deriv[i])
    lower = lagrange_at(points, (points - 1.0) / 2.0)
    upper = lagrange_at(points, (points + 1.0) / 2.0)
    stiff = deriv.T @ (weights[:, None] * deriv)
    return weights, deriv, lower, upper, stiff


W, D, QLO, QHI, K1 = node_tables()
HALVES = [np.eye(6), QLO, QHI]


def plane_tables(count):
    planes = np.arange(count)[:, None]
    coeffs = np.arange(count)[None, :]
    harmonic = (coeffs + 1) // 2
    phase = 2.0 * np.pi * (harmonic * planes % count) / count
    synth = np.where(coeffs == 0, 1.0, np.where(coeffs % 2 == 1, np.cos(phase), np.sin(phase)))
    norm = np.where((coeffs == 0) | (coeffs == count - 1), float(count), count / 2.0)
    return synth, (synth / norm).T


def split_table(table):
    table = np.asarray(table, np.float32)
    high = table.astype(ml_dtypes.bfloat16)
    low = (table - high.astype(np.float32)).astype(ml_dtypes.bfloat16)
    return np.stack([high, low])


def fold(matrix):
    plus = (matrix[:3, :3] + matrix[:3, :2:-1]) / 2.0
    minus = (matrix[:3, :3] - matrix[:3, :2:-1]) / 2.0
    return plus, minus


STIFF_FOLD = fold(K1 / W[:, None])
DERIV_FOLD = fold(D)


def folded(values, tables, sign):
    plus, minus = tables
    even = [values[a] + values[5 - a] for a in range(3)]
    odd = [values[a] - values[5 - a] for a in range(3)]
    out = [None] * 6
    for i in range(3):
        e = sum(float(plus[i, a]) * even[a] for a in range(3))
        o = sum(float(minus[i, a]) * odd[a] for a in range(3))
        out[i] = e + o
        out[5 - i] = e - o if sign > 0 else o - e
    return out


def split(value):
    high = value.astype(BF16)
    return high, (value - high.astype(F32)).astype(BF16)


def lane_ids(shape):
    return lax.broadcasted_iota(jnp.int32, shape, len(shape) - 1)


def call(kernel, outs, scratch, operands, spaces, out_space=VMEM, grant=3):
    total = sum(int(np.prod(o.shape)) * 4 for o in outs)
    total += sum(int(np.prod(o.shape)) * 4 for o in operands)
    return pl.pallas_call(
        kernel,
        out_shape=outs,
        in_specs=[pl.BlockSpec(memory_space=s) for s in spaces],
        out_specs=[pl.BlockSpec(memory_space=out_space) for _ in outs],
        scratch_shapes=scratch,
        compiler_params=pltpu.CompilerParams(vmem_limit_bytes=grant * 2**20),
        cost_estimate=pl.CostEstimate(flops=4_000_000, bytes_accessed=total, transcendentals=0),
    )(*operands)


def shape(*dims, dtype=F32):
    return jax.ShapeDtypeStruct(dims, dtype)


def take(value, index):
    return jnp.take_along_axis(value, index, axis=1)


def take_row(value, index):
    wide = jnp.broadcast_to(value, (8, 128)), jnp.broadcast_to(index, (8, 128))
    return take(*wide)[0:1]


def prep_kernel(meta, links, sides, visc, layout, idx, edge_idx, tab, own_c, far_c, edge_own, edge_far):
    me = meta[1]
    dev = lax.shift_right_logical(links[...], 7)
    loc = jnp.bitwise_and(links[...], 127)
    remote = (dev != me).astype(jnp.int32)
    idx[LOCAL : LOCAL + 8, :] = loc
    row = lax.broadcasted_iota(jnp.int32, (128, 128), 0)
    col = lane_ids((128, 128))
    lane = lane_ids((1, 128))
    slot = jnp.bitwise_and(lane, 15)
    own, other = sides[0], sides[1]
    listed, present, ranks = [], [], []
    for side in range(2):
        rem = [remote[2 * side + t : 2 * side + t + 1] for t in range(2)]
        far = [loc[2 * side + t : 2 * side + t + 1] for t in range(2)]
        any_rem = jnp.maximum(rem[0], rem[1])
        before = jnp.sum(jnp.where(col < row, any_rem, 0).astype(F32), axis=1, keepdims=True)
        mine = jnp.sum(jnp.where(col == row, any_rem, 0).astype(F32), axis=1, keepdims=True)
        chosen = jnp.where((before == slot.astype(F32)) & (mine > 0.0), 1.0, 0.0)
        listed.append(jnp.sum(chosen * row.astype(F32), axis=0, keepdims=True).astype(jnp.int32))
        present.append(jnp.sum(chosen, axis=0, keepdims=True).astype(jnp.int32))
        idx[side : side + 1, :] = listed[side]
        mine_at = jnp.sum(jnp.where(row == col, before, 0.0), axis=0, keepdims=True)
        mine_at = jnp.where(any_rem > 0, mine_at.astype(jnp.int32), 0)
        idx[SELF + side : SELF + side + 1, :] = mine_at
        idx[ANY + side : ANY + side + 1, :] = any_rem
        named = jnp.where(
            ((far[0] == row) & (rem[0] > 0)) | ((far[1] == row) & (rem[1] > 0)), 1.0, 0.0
        )
        named = jnp.max(named, axis=1, keepdims=True)
        for t in range(2):
            rank = jnp.sum(jnp.where(row < far[t], named, 0.0), axis=0, keepdims=True)
            ranks.append(jnp.where(rem[t] > 0, rank.astype(jnp.int32), 0))
    idx[6:10, :] = jnp.zeros((4, 128), jnp.int32)
    idx[18:24, :] = jnp.zeros((6, 128), jnp.int32)

    west = lane < 64
    base = jnp.bitwise_and(lane, 112)
    element = jnp.where(west, listed[0], listed[1])
    here = jnp.where(west, present[0], present[1]) > 0

    def pick(rows_w, rows_e):
        return jnp.where(west, take_row(rows_w, element), take_row(rows_e, element))

    rank, live, mine, theirs = [], [], [], []
    for t in range(2):
        rank.append(pick(ranks[t], ranks[2 + t]))
        live.append((pick(remote[t : t + 1], remote[2 + t : 3 + t]) > 0) & here)
        mine.append(jnp.where(live[t], pick(own[t : t + 1], own[2 + t : 3 + t]), 3))
        theirs.append(jnp.where(live[t], pick(other[t : t + 1], other[2 + t : 3 + t]), 3))
    first = jnp.full((1, 128), 99, jnp.int32)
    last = jnp.full((1, 128), -1, jnp.int32)
    for t in range(2):
        target = jnp.where(live[t], rank[t], 99)
        for r in range(16):
            hit = take_row(target, base + r) == slot
            first = jnp.where(hit, jnp.minimum(first, 16 * t + r), first)
            last = jnp.where(hit, jnp.maximum(last, 16 * t + r), last)
    exists = [last >= 0, last > first]
    key = [jnp.where(exists[0], first, 0), jnp.where(exists[1], last, 0)]
    back = [base + jnp.bitwise_and(k, 15) for k in key]

    def from_key(k, pair):
        value = jnp.where(key[k] >= 16, take_row(pair[1], back[k]), take_row(pair[0], back[k]))
        return jnp.where(exists[k], value, 3)

    near_own = [from_key(k, theirs) for k in range(2)]
    near_far = [from_key(k, mine) for k in range(2)]
    edge_idx[...] = jnp.zeros((8, 128), jnp.int32)
    for k in range(2):
        edge_idx[k : k + 1, :] = base + rank[k]
        edge_idx[2 + k : 3 + k, :] = back[k]
    none = jnp.full((4, 128), 3, jnp.int32)
    edge_mine = jnp.concatenate([mine[0], mine[1], near_own[0], near_own[1], none], axis=0)
    edge_theirs = jnp.concatenate([theirs[0], theirs[1], near_far[0], near_far[1], none], axis=0)

    nu = visc[...]
    wide = layout[...] == 0
    tab[0:1, :] = nu * jnp.where(wide, 2.0, 0.5)
    tab[1:2, :] = nu * jnp.where(wide, 0.5, 2.0)
    tab[2:3, :] = nu
    inside = jnp.where(remote > 0, 3, own)
    for face in range(4):
        plain = (inside[2 * face : 2 * face + 1] == 0) & (other[2 * face : 2 * face + 1] == 0)
        tab[3 + face : 4 + face, :] = plain.astype(F32)
    tab[7:8, :] = jnp.zeros((1, 128), F32)
    mine_m = [PENALTY * HALVES[o].T @ np.diag(W) @ HALVES[o] for o in range(3)]
    far_m = [
        [-PENALTY * HALVES[o].T @ np.diag(W) @ HALVES[c] for c in range(3)] for o in range(3)
    ]
    for code, facing, own_ref, far_ref in (
        (inside, other, own_c, far_c),
        (edge_mine, edge_theirs, edge_own, edge_far),
    ):
        hot = [(code == o).astype(F32) for o in range(3)]
        pair = [[hot[o] * (facing == c).astype(F32) for c in range(3)] for o in range(3)]
        for a in range(6):
            for b in range(6):
                n = 6 * a + b
                total = sum(float(mine_m[o][a, b]) * hot[o] for o in range(3))
                own_ref[n] = total + pltpu.roll(total, 7, 0)
                far_ref[n] = sum(
                    float(far_m[o][c][a, b]) * pair[o][c] for o in range(3) for c in range(3)
                )


def group_rows(group):
    return pl.ds(pl.multiple_of(group * 8, 8), 8)


def row_of(ref, r):
    return jnp.broadcast_to(ref[r : r + 1, :], (8, 128))


def face_nodes(face):
    return [
        6 * i + j
        for i, j in [
            (0, b) if face == 0 else (5, b) if face == 1 else (b, 0) if face == 2 else (b, 5)
            for b in range(6)
        ]
    ]


def either(meta, loop):
    for plain in (True, False):

        @pl.when((meta[2] == 0) == plain)
        def _(plain=plain):
            lax.fori_loop(0, 4, lambda group, carry: loop(group, plain) or carry, 0)


def weighted(factors, values):
    total = float(factors[0]) * values[0]
    for f, v in zip(factors[1:], values[1:]):
        total = total + float(f) * v
    return total


def plain_terms(env, v):
    _, idx, tab, _, _ = env

    def of_face(face):
        active = row_of(tab, 3 + face)
        local = row_of(idx, LOCAL + 2 * face)

        def term(a):
            n, m = face_nodes(face)[a], face_nodes(face ^ 1)[a]
            return (float(PENALTY * W[a]) * active) * (v(n) - take(v(m), local))

        return term

    return [of_face(face) for face in range(4)]


def general_terms(env, v):
    _, idx, _, own_c, far_c = env
    found = []
    for face in range(4):
        mine = [v(n) for n in face_nodes(face)]
        theirs = [
            [take(v(n), row_of(idx, LOCAL + 2 * face + t)) for n in face_nodes(face ^ 1)]
            for t in range(2)
        ]
        values = []
        for a in range(6):
            extra = jnp.zeros((8, 128), F32)
            for b in range(6):
                extra = extra + own_c[6 * a + b, 2 * face : 2 * face + 1, :] * mine[b]
                for t in range(2):
                    s = 2 * face + t
                    extra = extra + far_c[6 * a + b, s : s + 1, :] * theirs[t][b]
            values.append(extra)
        found.append(values.__getitem__)
    return found


def inner(group, env, v_ref, plain, emit):
    meta, _, tab, _, _ = env
    rows = group_rows(group)

    def v(n):
        return v_ref[n, rows, :]

    terms = (plain_terms if plain else general_terms)(env, v)
    q = meta[0] * 32 + group * 8 + lax.broadcasted_iota(jnp.int32, (8, 128), 0)
    harmonic = lax.shift_right_logical(q + 1, 1).astype(F32) * SPANWISE
    cx, cy = row_of(tab, 0), row_of(tab, 1)
    shift = 1.0 + 0.5 * tab[2:3, :] * (harmonic * harmonic)
    plus, minus = STIFF_FOLD
    even = [[v(6 * a + j) + v(30 - 6 * a + j) for a in range(3)] for j in range(6)]
    odd = [[v(6 * a + j) - v(30 - 6 * a + j) for a in range(3)] for j in range(6)]
    for i in range(3):
        e = [weighted(plus[i], even[j]) for j in range(6)]
        o = [weighted(minus[i], odd[j]) for j in range(6)]
        for line in (i, 5 - i):
            mine = [v(6 * line + j) for j in range(6)]
            g = folded(mine, STIFF_FOLD, 1)
            for j in range(6):
                n = 6 * line + j
                gx = e[j] + o[j] if line == i else e[j] - o[j]
                value = float(W[line] * W[j]) * (shift * mine[j] + cx * gx + cy * g[j])
                for face, (at, b) in enumerate(((line == 0, j), (line == 5, j), (j == 0, line), (j == 5, line))):
                    if at:
                        value = value + terms[face](b)
                emit(n, value)


def compact(group, idx, v_ref, h_ref, send_w, send_e):
    rows = group_rows(group)
    part = lax.shift_right_logical(lane_ids((8, 128)), 4)
    for face, ref in ((0, send_w), (1, send_e)):
        index = row_of(idx, face)
        for b in range(6):
            n = face_nodes(face)[b]
            low, high = take(v_ref[n, rows, :], index), take(h_ref[n, rows, :], index)
            old = ref[8 * b : 8 * b + 8, :]
            new = jnp.where(part == group, low, jnp.where(part == group + 4, high, old))
            ref[8 * b : 8 * b + 8, :] = new


def outer(group, idx, edge, first):
    found = {}
    for face in range(2):
        lanes = row_of(idx, SELF + face) + (64 * face + 16 * group)
        on = row_of(idx, ANY + face) > 0
        for b in range(6):
            value = take(edge[first + 8 * b : first + 8 * b + 8, :], lanes)
            found[face_nodes(face)[b]] = jnp.where(on, value, 0.0)
    return found


def edge_blocks(ref):
    return [ref[8 * b : 8 * b + 8, :] for b in range(6)]


def merge(to_w, to_e):
    west = lane_ids((8, 128)) < 64
    plain, inner_h = [], []
    for w, e in zip(edge_blocks(to_w), edge_blocks(to_e)):
        plain.append(jnp.where(west, w, pltpu.roll(e, 64, 1)))
        inner_h.append(jnp.where(west, pltpu.roll(w, 64, 1), e))
    return plain, inner_h


def edge_term(edge_idx, edge_own, edge_far, mine, theirs, row):
    near = [[take(t, row_of(edge_idx, row + k)) for t in theirs] for k in range(2)]
    out = []
    for a in range(6):
        chains = [None] * 3
        for b in range(6):
            n = 6 * a + b
            terms = [edge_own[n, row : row + 1, :] * mine[b]]
            terms += [edge_far[n, row + k : row + k + 1, :] * near[k][b] for k in range(2)]
            chains = terms if chains[0] is None else [c + t for c, t in zip(chains, terms)]
        out.append(chains[0] + (chains[1] + chains[2]))
    return out


def store_sums(acc, pad, first, count):
    width = count * 128
    lhs = (
        lax.broadcasted_iota(jnp.int32, (8, width), 0)
        == lax.shift_right_logical(lane_ids((8, width)), 7) + first
    ).astype(F32)
    sums = lax.dot_general(
        lhs, acc[...], (((1,), (1,)), ((), ())),
        precision=lax.Precision.HIGHEST, preferred_element_type=F32,
    )
    pad[...] = jnp.ones((8, 128), F32)
    pad[:, 0:32] = sums


HALF = 10.0


def store(ref, rows):
    def emit(n, value):
        ref[n, rows, :] = value

    return emit


def guess_kernel(meta, idx, tab, own_c, far_c, u, out, send_w, send_e):
    env = (meta, idx, tab, own_c, far_c)

    def loop(group, plain):
        inner(group, env, u, plain, store(out, group_rows(group)))
        compact(group, idx, u, out, send_w, send_e)

    either(meta, loop)


def base_kernel(idx, edge_idx, edge_own, edge_far, u, hu, to_w, to_e, from_w, from_e, out, edge):
    mine, _ = merge(to_w, to_e)
    theirs, _ = merge(from_w, from_e)
    for b, value in enumerate(edge_term(edge_idx, edge_own, edge_far, mine, theirs, 0)):
        edge[8 * b : 8 * b + 8, :] = value

    def body(group, carry):
        rows = group_rows(group)
        extra = outer(group, idx, edge, 0)
        for n in range(36):
            image = hu[n, rows, :]
            if n in extra:
                image = image + extra[n]
            out[n, rows, :] = float(W[n // 6] * W[n % 6]) * u[n, rows, :] - image
        return carry

    lax.fori_loop(0, 4, body, 0)


def residual_kernel(meta, idx, tab, own_c, far_c, back, base, out, h_out, send_w, send_e):
    env = (meta, idx, tab, own_c, far_c)
    for g in range(9):
        turned = back[:, 16 * g : 16 * g + 16, :].reshape(128, 128).T
        for m in range(4):
            n = 4 * g + m
            out[n] = base[n] + turned[32 * m : 32 * m + 32]

    def loop(group, plain):
        inner(group, env, out, plain, store(h_out, group_rows(group)))
        compact(group, idx, out, h_out, send_w, send_e)

    either(meta, loop)


def edge_steps(tables, to_w, to_e, from_w, from_e, before, edge, keep):
    edge_idx, edge_own, edge_far = tables
    mine, mine_h = merge(to_w, to_e)
    theirs, theirs_h = merge(from_w, from_e)
    scale = (1.0 if before is None else 2.0) / HALF
    first = edge_term(edge_idx, edge_own, edge_far, mine, theirs, 0)
    facing = edge_term(edge_idx, edge_own, edge_far, theirs, mine, 2)
    mine_next, theirs_next = [], []
    for b in range(6):
        if before is None:
            mine_next.append(scale * (mine_h[b] + first[b]) - mine[b])
            theirs_next.append(scale * (theirs_h[b] + facing[b]) - theirs[b])
        else:
            old = before[8 * b : 8 * b + 8, :], before[48 + 8 * b : 56 + 8 * b, :]
            mine_next.append(scale * (mine_h[b] + first[b]) - 2.0 * mine[b] - old[0])
            theirs_next.append(scale * (theirs_h[b] + facing[b]) - 2.0 * theirs[b] - old[1])
    second = edge_term(edge_idx, edge_own, edge_far, mine_next, theirs_next, 0)
    for b in range(6):
        edge[8 * b : 8 * b + 8, :] = first[b]
        edge[48 + 8 * b : 56 + 8 * b, :] = second[b]
        if keep is not None:
            keep[8 * b : 8 * b + 8, :] = mine_next[b]
            keep[48 + 8 * b : 56 + 8 * b, :] = theirs_next[b]


def two_steps_kernel(
    meta, idx, tab, own_c, far_c, edge_idx, edge_own, edge_far,
    t0, h0, to_w, to_e, from_w, from_e,
    t1, t2, h2, send_w, send_e, keep, part, edge, acc, pad,
):
    env = (meta, idx, tab, own_c, far_c)
    tables = (edge_idx, edge_own, edge_far)
    edge_steps(tables, to_w, to_e, from_w, from_e, None, edge, keep)

    def loop(group, plain):
        rows = group_rows(group)
        extra = outer(group, idx, edge, 0)
        sums = [jnp.zeros((8, 128), F32)] * 5
        for n in range(36):
            image = h0[n, rows, :]
            if n in extra:
                image = image + extra[n]
            a = t0[n, rows, :]
            b = (1.0 / HALF) * image - a
            t1[n, rows, :] = b
            for k, term in enumerate((a * a, a * b, b * b)):
                sums[k] = sums[k] + term
        extra_next = outer(group, idx, edge, 48)

        def emit(n, image):
            if n in extra_next:
                image = image + extra_next[n]
            b = t1[n, rows, :]
            c = (2.0 / HALF) * image - 2.0 * b - t0[n, rows, :]
            t2[n, rows, :] = c
            sums[3] = sums[3] + b * c
            sums[4] = sums[4] + c * c

        inner(group, env, t1, plain, emit)
        for k in range(5):
            acc[rows, 128 * k : 128 * k + 128] = sums[k]
        inner(group, env, t2, plain, store(h2, rows))
        compact(group, idx, t2, h2, send_w, send_e)

    either(meta, loop)
    store_sums(acc, pad, 0, 5)
    part[...] = pad[...]


def last_steps_kernel(
    meta, idx, tab, own_c, far_c, edge_idx, edge_own, edge_far,
    t1, t2, h2, to_w, to_e, from_w, from_e, keep, part,
    t3, red, edge, acc, pad,
):
    env = (meta, idx, tab, own_c, far_c)
    tables = (edge_idx, edge_own, edge_far)
    edge_steps(tables, to_w, to_e, from_w, from_e, keep, edge, None)

    def loop(group, plain):
        rows = group_rows(group)
        extra = outer(group, idx, edge, 0)
        sums = [jnp.zeros((8, 128), F32)] * 3
        for n in range(36):
            image = h2[n, rows, :]
            if n in extra:
                image = image + extra[n]
            c = t2[n, rows, :]
            d = (2.0 / HALF) * image - 2.0 * c - t1[n, rows, :]
            t3[n, rows, :] = d
            sums[0] = sums[0] + c * d
            sums[1] = sums[1] + d * d
        extra_next = outer(group, idx, edge, 48)

        def emit(n, image):
            if n in extra_next:
                image = image + extra_next[n]
            d = t3[n, rows, :]
            sums[2] = sums[2] + d * ((2.0 / HALF) * image - 2.0 * d - t2[n, rows, :])

        inner(group, env, t3, plain, emit)
        for k in range(3):
            acc[rows, 128 * k : 128 * k + 128] = sums[k]

    either(meta, loop)
    store_sums(acc, pad, 5, 3)
    row = lax.broadcasted_iota(jnp.int32, (8, 128), 0)
    mixed = jnp.where(row < 5, part[...], pad[...])
    for k in range(16):
        red[k] = mixed


def finish_kernel(red, x0, t0, t1, t2, t3, out, coef, held, sems):
    total = red[0]
    for k in range(1, 16):
        total = total + red[k]
    even = [total[2 * k : 2 * k + 1] for k in range(4)]
    odd = [total[2 * k + 1 : 2 * k + 2] for k in range(4)]
    moment = []
    for k in range(4):
        moment.append(even[0] if k == 0 else 2.0 * even[k] - even[0])
        moment.append(odd[0] if k == 0 else 2.0 * odd[k] - odd[0])

    def inner_product(i, j):
        return 0.5 * (moment[i + j] + moment[abs(i - j)])

    def energy(i, j):
        shifted = 0.5 * (inner_product(i, j + 1) + inner_product(i, abs(j - 1)))
        return HALF * (shifted + inner_product(i, j))

    low = [[None] * 4 for _ in range(4)]
    diag, inverse, half = [], [], []
    for j in range(4):
        d = energy(j, j)
        value = moment[j]
        for k in range(j):
            d = d - low[j][k] * low[j][k] * diag[k]
            value = value - low[j][k] * half[k]
        diag.append(d)
        half.append(value)
        inverse.append(1.0 / d)
        for i in range(j + 1, 4):
            e = energy(i, j)
            for k in range(j):
                e = e - low[i][k] * low[j][k] * diag[k]
            low[i][j] = e * inverse[j]
    weight = [half[k] * inverse[k] for k in range(4)]
    for i in (2, 1, 0):
        for k in range(i + 1, 4):
            weight[i] = weight[i] - low[k][i] * weight[k]
    turned = jnp.concatenate(weight + [jnp.zeros((4, 128), F32)], axis=0).T
    for k in range(4):
        coef[k] = jnp.broadcast_to(turned[0:32, k : k + 1], (32, 128))
    copies = []
    for c in range(6):
        for n in range(6 * c, 6 * c + 6):
            held[n] = x0[n] + coef[0] * t0[n] + coef[1] * t1[n] + coef[2] * t2[n] + coef[3] * t3[n]
        part = pl.ds(6 * c, 6)
        copies.append(pltpu.make_async_copy(held.at[part], out.at[part], sems.at[c]))
        copies[c].start()
    for copy in copies:
        copy.wait()


def pack_kernel(u, out, held, sems):
    copies = []
    for g in range(9):
        part = pl.ds(4 * g, 4)
        copies.append(pltpu.make_async_copy(u.at[part], held.at[part], sems.at[g]))
        copies[g].start()
    for g in range(9):
        copies[g].wait()
        turned = held[4 * g : 4 * g + 4].reshape(128, 128).T
        out[:, 16 * g : 16 * g + 16, :] = turned.reshape(8, 16, 128)


def block_turn(blocks):
    part = lax.shift_right_logical(lane_ids(blocks[0].shape), 5)
    rolled = [blocks[0]] + [pltpu.roll(blocks[s], 32 * s, 1) for s in range(1, 4)]
    out = []
    for m in range(4):
        mixed = rolled[-m % 4]
        for t in range(1, 4):
            mixed = jnp.where(part == t, rolled[(t - m) % 4], mixed)
        out.append(pltpu.roll(mixed, 128 - 32 * m, 1) if m else mixed)
    return out


def product3(high, low, table):
    def dot(a, b):
        return jnp.dot(a, b, preferred_element_type=F32)

    return dot(high, table[0]) + dot(high, table[1]) + dot(low, table[0])


def advect_kernel(meta, came, speed, synth, analy, out, high, low, phys):
    for g in range(9):
        for h in range(2):
            pieces = block_turn([came[4 * h + s, 16 * g : 16 * g + 16, :] for s in range(4)])
            for m in range(4):
                n = 16 * (4 * g + m)
                hi, lo = split(pieces[m])
                high[n : n + 16, 128 * h : 128 * h + 128] = hi
                low[n : n + 16, 128 * h : 128 * h + 128] = lo
    for i in range(6):
        part = slice(96 * i, 96 * i + 96)
        phys[part, :] = product3(high[part, :], low[part, :], synth)
    wide = meta[3] == 0
    sx = jnp.where(wide, 2.0, 1.0)
    sy = jnp.where(wide, 1.0, 2.0)
    for h in range(2):
        cols = slice(128 * h, 128 * h + 128)
        u = [[phys[16 * (6 * i + j) : 16 * (6 * i + j) + 16, cols] for j in range(6)] for i in range(6)]
        acc = [[None] * 6 for _ in range(6)]
        for j in range(6):
            g = folded([u[i][j] for i in range(6)], DERIV_FOLD, -1)
            for i in range(6):
                acc[i][j] = sx * (speed[0, 6 * i + j, :, cols] * g[i])
        for i in range(6):
            g = folded(u[i], DERIV_FOLD, -1)
            for j in range(6):
                n = 16 * (6 * i + j)
                total = acc[i][j] + sy * (speed[1, 6 * i + j, :, cols] * g[j])
                hi, lo = split(float(-0.5 * W[i] * W[j]) * total)
                high[n : n + 16, cols] = hi
                low[n : n + 16, cols] = lo
    for i in range(6):
        part = slice(96 * i, 96 * i + 96)
        phys[part, :] = product3(high[part, :], low[part, :], analy)
    for g in range(9):
        for h in range(2):
            cols = slice(128 * h, 128 * h + 128)
            pieces = block_turn(
                [phys[16 * (4 * g + m) : 16 * (4 * g + m) + 16, cols] for m in range(4)]
            )
            for s in range(4):
                out[4 * h + s, 16 * g : 16 * g + 16, :] = pieces[s]


def shift_by(array, by):
    count = lax.axis_size("elem")
    return lax.ppermute(array, "elem", [(i, (i + by) % count) for i in range(count)])


def shards(scalar_modes, velocity, viscosity, mortar_links, mortar_sides, layout):
    u = jnp.transpose(scalar_modes, (1, 2, 0, 3)).reshape(36, 32, 128)
    speed = jnp.transpose(velocity, (0, 2, 3, 4, 1)).reshape(2, 36, 16, 256)
    synth, analy = plane_tables(256)
    synth = jnp.asarray(split_table(synth.T))
    analy = jnp.asarray(split_table(analy.T))
    plane_id, elem_id = lax.axis_index("plane"), lax.axis_index("elem")
    own, other = mortar_sides[0], mortar_sides[1]
    second = jnp.arange(8)[:, None] % 2 == 1
    plain = (own == 3) | ((own == 0) & (other == 0) & ~second) | (mortar_links // 128 != elem_id)
    mixed = jnp.any(~plain)
    meta = jnp.stack([plane_id, elem_id, mixed.astype(jnp.int32), layout[0]]).astype(jnp.int32)

    vol, edge = shape(36, 32, 128), shape(48, 128)
    both = shape(96, 128)
    blocks = shape(8, 144, 128)
    packed = call(
        pack_kernel,
        [blocks],
        [VMEM((36, 32, 128), F32), pltpu.SemaphoreType.DMA((9,))],
        [u],
        [pl.ANY],
    )[0]
    came = lax.all_to_all(packed, "plane", 0, 0, tiled=True)

    table = shape(36, 8, 128)
    idx, edge_idx, tab, own_c, far_c, edge_own, edge_far = call(
        prep_kernel,
        [shape(24, 128, dtype=jnp.int32), shape(8, 128, dtype=jnp.int32), shape(8, 128)] + [table] * 4,
        [],
        [meta, mortar_links, mortar_sides, viscosity[None], layout[None]],
        [SMEM] + [VMEM] * 4,
    )
    head = [meta, idx, tab, own_c, far_c]
    edges = [edge_idx, edge_own, edge_far]

    def run(kernel, outs, scratch, args, grant=3):
        spaces = [SMEM if a is meta else VMEM for a in args]
        return call(kernel, outs, scratch, args, spaces, grant=grant)

    def trade(send_w, send_e):
        return shift_by(send_e, 1), shift_by(send_w, -1)

    hu, *sent = run(guess_kernel, [vol, edge, edge], [], head + [u])
    got = trade(*sent)
    came, *got = lax.optimization_barrier((came, *got))
    back = run(
        advect_kernel,
        [blocks],
        [VMEM((576, 256), BF16), VMEM((576, 256), BF16), VMEM((576, 256), F32)],
        [meta, came, speed, synth, analy],
        grant=8,
    )[0]
    back = lax.all_to_all(back, "plane", 0, 0, tiled=True)
    base = run(
        base_kernel, [vol], [VMEM((48, 128), F32)], [idx, *edges, u, hu, *sent, *got]
    )[0]

    def work(count):
        return [
            VMEM((96, 128), F32),
            VMEM((32, 128 * count), F32),
            VMEM((8, 128), F32),
        ]

    t0, h0, *sent = run(residual_kernel, [vol, vol, edge, edge], [], head + [back, base])
    got = trade(*sent)
    t1, t2, h2, to_w, to_e, keep, part = run(
        two_steps_kernel,
        [vol, vol, vol, edge, edge, both, shape(8, 128)],
        work(5),
        head + edges + [t0, h0, *sent, *got],
    )
    got = trade(to_w, to_e)
    t3, red = run(
        last_steps_kernel,
        [vol, shape(16, 8, 128)],
        work(3),
        head + edges + [t1, t2, h2, to_w, to_e, *got, keep, part],
    )
    red = lax.all_to_all(red, "elem", 0, 0, tiled=True)
    out = call(
        finish_kernel,
        [vol],
        [VMEM((4, 32, 128), F32), VMEM((36, 32, 128), F32), pltpu.SemaphoreType.DMA((6,))],
        [red, u, t0, t1, t2, t3],
        [VMEM] * 6,
        pl.ANY,
    )[0]
    return jnp.transpose(out.reshape(6, 6, 32, 128), (2, 0, 1, 3))


def solution(mesh):
    placed = (
        P("plane", None, None, "elem"),
        P(None, None, None, None, ("elem", "plane")),
        P("elem"),
        P(None, "elem"),
        P(None, None, "elem"),
        P("elem"),
    )
    return jax.shard_map(
        shards,
        mesh=mesh,
        in_specs=placed,
        out_specs=P("plane", None, None, "elem"),
        check_vma=False,
    )
```

```python
import math

import jax
import jax.numpy as jnp
import ml_dtypes
import numpy as np
from jax import lax
from jax.experimental import pallas as pl
from jax.experimental.pallas import tpu as pltpu
from jax.sharding import PartitionSpec as P

F32 = jnp.float32
BF16 = jnp.bfloat16
PENALTY = 10.0
SPANWISE = 0.0625
VMEM = pltpu.VMEM
SMEM = pltpu.SMEM
HBM = pltpu.HBM
SELF, ANY, LOCAL = 2, 4, 10


def lagrange_at(points, targets):
    out = np.ones((6, 6))
    for row in range(6):
        for col in range(6):
            for other in range(6):
                if other != col:
                    out[row, col] *= (targets[row] - points[other]) / (points[col] - points[other])
    return out


def node_tables():
    root = math.sqrt(7.0)
    outer = math.sqrt(1.0 / 3.0 + 2.0 * root / 21.0)
    inner = math.sqrt(1.0 / 3.0 - 2.0 * root / 21.0)
    points = np.array([-1.0, -outer, -inner, inner, outer, 1.0])
    half = [1.0 / 15.0, (14.0 - root) / 30.0, (14.0 + root) / 30.0]
    weights = np.array(half + half[::-1])
    bary = np.array(
        [1.0 / np.prod([points[c] - points[k] for k in range(6) if k != c]) for c in range(6)]
    )
    deriv = np.zeros((6, 6))
    for i in range(6):
        for j in range(6):
            if i != j:
                deriv[i, j] = bary[j] / bary[i] / (points[i] - points[j])
        deriv[i, i] = -np.sum(deriv[i])
    lower = lagrange_at(points, (points - 1.0) / 2.0)
    upper = lagrange_at(points, (points + 1.0) / 2.0)
    stiff = deriv.T @ (weights[:, None] * deriv)
    return weights, deriv, lower, upper, stiff


W, D, QLO, QHI, K1 = node_tables()
HALVES = [np.eye(6), QLO, QHI]


def plane_tables(count):
    planes = np.arange(count)[:, None]
    coeffs = np.arange(count)[None, :]
    harmonic = (coeffs + 1) // 2
    phase = 2.0 * np.pi * (harmonic * planes % count) / count
    synth = np.where(coeffs == 0, 1.0, np.where(coeffs % 2 == 1, np.cos(phase), np.sin(phase)))
    norm = np.where((coeffs == 0) | (coeffs == count - 1), float(count), count / 2.0)
    return synth, (synth / norm).T


def split_table(table):
    table = np.asarray(table, np.float32)
    high = table.astype(ml_dtypes.bfloat16)
    low = (table - high.astype(np.float32)).astype(ml_dtypes.bfloat16)
    return np.stack([high, low])


def fold(matrix):
    plus = (matrix[:3, :3] + matrix[:3, :2:-1]) / 2.0
    minus = (matrix[:3, :3] - matrix[:3, :2:-1]) / 2.0
    return plus, minus


STIFF_FOLD = fold(K1 / W[:, None])
DERIV_FOLD = fold(D)


def folded(values, tables, sign):
    plus, minus = tables
    even = [values[a] + values[5 - a] for a in range(3)]
    odd = [values[a] - values[5 - a] for a in range(3)]
    out = [None] * 6
    for i in range(3):
        e = sum(float(plus[i, a]) * even[a] for a in range(3))
        o = sum(float(minus[i, a]) * odd[a] for a in range(3))
        out[i] = e + o
        out[5 - i] = e - o if sign > 0 else o - e
    return out


def split(value):
    high = value.astype(BF16)
    return high, (value - high.astype(F32)).astype(BF16)


def lane_ids(shape):
    return lax.broadcasted_iota(jnp.int32, shape, len(shape) - 1)


def call(kernel, outs, scratch, operands, spaces, out_spaces=None, grant=3):
    total = sum(int(np.prod(o.shape)) * 4 for o in outs)
    total += sum(int(np.prod(o.shape)) * 4 for o in operands)
    return pl.pallas_call(
        kernel,
        out_shape=outs,
        in_specs=[pl.BlockSpec(memory_space=s) for s in spaces],
        out_specs=[pl.BlockSpec(memory_space=s) for s in out_spaces or [VMEM] * len(outs)],
        scratch_shapes=scratch,
        compiler_params=pltpu.CompilerParams(vmem_limit_bytes=grant * 2**20),
        cost_estimate=pl.CostEstimate(flops=4_000_000, bytes_accessed=total, transcendentals=0),
    )(*[far(a) if s == HBM else a for a, s in zip(operands, spaces)])


def far(array):
    return pltpu.with_memory_space_constraint(array, HBM)


def shape(*dims, dtype=F32):
    return jax.ShapeDtypeStruct(dims, dtype)


def take(value, index):
    return jnp.take_along_axis(value, index, axis=1)


def take_row(value, index):
    wide = jnp.broadcast_to(value, (8, 128)), jnp.broadcast_to(index, (8, 128))
    return take(*wide)[0:1]


def prep_kernel(
    place, links, sides, visc, layout, meta, idx, edge_idx, tab, own_c, far_c, edge_own, edge_far
):
    me = place[1]
    dev = lax.shift_right_logical(links[...], 7)
    loc = jnp.bitwise_and(links[...], 127)
    remote = (dev != me).astype(jnp.int32)
    idx[LOCAL : LOCAL + 8, :] = loc
    own, other = sides[0], sides[1]
    inside = jnp.where(remote > 0, 3, own)
    whole = (inside == 0) & (other == 0)
    second = jnp.bitwise_and(lax.broadcasted_iota(jnp.int32, (8, 128), 0), 1) == 1
    odd_one = jnp.where(inside == 3, 0.0, jnp.where(whole & ~second, 0.0, 1.0))
    meta[0] = place[0]
    meta[1] = place[1]
    meta[2] = jnp.max(odd_one).astype(jnp.int32)
    meta[3] = jnp.max(layout[...].astype(F32)).astype(jnp.int32)
    row = lax.broadcasted_iota(jnp.int32, (128, 128), 0)
    col = lane_ids((128, 128))
    lane = lane_ids((1, 128))
    slot = jnp.bitwise_and(lane, 15)
    listed, present, ranks = [], [], []
    for side in range(2):
        rem = [remote[2 * side + t : 2 * side + t + 1] for t in range(2)]
        far = [loc[2 * side + t : 2 * side + t + 1] for t in range(2)]
        any_rem = jnp.maximum(rem[0], rem[1])
        before = jnp.sum(jnp.where(col < row, any_rem, 0).astype(F32), axis=1, keepdims=True)
        mine = jnp.sum(jnp.where(col == row, any_rem, 0).astype(F32), axis=1, keepdims=True)
        chosen = jnp.where((before == slot.astype(F32)) & (mine > 0.0), 1.0, 0.0)
        listed.append(jnp.sum(chosen * row.astype(F32), axis=0, keepdims=True).astype(jnp.int32))
        present.append(jnp.sum(chosen, axis=0, keepdims=True).astype(jnp.int32))
        idx[side : side + 1, :] = listed[side]
        mine_at = jnp.sum(jnp.where(row == col, before, 0.0), axis=0, keepdims=True)
        mine_at = jnp.where(any_rem > 0, mine_at.astype(jnp.int32), 0)
        idx[SELF + side : SELF + side + 1, :] = mine_at
        idx[ANY + side : ANY + side + 1, :] = any_rem
        named = jnp.where(
            ((far[0] == row) & (rem[0] > 0)) | ((far[1] == row) & (rem[1] > 0)), 1.0, 0.0
        )
        named = jnp.max(named, axis=1, keepdims=True)
        for t in range(2):
            rank = jnp.sum(jnp.where(row < far[t], named, 0.0), axis=0, keepdims=True)
            ranks.append(jnp.where(rem[t] > 0, rank.astype(jnp.int32), 0))
    idx[6:10, :] = jnp.zeros((4, 128), jnp.int32)
    idx[18:24, :] = jnp.zeros((6, 128), jnp.int32)

    west = lane < 64
    base = jnp.bitwise_and(lane, 112)
    element = jnp.where(west, listed[0], listed[1])
    here = jnp.where(west, present[0], present[1]) > 0

    def pick(rows_w, rows_e):
        return jnp.where(west, take_row(rows_w, element), take_row(rows_e, element))

    rank, live, mine, theirs = [], [], [], []
    for t in range(2):
        rank.append(pick(ranks[t], ranks[2 + t]))
        live.append((pick(remote[t : t + 1], remote[2 + t : 3 + t]) > 0) & here)
        mine.append(jnp.where(live[t], pick(own[t : t + 1], own[2 + t : 3 + t]), 3))
        theirs.append(jnp.where(live[t], pick(other[t : t + 1], other[2 + t : 3 + t]), 3))
    first = jnp.full((1, 128), 99, jnp.int32)
    last = jnp.full((1, 128), -1, jnp.int32)
    for t in range(2):
        target = jnp.where(live[t], rank[t], 99)
        for r in range(16):
            hit = take_row(target, base + r) == slot
            first = jnp.where(hit, jnp.minimum(first, 16 * t + r), first)
            last = jnp.where(hit, jnp.maximum(last, 16 * t + r), last)
    exists = [last >= 0, last > first]
    key = [jnp.where(exists[0], first, 0), jnp.where(exists[1], last, 0)]
    back = [base + jnp.bitwise_and(k, 15) for k in key]

    def from_key(k, pair):
        value = jnp.where(key[k] >= 16, take_row(pair[1], back[k]), take_row(pair[0], back[k]))
        return jnp.where(exists[k], value, 3)

    near_own = [from_key(k, theirs) for k in range(2)]
    near_far = [from_key(k, mine) for k in range(2)]
    edge_idx[...] = jnp.zeros((8, 128), jnp.int32)
    for k in range(2):
        edge_idx[k : k + 1, :] = base + rank[k]
        edge_idx[2 + k : 3 + k, :] = back[k]
    none = jnp.full((4, 128), 3, jnp.int32)
    edge_mine = jnp.concatenate([mine[0], mine[1], near_own[0], near_own[1], none], axis=0)
    edge_theirs = jnp.concatenate([theirs[0], theirs[1], near_far[0], near_far[1], none], axis=0)

    nu = visc[...]
    wide = layout[...] == 0
    tab[0:1, :] = nu * jnp.where(wide, 2.0, 0.5)
    tab[1:2, :] = nu * jnp.where(wide, 0.5, 2.0)
    tab[2:3, :] = nu
    for face in range(4):
        tab[3 + face : 4 + face, :] = whole[2 * face : 2 * face + 1].astype(F32)
    tab[7:8, :] = jnp.zeros((1, 128), F32)
    mine_m = [PENALTY * HALVES[o].T @ np.diag(W) @ HALVES[o] for o in range(3)]
    far_m = [
        [-PENALTY * HALVES[o].T @ np.diag(W) @ HALVES[c] for c in range(3)] for o in range(3)
    ]
    for code, facing, own_ref, far_ref in (
        (inside, other, own_c, far_c),
        (edge_mine, edge_theirs, edge_own, edge_far),
    ):
        hot = [(code == o).astype(F32) for o in range(3)]
        pair = [[hot[o] * (facing == c).astype(F32) for c in range(3)] for o in range(3)]
        for a in range(6):
            for b in range(6):
                n = 6 * a + b
                total = sum(float(mine_m[o][a, b]) * hot[o] for o in range(3))
                own_ref[n] = total + pltpu.roll(total, 7, 0)
                far_ref[n] = sum(
                    float(far_m[o][c][a, b]) * pair[o][c] for o in range(3) for c in range(3)
                )


def group_rows(group):
    return pl.ds(pl.multiple_of(group * 8, 8), 8)


def row_of(ref, r):
    return jnp.broadcast_to(ref[r : r + 1, :], (8, 128))


def face_nodes(face):
    return [
        6 * i + j
        for i, j in [
            (0, b) if face == 0 else (5, b) if face == 1 else (b, 0) if face == 2 else (b, 5)
            for b in range(6)
        ]
    ]


def either(meta, loop):
    for plain in (True, False):

        @pl.when((meta[2] == 0) == plain)
        def _(plain=plain):
            lax.fori_loop(0, 4, lambda group, carry: loop(group, plain) or carry, 0)


def weighted(factors, values):
    total = float(factors[0]) * values[0]
    for f, v in zip(factors[1:], values[1:]):
        total = total + float(f) * v
    return total


def plain_terms(env, v):
    _, idx, tab, _, _ = env

    def of_face(face):
        active = row_of(tab, 3 + face)
        local = row_of(idx, LOCAL + 2 * face)

        def term(a):
            n, m = face_nodes(face)[a], face_nodes(face ^ 1)[a]
            return (float(PENALTY * W[a]) * active) * (v(n) - take(v(m), local))

        return term

    return [of_face(face) for face in range(4)]


def general_terms(env, v):
    _, idx, _, own_c, far_c = env
    found = []
    for face in range(4):
        mine = [v(n) for n in face_nodes(face)]
        theirs = [
            [take(v(n), row_of(idx, LOCAL + 2 * face + t)) for n in face_nodes(face ^ 1)]
            for t in range(2)
        ]
        values = []
        for a in range(6):
            extra = jnp.zeros((8, 128), F32)
            for b in range(6):
                extra = extra + own_c[6 * a + b, 2 * face : 2 * face + 1, :] * mine[b]
                for t in range(2):
                    s = 2 * face + t
                    extra = extra + far_c[6 * a + b, s : s + 1, :] * theirs[t][b]
            values.append(extra)
        found.append(values.__getitem__)
    return found


def inner(group, env, v_ref, plain, emit):
    meta, _, tab, _, _ = env
    rows = group_rows(group)

    def v(n):
        return v_ref[n, rows, :]

    terms = (plain_terms if plain else general_terms)(env, v)
    q = meta[0] * 32 + group * 8 + lax.broadcasted_iota(jnp.int32, (8, 128), 0)
    harmonic = lax.shift_right_logical(q + 1, 1).astype(F32) * SPANWISE
    cx, cy = row_of(tab, 0), row_of(tab, 1)
    shift = 1.0 + 0.5 * tab[2:3, :] * (harmonic * harmonic)
    plus, minus = STIFF_FOLD
    even = [[v(6 * a + j) + v(30 - 6 * a + j) for a in range(3)] for j in range(6)]
    odd = [[v(6 * a + j) - v(30 - 6 * a + j) for a in range(3)] for j in range(6)]
    for i in range(3):
        e = [weighted(plus[i], even[j]) for j in range(6)]
        o = [weighted(minus[i], odd[j]) for j in range(6)]
        for line in (i, 5 - i):
            mine = [v(6 * line + j) for j in range(6)]
            g = folded(mine, STIFF_FOLD, 1)
            for j in range(6):
                n = 6 * line + j
                gx = e[j] + o[j] if line == i else e[j] - o[j]
                value = float(W[line] * W[j]) * (shift * mine[j] + cx * gx + cy * g[j])
                for face, (at, b) in enumerate(((line == 0, j), (line == 5, j), (j == 0, line), (j == 5, line))):
                    if at:
                        value = value + terms[face](b)
                emit(n, value)


def compact(group, idx, v_ref, h_ref, send_w, send_e):
    rows = group_rows(group)
    part = lax.shift_right_logical(lane_ids((8, 128)), 4)
    for face, ref in ((0, send_w), (1, send_e)):
        index = row_of(idx, face)
        for b in range(6):
            n = face_nodes(face)[b]
            low, high = take(v_ref[n, rows, :], index), take(h_ref[n, rows, :], index)
            old = ref[8 * b : 8 * b + 8, :]
            new = jnp.where(part == group, low, jnp.where(part == group + 4, high, old))
            ref[8 * b : 8 * b + 8, :] = new


def outer(group, idx, edge, first):
    found = {}
    for face in range(2):
        lanes = row_of(idx, SELF + face) + (64 * face + 16 * group)
        on = row_of(idx, ANY + face) > 0
        for b in range(6):
            value = take(edge[first + 8 * b : first + 8 * b + 8, :], lanes)
            found[face_nodes(face)[b]] = jnp.where(on, value, 0.0)
    return found


def edge_blocks(ref):
    return [ref[8 * b : 8 * b + 8, :] for b in range(6)]


def merge(to_w, to_e):
    west = lane_ids((8, 128)) < 64
    plain, inner_h = [], []
    for w, e in zip(edge_blocks(to_w), edge_blocks(to_e)):
        plain.append(jnp.where(west, w, pltpu.roll(e, 64, 1)))
        inner_h.append(jnp.where(west, pltpu.roll(w, 64, 1), e))
    return plain, inner_h


def edge_term(edge_idx, edge_own, edge_far, mine, theirs, row):
    near = [[take(t, row_of(edge_idx, row + k)) for t in theirs] for k in range(2)]
    out = []
    for a in range(6):
        chains = [None] * 3
        for b in range(6):
            n = 6 * a + b
            terms = [edge_own[n, row : row + 1, :] * mine[b]]
            terms += [edge_far[n, row + k : row + k + 1, :] * near[k][b] for k in range(2)]
            chains = terms if chains[0] is None else [c + t for c, t in zip(chains, terms)]
        out.append(chains[0] + (chains[1] + chains[2]))
    return out


def store_sums(acc, pad, first, count):
    width = count * 128
    lhs = (
        lax.broadcasted_iota(jnp.int32, (8, width), 0)
        == lax.shift_right_logical(lane_ids((8, width)), 7) + first
    ).astype(F32)
    sums = lax.dot_general(
        lhs, acc[...], (((1,), (1,)), ((), ())),
        precision=lax.Precision.HIGHEST, preferred_element_type=F32,
    )
    pad[...] = jnp.ones((8, 128), F32)
    pad[:, 0:32] = sums


HALF = 10.0


def store(ref, rows):
    def emit(n, value):
        ref[n, rows, :] = value

    return emit


def guess_kernel(meta, idx, tab, own_c, far_c, u, out, send_w, send_e):
    env = (meta, idx, tab, own_c, far_c)

    def loop(group, plain):
        inner(group, env, u, plain, store(out, group_rows(group)))
        compact(group, idx, u, out, send_w, send_e)

    either(meta, loop)


def base_kernel(idx, edge_idx, edge_own, edge_far, u, hu, to_w, to_e, from_w, from_e, out, edge):
    mine, _ = merge(to_w, to_e)
    theirs, _ = merge(from_w, from_e)
    for b, value in enumerate(edge_term(edge_idx, edge_own, edge_far, mine, theirs, 0)):
        edge[8 * b : 8 * b + 8, :] = value

    def body(group, carry):
        rows = group_rows(group)
        extra = outer(group, idx, edge, 0)
        for n in range(36):
            image = hu[n, rows, :]
            if n in extra:
                image = image + extra[n]
            out[n, rows, :] = float(W[n // 6] * W[n % 6]) * u[n, rows, :] - image
        return carry

    lax.fori_loop(0, 4, body, 0)


def residual_kernel(meta, idx, tab, own_c, far_c, back, base, out, h_out, send_w, send_e):
    env = (meta, idx, tab, own_c, far_c)
    for g in range(9):
        turned = back[:, 16 * g : 16 * g + 16, :].reshape(128, 128).T
        for m in range(4):
            n = 4 * g + m
            out[n] = base[n] + turned[32 * m : 32 * m + 32]

    def loop(group, plain):
        inner(group, env, out, plain, store(h_out, group_rows(group)))
        compact(group, idx, out, h_out, send_w, send_e)

    either(meta, loop)


def edge_steps(tables, to_w, to_e, from_w, from_e, before, edge, keep):
    edge_idx, edge_own, edge_far = tables
    mine, mine_h = merge(to_w, to_e)
    theirs, theirs_h = merge(from_w, from_e)
    scale = (1.0 if before is None else 2.0) / HALF
    first = edge_term(edge_idx, edge_own, edge_far, mine, theirs, 0)
    facing = edge_term(edge_idx, edge_own, edge_far, theirs, mine, 2)
    mine_next, theirs_next = [], []
    for b in range(6):
        if before is None:
            mine_next.append(scale * (mine_h[b] + first[b]) - mine[b])
            theirs_next.append(scale * (theirs_h[b] + facing[b]) - theirs[b])
        else:
            old = before[8 * b : 8 * b + 8, :], before[48 + 8 * b : 56 + 8 * b, :]
            mine_next.append(scale * (mine_h[b] + first[b]) - 2.0 * mine[b] - old[0])
            theirs_next.append(scale * (theirs_h[b] + facing[b]) - 2.0 * theirs[b] - old[1])
    second = edge_term(edge_idx, edge_own, edge_far, mine_next, theirs_next, 0)
    for b in range(6):
        edge[8 * b : 8 * b + 8, :] = first[b]
        edge[48 + 8 * b : 56 + 8 * b, :] = second[b]
        if keep is not None:
            keep[8 * b : 8 * b + 8, :] = mine_next[b]
            keep[48 + 8 * b : 56 + 8 * b, :] = theirs_next[b]


def two_steps_kernel(
    meta, idx, tab, own_c, far_c, edge_idx, edge_own, edge_far,
    t0, h0, to_w, to_e, from_w, from_e,
    t1, t2, h2, send_w, send_e, keep, part, edge, acc, pad,
):
    env = (meta, idx, tab, own_c, far_c)
    tables = (edge_idx, edge_own, edge_far)
    edge_steps(tables, to_w, to_e, from_w, from_e, None, edge, keep)

    def loop(group, plain):
        rows = group_rows(group)
        extra = outer(group, idx, edge, 0)
        sums = [jnp.zeros((8, 128), F32)] * 5
        for n in range(36):
            image = h0[n, rows, :]
            if n in extra:
                image = image + extra[n]
            a = t0[n, rows, :]
            b = (1.0 / HALF) * image - a
            t1[n, rows, :] = b
            for k, term in enumerate((a * a, a * b, b * b)):
                sums[k] = sums[k] + term
        extra_next = outer(group, idx, edge, 48)

        def emit(n, image):
            if n in extra_next:
                image = image + extra_next[n]
            b = t1[n, rows, :]
            c = (2.0 / HALF) * image - 2.0 * b - t0[n, rows, :]
            t2[n, rows, :] = c
            sums[3] = sums[3] + b * c
            sums[4] = sums[4] + c * c

        inner(group, env, t1, plain, emit)
        for k in range(5):
            acc[rows, 128 * k : 128 * k + 128] = sums[k]
        inner(group, env, t2, plain, store(h2, rows))
        compact(group, idx, t2, h2, send_w, send_e)

    either(meta, loop)
    store_sums(acc, pad, 0, 5)
    part[...] = pad[...]


def last_steps_kernel(
    meta, idx, tab, own_c, far_c, edge_idx, edge_own, edge_far,
    t1, t2, h2, to_w, to_e, from_w, from_e, keep, part,
    t3, red, edge, acc, pad,
):
    env = (meta, idx, tab, own_c, far_c)
    tables = (edge_idx, edge_own, edge_far)
    edge_steps(tables, to_w, to_e, from_w, from_e, keep, edge, None)

    def loop(group, plain):
        rows = group_rows(group)
        extra = outer(group, idx, edge, 0)
        sums = [jnp.zeros((8, 128), F32)] * 3
        for n in range(36):
            image = h2[n, rows, :]
            if n in extra:
                image = image + extra[n]
            c = t2[n, rows, :]
            d = (2.0 / HALF) * image - 2.0 * c - t1[n, rows, :]
            t3[n, rows, :] = d
            sums[0] = sums[0] + c * d
            sums[1] = sums[1] + d * d
        extra_next = outer(group, idx, edge, 48)

        def emit(n, image):
            if n in extra_next:
                image = image + extra_next[n]
            d = t3[n, rows, :]
            sums[2] = sums[2] + d * ((2.0 / HALF) * image - 2.0 * d - t2[n, rows, :])

        inner(group, env, t3, plain, emit)
        for k in range(3):
            acc[rows, 128 * k : 128 * k + 128] = sums[k]

    either(meta, loop)
    store_sums(acc, pad, 5, 3)
    row = lax.broadcasted_iota(jnp.int32, (8, 128), 0)
    mixed = jnp.where(row < 5, part[...], pad[...])
    for k in range(16):
        red[k] = mixed


def finish_kernel(red, x0, t0, t1, t2, t3, out, coef, held, sems):
    total = red[0]
    for k in range(1, 16):
        total = total + red[k]
    even = [total[2 * k : 2 * k + 1] for k in range(4)]
    odd = [total[2 * k + 1 : 2 * k + 2] for k in range(4)]
    moment = []
    for k in range(4):
        moment.append(even[0] if k == 0 else 2.0 * even[k] - even[0])
        moment.append(odd[0] if k == 0 else 2.0 * odd[k] - odd[0])

    def inner_product(i, j):
        return 0.5 * (moment[i + j] + moment[abs(i - j)])

    def energy(i, j):
        shifted = 0.5 * (inner_product(i, j + 1) + inner_product(i, abs(j - 1)))
        return HALF * (shifted + inner_product(i, j))

    low = [[None] * 4 for _ in range(4)]
    diag, inverse, half = [], [], []
    for j in range(4):
        d = energy(j, j)
        value = moment[j]
        for k in range(j):
            d = d - low[j][k] * low[j][k] * diag[k]
            value = value - low[j][k] * half[k]
        diag.append(d)
        half.append(value)
        inverse.append(1.0 / d)
        for i in range(j + 1, 4):
            e = energy(i, j)
            for k in range(j):
                e = e - low[i][k] * low[j][k] * diag[k]
            low[i][j] = e * inverse[j]
    weight = [half[k] * inverse[k] for k in range(4)]
    for i in (2, 1, 0):
        for k in range(i + 1, 4):
            weight[i] = weight[i] - low[k][i] * weight[k]
    turned = jnp.concatenate(weight + [jnp.zeros((4, 128), F32)], axis=0).T
    for k in range(4):
        coef[k] = jnp.broadcast_to(turned[0:32, k : k + 1], (32, 128))
    copies = []
    for c in range(6):
        for n in range(6 * c, 6 * c + 6):
            held[n] = x0[n] + coef[0] * t0[n] + coef[1] * t1[n] + coef[2] * t2[n] + coef[3] * t3[n]
        part = pl.ds(6 * c, 6)
        copies.append(pltpu.make_async_copy(held.at[part], out.at[part], sems.at[c]))
        copies[c].start()
    for copy in copies:
        copy.wait()


def pack_kernel(u, out, held, ready, sems):
    copies = []
    for g in range(9):
        part = pl.ds(4 * g, 4)
        copies.append(pltpu.make_async_copy(u.at[part], held.at[part], sems.at[g]))
        copies[g].start()
    for g in range(9):
        copies[g].wait()
        turned = held[4 * g : 4 * g + 4].reshape(128, 128).T
        ready[:, 16 * g : 16 * g + 16, :] = turned.reshape(8, 16, 128)
        part = pl.ds(16 * g, 16)
        copies[g] = pltpu.make_async_copy(ready.at[:, part], out.at[:, part], sems.at[9 + g])
        copies[g].start()
    for copy in copies:
        copy.wait()


def block_turn(blocks):
    part = lax.shift_right_logical(lane_ids(blocks[0].shape), 5)
    rolled = [blocks[0]] + [pltpu.roll(blocks[s], 32 * s, 1) for s in range(1, 4)]
    out = []
    for m in range(4):
        mixed = rolled[-m % 4]
        for t in range(1, 4):
            mixed = jnp.where(part == t, rolled[(t - m) % 4], mixed)
        out.append(pltpu.roll(mixed, 128 - 32 * m, 1) if m else mixed)
    return out


def product3(high, low, table):
    def dot(a, b):
        return jnp.dot(a, b, preferred_element_type=F32)

    return dot(high, table[0]) + dot(high, table[1]) + dot(low, table[0])


def advect_kernel(
    meta, came, speed_far, synth_far, analy_far, out,
    high, low, phys, speed, synth, analy, ready, sems,
):
    loads = [
        pltpu.make_async_copy(far, near, sems.at[k])
        for k, (far, near) in enumerate(
            ((synth_far, synth), (speed_far, speed), (analy_far, analy))
        )
    ]
    for load in loads:
        load.start()
    for g in range(9):
        for h in range(2):
            pieces = block_turn([came[4 * h + s, 16 * g : 16 * g + 16, :] for s in range(4)])
            for m in range(4):
                n = 16 * (4 * g + m)
                hi, lo = split(pieces[m])
                high[n : n + 16, 128 * h : 128 * h + 128] = hi
                low[n : n + 16, 128 * h : 128 * h + 128] = lo
    loads[0].wait()
    for i in range(2):
        part = slice(288 * i, 288 * i + 288)
        phys[part, :] = product3(high[part, :], low[part, :], synth)
    loads[1].wait()
    wide = meta[3] == 0
    sx = jnp.where(wide, 2.0, 1.0)
    sy = jnp.where(wide, 1.0, 2.0)
    for h in range(2):
        cols = slice(128 * h, 128 * h + 128)
        u = [[phys[16 * (6 * i + j) : 16 * (6 * i + j) + 16, cols] for j in range(6)] for i in range(6)]
        acc = [[None] * 6 for _ in range(6)]
        for j in range(6):
            g = folded([u[i][j] for i in range(6)], DERIV_FOLD, -1)
            for i in range(6):
                acc[i][j] = sx * (speed[0, 6 * i + j, :, cols] * g[i])
        for i in range(6):
            g = folded(u[i], DERIV_FOLD, -1)
            for j in range(6):
                n = 16 * (6 * i + j)
                total = acc[i][j] + sy * (speed[1, 6 * i + j, :, cols] * g[j])
                hi, lo = split(float(-0.5 * W[i] * W[j]) * total)
                high[n : n + 16, cols] = hi
                low[n : n + 16, cols] = lo
    loads[2].wait()
    for i in range(2):
        part = slice(288 * i, 288 * i + 288)
        phys[part, :] = product3(high[part, :], low[part, :], analy)
    stores = []
    for g in range(9):
        for h in range(2):
            cols = slice(128 * h, 128 * h + 128)
            pieces = block_turn(
                [phys[16 * (4 * g + m) : 16 * (4 * g + m) + 16, cols] for m in range(4)]
            )
            for s in range(4):
                ready[4 * h + s, 16 * g : 16 * g + 16, :] = pieces[s]
        part = pl.ds(16 * g, 16)
        stores.append(pltpu.make_async_copy(ready.at[:, part], out.at[:, part], sems.at[3 + g]))
        stores[g].start()
    for store_ in stores:
        store_.wait()


def shift_by(array, by):
    count = lax.axis_size("elem")
    return lax.ppermute(array, "elem", [(i, (i + by) % count) for i in range(count)])


def shards(scalar_modes, velocity, viscosity, mortar_links, mortar_sides, layout):
    u = jnp.transpose(scalar_modes, (1, 2, 0, 3)).reshape(36, 32, 128)
    speed = jnp.transpose(velocity, (0, 2, 3, 4, 1)).reshape(2, 36, 16, 256)
    synth, analy = plane_tables(256)
    synth = jnp.asarray(split_table(synth.T))
    analy = jnp.asarray(split_table(analy.T))
    place = jnp.stack([lax.axis_index("plane"), lax.axis_index("elem")]).astype(jnp.int32)

    vol, edge = shape(36, 32, 128), shape(48, 128)
    both = shape(96, 128)
    blocks = shape(8, 144, 128)
    packed = call(
        pack_kernel,
        [blocks],
        [VMEM((36, 32, 128), F32), VMEM((8, 144, 128), F32), pltpu.SemaphoreType.DMA((18,))],
        [u],
        [HBM],
        [HBM],
    )[0]
    came = lax.all_to_all(packed, "plane", 0, 0, tiled=True)

    table = shape(36, 8, 128)
    meta, idx, edge_idx, tab, own_c, far_c, edge_own, edge_far = call(
        prep_kernel,
        [
            shape(4, dtype=jnp.int32),
            shape(24, 128, dtype=jnp.int32),
            shape(8, 128, dtype=jnp.int32),
            shape(8, 128),
        ]
        + [table] * 4,
        [],
        [place, mortar_links, mortar_sides, viscosity[None], layout[None]],
        [SMEM] + [VMEM] * 4,
        [SMEM] + [VMEM] * 7,
    )
    head = [meta, idx, tab, own_c, far_c]
    edges = [edge_idx, edge_own, edge_far]

    def run(kernel, outs, scratch, args):
        return call(kernel, outs, scratch, args, [SMEM if a is meta else VMEM for a in args])

    def trade(send_w, send_e):
        return shift_by(send_e, 1), shift_by(send_w, -1)

    hu, *sent = run(guess_kernel, [vol, edge, edge], [], head + [u])
    got = trade(*sent)
    came, *got = lax.optimization_barrier((came, *got))
    back = call(
        advect_kernel,
        [blocks],
        [
            VMEM((576, 256), BF16),
            VMEM((576, 256), BF16),
            VMEM((576, 256), F32),
            VMEM((2, 36, 16, 256), F32),
            VMEM((2, 256, 256), BF16),
            VMEM((2, 256, 256), BF16),
            VMEM((8, 144, 128), F32),
            pltpu.SemaphoreType.DMA((12,)),
        ],
        [meta, came, speed, synth, analy],
        [SMEM, VMEM, HBM, HBM, HBM],
        [HBM],
        grant=12,
    )[0]
    back = lax.all_to_all(back, "plane", 0, 0, tiled=True)
    base = run(
        base_kernel, [vol], [VMEM((48, 128), F32)], [idx, *edges, u, hu, *sent, *got]
    )[0]

    def work(count):
        return [
            VMEM((96, 128), F32),
            VMEM((32, 128 * count), F32),
            VMEM((8, 128), F32),
        ]

    t0, h0, *sent = run(residual_kernel, [vol, vol, edge, edge], [], head + [back, base])
    got = trade(*sent)
    t1, t2, h2, to_w, to_e, keep, part = run(
        two_steps_kernel,
        [vol, vol, vol, edge, edge, both, shape(8, 128)],
        work(5),
        head + edges + [t0, h0, *sent, *got],
    )
    got = trade(to_w, to_e)
    t3, red = run(
        last_steps_kernel,
        [vol, shape(16, 8, 128)],
        work(3),
        head + edges + [t1, t2, h2, to_w, to_e, *got, keep, part],
    )
    red = lax.all_to_all(red, "elem", 0, 0, tiled=True)
    out = call(
        finish_kernel,
        [vol],
        [VMEM((4, 32, 128), F32), VMEM((36, 32, 128), F32), pltpu.SemaphoreType.DMA((6,))],
        [red, u, t0, t1, t2, t3],
        [VMEM] * 6,
        [HBM],
    )[0]
    return jnp.transpose(out.reshape(6, 6, 32, 128), (2, 0, 1, 3))


def solution(mesh):
    placed = (
        P("plane", None, None, "elem"),
        P(None, None, None, None, ("elem", "plane")),
        P("elem"),
        P(None, "elem"),
        P(None, None, "elem"),
        P("elem"),
    )
    return jax.shard_map(
        shards,
        mesh=mesh,
        in_specs=placed,
        out_specs=P("plane", None, None, "elem"),
        check_vma=False,
    )
```

```python
import math

import jax
import jax.numpy as jnp
import ml_dtypes
import numpy as np
from jax import lax
from jax.experimental import pallas as pl
from jax.experimental.pallas import tpu as pltpu
from jax.sharding import PartitionSpec as P

F32 = jnp.float32
BF16 = jnp.bfloat16
PENALTY = 10.0
SPANWISE = 0.0625
VMEM = pltpu.VMEM
SMEM = pltpu.SMEM
HBM = pltpu.HBM
SELF, ANY, LOCAL = 2, 4, 10


def lagrange_at(points, targets):
    out = np.ones((6, 6))
    for row in range(6):
        for col in range(6):
            for other in range(6):
                if other != col:
                    out[row, col] *= (targets[row] - points[other]) / (points[col] - points[other])
    return out


def node_tables():
    root = math.sqrt(7.0)
    outer = math.sqrt(1.0 / 3.0 + 2.0 * root / 21.0)
    inner = math.sqrt(1.0 / 3.0 - 2.0 * root / 21.0)
    points = np.array([-1.0, -outer, -inner, inner, outer, 1.0])
    half = [1.0 / 15.0, (14.0 - root) / 30.0, (14.0 + root) / 30.0]
    weights = np.array(half + half[::-1])
    bary = np.array(
        [1.0 / np.prod([points[c] - points[k] for k in range(6) if k != c]) for c in range(6)]
    )
    deriv = np.zeros((6, 6))
    for i in range(6):
        for j in range(6):
            if i != j:
                deriv[i, j] = bary[j] / bary[i] / (points[i] - points[j])
        deriv[i, i] = -np.sum(deriv[i])
    lower = lagrange_at(points, (points - 1.0) / 2.0)
    upper = lagrange_at(points, (points + 1.0) / 2.0)
    stiff = deriv.T @ (weights[:, None] * deriv)
    return weights, deriv, lower, upper, stiff


W, D, QLO, QHI, K1 = node_tables()
HALVES = [np.eye(6), QLO, QHI]


def plane_tables(count):
    planes = np.arange(count)[:, None]
    coeffs = np.arange(count)[None, :]
    harmonic = (coeffs + 1) // 2
    phase = 2.0 * np.pi * (harmonic * planes % count) / count
    synth = np.where(coeffs == 0, 1.0, np.where(coeffs % 2 == 1, np.cos(phase), np.sin(phase)))
    return synth


def split_table(table):
    table = np.asarray(table, np.float32)
    high = table.astype(ml_dtypes.bfloat16)
    low = (table - high.astype(np.float32)).astype(ml_dtypes.bfloat16)
    return np.stack([high, low])


def fold(matrix):
    plus = (matrix[:3, :3] + matrix[:3, :2:-1]) / 2.0
    minus = (matrix[:3, :3] - matrix[:3, :2:-1]) / 2.0
    return plus, minus


STIFF_FOLD = fold(K1 / W[:, None])
DERIV_FOLD = fold(D)


def folded(values, tables, sign):
    plus, minus = tables
    even = [values[a] + values[5 - a] for a in range(3)]
    odd = [values[a] - values[5 - a] for a in range(3)]
    out = [None] * 6
    for i in range(3):
        e = sum(float(plus[i, a]) * even[a] for a in range(3))
        o = sum(float(minus[i, a]) * odd[a] for a in range(3))
        out[i] = e + o
        out[5 - i] = e - o if sign > 0 else o - e
    return out


def split(value):
    high = value.astype(BF16)
    return high, (value - high.astype(F32)).astype(BF16)


def lane_ids(shape):
    return lax.broadcasted_iota(jnp.int32, shape, len(shape) - 1)


def call(kernel, outs, scratch, operands, spaces, out_spaces=None, grant=3):
    total = sum(int(np.prod(o.shape)) * 4 for o in outs)
    total += sum(int(np.prod(o.shape)) * 4 for o in operands)
    return pl.pallas_call(
        kernel,
        out_shape=outs,
        in_specs=[pl.BlockSpec(memory_space=s) for s in spaces],
        out_specs=[pl.BlockSpec(memory_space=s) for s in out_spaces or [VMEM] * len(outs)],
        scratch_shapes=scratch,
        compiler_params=pltpu.CompilerParams(vmem_limit_bytes=grant * 2**20),
        cost_estimate=pl.CostEstimate(flops=4_000_000, bytes_accessed=total, transcendentals=0),
    )(*[far(a) if s == HBM else a for a, s in zip(operands, spaces)])


def far(array):
    return pltpu.with_memory_space_constraint(array, HBM)


def shape(*dims, dtype=F32):
    return jax.ShapeDtypeStruct(dims, dtype)


def take(value, index):
    return jnp.take_along_axis(value, index, axis=1)


def take_row(value, index):
    wide = jnp.broadcast_to(value, (8, 128)), jnp.broadcast_to(index, (8, 128))
    return take(*wide)[0:1]


def prep_kernel(
    place, links, sides, visc, layout, meta, idx, edge_idx, tab, own_c, far_c, edge_own, edge_far
):
    me = place[1]
    dev = lax.shift_right_logical(links[...], 7)
    loc = jnp.bitwise_and(links[...], 127)
    remote = (dev != me).astype(jnp.int32)
    idx[LOCAL : LOCAL + 8, :] = loc
    own, other = sides[0], sides[1]
    inside = jnp.where(remote > 0, 3, own)
    whole = (inside == 0) & (other == 0)
    second = jnp.bitwise_and(lax.broadcasted_iota(jnp.int32, (8, 128), 0), 1) == 1
    odd_one = jnp.where(inside == 3, 0.0, jnp.where(whole & ~second, 0.0, 1.0))
    meta[0] = place[0]
    meta[1] = place[1]
    meta[2] = jnp.max(odd_one).astype(jnp.int32)
    meta[3] = jnp.max(layout[...].astype(F32)).astype(jnp.int32)
    row = lax.broadcasted_iota(jnp.int32, (128, 128), 0)
    col = lane_ids((128, 128))
    lane = lane_ids((1, 128))
    slot = jnp.bitwise_and(lane, 15)
    listed, present, ranks = [], [], []
    for side in range(2):
        rem = [remote[2 * side + t : 2 * side + t + 1] for t in range(2)]
        far = [loc[2 * side + t : 2 * side + t + 1] for t in range(2)]
        any_rem = jnp.maximum(rem[0], rem[1])
        before = jnp.sum(jnp.where(col < row, any_rem, 0).astype(F32), axis=1, keepdims=True)
        mine = jnp.sum(jnp.where(col == row, any_rem, 0).astype(F32), axis=1, keepdims=True)
        chosen = jnp.where((before == slot.astype(F32)) & (mine > 0.0), 1.0, 0.0)
        listed.append(jnp.sum(chosen * row.astype(F32), axis=0, keepdims=True).astype(jnp.int32))
        present.append(jnp.sum(chosen, axis=0, keepdims=True).astype(jnp.int32))
        idx[side : side + 1, :] = listed[side]
        mine_at = jnp.sum(jnp.where(row == col, before, 0.0), axis=0, keepdims=True)
        mine_at = jnp.where(any_rem > 0, mine_at.astype(jnp.int32), 0)
        idx[SELF + side : SELF + side + 1, :] = mine_at
        idx[ANY + side : ANY + side + 1, :] = any_rem
        named = jnp.where(
            ((far[0] == row) & (rem[0] > 0)) | ((far[1] == row) & (rem[1] > 0)), 1.0, 0.0
        )
        named = jnp.max(named, axis=1, keepdims=True)
        for t in range(2):
            rank = jnp.sum(jnp.where(row < far[t], named, 0.0), axis=0, keepdims=True)
            ranks.append(jnp.where(rem[t] > 0, rank.astype(jnp.int32), 0))
    idx[6:10, :] = jnp.zeros((4, 128), jnp.int32)
    idx[18:24, :] = jnp.zeros((6, 128), jnp.int32)

    west = lane < 64
    base = jnp.bitwise_and(lane, 112)
    element = jnp.where(west, listed[0], listed[1])
    here = jnp.where(west, present[0], present[1]) > 0

    def pick(rows_w, rows_e):
        return jnp.where(west, take_row(rows_w, element), take_row(rows_e, element))

    rank, live, mine, theirs = [], [], [], []
    for t in range(2):
        rank.append(pick(ranks[t], ranks[2 + t]))
        live.append((pick(remote[t : t + 1], remote[2 + t : 3 + t]) > 0) & here)
        mine.append(jnp.where(live[t], pick(own[t : t + 1], own[2 + t : 3 + t]), 3))
        theirs.append(jnp.where(live[t], pick(other[t : t + 1], other[2 + t : 3 + t]), 3))
    first = jnp.full((1, 128), 99, jnp.int32)
    last = jnp.full((1, 128), -1, jnp.int32)
    for t in range(2):
        target = jnp.where(live[t], rank[t], 99)
        for r in range(16):
            hit = take_row(target, base + r) == slot
            first = jnp.where(hit, jnp.minimum(first, 16 * t + r), first)
            last = jnp.where(hit, jnp.maximum(last, 16 * t + r), last)
    exists = [last >= 0, last > first]
    key = [jnp.where(exists[0], first, 0), jnp.where(exists[1], last, 0)]
    back = [base + jnp.bitwise_and(k, 15) for k in key]

    def from_key(k, pair):
        value = jnp.where(key[k] >= 16, take_row(pair[1], back[k]), take_row(pair[0], back[k]))
        return jnp.where(exists[k], value, 3)

    near_own = [from_key(k, theirs) for k in range(2)]
    near_far = [from_key(k, mine) for k in range(2)]
    edge_idx[...] = jnp.zeros((8, 128), jnp.int32)
    for k in range(2):
        edge_idx[k : k + 1, :] = base + rank[k]
        edge_idx[2 + k : 3 + k, :] = back[k]
    none = jnp.full((4, 128), 3, jnp.int32)
    edge_mine = jnp.concatenate([mine[0], mine[1], near_own[0], near_own[1], none], axis=0)
    edge_theirs = jnp.concatenate([theirs[0], theirs[1], near_far[0], near_far[1], none], axis=0)

    nu = visc[...]
    wide = layout[...] == 0
    tab[0:1, :] = nu * jnp.where(wide, 2.0, 0.5)
    tab[1:2, :] = nu * jnp.where(wide, 0.5, 2.0)
    tab[2:3, :] = nu
    for face in range(4):
        tab[3 + face : 4 + face, :] = whole[2 * face : 2 * face + 1].astype(F32)
    tab[7:8, :] = jnp.zeros((1, 128), F32)
    mine_m = [PENALTY * HALVES[o].T @ np.diag(W) @ HALVES[o] for o in range(3)]
    far_m = [
        [-PENALTY * HALVES[o].T @ np.diag(W) @ HALVES[c] for c in range(3)] for o in range(3)
    ]
    for code, facing, own_ref, far_ref in (
        (inside, other, own_c, far_c),
        (edge_mine, edge_theirs, edge_own, edge_far),
    ):
        hot = [(code == o).astype(F32) for o in range(3)]
        pair = [[hot[o] * (facing == c).astype(F32) for c in range(3)] for o in range(3)]
        for a in range(6):
            for b in range(6):
                n = 6 * a + b
                total = sum(float(mine_m[o][a, b]) * hot[o] for o in range(3))
                own_ref[n] = total + pltpu.roll(total, 7, 0)
                far_ref[n] = sum(
                    float(far_m[o][c][a, b]) * pair[o][c] for o in range(3) for c in range(3)
                )


def group_rows(group):
    return pl.ds(pl.multiple_of(group * 8, 8), 8)


def row_of(ref, r):
    return jnp.broadcast_to(ref[r : r + 1, :], (8, 128))


def face_nodes(face):
    return [
        6 * i + j
        for i, j in [
            (0, b) if face == 0 else (5, b) if face == 1 else (b, 0) if face == 2 else (b, 5)
            for b in range(6)
        ]
    ]


def either(meta, loop):
    for plain in (True, False):

        @pl.when((meta[2] == 0) == plain)
        def _(plain=plain):
            lax.fori_loop(0, 4, lambda group, carry: loop(group, plain) or carry, 0)


def weighted(factors, values):
    total = float(factors[0]) * values[0]
    for f, v in zip(factors[1:], values[1:]):
        total = total + float(f) * v
    return total


def plain_terms(env, v):
    _, idx, tab, _, _ = env

    def of_face(face):
        active = row_of(tab, 3 + face)
        local = row_of(idx, LOCAL + 2 * face)

        def term(a):
            n, m = face_nodes(face)[a], face_nodes(face ^ 1)[a]
            return (float(PENALTY * W[a]) * active) * (v(n) - take(v(m), local))

        return term

    return [of_face(face) for face in range(4)]


def general_terms(env, v):
    _, idx, _, own_c, far_c = env
    found = []
    for face in range(4):
        mine = [v(n) for n in face_nodes(face)]
        theirs = [
            [take(v(n), row_of(idx, LOCAL + 2 * face + t)) for n in face_nodes(face ^ 1)]
            for t in range(2)
        ]
        values = []
        for a in range(6):
            extra = jnp.zeros((8, 128), F32)
            for b in range(6):
                extra = extra + own_c[6 * a + b, 2 * face : 2 * face + 1, :] * mine[b]
                for t in range(2):
                    s = 2 * face + t
                    extra = extra + far_c[6 * a + b, s : s + 1, :] * theirs[t][b]
            values.append(extra)
        found.append(values.__getitem__)
    return found


def inner(group, env, v_ref, plain, emit):
    meta, _, tab, _, _ = env
    rows = group_rows(group)

    def v(n):
        return v_ref[n, rows, :]

    terms = (plain_terms if plain else general_terms)(env, v)
    q = meta[0] * 32 + group * 8 + lax.broadcasted_iota(jnp.int32, (8, 128), 0)
    harmonic = lax.shift_right_logical(q + 1, 1).astype(F32) * SPANWISE
    cx, cy = row_of(tab, 0), row_of(tab, 1)
    shift = 1.0 + 0.5 * tab[2:3, :] * (harmonic * harmonic)
    plus, minus = STIFF_FOLD
    even = [[v(6 * a + j) + v(30 - 6 * a + j) for a in range(3)] for j in range(6)]
    odd = [[v(6 * a + j) - v(30 - 6 * a + j) for a in range(3)] for j in range(6)]
    for i in range(3):
        e = [weighted(plus[i], even[j]) for j in range(6)]
        o = [weighted(minus[i], odd[j]) for j in range(6)]
        for line in (i, 5 - i):
            mine = [v(6 * line + j) for j in range(6)]
            g = folded(mine, STIFF_FOLD, 1)
            for j in range(6):
                n = 6 * line + j
                gx = e[j] + o[j] if line == i else e[j] - o[j]
                value = float(W[line] * W[j]) * (shift * mine[j] + cx * gx + cy * g[j])
                for face, (at, b) in enumerate(((line == 0, j), (line == 5, j), (j == 0, line), (j == 5, line))):
                    if at:
                        value = value + terms[face](b)
                emit(n, value)


def compact(group, idx, v_ref, h_ref, send_w, send_e):
    rows = group_rows(group)
    part = lax.shift_right_logical(lane_ids((8, 128)), 4)
    for face, ref in ((0, send_w), (1, send_e)):
        index = row_of(idx, face)
        for b in range(6):
            n = face_nodes(face)[b]
            low, high = take(v_ref[n, rows, :], index), take(h_ref[n, rows, :], index)
            old = ref[8 * b : 8 * b + 8, :]
            new = jnp.where(part == group, low, jnp.where(part == group + 4, high, old))
            ref[8 * b : 8 * b + 8, :] = new


def outer(group, idx, edge, first):
    found = {}
    for face in range(2):
        lanes = row_of(idx, SELF + face) + (64 * face + 16 * group)
        on = row_of(idx, ANY + face) > 0
        for b in range(6):
            value = take(edge[first + 8 * b : first + 8 * b + 8, :], lanes)
            found[face_nodes(face)[b]] = jnp.where(on, value, 0.0)
    return found


def edge_blocks(ref):
    return [ref[8 * b : 8 * b + 8, :] for b in range(6)]


def merge(to_w, to_e):
    west = lane_ids((8, 128)) < 64
    plain, inner_h = [], []
    for w, e in zip(edge_blocks(to_w), edge_blocks(to_e)):
        plain.append(jnp.where(west, w, pltpu.roll(e, 64, 1)))
        inner_h.append(jnp.where(west, pltpu.roll(w, 64, 1), e))
    return plain, inner_h


def edge_term(edge_idx, edge_own, edge_far, mine, theirs, row):
    near = [[take(t, row_of(edge_idx, row + k)) for t in theirs] for k in range(2)]
    out = []
    for a in range(6):
        chains = [None] * 3
        for b in range(6):
            n = 6 * a + b
            terms = [edge_own[n, row : row + 1, :] * mine[b]]
            terms += [edge_far[n, row + k : row + k + 1, :] * near[k][b] for k in range(2)]
            chains = terms if chains[0] is None else [c + t for c, t in zip(chains, terms)]
        out.append(chains[0] + (chains[1] + chains[2]))
    return out


def store_sums(acc, pad, first, count):
    width = count * 128
    lhs = (
        lax.broadcasted_iota(jnp.int32, (8, width), 0)
        == lax.shift_right_logical(lane_ids((8, width)), 7) + first
    ).astype(F32)
    sums = lax.dot_general(
        lhs, acc[...], (((1,), (1,)), ((), ())),
        precision=lax.Precision.HIGHEST, preferred_element_type=F32,
    )
    pad[...] = jnp.ones((8, 128), F32)
    pad[:, 0:32] = sums


HALF = 10.0


def store(ref, rows):
    def emit(n, value):
        ref[n, rows, :] = value

    return emit


def guess_kernel(meta, idx, tab, own_c, far_c, u_far, out, send_w, send_e, u, sem):
    env = (meta, idx, tab, own_c, far_c)
    copy = pltpu.make_async_copy(u_far, u, sem)
    copy.start()
    copy.wait()

    def loop(group, plain):
        rows = group_rows(group)

        def emit(n, value):
            out[n, rows, :] = float(W[n // 6] * W[n % 6]) * u[n, rows, :] - value

        inner(group, env, u, plain, emit)
        compact(group, idx, u, u, send_w, send_e)

    either(meta, loop)


def guess_edge_kernel(edge_idx, edge_own, edge_far, to_w, to_e, from_w, from_e, edge):
    mine, _ = merge(to_w, to_e)
    theirs, _ = merge(from_w, from_e)
    for b, value in enumerate(edge_term(edge_idx, edge_own, edge_far, mine, theirs, 0)):
        edge[8 * b : 8 * b + 8, :] = value


def residual_kernel(
    meta, idx, tab, own_c, far_c, back, base, edge, out, h_out, send_w, send_e
):
    env = (meta, idx, tab, own_c, far_c)
    for g in range(9):
        turned = back[:, 16 * g : 16 * g + 16, :].reshape(128, 128).T
        for m in range(4):
            n = 4 * g + m
            out[n] = base[n] + turned[32 * m : 32 * m + 32]

    def loop(group, plain):
        rows = group_rows(group)
        for n, extra in outer(group, idx, edge, 0).items():
            out[n, rows, :] -= extra
        inner(group, env, out, plain, store(h_out, rows))
        compact(group, idx, out, h_out, send_w, send_e)

    either(meta, loop)


def edge_steps(tables, to_w, to_e, from_w, from_e, before, edge, keep):
    edge_idx, edge_own, edge_far = tables
    mine, mine_h = merge(to_w, to_e)
    theirs, theirs_h = merge(from_w, from_e)
    scale = (1.0 if before is None else 2.0) / HALF
    first = edge_term(edge_idx, edge_own, edge_far, mine, theirs, 0)
    facing = edge_term(edge_idx, edge_own, edge_far, theirs, mine, 2)
    mine_next, theirs_next = [], []
    for b in range(6):
        if before is None:
            mine_next.append(scale * (mine_h[b] + first[b]) - mine[b])
            theirs_next.append(scale * (theirs_h[b] + facing[b]) - theirs[b])
        else:
            old = before[8 * b : 8 * b + 8, :], before[48 + 8 * b : 56 + 8 * b, :]
            mine_next.append(scale * (mine_h[b] + first[b]) - 2.0 * mine[b] - old[0])
            theirs_next.append(scale * (theirs_h[b] + facing[b]) - 2.0 * theirs[b] - old[1])
    second = edge_term(edge_idx, edge_own, edge_far, mine_next, theirs_next, 0)
    for b in range(6):
        edge[8 * b : 8 * b + 8, :] = first[b]
        edge[48 + 8 * b : 56 + 8 * b, :] = second[b]
        if keep is not None:
            keep[8 * b : 8 * b + 8, :] = mine_next[b]
            keep[48 + 8 * b : 56 + 8 * b, :] = theirs_next[b]


def two_steps_kernel(
    meta, idx, tab, own_c, far_c, edge_idx, edge_own, edge_far,
    t0, h0, to_w, to_e, from_w, from_e,
    t1, t2, h2, send_w, send_e, keep, part, edge, acc, pad,
):
    env = (meta, idx, tab, own_c, far_c)
    tables = (edge_idx, edge_own, edge_far)
    edge_steps(tables, to_w, to_e, from_w, from_e, None, edge, keep)

    def loop(group, plain):
        rows = group_rows(group)
        extra = outer(group, idx, edge, 0)
        sums = [jnp.zeros((8, 128), F32)] * 5
        for n in range(36):
            image = h0[n, rows, :]
            if n in extra:
                image = image + extra[n]
            a = t0[n, rows, :]
            b = (1.0 / HALF) * image - a
            t1[n, rows, :] = b
            for k, term in enumerate((a * a, a * b, b * b)):
                sums[k] = sums[k] + term
        extra_next = outer(group, idx, edge, 48)

        def emit(n, image):
            if n in extra_next:
                image = image + extra_next[n]
            b = t1[n, rows, :]
            c = (2.0 / HALF) * image - 2.0 * b - t0[n, rows, :]
            t2[n, rows, :] = c
            sums[3] = sums[3] + b * c
            sums[4] = sums[4] + c * c

        inner(group, env, t1, plain, emit)
        for k in range(5):
            acc[rows, 128 * k : 128 * k + 128] = sums[k]
        inner(group, env, t2, plain, store(h2, rows))
        compact(group, idx, t2, h2, send_w, send_e)

    either(meta, loop)
    store_sums(acc, pad, 0, 5)
    part[...] = pad[...]


def last_steps_kernel(
    meta, idx, tab, own_c, far_c, edge_idx, edge_own, edge_far,
    t1, t2, h2, to_w, to_e, from_w, from_e, keep, part,
    t3, red, edge, acc, pad,
):
    env = (meta, idx, tab, own_c, far_c)
    tables = (edge_idx, edge_own, edge_far)
    edge_steps(tables, to_w, to_e, from_w, from_e, keep, edge, None)

    def loop(group, plain):
        rows = group_rows(group)
        extra = outer(group, idx, edge, 0)
        sums = [jnp.zeros((8, 128), F32)] * 3
        for n in range(36):
            image = h2[n, rows, :]
            if n in extra:
                image = image + extra[n]
            c = t2[n, rows, :]
            d = (2.0 / HALF) * image - 2.0 * c - t1[n, rows, :]
            t3[n, rows, :] = d
            sums[0] = sums[0] + c * d
            sums[1] = sums[1] + d * d
        extra_next = outer(group, idx, edge, 48)

        def emit(n, image):
            if n in extra_next:
                image = image + extra_next[n]
            d = t3[n, rows, :]
            sums[2] = sums[2] + d * ((2.0 / HALF) * image - 2.0 * d - t2[n, rows, :])

        inner(group, env, t3, plain, emit)
        for k in range(3):
            acc[rows, 128 * k : 128 * k + 128] = sums[k]

    either(meta, loop)
    store_sums(acc, pad, 5, 3)
    row = lax.broadcasted_iota(jnp.int32, (8, 128), 0)
    mixed = jnp.where(row < 5, part[...], pad[...])
    for k in range(16):
        red[k] = mixed


def finish_kernel(red, x0, t0, t1, t2, t3, out, coef, held, sems):
    total = red[0]
    for k in range(1, 16):
        total = total + red[k]
    even = [total[2 * k : 2 * k + 1] for k in range(4)]
    odd = [total[2 * k + 1 : 2 * k + 2] for k in range(4)]
    moment = []
    for k in range(4):
        moment.append(even[0] if k == 0 else 2.0 * even[k] - even[0])
        moment.append(odd[0] if k == 0 else 2.0 * odd[k] - odd[0])

    def inner_product(i, j):
        return 0.5 * (moment[i + j] + moment[abs(i - j)])

    def energy(i, j):
        shifted = 0.5 * (inner_product(i, j + 1) + inner_product(i, abs(j - 1)))
        return HALF * (shifted + inner_product(i, j))

    low = [[None] * 4 for _ in range(4)]
    diag, inverse, half = [], [], []
    for j in range(4):
        d = energy(j, j)
        value = moment[j]
        for k in range(j):
            d = d - low[j][k] * low[j][k] * diag[k]
            value = value - low[j][k] * half[k]
        diag.append(d)
        half.append(value)
        inverse.append(1.0 / d)
        for i in range(j + 1, 4):
            e = energy(i, j)
            for k in range(j):
                e = e - low[i][k] * low[j][k] * diag[k]
            low[i][j] = e * inverse[j]
    weight = [half[k] * inverse[k] for k in range(4)]
    for i in (2, 1, 0):
        for k in range(i + 1, 4):
            weight[i] = weight[i] - low[k][i] * weight[k]
    turned = jnp.concatenate(weight + [jnp.zeros((4, 128), F32)], axis=0).T
    for k in range(4):
        coef[k] = jnp.broadcast_to(turned[0:32, k : k + 1], (32, 128))
    copies = []
    for c in range(3):
        for n in range(12 * c, 12 * c + 12):
            held[n] = x0[n] + coef[0] * t0[n] + coef[1] * t1[n] + coef[2] * t2[n] + coef[3] * t3[n]
        part = pl.ds(12 * c, 12)
        copies.append(pltpu.make_async_copy(held.at[part], out.at[part], sems.at[c]))
        copies[c].start()
    for copy in copies:
        copy.wait()


def pack_kernel(u, out, held, ready, sems):
    loads, stores = [], []
    for c in range(3):
        part = pl.ds(12 * c, 12)
        loads.append(pltpu.make_async_copy(u.at[part], held.at[part], sems.at[c]))
        loads[c].start()
    for c in range(3):
        loads[c].wait()
        for g in range(3 * c, 3 * c + 3):
            turned = held[4 * g : 4 * g + 4].reshape(128, 128).T
            ready[:, 16 * g : 16 * g + 16, :] = turned.reshape(8, 16, 128)
        part = pl.ds(48 * c, 48)
        stores.append(pltpu.make_async_copy(ready.at[:, part], out.at[:, part], sems.at[3 + c]))
        stores[c].start()
    for copy in stores:
        copy.wait()


def block_turn(blocks):
    part = lax.shift_right_logical(lane_ids(blocks[0].shape), 5)
    rolled = [blocks[0]] + [pltpu.roll(blocks[s], 32 * s, 1) for s in range(1, 4)]
    out = []
    for m in range(4):
        mixed = rolled[-m % 4]
        for t in range(1, 4):
            mixed = jnp.where(part == t, rolled[(t - m) % 4], mixed)
        out.append(pltpu.roll(mixed, 128 - 32 * m, 1) if m else mixed)
    return out


def product3(high, low, table, dim):
    def dot(a, b):
        return lax.dot_general(a, b, (((1,), (dim,)), ((), ())), preferred_element_type=F32)

    return dot(high, table[0]) + dot(high, table[1]) + dot(low, table[0])


def advect_kernel(meta, came, speed, synth, out, high, low, phys, ready, sem):
    for g in range(9):
        for h in range(2):
            pieces = block_turn([came[4 * h + s, 16 * g : 16 * g + 16, :] for s in range(4)])
            for m in range(4):
                n = 16 * (4 * g + m)
                hi, lo = split(pieces[m])
                high[n : n + 16, 128 * h : 128 * h + 128] = hi
                low[n : n + 16, 128 * h : 128 * h + 128] = lo
    for i in range(2):
        part = slice(288 * i, 288 * i + 288)
        phys[part, :] = product3(high[part, :], low[part, :], synth, 1)
    wide = meta[3] == 0
    sx = jnp.where(wide, 2.0, 1.0)
    sy = jnp.where(wide, 1.0, 2.0)
    for h in range(2):
        cols = slice(128 * h, 128 * h + 128)
        u = [[phys[16 * (6 * i + j) : 16 * (6 * i + j) + 16, cols] for j in range(6)] for i in range(6)]
        acc = [[None] * 6 for _ in range(6)]
        for j in range(6):
            g = folded([u[i][j] for i in range(6)], DERIV_FOLD, -1)
            for i in range(6):
                acc[i][j] = sx * (speed[0, 6 * i + j, :, cols] * g[i])
        for i in range(6):
            g = folded(u[i], DERIV_FOLD, -1)
            for j in range(6):
                n = 16 * (6 * i + j)
                total = acc[i][j] + sy * (speed[1, 6 * i + j, :, cols] * g[j])
                hi, lo = split(float(-0.5 * W[i] * W[j]) * total)
                high[n : n + 16, cols] = hi
                low[n : n + 16, cols] = lo
    for i in range(2):
        part = slice(288 * i, 288 * i + 288)
        phys[part, :] = product3(high[part, :], low[part, :], synth, 0)
    for h in range(2):
        q = lane_ids((16, 128)) + 128 * h
        norm = jnp.where((q == 0) | (q == 255), 1.0 / 256, 1.0 / 128)
        cols = slice(128 * h, 128 * h + 128)
        for g in range(9):
            pieces = block_turn(
                [norm * phys[16 * (4 * g + m) : 16 * (4 * g + m) + 16, cols] for m in range(4)]
            )
            for s in range(4):
                ready[4 * h + s, 16 * g : 16 * g + 16, :] = pieces[s]
    copy = pltpu.make_async_copy(ready, out, sem)
    copy.start()
    copy.wait()


def shift_by(array, by):
    count = lax.axis_size("elem")
    return lax.ppermute(array, "elem", [(i, (i + by) % count) for i in range(count)])


def shards(scalar_modes, velocity, viscosity, mortar_links, mortar_sides, layout):
    u = jnp.transpose(scalar_modes, (1, 2, 0, 3)).reshape(36, 32, 128)
    speed = jnp.transpose(velocity, (0, 2, 3, 4, 1)).reshape(2, 36, 16, 256)
    synth = jnp.asarray(split_table(plane_tables(256)))
    place = jnp.stack([lax.axis_index("plane"), lax.axis_index("elem")]).astype(jnp.int32)

    vol, edge = shape(36, 32, 128), shape(48, 128)
    both = shape(96, 128)
    blocks = shape(8, 144, 128)
    packed = call(
        pack_kernel,
        [blocks],
        [VMEM((36, 32, 128), F32), VMEM((8, 144, 128), F32), pltpu.SemaphoreType.DMA((6,))],
        [u],
        [HBM],
        [HBM],
    )[0]
    came = lax.all_to_all(packed, "plane", 0, 0, tiled=True)

    table = shape(36, 8, 128)
    meta, idx, edge_idx, tab, own_c, far_c, edge_own, edge_far = call(
        prep_kernel,
        [
            shape(4, dtype=jnp.int32),
            shape(24, 128, dtype=jnp.int32),
            shape(8, 128, dtype=jnp.int32),
            shape(8, 128),
        ]
        + [table] * 4,
        [],
        [place, mortar_links, mortar_sides, viscosity[None], layout[None]],
        [SMEM] + [VMEM] * 4,
        [SMEM] + [VMEM] * 7,
    )
    head = [meta, idx, tab, own_c, far_c]
    edges = [edge_idx, edge_own, edge_far]

    def run(kernel, outs, scratch, args):
        return call(kernel, outs, scratch, args, [SMEM if a is meta else VMEM for a in args])

    def trade(send_w, send_e):
        return shift_by(send_e, 1), shift_by(send_w, -1)

    base, *sent = call(
        guess_kernel,
        [vol, edge, edge],
        [VMEM((36, 32, 128), F32), pltpu.SemaphoreType.DMA],
        head + [u],
        [SMEM] + [VMEM] * 4 + [HBM],
    )
    came, *sent = lax.optimization_barrier((came, *sent))
    back = call(
        advect_kernel,
        [blocks],
        [
            VMEM((576, 256), BF16),
            VMEM((576, 256), BF16),
            VMEM((576, 256), F32),
            VMEM((8, 144, 128), F32),
            pltpu.SemaphoreType.DMA,
        ],
        [meta, came, speed, synth],
        [SMEM, VMEM, VMEM, VMEM],
        [HBM],
        grant=8,
    )[0]
    back, *sent = lax.optimization_barrier((back, *sent))
    back = lax.all_to_all(back, "plane", 0, 0, tiled=True)
    guess_edge = run(guess_edge_kernel, [shape(48, 128)], [], [*edges, *sent, *trade(*sent)])[0]

    def work(count):
        return [
            VMEM((96, 128), F32),
            VMEM((32, 128 * count), F32),
            VMEM((8, 128), F32),
        ]

    t0, h0, *sent = run(residual_kernel, [vol, vol, edge, edge], [], head + [back, base, guess_edge])
    got = trade(*sent)
    t1, t2, h2, to_w, to_e, keep, part = run(
        two_steps_kernel,
        [vol, vol, vol, edge, edge, both, shape(8, 128)],
        work(5),
        head + edges + [t0, h0, *sent, *got],
    )
    got = trade(to_w, to_e)
    t3, red = run(
        last_steps_kernel,
        [vol, shape(16, 8, 128)],
        work(3),
        head + edges + [t1, t2, h2, to_w, to_e, *got, keep, part],
    )
    red = lax.all_to_all(red, "elem", 0, 0, tiled=True)
    out = call(
        finish_kernel,
        [vol],
        [VMEM((4, 32, 128), F32), VMEM((36, 32, 128), F32), pltpu.SemaphoreType.DMA((3,))],
        [red, u, t0, t1, t2, t3],
        [VMEM] * 6,
        [HBM],
    )[0]
    return jnp.transpose(out.reshape(6, 6, 32, 128), (2, 0, 1, 3))


def solution(mesh):
    placed = (
        P("plane", None, None, "elem"),
        P(None, None, None, None, ("elem", "plane")),
        P("elem"),
        P(None, "elem"),
        P(None, None, "elem"),
        P("elem"),
    )
    return jax.shard_map(
        shards,
        mesh=mesh,
        in_specs=placed,
        out_specs=P("plane", None, None, "elem"),
        check_vma=False,
    )
```

```python
import math

import jax
import jax.numpy as jnp
import ml_dtypes
import numpy as np
from jax import lax
from jax.experimental import pallas as pl
from jax.experimental.pallas import tpu as pltpu
from jax.sharding import PartitionSpec as P

F32 = jnp.float32
BF16 = jnp.bfloat16
PENALTY = 10.0
SPANWISE = 0.0625
VMEM = pltpu.VMEM
SMEM = pltpu.SMEM
HBM = pltpu.HBM
SELF, ANY, LOCAL = 2, 4, 10


def lagrange_at(points, targets):
    out = np.ones((6, 6))
    for row in range(6):
        for col in range(6):
            for other in range(6):
                if other != col:
                    out[row, col] *= (targets[row] - points[other]) / (points[col] - points[other])
    return out


def node_tables():
    root = math.sqrt(7.0)
    outer = math.sqrt(1.0 / 3.0 + 2.0 * root / 21.0)
    inner = math.sqrt(1.0 / 3.0 - 2.0 * root / 21.0)
    points = np.array([-1.0, -outer, -inner, inner, outer, 1.0])
    half = [1.0 / 15.0, (14.0 - root) / 30.0, (14.0 + root) / 30.0]
    weights = np.array(half + half[::-1])
    bary = np.array(
        [1.0 / np.prod([points[c] - points[k] for k in range(6) if k != c]) for c in range(6)]
    )
    deriv = np.zeros((6, 6))
    for i in range(6):
        for j in range(6):
            if i != j:
                deriv[i, j] = bary[j] / bary[i] / (points[i] - points[j])
        deriv[i, i] = -np.sum(deriv[i])
    lower = lagrange_at(points, (points - 1.0) / 2.0)
    upper = lagrange_at(points, (points + 1.0) / 2.0)
    stiff = deriv.T @ (weights[:, None] * deriv)
    return weights, deriv, lower, upper, stiff


W, D, QLO, QHI, K1 = node_tables()
HALVES = [np.eye(6), QLO, QHI]


def plane_tables(count):
    planes = np.arange(count)[:, None]
    coeffs = np.arange(count)[None, :]
    harmonic = (coeffs + 1) // 2
    phase = 2.0 * np.pi * (harmonic * planes % count) / count
    synth = np.where(coeffs == 0, 1.0, np.where(coeffs % 2 == 1, np.cos(phase), np.sin(phase)))
    return synth


def split_table(table):
    table = np.asarray(table, np.float32)
    high = table.astype(ml_dtypes.bfloat16)
    low = (table - high.astype(np.float32)).astype(ml_dtypes.bfloat16)
    return np.stack([high, low])


def fold(matrix):
    plus = (matrix[:3, :3] + matrix[:3, :2:-1]) / 2.0
    minus = (matrix[:3, :3] - matrix[:3, :2:-1]) / 2.0
    return plus, minus


STIFF_FOLD = fold(K1 / W[:, None])
DERIV_FOLD = fold(D)


def folded(values, tables, sign):
    plus, minus = tables
    even = [values[a] + values[5 - a] for a in range(3)]
    odd = [values[a] - values[5 - a] for a in range(3)]
    out = [None] * 6
    for i in range(3):
        e = sum(float(plus[i, a]) * even[a] for a in range(3))
        o = sum(float(minus[i, a]) * odd[a] for a in range(3))
        out[i] = e + o
        out[5 - i] = e - o if sign > 0 else o - e
    return out


def split(value):
    high = value.astype(BF16)
    return high, (value - high.astype(F32)).astype(BF16)


def lane_ids(shape):
    return lax.broadcasted_iota(jnp.int32, shape, len(shape) - 1)


def call(kernel, outs, scratch, operands, spaces, out_spaces=None, grant=3):
    total = sum(int(np.prod(o.shape)) * 4 for o in outs)
    total += sum(int(np.prod(o.shape)) * 4 for o in operands)
    return pl.pallas_call(
        kernel,
        out_shape=outs,
        in_specs=[pl.BlockSpec(memory_space=s) for s in spaces],
        out_specs=[pl.BlockSpec(memory_space=s) for s in out_spaces or [VMEM] * len(outs)],
        scratch_shapes=scratch,
        compiler_params=pltpu.CompilerParams(vmem_limit_bytes=grant * 2**20),
        cost_estimate=pl.CostEstimate(flops=4_000_000, bytes_accessed=total, transcendentals=0),
    )(*[far(a) if s == HBM else a for a, s in zip(operands, spaces)])


def far(array):
    return pltpu.with_memory_space_constraint(array, HBM)


def shape(*dims, dtype=F32):
    return jax.ShapeDtypeStruct(dims, dtype)


def take(value, index):
    return jnp.take_along_axis(value, index, axis=1)


def take_row(value, index):
    wide = jnp.broadcast_to(value, (8, 128)), jnp.broadcast_to(index, (8, 128))
    return take(*wide)[0:1]


def prep_kernel(
    place, links, sides, visc, layout, meta, idx, edge_idx, tab, own_c, far_c, edge_own, edge_far
):
    me = place[1]
    dev = lax.shift_right_logical(links[...], 7)
    loc = jnp.bitwise_and(links[...], 127)
    remote = (dev != me).astype(jnp.int32)
    idx[LOCAL : LOCAL + 8, :] = loc
    own, other = sides[0], sides[1]
    inside = jnp.where(remote > 0, 3, own)
    whole = (inside == 0) & (other == 0)
    second = jnp.bitwise_and(lax.broadcasted_iota(jnp.int32, (8, 128), 0), 1) == 1
    odd_one = jnp.where(inside == 3, 0.0, jnp.where(whole & ~second, 0.0, 1.0))
    meta[0] = place[0]
    meta[1] = place[1]
    meta[2] = jnp.max(odd_one).astype(jnp.int32)
    meta[3] = jnp.max(layout[...].astype(F32)).astype(jnp.int32)
    row = lax.broadcasted_iota(jnp.int32, (128, 128), 0)
    col = lane_ids((128, 128))
    lane = lane_ids((1, 128))
    slot = jnp.bitwise_and(lane, 15)
    listed, present, ranks = [], [], []
    for side in range(2):
        rem = [remote[2 * side + t : 2 * side + t + 1] for t in range(2)]
        far = [loc[2 * side + t : 2 * side + t + 1] for t in range(2)]
        any_rem = jnp.maximum(rem[0], rem[1])
        before = jnp.sum(jnp.where(col < row, any_rem, 0).astype(F32), axis=1, keepdims=True)
        mine = jnp.sum(jnp.where(col == row, any_rem, 0).astype(F32), axis=1, keepdims=True)
        chosen = jnp.where((before == slot.astype(F32)) & (mine > 0.0), 1.0, 0.0)
        listed.append(jnp.sum(chosen * row.astype(F32), axis=0, keepdims=True).astype(jnp.int32))
        present.append(jnp.sum(chosen, axis=0, keepdims=True).astype(jnp.int32))
        idx[side : side + 1, :] = listed[side]
        mine_at = jnp.sum(jnp.where(row == col, before, 0.0), axis=0, keepdims=True)
        mine_at = jnp.where(any_rem > 0, mine_at.astype(jnp.int32), 0)
        idx[SELF + side : SELF + side + 1, :] = mine_at
        idx[ANY + side : ANY + side + 1, :] = any_rem
        named = jnp.where(
            ((far[0] == row) & (rem[0] > 0)) | ((far[1] == row) & (rem[1] > 0)), 1.0, 0.0
        )
        named = jnp.max(named, axis=1, keepdims=True)
        for t in range(2):
            rank = jnp.sum(jnp.where(row < far[t], named, 0.0), axis=0, keepdims=True)
            ranks.append(jnp.where(rem[t] > 0, rank.astype(jnp.int32), 0))
    idx[6:10, :] = jnp.zeros((4, 128), jnp.int32)
    idx[18:24, :] = jnp.zeros((6, 128), jnp.int32)

    west = lane < 64
    base = jnp.bitwise_and(lane, 112)
    element = jnp.where(west, listed[0], listed[1])
    here = jnp.where(west, present[0], present[1]) > 0

    def pick(rows_w, rows_e):
        return jnp.where(west, take_row(rows_w, element), take_row(rows_e, element))

    rank, live, mine, theirs = [], [], [], []
    for t in range(2):
        rank.append(pick(ranks[t], ranks[2 + t]))
        live.append((pick(remote[t : t + 1], remote[2 + t : 3 + t]) > 0) & here)
        mine.append(jnp.where(live[t], pick(own[t : t + 1], own[2 + t : 3 + t]), 3))
        theirs.append(jnp.where(live[t], pick(other[t : t + 1], other[2 + t : 3 + t]), 3))
    first = jnp.full((1, 128), 99, jnp.int32)
    last = jnp.full((1, 128), -1, jnp.int32)
    for t in range(2):
        target = jnp.where(live[t], rank[t], 99)
        for r in range(16):
            hit = take_row(target, base + r) == slot
            first = jnp.where(hit, jnp.minimum(first, 16 * t + r), first)
            last = jnp.where(hit, jnp.maximum(last, 16 * t + r), last)
    exists = [last >= 0, last > first]
    key = [jnp.where(exists[0], first, 0), jnp.where(exists[1], last, 0)]
    back = [base + jnp.bitwise_and(k, 15) for k in key]

    def from_key(k, pair):
        value = jnp.where(key[k] >= 16, take_row(pair[1], back[k]), take_row(pair[0], back[k]))
        return jnp.where(exists[k], value, 3)

    near_own = [from_key(k, theirs) for k in range(2)]
    near_far = [from_key(k, mine) for k in range(2)]
    edge_idx[...] = jnp.zeros((8, 128), jnp.int32)
    for k in range(2):
        edge_idx[k : k + 1, :] = base + rank[k]
        edge_idx[2 + k : 3 + k, :] = back[k]
    none = jnp.full((4, 128), 3, jnp.int32)
    edge_mine = jnp.concatenate([mine[0], mine[1], near_own[0], near_own[1], none], axis=0)
    edge_theirs = jnp.concatenate([theirs[0], theirs[1], near_far[0], near_far[1], none], axis=0)

    nu = visc[...]
    wide = layout[...] == 0
    tab[0:1, :] = nu * jnp.where(wide, 2.0, 0.5)
    tab[1:2, :] = nu * jnp.where(wide, 0.5, 2.0)
    tab[2:3, :] = nu
    for face in range(4):
        tab[3 + face : 4 + face, :] = whole[2 * face : 2 * face + 1].astype(F32)
    tab[7:8, :] = jnp.zeros((1, 128), F32)
    mine_m = [PENALTY * HALVES[o].T @ np.diag(W) @ HALVES[o] for o in range(3)]
    far_m = [
        [-PENALTY * HALVES[o].T @ np.diag(W) @ HALVES[c] for c in range(3)] for o in range(3)
    ]
    for code, facing, own_ref, far_ref in (
        (inside, other, own_c, far_c),
        (edge_mine, edge_theirs, edge_own, edge_far),
    ):
        hot = [(code == o).astype(F32) for o in range(3)]
        pair = [[hot[o] * (facing == c).astype(F32) for c in range(3)] for o in range(3)]
        for a in range(6):
            for b in range(6):
                n = 6 * a + b
                total = sum(float(mine_m[o][a, b]) * hot[o] for o in range(3))
                own_ref[n] = total + pltpu.roll(total, 7, 0)
                far_ref[n] = sum(
                    float(far_m[o][c][a, b]) * pair[o][c] for o in range(3) for c in range(3)
                )


def group_rows(group):
    return pl.ds(pl.multiple_of(group * 8, 8), 8)


def row_of(ref, r):
    return jnp.broadcast_to(ref[r : r + 1, :], (8, 128))


def face_nodes(face):
    return [
        6 * i + j
        for i, j in [
            (0, b) if face == 0 else (5, b) if face == 1 else (b, 0) if face == 2 else (b, 5)
            for b in range(6)
        ]
    ]


def either(meta, loop):
    for plain in (True, False):

        @pl.when((meta[2] == 0) == plain)
        def _(plain=plain):
            lax.fori_loop(
                0, 4, lambda group, carry: loop(group, plain) or carry, 0, unroll=2 if plain else 1
            )


def weighted(factors, values):
    total = float(factors[0]) * values[0]
    for f, v in zip(factors[1:], values[1:]):
        total = total + float(f) * v
    return total


def plain_terms(env, v):
    _, idx, tab, _, _ = env

    def of_face(face):
        active = row_of(tab, 3 + face)
        local = row_of(idx, LOCAL + 2 * face)

        def term(a):
            n, m = face_nodes(face)[a], face_nodes(face ^ 1)[a]
            return (float(PENALTY * W[a]) * active) * (v(n) - take(v(m), local))

        return term

    return [of_face(face) for face in range(4)]


def general_terms(env, v):
    _, idx, _, own_c, far_c = env
    found = []
    for face in range(4):
        mine = [v(n) for n in face_nodes(face)]
        theirs = [
            [take(v(n), row_of(idx, LOCAL + 2 * face + t)) for n in face_nodes(face ^ 1)]
            for t in range(2)
        ]
        values = []
        for a in range(6):
            extra = jnp.zeros((8, 128), F32)
            for b in range(6):
                extra = extra + own_c[6 * a + b, 2 * face : 2 * face + 1, :] * mine[b]
                for t in range(2):
                    s = 2 * face + t
                    extra = extra + far_c[6 * a + b, s : s + 1, :] * theirs[t][b]
            values.append(extra)
        found.append(values.__getitem__)
    return found


def inner(group, env, v_ref, plain, emit):
    meta, _, tab, _, _ = env
    rows = group_rows(group)

    def v(n):
        return v_ref[n, rows, :]

    terms = (plain_terms if plain else general_terms)(env, v)
    q = meta[0] * 32 + group * 8 + lax.broadcasted_iota(jnp.int32, (8, 128), 0)
    harmonic = lax.shift_right_logical(q + 1, 1).astype(F32) * SPANWISE
    cx, cy = row_of(tab, 0), row_of(tab, 1)
    shift = 1.0 + 0.5 * tab[2:3, :] * (harmonic * harmonic)
    plus, minus = STIFF_FOLD
    even = [[v(6 * a + j) + v(30 - 6 * a + j) for a in range(3)] for j in range(6)]
    odd = [[v(6 * a + j) - v(30 - 6 * a + j) for a in range(3)] for j in range(6)]
    for i in range(3):
        e = [weighted(plus[i], even[j]) for j in range(6)]
        o = [weighted(minus[i], odd[j]) for j in range(6)]
        for line in (i, 5 - i):
            mine = [v(6 * line + j) for j in range(6)]
            g = folded(mine, STIFF_FOLD, 1)
            for j in range(6):
                n = 6 * line + j
                gx = e[j] + o[j] if line == i else e[j] - o[j]
                value = float(W[line] * W[j]) * (shift * mine[j] + cx * gx + cy * g[j])
                for face, (at, b) in enumerate(((line == 0, j), (line == 5, j), (j == 0, line), (j == 5, line))):
                    if at:
                        value = value + terms[face](b)
                emit(n, value)


def compact(idx, v_ref, h_ref, send_w, send_e):
    part = lax.shift_right_logical(lane_ids((8, 128)), 4)
    for face, ref in ((0, send_w), (1, send_e)):
        index = row_of(idx, face)
        for b in range(6):
            n = face_nodes(face)[b]
            value = take(v_ref[n, 0:8, :], index)
            for k in range(1, 8):
                source = v_ref if k < 4 else h_ref
                other = take(source[n, 8 * (k % 4) : 8 * (k % 4) + 8, :], index)
                value = jnp.where(part == k, other, value)
            ref[8 * b : 8 * b + 8, :] = value


def outer(group, idx, edge, first):
    found = {}
    for face in range(2):
        lanes = row_of(idx, SELF + face) + (64 * face + 16 * group)
        on = row_of(idx, ANY + face) > 0
        for b in range(6):
            value = take(edge[first + 8 * b : first + 8 * b + 8, :], lanes)
            found[face_nodes(face)[b]] = jnp.where(on, value, 0.0)
    return found


def edge_blocks(ref):
    return [ref[8 * b : 8 * b + 8, :] for b in range(6)]


def merge(to_w, to_e):
    west = lane_ids((8, 128)) < 64
    plain, inner_h = [], []
    for w, e in zip(edge_blocks(to_w), edge_blocks(to_e)):
        plain.append(jnp.where(west, w, pltpu.roll(e, 64, 1)))
        inner_h.append(jnp.where(west, pltpu.roll(w, 64, 1), e))
    return plain, inner_h


def edge_term(edge_idx, edge_own, edge_far, mine, theirs, row):
    near = [[take(t, row_of(edge_idx, row + k)) for t in theirs] for k in range(2)]
    out = []
    for a in range(6):
        chains = [None] * 3
        for b in range(6):
            n = 6 * a + b
            terms = [edge_own[n, row : row + 1, :] * mine[b]]
            terms += [edge_far[n, row + k : row + k + 1, :] * near[k][b] for k in range(2)]
            chains = terms if chains[0] is None else [c + t for c, t in zip(chains, terms)]
        out.append(chains[0] + (chains[1] + chains[2]))
    return out


def store_sums(acc, pad, first, count):
    width = count * 128
    lhs = (
        lax.broadcasted_iota(jnp.int32, (8, width), 0)
        == lax.shift_right_logical(lane_ids((8, width)), 7) + first
    ).astype(F32)
    sums = lax.dot_general(
        lhs, acc[...], (((1,), (1,)), ((), ())),
        precision=lax.Precision.HIGHEST, preferred_element_type=F32,
    )
    pad[...] = jnp.ones((8, 128), F32)
    pad[:, 0:32] = sums


HALF = 10.0


def store(ref, rows):
    def emit(n, value):
        ref[n, rows, :] = value

    return emit


def guess_kernel(meta, idx, tab, own_c, far_c, u_far, out, send_w, send_e, u, sem):
    env = (meta, idx, tab, own_c, far_c)
    copy = pltpu.make_async_copy(u_far, u, sem)
    copy.start()
    copy.wait()

    def loop(group, plain):
        rows = group_rows(group)

        def emit(n, value):
            out[n, rows, :] = float(W[n // 6] * W[n % 6]) * u[n, rows, :] - value

        inner(group, env, u, plain, emit)

    either(meta, loop)
    compact(idx, u, u, send_w, send_e)


def guess_edge_kernel(edge_idx, edge_own, edge_far, to_w, to_e, from_w, from_e, edge):
    mine, _ = merge(to_w, to_e)
    theirs, _ = merge(from_w, from_e)
    for b, value in enumerate(edge_term(edge_idx, edge_own, edge_far, mine, theirs, 0)):
        edge[8 * b : 8 * b + 8, :] = value


def residual_kernel(
    meta, idx, tab, own_c, far_c, back, base, edge, out, h_out, send_w, send_e
):
    env = (meta, idx, tab, own_c, far_c)

    def turn(g, carry):
        part = pl.ds(pl.multiple_of(16 * g, 16), 16)
        turned = back[:, part, :].reshape(128, 128).T
        for m in range(4):
            out[4 * g + m] = base[4 * g + m] + turned[32 * m : 32 * m + 32]
        return carry

    lax.fori_loop(0, 9, turn, 0, unroll=3)

    def loop(group, plain):
        rows = group_rows(group)
        for n, extra in outer(group, idx, edge, 0).items():
            out[n, rows, :] -= extra
        inner(group, env, out, plain, store(h_out, rows))

    either(meta, loop)
    compact(idx, out, h_out, send_w, send_e)


def edge_steps(tables, to_w, to_e, from_w, from_e, before, edge, keep):
    edge_idx, edge_own, edge_far = tables
    mine, mine_h = merge(to_w, to_e)
    theirs, theirs_h = merge(from_w, from_e)
    scale = (1.0 if before is None else 2.0) / HALF
    first = edge_term(edge_idx, edge_own, edge_far, mine, theirs, 0)
    facing = edge_term(edge_idx, edge_own, edge_far, theirs, mine, 2)
    mine_next, theirs_next = [], []
    for b in range(6):
        if before is None:
            mine_next.append(scale * (mine_h[b] + first[b]) - mine[b])
            theirs_next.append(scale * (theirs_h[b] + facing[b]) - theirs[b])
        else:
            old = before[8 * b : 8 * b + 8, :], before[48 + 8 * b : 56 + 8 * b, :]
            mine_next.append(scale * (mine_h[b] + first[b]) - 2.0 * mine[b] - old[0])
            theirs_next.append(scale * (theirs_h[b] + facing[b]) - 2.0 * theirs[b] - old[1])
    second = edge_term(edge_idx, edge_own, edge_far, mine_next, theirs_next, 0)
    for b in range(6):
        edge[8 * b : 8 * b + 8, :] = first[b]
        edge[48 + 8 * b : 56 + 8 * b, :] = second[b]
        if keep is not None:
            keep[8 * b : 8 * b + 8, :] = mine_next[b]
            keep[48 + 8 * b : 56 + 8 * b, :] = theirs_next[b]


def two_steps_kernel(
    meta, idx, tab, own_c, far_c, edge_idx, edge_own, edge_far,
    t0, h0, to_w, to_e, from_w, from_e,
    t1, t2, h2, send_w, send_e, keep, edge,
):
    env = (meta, idx, tab, own_c, far_c)
    tables = (edge_idx, edge_own, edge_far)
    edge_steps(tables, to_w, to_e, from_w, from_e, None, edge, keep)

    def loop(group, plain):
        rows = group_rows(group)
        extra = outer(group, idx, edge, 0)
        for n in range(36):
            image = h0[n, rows, :]
            if n in extra:
                image = image + extra[n]
            t1[n, rows, :] = (1.0 / HALF) * image - t0[n, rows, :]
        extra_next = outer(group, idx, edge, 48)

        def emit(n, image):
            if n in extra_next:
                image = image + extra_next[n]
            t2[n, rows, :] = (2.0 / HALF) * image - 2.0 * t1[n, rows, :] - t0[n, rows, :]

        inner(group, env, t1, plain, emit)
        inner(group, env, t2, plain, store(h2, rows))

    either(meta, loop)
    compact(idx, t2, h2, send_w, send_e)


def sums_kernel(t0, t1, t2, part, acc, pad):
    def body(group, carry):
        rows = group_rows(group)
        sums = [jnp.zeros((8, 128), F32)] * 5
        for n in range(36):
            a, b, c = t0[n, rows, :], t1[n, rows, :], t2[n, rows, :]
            for k, term in enumerate((a * a, a * b, b * b, b * c, c * c)):
                sums[k] = sums[k] + term
        for k in range(5):
            acc[rows, 128 * k : 128 * k + 128] = sums[k]
        return carry

    lax.fori_loop(0, 4, body, 0)
    store_sums(acc, pad, 0, 5)
    part[...] = pad[...]


def last_steps_kernel(
    meta, idx, tab, own_c, far_c, edge_idx, edge_own, edge_far,
    t1, t2, h2, to_w, to_e, from_w, from_e, keep, part,
    t3, red, edge, acc, pad,
):
    env = (meta, idx, tab, own_c, far_c)
    tables = (edge_idx, edge_own, edge_far)
    edge_steps(tables, to_w, to_e, from_w, from_e, keep, edge, None)

    def loop(group, plain):
        rows = group_rows(group)
        extra = outer(group, idx, edge, 0)
        sums = [jnp.zeros((8, 128), F32)] * 3
        for n in range(36):
            image = h2[n, rows, :]
            if n in extra:
                image = image + extra[n]
            c = t2[n, rows, :]
            d = (2.0 / HALF) * image - 2.0 * c - t1[n, rows, :]
            t3[n, rows, :] = d
            sums[0] = sums[0] + c * d
            sums[1] = sums[1] + d * d
        extra_next = outer(group, idx, edge, 48)

        def emit(n, image):
            if n in extra_next:
                image = image + extra_next[n]
            d = t3[n, rows, :]
            sums[2] = sums[2] + d * ((2.0 / HALF) * image - 2.0 * d - t2[n, rows, :])

        inner(group, env, t3, plain, emit)
        for k in range(3):
            acc[rows, 128 * k : 128 * k + 128] = sums[k]

    either(meta, loop)
    store_sums(acc, pad, 5, 3)
    row = lax.broadcasted_iota(jnp.int32, (8, 128), 0)
    mixed = jnp.where(row < 5, part[...], pad[...])
    for k in range(16):
        red[k] = mixed


def finish_kernel(red, x0, t0, t1, t2, t3, out, coef, held, sems):
    total = red[0]
    for k in range(1, 16):
        total = total + red[k]
    even = [total[2 * k : 2 * k + 1] for k in range(4)]
    odd = [total[2 * k + 1 : 2 * k + 2] for k in range(4)]
    moment = []
    for k in range(4):
        moment.append(even[0] if k == 0 else 2.0 * even[k] - even[0])
        moment.append(odd[0] if k == 0 else 2.0 * odd[k] - odd[0])

    def inner_product(i, j):
        return 0.5 * (moment[i + j] + moment[abs(i - j)])

    def energy(i, j):
        shifted = 0.5 * (inner_product(i, j + 1) + inner_product(i, abs(j - 1)))
        return HALF * (shifted + inner_product(i, j))

    low = [[None] * 4 for _ in range(4)]
    diag, inverse, half = [], [], []
    for j in range(4):
        d = energy(j, j)
        value = moment[j]
        for k in range(j):
            d = d - low[j][k] * low[j][k] * diag[k]
            value = value - low[j][k] * half[k]
        diag.append(d)
        half.append(value)
        inverse.append(1.0 / d)
        for i in range(j + 1, 4):
            e = energy(i, j)
            for k in range(j):
                e = e - low[i][k] * low[j][k] * diag[k]
            low[i][j] = e * inverse[j]
    weight = [half[k] * inverse[k] for k in range(4)]
    for i in (2, 1, 0):
        for k in range(i + 1, 4):
            weight[i] = weight[i] - low[k][i] * weight[k]
    turned = jnp.concatenate(weight + [jnp.zeros((4, 128), F32)], axis=0).T
    for k in range(4):
        coef[k] = jnp.broadcast_to(turned[0:32, k : k + 1], (32, 128))
    copies = []
    for c in range(3):
        def add(n, carry):
            terms = coef[0] * t0[n] + coef[1] * t1[n] + coef[2] * t2[n] + coef[3] * t3[n]
            held[n] = x0[n] + terms
            return carry

        lax.fori_loop(12 * c, 12 * c + 12, add, 0, unroll=3)
        part = pl.ds(12 * c, 12)
        copies.append(pltpu.make_async_copy(held.at[part], out.at[part], sems.at[c]))
        copies[c].start()
    for copy in copies:
        copy.wait()


def pack_kernel(u, out, held, ready, sems):
    loads, stores = [], []
    for c in range(3):
        part = pl.ds(12 * c, 12)
        loads.append(pltpu.make_async_copy(u.at[part], held.at[part], sems.at[c]))
        loads[c].start()
    for c in range(3):
        loads[c].wait()

        def turn(g, carry):
            turned = held[pl.ds(4 * g, 4)].reshape(128, 128).T
            part = pl.ds(pl.multiple_of(16 * g, 16), 16)
            ready[:, part, :] = turned.reshape(8, 16, 128)
            return carry

        lax.fori_loop(3 * c, 3 * c + 3, turn, 0)
        part = pl.ds(48 * c, 48)
        stores.append(pltpu.make_async_copy(ready.at[:, part], out.at[:, part], sems.at[3 + c]))
        stores[c].start()
    for copy in stores:
        copy.wait()


def block_turn(blocks):
    part = lax.shift_right_logical(lane_ids(blocks[0].shape), 5)
    rolled = [blocks[0]] + [pltpu.roll(blocks[s], 32 * s, 1) for s in range(1, 4)]
    out = []
    for m in range(4):
        mixed = rolled[-m % 4]
        for t in range(1, 4):
            mixed = jnp.where(part == t, rolled[(t - m) % 4], mixed)
        out.append(pltpu.roll(mixed, 128 - 32 * m, 1) if m else mixed)
    return out


def product3(high, low, table, dim):
    def dot(a, b):
        return lax.dot_general(a, b, (((1,), (dim,)), ((), ())), preferred_element_type=F32)

    return dot(high, table[0]) + dot(high, table[1]) + dot(low, table[0])


def advect_kernel(meta, came, speed, synth, out, high, low, phys, grad, ready, sems):
    def rows_of(n):
        return pl.ds(pl.multiple_of(16 * n, 16), 16)

    def spread(g, carry):
        for h in range(2):
            cols = slice(128 * h, 128 * h + 128)
            pieces = block_turn([came[4 * h + s, rows_of(g), :] for s in range(4)])
            for m in range(4):
                hi, lo = split(pieces[m])
                high[rows_of(4 * g + m), cols] = hi
                low[rows_of(4 * g + m), cols] = lo
        return carry

    lax.fori_loop(0, 9, spread, 0)
    for i in range(2):
        part = slice(288 * i, 288 * i + 288)
        phys[part, :] = product3(high[part, :], low[part, :], synth, 1)
    wide = meta[3] == 0
    sx = jnp.where(wide, 2.0, 1.0)
    sy = jnp.where(wide, 1.0, 2.0)

    def advance(h, carry):
        cols = pl.ds(pl.multiple_of(128 * h, 128), 128)

        def line_x(j, carry):
            g = folded([phys[rows_of(6 * i + j), cols] for i in range(6)], DERIV_FOLD, -1)
            for i in range(6):
                n = 6 * i + j
                grad[rows_of(n), cols] = sx * (speed[0, n, :, cols] * g[i])
            return carry

        lax.fori_loop(0, 6, line_x, 0, unroll=2)
        for i in range(6):
            g = folded([phys[rows_of(6 * i + j), cols] for j in range(6)], DERIV_FOLD, -1)
            for j in range(6):
                n = 6 * i + j
                total = grad[rows_of(n), cols] + sy * (speed[1, n, :, cols] * g[j])
                hi, lo = split(float(-0.5 * W[i] * W[j]) * total)
                high[rows_of(n), cols] = hi
                low[rows_of(n), cols] = lo
        return carry

    lax.fori_loop(0, 2, advance, 0)
    for i in range(2):
        part = slice(288 * i, 288 * i + 288)
        phys[part, :] = product3(high[part, :], low[part, :], synth, 0)

    def gather(g, carry):
        for h in range(2):
            q = lane_ids((16, 128)) + 128 * h
            norm = jnp.where((q == 0) | (q == 255), 1.0 / 256, 1.0 / 128)
            cols = slice(128 * h, 128 * h + 128)
            pieces = block_turn([norm * phys[rows_of(4 * g + m), cols] for m in range(4)])
            for s in range(4):
                ready[4 * h + s, rows_of(g), :] = pieces[s]
        return carry

    copies = []
    for c in range(3):
        lax.fori_loop(3 * c, 3 * c + 3, gather, 0)
        part = pl.ds(48 * c, 48)
        copies.append(pltpu.make_async_copy(ready.at[:, part], out.at[:, part], sems.at[c]))
        copies[c].start()
    for copy in copies:
        copy.wait()


def shift_by(array, by):
    count = lax.axis_size("elem")
    return lax.ppermute(array, "elem", [(i, (i + by) % count) for i in range(count)])


def shards(scalar_modes, velocity, viscosity, mortar_links, mortar_sides, layout):
    u = jnp.transpose(scalar_modes, (1, 2, 0, 3)).reshape(36, 32, 128)
    speed = jnp.transpose(velocity, (0, 2, 3, 4, 1)).reshape(2, 36, 16, 256)
    synth = jnp.asarray(split_table(plane_tables(256)))
    place = jnp.stack([lax.axis_index("plane"), lax.axis_index("elem")]).astype(jnp.int32)

    vol, edge = shape(36, 32, 128), shape(48, 128)
    both = shape(96, 128)
    blocks = shape(8, 144, 128)
    packed = call(
        pack_kernel,
        [blocks],
        [VMEM((36, 32, 128), F32), VMEM((8, 144, 128), F32), pltpu.SemaphoreType.DMA((6,))],
        [u],
        [HBM],
        [HBM],
    )[0]
    came = lax.all_to_all(packed, "plane", 0, 0, tiled=True)

    table = shape(36, 8, 128)
    meta, idx, edge_idx, tab, own_c, far_c, edge_own, edge_far = call(
        prep_kernel,
        [
            shape(4, dtype=jnp.int32),
            shape(24, 128, dtype=jnp.int32),
            shape(8, 128, dtype=jnp.int32),
            shape(8, 128),
        ]
        + [table] * 4,
        [],
        [place, mortar_links, mortar_sides, viscosity[None], layout[None]],
        [SMEM] + [VMEM] * 4,
        [SMEM] + [VMEM] * 7,
    )
    head = [meta, idx, tab, own_c, far_c]
    edges = [edge_idx, edge_own, edge_far]

    def run(kernel, outs, scratch, args):
        return call(kernel, outs, scratch, args, [SMEM if a is meta else VMEM for a in args])

    def trade(send_w, send_e):
        return shift_by(send_e, 1), shift_by(send_w, -1)

    base, *sent = call(
        guess_kernel,
        [vol, edge, edge],
        [VMEM((36, 32, 128), F32), pltpu.SemaphoreType.DMA],
        head + [u],
        [SMEM] + [VMEM] * 4 + [HBM],
    )
    came, *sent = lax.optimization_barrier((came, *sent))
    back = call(
        advect_kernel,
        [blocks],
        [
            VMEM((576, 256), BF16),
            VMEM((576, 256), BF16),
            VMEM((576, 256), F32),
            VMEM((576, 256), F32),
            VMEM((8, 144, 128), F32),
            pltpu.SemaphoreType.DMA((3,)),
        ],
        [meta, came, speed, synth],
        [SMEM, VMEM, VMEM, VMEM],
        [HBM],
        grant=8,
    )[0]
    back, *sent = lax.optimization_barrier((back, *sent))
    back = lax.all_to_all(back, "plane", 0, 0, tiled=True)
    guess_edge = run(guess_edge_kernel, [shape(48, 128)], [], [*edges, *sent, *trade(*sent)])[0]

    def work(count):
        return [
            VMEM((96, 128), F32),
            VMEM((32, 128 * count), F32),
            VMEM((8, 128), F32),
        ]

    t0, h0, *sent = run(residual_kernel, [vol, vol, edge, edge], [], head + [back, base, guess_edge])
    got = trade(*sent)
    t1, t2, h2, to_w, to_e, keep = run(
        two_steps_kernel,
        [vol, vol, vol, edge, edge, both],
        [VMEM((96, 128), F32)],
        head + edges + [t0, h0, *sent, *got],
    )
    got = trade(to_w, to_e)
    part = run(sums_kernel, [shape(8, 128)], work(5)[1:], [t0, t1, t2])[0]
    t3, red = run(
        last_steps_kernel,
        [vol, shape(16, 8, 128)],
        work(3),
        head + edges + [t1, t2, h2, to_w, to_e, *got, keep, part],
    )
    red = lax.all_to_all(red, "elem", 0, 0, tiled=True)
    out = call(
        finish_kernel,
        [vol],
        [VMEM((4, 32, 128), F32), VMEM((36, 32, 128), F32), pltpu.SemaphoreType.DMA((3,))],
        [red, u, t0, t1, t2, t3],
        [VMEM] * 6,
        [HBM],
    )[0]
    return jnp.transpose(out.reshape(6, 6, 32, 128), (2, 0, 1, 3))


def solution(mesh):
    placed = (
        P("plane", None, None, "elem"),
        P(None, None, None, None, ("elem", "plane")),
        P("elem"),
        P(None, "elem"),
        P(None, None, "elem"),
        P("elem"),
    )
    return jax.shard_map(
        shards,
        mesh=mesh,
        in_specs=placed,
        out_specs=P("plane", None, None, "elem"),
        check_vma=False,
    )
```

```python
import math

import jax
import jax.numpy as jnp
import ml_dtypes
import numpy as np
from jax import lax
from jax.experimental import pallas as pl
from jax.experimental.pallas import tpu as pltpu
from jax.sharding import PartitionSpec as P

F32 = jnp.float32
BF16 = jnp.bfloat16
PENALTY = 10.0
SPANWISE = 0.0625
VMEM = pltpu.VMEM
SMEM = pltpu.SMEM
HBM = pltpu.HBM
MIXED = 7
SELF, ANY, FIRST, LAYOUT, LOCAL = 2, 4, 6, 7, 10


def lagrange_at(points, targets):
    out = np.ones((6, 6))
    for row in range(6):
        for col in range(6):
            for other in range(6):
                if other != col:
                    out[row, col] *= (targets[row] - points[other]) / (points[col] - points[other])
    return out


def node_tables():
    root = math.sqrt(7.0)
    outer = math.sqrt(1.0 / 3.0 + 2.0 * root / 21.0)
    inner = math.sqrt(1.0 / 3.0 - 2.0 * root / 21.0)
    points = np.array([-1.0, -outer, -inner, inner, outer, 1.0])
    half = [1.0 / 15.0, (14.0 - root) / 30.0, (14.0 + root) / 30.0]
    weights = np.array(half + half[::-1])
    bary = np.array(
        [1.0 / np.prod([points[c] - points[k] for k in range(6) if k != c]) for c in range(6)]
    )
    deriv = np.zeros((6, 6))
    for i in range(6):
        for j in range(6):
            if i != j:
                deriv[i, j] = bary[j] / bary[i] / (points[i] - points[j])
        deriv[i, i] = -np.sum(deriv[i])
    lower = lagrange_at(points, (points - 1.0) / 2.0)
    upper = lagrange_at(points, (points + 1.0) / 2.0)
    stiff = deriv.T @ (weights[:, None] * deriv)
    return weights, deriv, lower, upper, stiff


W, D, QLO, QHI, K1 = node_tables()
HALVES = [np.eye(6), QLO, QHI]


def plane_tables(count):
    planes = np.arange(count)[:, None]
    coeffs = np.arange(count)[None, :]
    harmonic = (coeffs + 1) // 2
    phase = 2.0 * np.pi * (harmonic * planes % count) / count
    synth = np.where(coeffs == 0, 1.0, np.where(coeffs % 2 == 1, np.cos(phase), np.sin(phase)))
    return synth


def split_table(table):
    table = np.asarray(table, np.float32)
    high = table.astype(ml_dtypes.bfloat16)
    low = (table - high.astype(np.float32)).astype(ml_dtypes.bfloat16)
    return np.stack([high, low])


def fold(matrix):
    plus = (matrix[:3, :3] + matrix[:3, :2:-1]) / 2.0
    minus = (matrix[:3, :3] - matrix[:3, :2:-1]) / 2.0
    return plus, minus


STIFF_FOLD = fold(K1 / W[:, None])
DERIV_FOLD = fold(D)


def folded(values, tables, sign):
    plus, minus = tables
    even = [values[a] + values[5 - a] for a in range(3)]
    odd = [values[a] - values[5 - a] for a in range(3)]
    out = [None] * 6
    for i in range(3):
        e = sum(float(plus[i, a]) * even[a] for a in range(3))
        o = sum(float(minus[i, a]) * odd[a] for a in range(3))
        out[i] = e + o
        out[5 - i] = e - o if sign > 0 else o - e
    return out


def split(value):
    high = value.astype(BF16)
    return high, (value - high.astype(F32)).astype(BF16)


def lane_ids(shape):
    return lax.broadcasted_iota(jnp.int32, shape, len(shape) - 1)


def call(kernel, outs, scratch, operands, spaces, out_spaces=None, grant=3):
    total = sum(int(np.prod(o.shape)) * 4 for o in outs)
    total += sum(int(np.prod(o.shape)) * 4 for o in operands)
    return pl.pallas_call(
        kernel,
        out_shape=outs,
        in_specs=[pl.BlockSpec(memory_space=s) for s in spaces],
        out_specs=[pl.BlockSpec(memory_space=s) for s in out_spaces or [VMEM] * len(outs)],
        scratch_shapes=scratch,
        compiler_params=pltpu.CompilerParams(vmem_limit_bytes=grant * 2**20),
        cost_estimate=pl.CostEstimate(flops=4_000_000, bytes_accessed=total, transcendentals=0),
    )(*[far(a) if s == HBM else a for a, s in zip(operands, spaces)])


def far(array):
    return pltpu.with_memory_space_constraint(array, HBM)


def shape(*dims, dtype=F32):
    return jax.ShapeDtypeStruct(dims, dtype)


def take(value, index):
    return jnp.take_along_axis(value, index, axis=1)


def take_row(value, index):
    wide = jnp.broadcast_to(value, (8, 128)), jnp.broadcast_to(index, (8, 128))
    return take(*wide)[0:1]


def prep_kernel(
    place, links, sides, visc, layout, idx, edge_idx, tab, own_c, far_c, edge_own, edge_far
):
    me = place[1]
    dev = lax.shift_right_logical(links[...], 7)
    loc = jnp.bitwise_and(links[...], 127)
    remote = (dev != me).astype(jnp.int32)
    idx[LOCAL : LOCAL + 8, :] = loc
    own, other = sides[0], sides[1]
    inside = jnp.where(remote > 0, 3, own)
    whole = (inside == 0) & (other == 0)
    second = jnp.bitwise_and(lax.broadcasted_iota(jnp.int32, (8, 128), 0), 1) == 1
    odd_one = jnp.where(inside == 3, 0.0, jnp.where(whole & ~second, 0.0, 1.0))
    idx[FIRST : FIRST + 1, :] = jnp.full((1, 128), 32 * place[0], jnp.int32)
    idx[LAYOUT : LAYOUT + 1, :] = layout[...]
    row = lax.broadcasted_iota(jnp.int32, (128, 128), 0)
    col = lane_ids((128, 128))
    lane = lane_ids((1, 128))
    slot = jnp.bitwise_and(lane, 15)
    listed, present, ranks = [], [], []
    for side in range(2):
        rem = [remote[2 * side + t : 2 * side + t + 1] for t in range(2)]
        far = [loc[2 * side + t : 2 * side + t + 1] for t in range(2)]
        any_rem = jnp.maximum(rem[0], rem[1])
        before = jnp.sum(jnp.where(col < row, any_rem, 0).astype(F32), axis=1, keepdims=True)
        mine = jnp.sum(jnp.where(col == row, any_rem, 0).astype(F32), axis=1, keepdims=True)
        chosen = jnp.where((before == slot.astype(F32)) & (mine > 0.0), 1.0, 0.0)
        listed.append(jnp.sum(chosen * row.astype(F32), axis=0, keepdims=True).astype(jnp.int32))
        present.append(jnp.sum(chosen, axis=0, keepdims=True).astype(jnp.int32))
        idx[side : side + 1, :] = listed[side]
        mine_at = jnp.sum(jnp.where(row == col, before, 0.0), axis=0, keepdims=True)
        mine_at = jnp.where(any_rem > 0, mine_at.astype(jnp.int32), 0)
        idx[SELF + side : SELF + side + 1, :] = mine_at
        idx[ANY + side : ANY + side + 1, :] = any_rem
        named = jnp.where(
            ((far[0] == row) & (rem[0] > 0)) | ((far[1] == row) & (rem[1] > 0)), 1.0, 0.0
        )
        named = jnp.max(named, axis=1, keepdims=True)
        for t in range(2):
            rank = jnp.sum(jnp.where(row < far[t], named, 0.0), axis=0, keepdims=True)
            ranks.append(jnp.where(rem[t] > 0, rank.astype(jnp.int32), 0))
    idx[8:10, :] = jnp.zeros((2, 128), jnp.int32)
    idx[18:24, :] = jnp.zeros((6, 128), jnp.int32)

    west = lane < 64
    base = jnp.bitwise_and(lane, 112)
    element = jnp.where(west, listed[0], listed[1])
    here = jnp.where(west, present[0], present[1]) > 0

    def pick(rows_w, rows_e):
        return jnp.where(west, take_row(rows_w, element), take_row(rows_e, element))

    rank, live, mine, theirs = [], [], [], []
    for t in range(2):
        rank.append(pick(ranks[t], ranks[2 + t]))
        live.append((pick(remote[t : t + 1], remote[2 + t : 3 + t]) > 0) & here)
        mine.append(jnp.where(live[t], pick(own[t : t + 1], own[2 + t : 3 + t]), 3))
        theirs.append(jnp.where(live[t], pick(other[t : t + 1], other[2 + t : 3 + t]), 3))
    first = jnp.full((1, 128), 99, jnp.int32)
    last = jnp.full((1, 128), -1, jnp.int32)
    for t in range(2):
        target = jnp.where(live[t], rank[t], 99)
        for r in range(16):
            hit = take_row(target, base + r) == slot
            first = jnp.where(hit, jnp.minimum(first, 16 * t + r), first)
            last = jnp.where(hit, jnp.maximum(last, 16 * t + r), last)
    exists = [last >= 0, last > first]
    key = [jnp.where(exists[0], first, 0), jnp.where(exists[1], last, 0)]
    back = [base + jnp.bitwise_and(k, 15) for k in key]

    def from_key(k, pair):
        value = jnp.where(key[k] >= 16, take_row(pair[1], back[k]), take_row(pair[0], back[k]))
        return jnp.where(exists[k], value, 3)

    near_own = [from_key(k, theirs) for k in range(2)]
    near_far = [from_key(k, mine) for k in range(2)]
    edge_idx[...] = jnp.zeros((8, 128), jnp.int32)
    for k in range(2):
        edge_idx[k : k + 1, :] = base + rank[k]
        edge_idx[2 + k : 3 + k, :] = back[k]
    none = jnp.full((4, 128), 3, jnp.int32)
    edge_mine = jnp.concatenate([mine[0], mine[1], near_own[0], near_own[1], none], axis=0)
    edge_theirs = jnp.concatenate([theirs[0], theirs[1], near_far[0], near_far[1], none], axis=0)

    nu = visc[...]
    wide = layout[...] == 0
    tab[0:1, :] = nu * jnp.where(wide, 2.0, 0.5)
    tab[1:2, :] = nu * jnp.where(wide, 0.5, 2.0)
    tab[2:3, :] = nu
    for face in range(4):
        tab[3 + face : 4 + face, :] = whole[2 * face : 2 * face + 1].astype(F32)
    tab[MIXED : MIXED + 1, :] = jnp.max(odd_one, axis=0, keepdims=True)
    mine_m = [PENALTY * HALVES[o].T @ np.diag(W) @ HALVES[o] for o in range(3)]
    far_m = [
        [-PENALTY * HALVES[o].T @ np.diag(W) @ HALVES[c] for c in range(3)] for o in range(3)
    ]
    for code, facing, own_ref, far_ref in (
        (inside, other, own_c, far_c),
        (edge_mine, edge_theirs, edge_own, edge_far),
    ):
        hot = [(code == o).astype(F32) for o in range(3)]
        pair = [[hot[o] * (facing == c).astype(F32) for c in range(3)] for o in range(3)]
        for a in range(6):
            for b in range(6):
                n = 6 * a + b
                total = sum(float(mine_m[o][a, b]) * hot[o] for o in range(3))
                own_ref[n] = total + pltpu.roll(total, 7, 0)
                far_ref[n] = sum(
                    float(far_m[o][c][a, b]) * pair[o][c] for o in range(3) for c in range(3)
                )


def group_rows(group):
    return pl.ds(pl.multiple_of(group * 8, 8), 8)


def row_of(ref, r):
    return jnp.broadcast_to(ref[r : r + 1, :], (8, 128))


def face_nodes(face):
    return [
        6 * i + j
        for i, j in [
            (0, b) if face == 0 else (5, b) if face == 1 else (b, 0) if face == 2 else (b, 5)
            for b in range(6)
        ]
    ]


def either(tab, loop):
    mixed = jnp.max(tab[MIXED : MIXED + 1, :]) > 0.5
    for plain in (True, False):

        @pl.when(mixed != plain)
        def _(plain=plain):
            lax.fori_loop(
                0, 4, lambda group, carry: loop(group, plain) or carry, 0, unroll=2 if plain else 1
            )


def weighted(factors, values):
    total = float(factors[0]) * values[0]
    for f, v in zip(factors[1:], values[1:]):
        total = total + float(f) * v
    return total


def plain_terms(env, v):
    idx, tab, _, _ = env

    def of_face(face):
        active = row_of(tab, 3 + face)
        local = row_of(idx, LOCAL + 2 * face)

        def term(a):
            n, m = face_nodes(face)[a], face_nodes(face ^ 1)[a]
            return (float(PENALTY * W[a]) * active) * (v(n) - take(v(m), local))

        return term

    return [of_face(face) for face in range(4)]


def general_terms(env, v):
    idx, _, own_c, far_c = env
    found = []
    for face in range(4):
        mine = [v(n) for n in face_nodes(face)]
        theirs = [
            [take(v(n), row_of(idx, LOCAL + 2 * face + t)) for n in face_nodes(face ^ 1)]
            for t in range(2)
        ]
        values = []
        for a in range(6):
            extra = jnp.zeros((8, 128), F32)
            for b in range(6):
                extra = extra + own_c[6 * a + b, 2 * face : 2 * face + 1, :] * mine[b]
                for t in range(2):
                    s = 2 * face + t
                    extra = extra + far_c[6 * a + b, s : s + 1, :] * theirs[t][b]
            values.append(extra)
        found.append(values.__getitem__)
    return found


def inner(group, env, v_ref, plain, emit):
    idx, tab, _, _ = env
    rows = group_rows(group)

    def v(n):
        return v_ref[n, rows, :]

    terms = (plain_terms if plain else general_terms)(env, v)
    q = row_of(idx, FIRST) + group * 8 + lax.broadcasted_iota(jnp.int32, (8, 128), 0)
    harmonic = lax.shift_right_logical(q + 1, 1).astype(F32) * SPANWISE
    cx, cy = row_of(tab, 0), row_of(tab, 1)
    shift = 1.0 + 0.5 * tab[2:3, :] * (harmonic * harmonic)
    plus, minus = STIFF_FOLD
    even = [[v(6 * a + j) + v(30 - 6 * a + j) for a in range(3)] for j in range(6)]
    odd = [[v(6 * a + j) - v(30 - 6 * a + j) for a in range(3)] for j in range(6)]
    for i in range(3):
        e = [weighted(plus[i], even[j]) for j in range(6)]
        o = [weighted(minus[i], odd[j]) for j in range(6)]
        for line in (i, 5 - i):
            mine = [v(6 * line + j) for j in range(6)]
            g = folded(mine, STIFF_FOLD, 1)
            for j in range(6):
                n = 6 * line + j
                gx = e[j] + o[j] if line == i else e[j] - o[j]
                value = float(W[line] * W[j]) * (shift * mine[j] + cx * gx + cy * g[j])
                for face, (at, b) in enumerate(((line == 0, j), (line == 5, j), (j == 0, line), (j == 5, line))):
                    if at:
                        value = value + terms[face](b)
                emit(n, value)


def compact(idx, v_ref, h_ref, send_w, send_e):
    part = lax.shift_right_logical(lane_ids((8, 128)), 4)
    for face, ref in ((0, send_w), (1, send_e)):
        index = row_of(idx, face)
        for b in range(6):
            n = face_nodes(face)[b]
            value = take(v_ref[n, 0:8, :], index)
            for k in range(1, 8):
                source = v_ref if k < 4 else h_ref
                other = take(source[n, 8 * (k % 4) : 8 * (k % 4) + 8, :], index)
                value = jnp.where(part == k, other, value)
            ref[8 * b : 8 * b + 8, :] = value


def outer(group, idx, edge, first):
    found = {}
    for face in range(2):
        lanes = row_of(idx, SELF + face) + (64 * face + 16 * group)
        on = row_of(idx, ANY + face) > 0
        for b in range(6):
            value = take(edge[first + 8 * b : first + 8 * b + 8, :], lanes)
            found[face_nodes(face)[b]] = jnp.where(on, value, 0.0)
    return found


def edge_blocks(ref):
    return [ref[8 * b : 8 * b + 8, :] for b in range(6)]


def merge(to_w, to_e):
    west = lane_ids((8, 128)) < 64
    plain, inner_h = [], []
    for w, e in zip(edge_blocks(to_w), edge_blocks(to_e)):
        plain.append(jnp.where(west, w, pltpu.roll(e, 64, 1)))
        inner_h.append(jnp.where(west, pltpu.roll(w, 64, 1), e))
    return plain, inner_h


def edge_term(edge_idx, edge_own, edge_far, mine, theirs, row):
    near = [[take(t, row_of(edge_idx, row + k)) for t in theirs] for k in range(2)]
    out = []
    for a in range(6):
        chains = [None] * 3
        for b in range(6):
            n = 6 * a + b
            terms = [edge_own[n, row : row + 1, :] * mine[b]]
            terms += [edge_far[n, row + k : row + k + 1, :] * near[k][b] for k in range(2)]
            chains = terms if chains[0] is None else [c + t for c, t in zip(chains, terms)]
        out.append(chains[0] + (chains[1] + chains[2]))
    return out


def store_sums(acc, pad, first, count):
    width = count * 128
    lhs = (
        lax.broadcasted_iota(jnp.int32, (8, width), 0)
        == lax.shift_right_logical(lane_ids((8, width)), 7) + first
    ).astype(F32)
    sums = lax.dot_general(
        lhs, acc[...], (((1,), (1,)), ((), ())),
        precision=lax.Precision.HIGHEST, preferred_element_type=F32,
    )
    pad[...] = jnp.ones((8, 128), F32)
    pad[:, 0:32] = sums


HALF = 10.0


def store(ref, rows):
    def emit(n, value):
        ref[n, rows, :] = value

    return emit


def guess_kernel(idx, tab, own_c, far_c, u_far, out, send_w, send_e, u, sem):
    env = (idx, tab, own_c, far_c)
    copy = pltpu.make_async_copy(u_far, u, sem)
    copy.start()
    copy.wait()

    def loop(group, plain):
        rows = group_rows(group)

        def emit(n, value):
            out[n, rows, :] = float(W[n // 6] * W[n % 6]) * u[n, rows, :] - value

        inner(group, env, u, plain, emit)

    either(tab, loop)
    compact(idx, u, u, send_w, send_e)


def guess_edge_kernel(edge_idx, edge_own, edge_far, to_w, to_e, from_w, from_e, edge):
    mine, _ = merge(to_w, to_e)
    theirs, _ = merge(from_w, from_e)
    for b, value in enumerate(edge_term(edge_idx, edge_own, edge_far, mine, theirs, 0)):
        edge[8 * b : 8 * b + 8, :] = value


def residual_kernel(
    idx, tab, own_c, far_c, back, base, edge, out, h_out, send_w, send_e
):
    env = (idx, tab, own_c, far_c)

    def turn(g, carry):
        part = pl.ds(pl.multiple_of(16 * g, 16), 16)
        turned = back[:, part, :].reshape(128, 128).T
        for m in range(4):
            out[4 * g + m] = base[4 * g + m] + turned[32 * m : 32 * m + 32]
        return carry

    lax.fori_loop(0, 9, turn, 0, unroll=3)

    def loop(group, plain):
        rows = group_rows(group)
        for n, extra in outer(group, idx, edge, 0).items():
            out[n, rows, :] -= extra
        inner(group, env, out, plain, store(h_out, rows))

    either(tab, loop)
    compact(idx, out, h_out, send_w, send_e)


def edge_steps(tables, to_w, to_e, from_w, from_e, before, edge, keep):
    edge_idx, edge_own, edge_far = tables
    mine, mine_h = merge(to_w, to_e)
    theirs, theirs_h = merge(from_w, from_e)
    scale = (1.0 if before is None else 2.0) / HALF
    first = edge_term(edge_idx, edge_own, edge_far, mine, theirs, 0)
    facing = edge_term(edge_idx, edge_own, edge_far, theirs, mine, 2)
    mine_next, theirs_next = [], []
    for b in range(6):
        if before is None:
            mine_next.append(scale * (mine_h[b] + first[b]) - mine[b])
            theirs_next.append(scale * (theirs_h[b] + facing[b]) - theirs[b])
        else:
            old = before[8 * b : 8 * b + 8, :], before[48 + 8 * b : 56 + 8 * b, :]
            mine_next.append(scale * (mine_h[b] + first[b]) - 2.0 * mine[b] - old[0])
            theirs_next.append(scale * (theirs_h[b] + facing[b]) - 2.0 * theirs[b] - old[1])
    second = edge_term(edge_idx, edge_own, edge_far, mine_next, theirs_next, 0)
    for b in range(6):
        edge[8 * b : 8 * b + 8, :] = first[b]
        edge[48 + 8 * b : 56 + 8 * b, :] = second[b]
        if keep is not None:
            keep[8 * b : 8 * b + 8, :] = mine_next[b]
            keep[48 + 8 * b : 56 + 8 * b, :] = theirs_next[b]


def two_steps_kernel(
    idx, tab, own_c, far_c, edge_idx, edge_own, edge_far,
    t0, h0, to_w, to_e, from_w, from_e,
    t1, t2, h2, send_w, send_e, keep, edge,
):
    env = (idx, tab, own_c, far_c)
    tables = (edge_idx, edge_own, edge_far)
    edge_steps(tables, to_w, to_e, from_w, from_e, None, edge, keep)

    def loop(group, plain):
        rows = group_rows(group)
        extra = outer(group, idx, edge, 0)
        for n in range(36):
            image = h0[n, rows, :]
            if n in extra:
                image = image + extra[n]
            t1[n, rows, :] = (1.0 / HALF) * image - t0[n, rows, :]
        extra_next = outer(group, idx, edge, 48)

        def emit(n, image):
            if n in extra_next:
                image = image + extra_next[n]
            t2[n, rows, :] = (2.0 / HALF) * image - 2.0 * t1[n, rows, :] - t0[n, rows, :]

        inner(group, env, t1, plain, emit)
        inner(group, env, t2, plain, store(h2, rows))

    either(tab, loop)
    compact(idx, t2, h2, send_w, send_e)


def sums_kernel(t0, t1, t2, part, acc, pad):
    def body(group, carry):
        rows = group_rows(group)
        sums = [jnp.zeros((8, 128), F32)] * 5
        for n in range(36):
            a, b, c = t0[n, rows, :], t1[n, rows, :], t2[n, rows, :]
            for k, term in enumerate((a * a, a * b, b * b, b * c, c * c)):
                sums[k] = sums[k] + term
        for k in range(5):
            acc[rows, 128 * k : 128 * k + 128] = sums[k]
        return carry

    lax.fori_loop(0, 4, body, 0)
    store_sums(acc, pad, 0, 5)
    part[...] = pad[...]


def last_steps_kernel(
    idx, tab, own_c, far_c, edge_idx, edge_own, edge_far,
    t1, t2, h2, to_w, to_e, from_w, from_e, keep, part,
    t3, red, edge, acc, pad,
):
    env = (idx, tab, own_c, far_c)
    tables = (edge_idx, edge_own, edge_far)
    edge_steps(tables, to_w, to_e, from_w, from_e, keep, edge, None)

    def loop(group, plain):
        rows = group_rows(group)
        extra = outer(group, idx, edge, 0)
        sums = [jnp.zeros((8, 128), F32)] * 3
        for n in range(36):
            image = h2[n, rows, :]
            if n in extra:
                image = image + extra[n]
            c = t2[n, rows, :]
            d = (2.0 / HALF) * image - 2.0 * c - t1[n, rows, :]
            t3[n, rows, :] = d
            sums[0] = sums[0] + c * d
            sums[1] = sums[1] + d * d
        extra_next = outer(group, idx, edge, 48)

        def emit(n, image):
            if n in extra_next:
                image = image + extra_next[n]
            d = t3[n, rows, :]
            sums[2] = sums[2] + d * ((2.0 / HALF) * image - 2.0 * d - t2[n, rows, :])

        inner(group, env, t3, plain, emit)
        for k in range(3):
            acc[rows, 128 * k : 128 * k + 128] = sums[k]

    either(tab, loop)
    store_sums(acc, pad, 5, 3)
    row = lax.broadcasted_iota(jnp.int32, (8, 128), 0)
    mixed = jnp.where(row < 5, part[...], pad[...])
    for k in range(16):
        red[k] = mixed


def finish_kernel(red, x0, t0, t1, t2, t3, out, coef, held, sems):
    total = red[0]
    for k in range(1, 16):
        total = total + red[k]
    even = [total[2 * k : 2 * k + 1] for k in range(4)]
    odd = [total[2 * k + 1 : 2 * k + 2] for k in range(4)]
    moment = []
    for k in range(4):
        moment.append(even[0] if k == 0 else 2.0 * even[k] - even[0])
        moment.append(odd[0] if k == 0 else 2.0 * odd[k] - odd[0])

    def inner_product(i, j):
        return 0.5 * (moment[i + j] + moment[abs(i - j)])

    def energy(i, j):
        shifted = 0.5 * (inner_product(i, j + 1) + inner_product(i, abs(j - 1)))
        return HALF * (shifted + inner_product(i, j))

    low = [[None] * 4 for _ in range(4)]
    diag, inverse, half = [], [], []
    for j in range(4):
        d = energy(j, j)
        value = moment[j]
        for k in range(j):
            d = d - low[j][k] * low[j][k] * diag[k]
            value = value - low[j][k] * half[k]
        diag.append(d)
        half.append(value)
        inverse.append(1.0 / d)
        for i in range(j + 1, 4):
            e = energy(i, j)
            for k in range(j):
                e = e - low[i][k] * low[j][k] * diag[k]
            low[i][j] = e * inverse[j]
    weight = [half[k] * inverse[k] for k in range(4)]
    for i in (2, 1, 0):
        for k in range(i + 1, 4):
            weight[i] = weight[i] - low[k][i] * weight[k]
    turned = jnp.concatenate(weight + [jnp.zeros((4, 128), F32)], axis=0).T
    for k in range(4):
        coef[k] = jnp.broadcast_to(turned[0:32, k : k + 1], (32, 128))
    copies = []
    for c in range(3):
        def add(n, carry):
            terms = coef[0] * t0[n] + coef[1] * t1[n] + coef[2] * t2[n] + coef[3] * t3[n]
            held[n] = x0[n] + terms
            return carry

        lax.fori_loop(12 * c, 12 * c + 12, add, 0, unroll=3)
        part = pl.ds(12 * c, 12)
        copies.append(pltpu.make_async_copy(held.at[part], out.at[part], sems.at[c]))
        copies[c].start()
    for copy in copies:
        copy.wait()


def pack_kernel(u, out, held, ready, sems):
    loads, stores = [], []
    for c in range(3):
        part = pl.ds(12 * c, 12)
        loads.append(pltpu.make_async_copy(u.at[part], held.at[part], sems.at[c]))
        loads[c].start()
    for c in range(3):
        loads[c].wait()
        for g in range(3 * c, 3 * c + 3):
            turned = held[4 * g : 4 * g + 4].reshape(128, 128).T
            ready[:, 16 * g : 16 * g + 16, :] = turned.reshape(8, 16, 128)
        part = pl.ds(48 * c, 48)
        stores.append(pltpu.make_async_copy(ready.at[:, part], out.at[:, part], sems.at[3 + c]))
        stores[c].start()
    for copy in stores:
        copy.wait()


def block_turn(blocks):
    part = lax.shift_right_logical(lane_ids(blocks[0].shape), 5)
    rolled = [blocks[0]] + [pltpu.roll(blocks[s], 32 * s, 1) for s in range(1, 4)]
    out = []
    for m in range(4):
        mixed = rolled[-m % 4]
        for t in range(1, 4):
            mixed = jnp.where(part == t, rolled[(t - m) % 4], mixed)
        out.append(pltpu.roll(mixed, 128 - 32 * m, 1) if m else mixed)
    return out


def product3(high, low, table, dim):
    def dot(a, b):
        return lax.dot_general(a, b, (((1,), (dim,)), ((), ())), preferred_element_type=F32)

    return dot(high, table[0]) + dot(high, table[1]) + dot(low, table[0])


def advect_kernel(idx, came, speed, synth, out, high, low, phys, ready, sem):
    for g in range(9):
        for h in range(2):
            pieces = block_turn([came[4 * h + s, 16 * g : 16 * g + 16, :] for s in range(4)])
            for m in range(4):
                n = 16 * (4 * g + m)
                hi, lo = split(pieces[m])
                high[n : n + 16, 128 * h : 128 * h + 128] = hi
                low[n : n + 16, 128 * h : 128 * h + 128] = lo
    for i in range(2):
        part = slice(288 * i, 288 * i + 288)
        phys[part, :] = product3(high[part, :], low[part, :], synth, 1)
    wide = jnp.broadcast_to(idx[LAYOUT : LAYOUT + 1, :], (16, 128)) == 0
    sx = jnp.where(wide, 2.0, 1.0)
    sy = jnp.where(wide, 1.0, 2.0)
    for h in range(2):
        cols = slice(128 * h, 128 * h + 128)
        u = [[phys[16 * (6 * i + j) : 16 * (6 * i + j) + 16, cols] for j in range(6)] for i in range(6)]
        acc = [[None] * 6 for _ in range(6)]
        for j in range(6):
            g = folded([u[i][j] for i in range(6)], DERIV_FOLD, -1)
            for i in range(6):
                acc[i][j] = sx * (speed[0, 6 * i + j, :, cols] * g[i])
        for i in range(6):
            g = folded(u[i], DERIV_FOLD, -1)
            for j in range(6):
                n = 16 * (6 * i + j)
                total = acc[i][j] + sy * (speed[1, 6 * i + j, :, cols] * g[j])
                hi, lo = split(float(-0.5 * W[i] * W[j]) * total)
                high[n : n + 16, cols] = hi
                low[n : n + 16, cols] = lo
    for i in range(2):
        part = slice(288 * i, 288 * i + 288)
        phys[part, :] = product3(high[part, :], low[part, :], synth, 0)
    for h in range(2):
        q = lane_ids((16, 128)) + 128 * h
        norm = jnp.where((q == 0) | (q == 255), 1.0 / 256, 1.0 / 128)
        cols = slice(128 * h, 128 * h + 128)
        for g in range(9):
            pieces = block_turn(
                [norm * phys[16 * (4 * g + m) : 16 * (4 * g + m) + 16, cols] for m in range(4)]
            )
            for s in range(4):
                ready[4 * h + s, 16 * g : 16 * g + 16, :] = pieces[s]
    copy = pltpu.make_async_copy(ready, out, sem)
    copy.start()
    copy.wait()


def shift_by(array, by):
    count = lax.axis_size("elem")
    return lax.ppermute(array, "elem", [(i, (i + by) % count) for i in range(count)])


def shards(scalar_modes, velocity, viscosity, mortar_links, mortar_sides, layout):
    u = jnp.transpose(scalar_modes, (1, 2, 0, 3)).reshape(36, 32, 128)
    speed = jnp.transpose(velocity, (0, 2, 3, 4, 1)).reshape(2, 36, 16, 256)
    synth = jnp.asarray(split_table(plane_tables(256)))
    place = jnp.stack([lax.axis_index("plane"), lax.axis_index("elem")]).astype(jnp.int32)

    vol, edge = shape(36, 32, 128), shape(48, 128)
    both = shape(96, 128)
    blocks = shape(8, 144, 128)
    packed = call(
        pack_kernel,
        [blocks],
        [VMEM((36, 32, 128), F32), VMEM((8, 144, 128), F32), pltpu.SemaphoreType.DMA((6,))],
        [u],
        [HBM],
        [HBM],
    )[0]
    came = lax.all_to_all(packed, "plane", 0, 0, tiled=True)

    table = shape(36, 8, 128)
    idx, edge_idx, tab, own_c, far_c, edge_own, edge_far = call(
        prep_kernel,
        [
            shape(24, 128, dtype=jnp.int32),
            shape(8, 128, dtype=jnp.int32),
            shape(8, 128),
        ]
        + [table] * 4,
        [],
        [place, mortar_links, mortar_sides, viscosity[None], layout[None]],
        [SMEM] + [VMEM] * 4,
    )
    head = [idx, tab, own_c, far_c]
    edges = [edge_idx, edge_own, edge_far]

    def run(kernel, outs, scratch, args):
        return call(kernel, outs, scratch, args, [VMEM] * len(args))

    def trade(send_w, send_e):
        return shift_by(send_e, 1), shift_by(send_w, -1)

    base, *sent = call(
        guess_kernel,
        [vol, edge, edge],
        [VMEM((36, 32, 128), F32), pltpu.SemaphoreType.DMA],
        head + [u],
        [VMEM] * 4 + [HBM],
    )
    came, *sent = lax.optimization_barrier((came, *sent))
    back = call(
        advect_kernel,
        [blocks],
        [
            VMEM((576, 256), BF16),
            VMEM((576, 256), BF16),
            VMEM((576, 256), F32),
            VMEM((8, 144, 128), F32),
            pltpu.SemaphoreType.DMA,
        ],
        [idx, came, speed, synth],
        [VMEM] * 4,
        [HBM],
        grant=8,
    )[0]
    back, *sent = lax.optimization_barrier((back, *sent))
    back = lax.all_to_all(back, "plane", 0, 0, tiled=True)
    guess_edge = run(guess_edge_kernel, [shape(48, 128)], [], [*edges, *sent, *trade(*sent)])[0]

    def work(count):
        return [
            VMEM((96, 128), F32),
            VMEM((32, 128 * count), F32),
            VMEM((8, 128), F32),
        ]

    t0, h0, *sent = run(residual_kernel, [vol, vol, edge, edge], [], head + [back, base, guess_edge])
    got = trade(*sent)
    t1, t2, h2, to_w, to_e, keep = run(
        two_steps_kernel,
        [vol, vol, vol, edge, edge, both],
        [VMEM((96, 128), F32)],
        head + edges + [t0, h0, *sent, *got],
    )
    got = trade(to_w, to_e)
    part = run(sums_kernel, [shape(8, 128)], work(5)[1:], [t0, t1, t2])[0]
    t3, red = run(
        last_steps_kernel,
        [vol, shape(16, 8, 128)],
        work(3),
        head + edges + [t1, t2, h2, to_w, to_e, *got, keep, part],
    )
    red = lax.all_to_all(red, "elem", 0, 0, tiled=True)
    out = call(
        finish_kernel,
        [vol],
        [VMEM((4, 32, 128), F32), VMEM((36, 32, 128), F32), pltpu.SemaphoreType.DMA((3,))],
        [red, u, t0, t1, t2, t3],
        [VMEM] * 6,
        [HBM],
    )[0]
    return jnp.transpose(out.reshape(6, 6, 32, 128), (2, 0, 1, 3))


def solution(mesh):
    placed = (
        P("plane", None, None, "elem"),
        P(None, None, None, None, ("elem", "plane")),
        P("elem"),
        P(None, "elem"),
        P(None, None, "elem"),
        P("elem"),
    )
    return jax.shard_map(
        shards,
        mesh=mesh,
        in_specs=placed,
        out_specs=P("plane", None, None, "elem"),
        check_vma=False,
    )
```

```python
import math

import jax
import jax.numpy as jnp
import ml_dtypes
import numpy as np
from jax import lax
from jax.experimental import pallas as pl
from jax.experimental.pallas import tpu as pltpu
from jax.sharding import PartitionSpec as P

F32 = jnp.float32
BF16 = jnp.bfloat16
PENALTY = 10.0
SPANWISE = 0.0625
VMEM = pltpu.VMEM
SMEM = pltpu.SMEM
HBM = pltpu.HBM
MIXED = 7
SELF, ANY, FIRST, LAYOUT, LOCAL = 2, 4, 6, 7, 10


def lagrange_at(points, targets):
    out = np.ones((6, 6))
    for row in range(6):
        for col in range(6):
            for other in range(6):
                if other != col:
                    out[row, col] *= (targets[row] - points[other]) / (points[col] - points[other])
    return out


def node_tables():
    root = math.sqrt(7.0)
    outer = math.sqrt(1.0 / 3.0 + 2.0 * root / 21.0)
    inner = math.sqrt(1.0 / 3.0 - 2.0 * root / 21.0)
    points = np.array([-1.0, -outer, -inner, inner, outer, 1.0])
    half = [1.0 / 15.0, (14.0 - root) / 30.0, (14.0 + root) / 30.0]
    weights = np.array(half + half[::-1])
    bary = np.array(
        [1.0 / np.prod([points[c] - points[k] for k in range(6) if k != c]) for c in range(6)]
    )
    deriv = np.zeros((6, 6))
    for i in range(6):
        for j in range(6):
            if i != j:
                deriv[i, j] = bary[j] / bary[i] / (points[i] - points[j])
        deriv[i, i] = -np.sum(deriv[i])
    lower = lagrange_at(points, (points - 1.0) / 2.0)
    upper = lagrange_at(points, (points + 1.0) / 2.0)
    stiff = deriv.T @ (weights[:, None] * deriv)
    return weights, deriv, lower, upper, stiff


W, D, QLO, QHI, K1 = node_tables()
HALVES = [np.eye(6), QLO, QHI]


def plane_tables(count):
    planes = np.arange(count)[:, None]
    coeffs = np.arange(count)[None, :]
    harmonic = (coeffs + 1) // 2
    phase = 2.0 * np.pi * (harmonic * planes % count) / count
    synth = np.where(coeffs == 0, 1.0, np.where(coeffs % 2 == 1, np.cos(phase), np.sin(phase)))
    return synth


def split_table(table):
    table = np.asarray(table, np.float32)
    high = table.astype(ml_dtypes.bfloat16)
    low = (table - high.astype(np.float32)).astype(ml_dtypes.bfloat16)
    return np.stack([high, low])


def fold(matrix):
    plus = (matrix[:3, :3] + matrix[:3, :2:-1]) / 2.0
    minus = (matrix[:3, :3] - matrix[:3, :2:-1]) / 2.0
    return plus, minus


STIFF_FOLD = fold(K1 / W[:, None])
DERIV_FOLD = fold(D)


def folded(values, tables, sign):
    plus, minus = tables
    even = [values[a] + values[5 - a] for a in range(3)]
    odd = [values[a] - values[5 - a] for a in range(3)]
    out = [None] * 6
    for i in range(3):
        e = sum(float(plus[i, a]) * even[a] for a in range(3))
        o = sum(float(minus[i, a]) * odd[a] for a in range(3))
        out[i] = e + o
        out[5 - i] = e - o if sign > 0 else o - e
    return out


def split(value):
    high = value.astype(BF16)
    return high, (value - high.astype(F32)).astype(BF16)


def lane_ids(shape):
    return lax.broadcasted_iota(jnp.int32, shape, len(shape) - 1)


def call(kernel, outs, scratch, operands, spaces, out_spaces=None, grant=3):
    total = sum(int(np.prod(o.shape)) * 4 for o in outs)
    total += sum(int(np.prod(o.shape)) * 4 for o in operands)
    return pl.pallas_call(
        kernel,
        out_shape=outs,
        in_specs=[pl.BlockSpec(memory_space=s) for s in spaces],
        out_specs=[pl.BlockSpec(memory_space=s) for s in out_spaces or [VMEM] * len(outs)],
        scratch_shapes=scratch,
        compiler_params=pltpu.CompilerParams(vmem_limit_bytes=grant * 2**20),
        cost_estimate=pl.CostEstimate(flops=4_000_000, bytes_accessed=total, transcendentals=0),
    )(*[far(a) if s == HBM else a for a, s in zip(operands, spaces)])


def far(array):
    return pltpu.with_memory_space_constraint(array, HBM)


def shape(*dims, dtype=F32):
    return jax.ShapeDtypeStruct(dims, dtype)


def take(value, index):
    return jnp.take_along_axis(value, index, axis=1)


def take_row(value, index):
    wide = jnp.broadcast_to(value, (8, 128)), jnp.broadcast_to(index, (8, 128))
    return take(*wide)[0:1]


def build_tables(
    links, sides, visc, layout, idx, edge_idx, tab, own_c, far_c, edge_own, edge_far
):
    me = lax.axis_index("elem")
    dev = lax.shift_right_logical(links[...], 7)
    loc = jnp.bitwise_and(links[...], 127)
    remote = (dev != me).astype(jnp.int32)
    idx[LOCAL : LOCAL + 8, :] = loc
    own, other = sides[0], sides[1]
    inside = jnp.where(remote > 0, 3, own)
    whole = (inside == 0) & (other == 0)
    second = jnp.bitwise_and(lax.broadcasted_iota(jnp.int32, (8, 128), 0), 1) == 1
    odd_one = jnp.where(inside == 3, 0.0, jnp.where(whole & ~second, 0.0, 1.0))
    idx[FIRST : FIRST + 1, :] = jnp.full((1, 128), 32 * lax.axis_index("plane"), jnp.int32)
    idx[LAYOUT : LAYOUT + 1, :] = layout[...]
    row = lax.broadcasted_iota(jnp.int32, (128, 128), 0)
    col = lane_ids((128, 128))
    lane = lane_ids((1, 128))
    slot = jnp.bitwise_and(lane, 15)
    listed, present, ranks = [], [], []
    for side in range(2):
        rem = [remote[2 * side + t : 2 * side + t + 1] for t in range(2)]
        far = [loc[2 * side + t : 2 * side + t + 1] for t in range(2)]
        any_rem = jnp.maximum(rem[0], rem[1])
        before = jnp.sum(jnp.where(col < row, any_rem, 0).astype(F32), axis=1, keepdims=True)
        mine = jnp.sum(jnp.where(col == row, any_rem, 0).astype(F32), axis=1, keepdims=True)
        chosen = jnp.where((before == slot.astype(F32)) & (mine > 0.0), 1.0, 0.0)
        listed.append(jnp.sum(chosen * row.astype(F32), axis=0, keepdims=True).astype(jnp.int32))
        present.append(jnp.sum(chosen, axis=0, keepdims=True).astype(jnp.int32))
        idx[side : side + 1, :] = listed[side]
        mine_at = jnp.sum(jnp.where(row == col, before, 0.0), axis=0, keepdims=True)
        mine_at = jnp.where(any_rem > 0, mine_at.astype(jnp.int32), 0)
        idx[SELF + side : SELF + side + 1, :] = mine_at
        idx[ANY + side : ANY + side + 1, :] = any_rem
        named = jnp.where(
            ((far[0] == row) & (rem[0] > 0)) | ((far[1] == row) & (rem[1] > 0)), 1.0, 0.0
        )
        named = jnp.max(named, axis=1, keepdims=True)
        for t in range(2):
            rank = jnp.sum(jnp.where(row < far[t], named, 0.0), axis=0, keepdims=True)
            ranks.append(jnp.where(rem[t] > 0, rank.astype(jnp.int32), 0))
    idx[8:10, :] = jnp.zeros((2, 128), jnp.int32)
    idx[18:24, :] = jnp.zeros((6, 128), jnp.int32)

    west = lane < 64
    base = jnp.bitwise_and(lane, 112)
    element = jnp.where(west, listed[0], listed[1])
    here = jnp.where(west, present[0], present[1]) > 0

    def pick(rows_w, rows_e):
        return jnp.where(west, take_row(rows_w, element), take_row(rows_e, element))

    rank, live, mine, theirs = [], [], [], []
    for t in range(2):
        rank.append(pick(ranks[t], ranks[2 + t]))
        live.append((pick(remote[t : t + 1], remote[2 + t : 3 + t]) > 0) & here)
        mine.append(jnp.where(live[t], pick(own[t : t + 1], own[2 + t : 3 + t]), 3))
        theirs.append(jnp.where(live[t], pick(other[t : t + 1], other[2 + t : 3 + t]), 3))
    first = jnp.full((1, 128), 99, jnp.int32)
    last = jnp.full((1, 128), -1, jnp.int32)
    for t in range(2):
        target = jnp.where(live[t], rank[t], 99)
        for r in range(16):
            hit = take_row(target, base + r) == slot
            first = jnp.where(hit, jnp.minimum(first, 16 * t + r), first)
            last = jnp.where(hit, jnp.maximum(last, 16 * t + r), last)
    exists = [last >= 0, last > first]
    key = [jnp.where(exists[0], first, 0), jnp.where(exists[1], last, 0)]
    back = [base + jnp.bitwise_and(k, 15) for k in key]

    def from_key(k, pair):
        value = jnp.where(key[k] >= 16, take_row(pair[1], back[k]), take_row(pair[0], back[k]))
        return jnp.where(exists[k], value, 3)

    near_own = [from_key(k, theirs) for k in range(2)]
    near_far = [from_key(k, mine) for k in range(2)]
    edge_idx[...] = jnp.zeros((8, 128), jnp.int32)
    for k in range(2):
        edge_idx[k : k + 1, :] = base + rank[k]
        edge_idx[2 + k : 3 + k, :] = back[k]
    none = jnp.full((4, 128), 3, jnp.int32)
    edge_mine = jnp.concatenate([mine[0], mine[1], near_own[0], near_own[1], none], axis=0)
    edge_theirs = jnp.concatenate([theirs[0], theirs[1], near_far[0], near_far[1], none], axis=0)

    nu = visc[...]
    wide = layout[...] == 0
    tab[0:1, :] = nu * jnp.where(wide, 2.0, 0.5)
    tab[1:2, :] = nu * jnp.where(wide, 0.5, 2.0)
    tab[2:3, :] = nu
    for face in range(4):
        tab[3 + face : 4 + face, :] = whole[2 * face : 2 * face + 1].astype(F32)
    tab[MIXED : MIXED + 1, :] = jnp.max(odd_one, axis=0, keepdims=True)
    mine_m = [PENALTY * HALVES[o].T @ np.diag(W) @ HALVES[o] for o in range(3)]
    far_m = [
        [-PENALTY * HALVES[o].T @ np.diag(W) @ HALVES[c] for c in range(3)] for o in range(3)
    ]
    for code, facing, own_ref, far_ref in (
        (inside, other, own_c, far_c),
        (edge_mine, edge_theirs, edge_own, edge_far),
    ):
        hot = [(code == o).astype(F32) for o in range(3)]
        pair = [[hot[o] * (facing == c).astype(F32) for c in range(3)] for o in range(3)]
        for a in range(6):
            for b in range(6):
                n = 6 * a + b
                total = sum(float(mine_m[o][a, b]) * hot[o] for o in range(3))
                own_ref[n] = total + pltpu.roll(total, 7, 0)
                far_ref[n] = sum(
                    float(far_m[o][c][a, b]) * pair[o][c] for o in range(3) for c in range(3)
                )


def group_rows(group):
    return pl.ds(pl.multiple_of(group * 8, 8), 8)


def row_of(ref, r):
    return jnp.broadcast_to(ref[r : r + 1, :], (8, 128))


def face_nodes(face):
    return [
        6 * i + j
        for i, j in [
            (0, b) if face == 0 else (5, b) if face == 1 else (b, 0) if face == 2 else (b, 5)
            for b in range(6)
        ]
    ]


def either(tab, loop):
    mixed = jnp.max(tab[MIXED : MIXED + 1, :]) > 0.5
    for plain in (True, False):

        @pl.when(mixed != plain)
        def _(plain=plain):
            lax.fori_loop(
                0, 4, lambda group, carry: loop(group, plain) or carry, 0, unroll=2 if plain else 1
            )


def weighted(factors, values):
    total = float(factors[0]) * values[0]
    for f, v in zip(factors[1:], values[1:]):
        total = total + float(f) * v
    return total


def plain_terms(env, v):
    idx, tab, _, _ = env

    def of_face(face):
        active = row_of(tab, 3 + face)
        local = row_of(idx, LOCAL + 2 * face)

        def term(a):
            n, m = face_nodes(face)[a], face_nodes(face ^ 1)[a]
            return (float(PENALTY * W[a]) * active) * (v(n) - take(v(m), local))

        return term

    return [of_face(face) for face in range(4)]


def general_terms(env, v):
    idx, _, own_c, far_c = env
    found = []
    for face in range(4):
        mine = [v(n) for n in face_nodes(face)]
        theirs = [
            [take(v(n), row_of(idx, LOCAL + 2 * face + t)) for n in face_nodes(face ^ 1)]
            for t in range(2)
        ]
        values = []
        for a in range(6):
            extra = jnp.zeros((8, 128), F32)
            for b in range(6):
                extra = extra + own_c[6 * a + b, 2 * face : 2 * face + 1, :] * mine[b]
                for t in range(2):
                    s = 2 * face + t
                    extra = extra + far_c[6 * a + b, s : s + 1, :] * theirs[t][b]
            values.append(extra)
        found.append(values.__getitem__)
    return found


def inner(group, env, v_ref, plain, emit):
    idx, tab, _, _ = env
    rows = group_rows(group)

    def v(n):
        return v_ref[n, rows, :]

    terms = (plain_terms if plain else general_terms)(env, v)
    q = row_of(idx, FIRST) + group * 8 + lax.broadcasted_iota(jnp.int32, (8, 128), 0)
    harmonic = lax.shift_right_logical(q + 1, 1).astype(F32) * SPANWISE
    cx, cy = row_of(tab, 0), row_of(tab, 1)
    shift = 1.0 + 0.5 * tab[2:3, :] * (harmonic * harmonic)
    plus, minus = STIFF_FOLD
    even = [[v(6 * a + j) + v(30 - 6 * a + j) for a in range(3)] for j in range(6)]
    odd = [[v(6 * a + j) - v(30 - 6 * a + j) for a in range(3)] for j in range(6)]
    for i in range(3):
        e = [weighted(plus[i], even[j]) for j in range(6)]
        o = [weighted(minus[i], odd[j]) for j in range(6)]
        for line in (i, 5 - i):
            mine = [v(6 * line + j) for j in range(6)]
            g = folded(mine, STIFF_FOLD, 1)
            for j in range(6):
                n = 6 * line + j
                gx = e[j] + o[j] if line == i else e[j] - o[j]
                value = float(W[line] * W[j]) * (shift * mine[j] + cx * gx + cy * g[j])
                for face, (at, b) in enumerate(((line == 0, j), (line == 5, j), (j == 0, line), (j == 5, line))):
                    if at:
                        value = value + terms[face](b)
                emit(n, value)


def compact(idx, v_ref, h_ref, send_w, send_e):
    part = lax.shift_right_logical(lane_ids((8, 128)), 4)
    for face, ref in ((0, send_w), (1, send_e)):
        index = row_of(idx, face)
        for b in range(6):
            n = face_nodes(face)[b]
            value = take(v_ref[n, 0:8, :], index)
            for k in range(1, 8):
                source = v_ref if k < 4 else h_ref
                other = take(source[n, 8 * (k % 4) : 8 * (k % 4) + 8, :], index)
                value = jnp.where(part == k, other, value)
            ref[8 * b : 8 * b + 8, :] = value


def outer(group, idx, edge, first):
    found = {}
    for face in range(2):
        lanes = row_of(idx, SELF + face) + (64 * face + 16 * group)
        on = row_of(idx, ANY + face) > 0
        for b in range(6):
            value = take(edge[first + 8 * b : first + 8 * b + 8, :], lanes)
            found[face_nodes(face)[b]] = jnp.where(on, value, 0.0)
    return found


def edge_blocks(ref):
    return [ref[8 * b : 8 * b + 8, :] for b in range(6)]


def merge(to_w, to_e):
    west = lane_ids((8, 128)) < 64
    plain, inner_h = [], []
    for w, e in zip(edge_blocks(to_w), edge_blocks(to_e)):
        plain.append(jnp.where(west, w, pltpu.roll(e, 64, 1)))
        inner_h.append(jnp.where(west, pltpu.roll(w, 64, 1), e))
    return plain, inner_h


def edge_term(edge_idx, edge_own, edge_far, mine, theirs, row):
    near = [[take(t, row_of(edge_idx, row + k)) for t in theirs] for k in range(2)]
    out = []
    for a in range(6):
        chains = [None] * 3
        for b in range(6):
            n = 6 * a + b
            terms = [edge_own[n, row : row + 1, :] * mine[b]]
            terms += [edge_far[n, row + k : row + k + 1, :] * near[k][b] for k in range(2)]
            chains = terms if chains[0] is None else [c + t for c, t in zip(chains, terms)]
        out.append(chains[0] + (chains[1] + chains[2]))
    return out


def store_sums(acc, pad, first, count):
    width = count * 128
    lhs = (
        lax.broadcasted_iota(jnp.int32, (8, width), 0)
        == lax.shift_right_logical(lane_ids((8, width)), 7) + first
    ).astype(F32)
    sums = lax.dot_general(
        lhs, acc[...], (((1,), (1,)), ((), ())),
        precision=lax.Precision.HIGHEST, preferred_element_type=F32,
    )
    pad[...] = jnp.ones((8, 128), F32)
    pad[:, 0:32] = sums


HALF = 10.0


def store(ref, rows):
    def emit(n, value):
        ref[n, rows, :] = value

    return emit


def guess_kernel(
    links, sides, visc, layout, u_far,
    idx, edge_idx, tab, own_c, far_c, edge_own, edge_far, out, send_w, send_e, u, sem,
):
    copy = pltpu.make_async_copy(u_far, u, sem)
    copy.start()
    build_tables(
        links, sides, visc, layout, idx, edge_idx, tab, own_c, far_c, edge_own, edge_far
    )
    copy.wait()
    env = (idx, tab, own_c, far_c)

    def loop(group, plain):
        rows = group_rows(group)

        def emit(n, value):
            out[n, rows, :] = float(W[n // 6] * W[n % 6]) * u[n, rows, :] - value

        inner(group, env, u, plain, emit)

    either(tab, loop)
    compact(idx, u, u, send_w, send_e)


def guess_edge_kernel(edge_idx, edge_own, edge_far, to_w, to_e, from_w, from_e, edge):
    mine, _ = merge(to_w, to_e)
    theirs, _ = merge(from_w, from_e)
    for b, value in enumerate(edge_term(edge_idx, edge_own, edge_far, mine, theirs, 0)):
        edge[8 * b : 8 * b + 8, :] = value


def residual_kernel(
    idx, tab, own_c, far_c, back, base, edge, out, h_out, send_w, send_e
):
    env = (idx, tab, own_c, far_c)

    def turn(g, carry):
        part = pl.ds(pl.multiple_of(16 * g, 16), 16)
        turned = back[:, part, :].reshape(128, 128).T
        for m in range(4):
            out[4 * g + m] = base[4 * g + m] + turned[32 * m : 32 * m + 32]
        return carry

    lax.fori_loop(0, 9, turn, 0, unroll=3)

    def loop(group, plain):
        rows = group_rows(group)
        for n, extra in outer(group, idx, edge, 0).items():
            out[n, rows, :] -= extra
        inner(group, env, out, plain, store(h_out, rows))

    either(tab, loop)
    compact(idx, out, h_out, send_w, send_e)


def edge_steps(tables, to_w, to_e, from_w, from_e, before, edge, keep):
    edge_idx, edge_own, edge_far = tables
    mine, mine_h = merge(to_w, to_e)
    theirs, theirs_h = merge(from_w, from_e)
    scale = (1.0 if before is None else 2.0) / HALF
    first = edge_term(edge_idx, edge_own, edge_far, mine, theirs, 0)
    facing = edge_term(edge_idx, edge_own, edge_far, theirs, mine, 2)
    mine_next, theirs_next = [], []
    for b in range(6):
        if before is None:
            mine_next.append(scale * (mine_h[b] + first[b]) - mine[b])
            theirs_next.append(scale * (theirs_h[b] + facing[b]) - theirs[b])
        else:
            old = before[8 * b : 8 * b + 8, :], before[48 + 8 * b : 56 + 8 * b, :]
            mine_next.append(scale * (mine_h[b] + first[b]) - 2.0 * mine[b] - old[0])
            theirs_next.append(scale * (theirs_h[b] + facing[b]) - 2.0 * theirs[b] - old[1])
    second = edge_term(edge_idx, edge_own, edge_far, mine_next, theirs_next, 0)
    for b in range(6):
        edge[8 * b : 8 * b + 8, :] = first[b]
        edge[48 + 8 * b : 56 + 8 * b, :] = second[b]
        if keep is not None:
            keep[8 * b : 8 * b + 8, :] = mine_next[b]
            keep[48 + 8 * b : 56 + 8 * b, :] = theirs_next[b]


def two_steps_kernel(
    idx, tab, own_c, far_c, edge_idx, edge_own, edge_far,
    t0, h0, to_w, to_e, from_w, from_e,
    t1, t2, h2, send_w, send_e, keep, edge,
):
    env = (idx, tab, own_c, far_c)
    tables = (edge_idx, edge_own, edge_far)
    edge_steps(tables, to_w, to_e, from_w, from_e, None, edge, keep)

    def loop(group, plain):
        rows = group_rows(group)
        extra = outer(group, idx, edge, 0)
        for n in range(36):
            image = h0[n, rows, :]
            if n in extra:
                image = image + extra[n]
            t1[n, rows, :] = (1.0 / HALF) * image - t0[n, rows, :]
        extra_next = outer(group, idx, edge, 48)

        def emit(n, image):
            if n in extra_next:
                image = image + extra_next[n]
            t2[n, rows, :] = (2.0 / HALF) * image - 2.0 * t1[n, rows, :] - t0[n, rows, :]

        inner(group, env, t1, plain, emit)
        inner(group, env, t2, plain, store(h2, rows))

    either(tab, loop)
    compact(idx, t2, h2, send_w, send_e)


def sums_kernel(t0, t1, t2, part, acc, pad):
    def body(group, carry):
        rows = group_rows(group)
        sums = [jnp.zeros((8, 128), F32)] * 5
        for n in range(36):
            a, b, c = t0[n, rows, :], t1[n, rows, :], t2[n, rows, :]
            for k, term in enumerate((a * a, a * b, b * b, b * c, c * c)):
                sums[k] = sums[k] + term
        for k in range(5):
            acc[rows, 128 * k : 128 * k + 128] = sums[k]
        return carry

    lax.fori_loop(0, 4, body, 0)
    store_sums(acc, pad, 0, 5)
    part[...] = pad[...]


def last_steps_kernel(
    idx, tab, own_c, far_c, edge_idx, edge_own, edge_far,
    t1, t2, h2, to_w, to_e, from_w, from_e, keep, part,
    t3, red, edge, acc, pad,
):
    env = (idx, tab, own_c, far_c)
    tables = (edge_idx, edge_own, edge_far)
    edge_steps(tables, to_w, to_e, from_w, from_e, keep, edge, None)

    def loop(group, plain):
        rows = group_rows(group)
        extra = outer(group, idx, edge, 0)
        sums = [jnp.zeros((8, 128), F32)] * 3
        for n in range(36):
            image = h2[n, rows, :]
            if n in extra:
                image = image + extra[n]
            c = t2[n, rows, :]
            d = (2.0 / HALF) * image - 2.0 * c - t1[n, rows, :]
            t3[n, rows, :] = d
            sums[0] = sums[0] + c * d
            sums[1] = sums[1] + d * d
        extra_next = outer(group, idx, edge, 48)

        def emit(n, image):
            if n in extra_next:
                image = image + extra_next[n]
            d = t3[n, rows, :]
            sums[2] = sums[2] + d * ((2.0 / HALF) * image - 2.0 * d - t2[n, rows, :])

        inner(group, env, t3, plain, emit)
        for k in range(3):
            acc[rows, 128 * k : 128 * k + 128] = sums[k]

    either(tab, loop)
    store_sums(acc, pad, 5, 3)
    row = lax.broadcasted_iota(jnp.int32, (8, 128), 0)
    mixed = jnp.where(row < 5, part[...], pad[...])
    for k in range(16):
        red[k] = mixed


def finish_kernel(red, x0, t0, t1, t2, t3, out, coef, held, sems):
    total = red[0]
    for k in range(1, 16):
        total = total + red[k]
    even = [total[2 * k : 2 * k + 1] for k in range(4)]
    odd = [total[2 * k + 1 : 2 * k + 2] for k in range(4)]
    moment = []
    for k in range(4):
        moment.append(even[0] if k == 0 else 2.0 * even[k] - even[0])
        moment.append(odd[0] if k == 0 else 2.0 * odd[k] - odd[0])

    def inner_product(i, j):
        return 0.5 * (moment[i + j] + moment[abs(i - j)])

    def energy(i, j):
        shifted = 0.5 * (inner_product(i, j + 1) + inner_product(i, abs(j - 1)))
        return HALF * (shifted + inner_product(i, j))

    low = [[None] * 4 for _ in range(4)]
    diag, inverse, half = [], [], []
    for j in range(4):
        d = energy(j, j)
        value = moment[j]
        for k in range(j):
            d = d - low[j][k] * low[j][k] * diag[k]
            value = value - low[j][k] * half[k]
        diag.append(d)
        half.append(value)
        inverse.append(1.0 / d)
        for i in range(j + 1, 4):
            e = energy(i, j)
            for k in range(j):
                e = e - low[i][k] * low[j][k] * diag[k]
            low[i][j] = e * inverse[j]
    weight = [half[k] * inverse[k] for k in range(4)]
    for i in (2, 1, 0):
        for k in range(i + 1, 4):
            weight[i] = weight[i] - low[k][i] * weight[k]
    turned = jnp.concatenate(weight + [jnp.zeros((4, 128), F32)], axis=0).T
    for k in range(4):
        coef[k] = jnp.broadcast_to(turned[0:32, k : k + 1], (32, 128))
    copies = []
    for c in range(3):
        def add(n, carry):
            terms = coef[0] * t0[n] + coef[1] * t1[n] + coef[2] * t2[n] + coef[3] * t3[n]
            held[n] = x0[n] + terms
            return carry

        lax.fori_loop(12 * c, 12 * c + 12, add, 0, unroll=3)
        part = pl.ds(12 * c, 12)
        copies.append(pltpu.make_async_copy(held.at[part], out.at[part], sems.at[c]))
        copies[c].start()
    for copy in copies:
        copy.wait()


def pack_kernel(u, out, held, ready, sems):
    loads, stores = [], []
    for c in range(3):
        part = pl.ds(12 * c, 12)
        loads.append(pltpu.make_async_copy(u.at[part], held.at[part], sems.at[c]))
        loads[c].start()
    for c in range(3):
        loads[c].wait()
        for g in range(3 * c, 3 * c + 3):
            turned = held[4 * g : 4 * g + 4].reshape(128, 128).T
            ready[:, 16 * g : 16 * g + 16, :] = turned.reshape(8, 16, 128)
        part = pl.ds(48 * c, 48)
        stores.append(pltpu.make_async_copy(ready.at[:, part], out.at[:, part], sems.at[3 + c]))
        stores[c].start()
    for copy in stores:
        copy.wait()


def block_turn(blocks):
    part = lax.shift_right_logical(lane_ids(blocks[0].shape), 5)
    rolled = [blocks[0]] + [pltpu.roll(blocks[s], 32 * s, 1) for s in range(1, 4)]
    out = []
    for m in range(4):
        mixed = rolled[-m % 4]
        for t in range(1, 4):
            mixed = jnp.where(part == t, rolled[(t - m) % 4], mixed)
        out.append(pltpu.roll(mixed, 128 - 32 * m, 1) if m else mixed)
    return out


def product3(high, low, table, dim):
    def dot(a, b):
        return lax.dot_general(a, b, (((1,), (dim,)), ((), ())), preferred_element_type=F32)

    return dot(high, table[0]) + dot(high, table[1]) + dot(low, table[0])


def advect_kernel(idx, came, speed, synth, out, high, low, phys):
    for g in range(9):
        for h in range(2):
            pieces = block_turn([came[4 * h + s, 16 * g : 16 * g + 16, :] for s in range(4)])
            for m in range(4):
                n = 16 * (4 * g + m)
                hi, lo = split(pieces[m])
                high[n : n + 16, 128 * h : 128 * h + 128] = hi
                low[n : n + 16, 128 * h : 128 * h + 128] = lo
    for i in range(2):
        part = slice(288 * i, 288 * i + 288)
        phys[part, :] = product3(high[part, :], low[part, :], synth, 1)
    wide = jnp.broadcast_to(idx[LAYOUT : LAYOUT + 1, :], (16, 128)) == 0
    sx = jnp.where(wide, 2.0, 1.0)
    sy = jnp.where(wide, 1.0, 2.0)
    for h in range(2):
        cols = slice(128 * h, 128 * h + 128)
        u = [[phys[16 * (6 * i + j) : 16 * (6 * i + j) + 16, cols] for j in range(6)] for i in range(6)]
        acc = [[None] * 6 for _ in range(6)]
        for j in range(6):
            g = folded([u[i][j] for i in range(6)], DERIV_FOLD, -1)
            for i in range(6):
                acc[i][j] = sx * (speed[0, 6 * i + j, :, cols] * g[i])
        for i in range(6):
            g = folded(u[i], DERIV_FOLD, -1)
            for j in range(6):
                n = 16 * (6 * i + j)
                total = acc[i][j] + sy * (speed[1, 6 * i + j, :, cols] * g[j])
                hi, lo = split(float(-0.5 * W[i] * W[j]) * total)
                high[n : n + 16, cols] = hi
                low[n : n + 16, cols] = lo
    for i in range(2):
        part = slice(288 * i, 288 * i + 288)
        phys[part, :] = product3(high[part, :], low[part, :], synth, 0)
    for h in range(2):
        q = lane_ids((16, 128)) + 128 * h
        norm = jnp.where((q == 0) | (q == 255), 1.0 / 256, 1.0 / 128)
        cols = slice(128 * h, 128 * h + 128)
        for g in range(9):
            pieces = block_turn(
                [norm * phys[16 * (4 * g + m) : 16 * (4 * g + m) + 16, cols] for m in range(4)]
            )
            for s in range(4):
                out[4 * h + s, 16 * g : 16 * g + 16, :] = pieces[s]


def shift_by(array, by):
    count = lax.axis_size("elem")
    return lax.ppermute(array, "elem", [(i, (i + by) % count) for i in range(count)])


def shards(scalar_modes, velocity, viscosity, mortar_links, mortar_sides, layout):
    u = jnp.transpose(scalar_modes, (1, 2, 0, 3)).reshape(36, 32, 128)
    speed = jnp.transpose(velocity, (0, 2, 3, 4, 1)).reshape(2, 36, 16, 256)
    synth = jnp.asarray(split_table(plane_tables(256)))
    vol, edge = shape(36, 32, 128), shape(48, 128)
    both = shape(96, 128)
    blocks = shape(8, 144, 128)
    packed = call(
        pack_kernel,
        [blocks],
        [VMEM((36, 32, 128), F32), VMEM((8, 144, 128), F32), pltpu.SemaphoreType.DMA((6,))],
        [u],
        [HBM],
        [HBM],
    )[0]
    came = lax.all_to_all(packed, "plane", 0, 0, tiled=True)

    table = shape(36, 8, 128)
    idx, edge_idx, tab, own_c, far_c, edge_own, edge_far, base, *sent = call(
        guess_kernel,
        [
            shape(24, 128, dtype=jnp.int32),
            shape(8, 128, dtype=jnp.int32),
            shape(8, 128),
        ]
        + [table] * 4
        + [vol, edge, edge],
        [VMEM((36, 32, 128), F32), pltpu.SemaphoreType.DMA],
        [mortar_links, mortar_sides, viscosity[None], layout[None], u],
        [VMEM] * 4 + [HBM],
    )
    head = [idx, tab, own_c, far_c]
    edges = [edge_idx, edge_own, edge_far]

    def run(kernel, outs, scratch, args):
        return call(kernel, outs, scratch, args, [VMEM] * len(args))

    def trade(send_w, send_e):
        return shift_by(send_e, 1), shift_by(send_w, -1)

    guess_edge = run(guess_edge_kernel, [shape(48, 128)], [], [*edges, *sent, *trade(*sent)])[0]
    came, guess_edge = lax.optimization_barrier((came, guess_edge))
    back = call(
        advect_kernel,
        [blocks],
        [
            VMEM((576, 256), BF16),
            VMEM((576, 256), BF16),
            VMEM((576, 256), F32),
        ],
        [idx, came, speed, synth],
        [VMEM] * 4,
        grant=8,
    )[0]
    back = lax.all_to_all(back, "plane", 0, 0, tiled=True)

    def work(count):
        return [
            VMEM((96, 128), F32),
            VMEM((32, 128 * count), F32),
            VMEM((8, 128), F32),
        ]

    t0, h0, *sent = run(residual_kernel, [vol, vol, edge, edge], [], head + [back, base, guess_edge])
    got = trade(*sent)
    t1, t2, h2, to_w, to_e, keep = run(
        two_steps_kernel,
        [vol, vol, vol, edge, edge, both],
        [VMEM((96, 128), F32)],
        head + edges + [t0, h0, *sent, *got],
    )
    got = trade(to_w, to_e)
    part = run(sums_kernel, [shape(8, 128)], work(5)[1:], [t0, t1, t2])[0]
    t3, red = run(
        last_steps_kernel,
        [vol, shape(16, 8, 128)],
        work(3),
        head + edges + [t1, t2, h2, to_w, to_e, *got, keep, part],
    )
    red = lax.all_to_all(red, "elem", 0, 0, tiled=True)
    out = call(
        finish_kernel,
        [vol],
        [VMEM((4, 32, 128), F32), VMEM((36, 32, 128), F32), pltpu.SemaphoreType.DMA((3,))],
        [red, u, t0, t1, t2, t3],
        [VMEM] * 6,
        [HBM],
    )[0]
    return jnp.transpose(out.reshape(6, 6, 32, 128), (2, 0, 1, 3))


def solution(mesh):
    placed = (
        P("plane", None, None, "elem"),
        P(None, None, None, None, ("elem", "plane")),
        P("elem"),
        P(None, "elem"),
        P(None, None, "elem"),
        P("elem"),
    )
    return jax.shard_map(
        shards,
        mesh=mesh,
        in_specs=placed,
        out_specs=P("plane", None, None, "elem"),
        check_vma=False,
    )
```

```python
import math

import jax
import jax.numpy as jnp
import ml_dtypes
import numpy as np
from jax import lax
from jax.experimental import pallas as pl
from jax.experimental.pallas import tpu as pltpu
from jax.sharding import PartitionSpec as P

F32 = jnp.float32
BF16 = jnp.bfloat16
PENALTY = 10.0
SPANWISE = 0.0625
VMEM = pltpu.VMEM
SMEM = pltpu.SMEM
HBM = pltpu.HBM
MIXED = 7
SELF, ANY, FIRST, LAYOUT, LOCAL = 2, 4, 6, 7, 10


def lagrange_at(points, targets):
    out = np.ones((6, 6))
    for row in range(6):
        for col in range(6):
            for other in range(6):
                if other != col:
                    out[row, col] *= (targets[row] - points[other]) / (points[col] - points[other])
    return out


def node_tables():
    root = math.sqrt(7.0)
    outer = math.sqrt(1.0 / 3.0 + 2.0 * root / 21.0)
    inner = math.sqrt(1.0 / 3.0 - 2.0 * root / 21.0)
    points = np.array([-1.0, -outer, -inner, inner, outer, 1.0])
    half = [1.0 / 15.0, (14.0 - root) / 30.0, (14.0 + root) / 30.0]
    weights = np.array(half + half[::-1])
    bary = np.array(
        [1.0 / np.prod([points[c] - points[k] for k in range(6) if k != c]) for c in range(6)]
    )
    deriv = np.zeros((6, 6))
    for i in range(6):
        for j in range(6):
            if i != j:
                deriv[i, j] = bary[j] / bary[i] / (points[i] - points[j])
        deriv[i, i] = -np.sum(deriv[i])
    lower = lagrange_at(points, (points - 1.0) / 2.0)
    upper = lagrange_at(points, (points + 1.0) / 2.0)
    stiff = deriv.T @ (weights[:, None] * deriv)
    return weights, deriv, lower, upper, stiff


W, D, QLO, QHI, K1 = node_tables()
HALVES = [np.eye(6), QLO, QHI]


def plane_tables(count):
    planes = np.arange(count)[:, None]
    coeffs = np.arange(count)[None, :]
    harmonic = (coeffs + 1) // 2
    phase = 2.0 * np.pi * (harmonic * planes % count) / count
    synth = np.where(coeffs == 0, 1.0, np.where(coeffs % 2 == 1, np.cos(phase), np.sin(phase)))
    return synth


def split_table(table):
    table = np.asarray(table, np.float32)
    high = table.astype(ml_dtypes.bfloat16)
    low = (table - high.astype(np.float32)).astype(ml_dtypes.bfloat16)
    return np.stack([high, low])


def fold(matrix):
    plus = (matrix[:3, :3] + matrix[:3, :2:-1]) / 2.0
    minus = (matrix[:3, :3] - matrix[:3, :2:-1]) / 2.0
    return plus, minus


STIFF_FOLD = fold(K1 / W[:, None])
DERIV_FOLD = fold(D)


def folded(values, tables, sign):
    plus, minus = tables
    even = [values[a] + values[5 - a] for a in range(3)]
    odd = [values[a] - values[5 - a] for a in range(3)]
    out = [None] * 6
    for i in range(3):
        e = sum(float(plus[i, a]) * even[a] for a in range(3))
        o = sum(float(minus[i, a]) * odd[a] for a in range(3))
        out[i] = e + o
        out[5 - i] = e - o if sign > 0 else o - e
    return out


def split(value):
    high = value.astype(BF16)
    return high, (value - high.astype(F32)).astype(BF16)


def lane_ids(shape):
    return lax.broadcasted_iota(jnp.int32, shape, len(shape) - 1)


def call(kernel, outs, scratch, operands, spaces, out_spaces=None, grant=3):
    total = sum(int(np.prod(o.shape)) * 4 for o in outs)
    total += sum(int(np.prod(o.shape)) * 4 for o in operands)
    return pl.pallas_call(
        kernel,
        out_shape=outs,
        in_specs=[pl.BlockSpec(memory_space=s) for s in spaces],
        out_specs=[pl.BlockSpec(memory_space=s) for s in out_spaces or [VMEM] * len(outs)],
        scratch_shapes=scratch,
        compiler_params=pltpu.CompilerParams(vmem_limit_bytes=grant * 2**20),
        cost_estimate=pl.CostEstimate(flops=4_000_000, bytes_accessed=total, transcendentals=0),
    )(*[far(a) if s == HBM else a for a, s in zip(operands, spaces)])


def far(array):
    return pltpu.with_memory_space_constraint(array, HBM)


def shape(*dims, dtype=F32):
    return jax.ShapeDtypeStruct(dims, dtype)


def take(value, index):
    return jnp.take_along_axis(value, index, axis=1)


def take_row(value, index):
    wide = jnp.broadcast_to(value, (8, 128)), jnp.broadcast_to(index, (8, 128))
    return take(*wide)[0:1]


def boundary(remote, side):
    row = lax.broadcasted_iota(jnp.int32, (128, 128), 0)
    col = lane_ids((128, 128))
    any_rem = jnp.maximum(remote[2 * side : 2 * side + 1], remote[2 * side + 1 : 2 * side + 2])
    before = jnp.sum(jnp.where(col < row, any_rem, 0).astype(F32), axis=1, keepdims=True)
    mine = jnp.sum(jnp.where(col == row, any_rem, 0).astype(F32), axis=1, keepdims=True)
    slot = jnp.bitwise_and(lane_ids((1, 128)), 15).astype(F32)
    chosen = jnp.where((before == slot) & (mine > 0.0), 1.0, 0.0)
    listed = jnp.sum(chosen * row.astype(F32), axis=0, keepdims=True)
    return listed, jnp.sum(chosen, axis=0, keepdims=True), before


def build_tables(
    links, sides, visc, layout, idx, edge_idx, tab, own_c, far_c, edge_own, edge_far
):
    me = lax.axis_index("elem")
    dev = lax.shift_right_logical(links[...], 7)
    loc = jnp.bitwise_and(links[...], 127)
    remote = (dev != me).astype(jnp.int32)
    idx[LOCAL : LOCAL + 8, :] = loc
    own, other = sides[0], sides[1]
    inside = jnp.where(remote > 0, 3, own)
    whole = (inside == 0) & (other == 0)
    second = jnp.bitwise_and(lax.broadcasted_iota(jnp.int32, (8, 128), 0), 1) == 1
    odd_one = jnp.where(inside == 3, 0.0, jnp.where(whole & ~second, 0.0, 1.0))
    idx[FIRST : FIRST + 1, :] = jnp.full((1, 128), 32 * lax.axis_index("plane"), jnp.int32)
    idx[LAYOUT : LAYOUT + 1, :] = layout[...]
    row = lax.broadcasted_iota(jnp.int32, (128, 128), 0)
    col = lane_ids((128, 128))
    lane = lane_ids((1, 128))
    slot = jnp.bitwise_and(lane, 15)
    listed, present, ranks = [], [], []
    for side in range(2):
        rem = [remote[2 * side + t : 2 * side + t + 1] for t in range(2)]
        far = [loc[2 * side + t : 2 * side + t + 1] for t in range(2)]
        any_rem = jnp.maximum(rem[0], rem[1])
        places, filled, before = boundary(remote, side)
        listed.append(places.astype(jnp.int32))
        present.append(filled.astype(jnp.int32))
        idx[side : side + 1, :] = listed[side]
        mine_at = jnp.sum(jnp.where(row == col, before, 0.0), axis=0, keepdims=True)
        mine_at = jnp.where(any_rem > 0, mine_at.astype(jnp.int32), 0)
        idx[SELF + side : SELF + side + 1, :] = mine_at
        idx[ANY + side : ANY + side + 1, :] = any_rem
        named = jnp.where(
            ((far[0] == row) & (rem[0] > 0)) | ((far[1] == row) & (rem[1] > 0)), 1.0, 0.0
        )
        named = jnp.max(named, axis=1, keepdims=True)
        for t in range(2):
            rank = jnp.sum(jnp.where(row < far[t], named, 0.0), axis=0, keepdims=True)
            ranks.append(jnp.where(rem[t] > 0, rank.astype(jnp.int32), 0))
    idx[8:10, :] = jnp.zeros((2, 128), jnp.int32)
    idx[18:24, :] = jnp.zeros((6, 128), jnp.int32)

    west = lane < 64
    base = jnp.bitwise_and(lane, 112)
    element = jnp.where(west, listed[0], listed[1])
    here = jnp.where(west, present[0], present[1]) > 0

    def pick(rows_w, rows_e):
        return jnp.where(west, take_row(rows_w, element), take_row(rows_e, element))

    rank, live, mine, theirs = [], [], [], []
    for t in range(2):
        rank.append(pick(ranks[t], ranks[2 + t]))
        live.append((pick(remote[t : t + 1], remote[2 + t : 3 + t]) > 0) & here)
        mine.append(jnp.where(live[t], pick(own[t : t + 1], own[2 + t : 3 + t]), 3))
        theirs.append(jnp.where(live[t], pick(other[t : t + 1], other[2 + t : 3 + t]), 3))
    first = jnp.full((1, 128), 99, jnp.int32)
    last = jnp.full((1, 128), -1, jnp.int32)
    for t in range(2):
        target = jnp.where(live[t], rank[t], 99)
        for r in range(16):
            hit = take_row(target, base + r) == slot
            first = jnp.where(hit, jnp.minimum(first, 16 * t + r), first)
            last = jnp.where(hit, jnp.maximum(last, 16 * t + r), last)
    exists = [last >= 0, last > first]
    key = [jnp.where(exists[0], first, 0), jnp.where(exists[1], last, 0)]
    back = [base + jnp.bitwise_and(k, 15) for k in key]

    def from_key(k, pair):
        value = jnp.where(key[k] >= 16, take_row(pair[1], back[k]), take_row(pair[0], back[k]))
        return jnp.where(exists[k], value, 3)

    near_own = [from_key(k, theirs) for k in range(2)]
    near_far = [from_key(k, mine) for k in range(2)]
    edge_idx[...] = jnp.zeros((8, 128), jnp.int32)
    for k in range(2):
        edge_idx[k : k + 1, :] = base + rank[k]
        edge_idx[2 + k : 3 + k, :] = back[k]
    none = jnp.full((4, 128), 3, jnp.int32)
    edge_mine = jnp.concatenate([mine[0], mine[1], near_own[0], near_own[1], none], axis=0)
    edge_theirs = jnp.concatenate([theirs[0], theirs[1], near_far[0], near_far[1], none], axis=0)

    nu = visc[...]
    wide = layout[...] == 0
    tab[0:1, :] = nu * jnp.where(wide, 2.0, 0.5)
    tab[1:2, :] = nu * jnp.where(wide, 0.5, 2.0)
    tab[2:3, :] = nu
    for face in range(4):
        tab[3 + face : 4 + face, :] = whole[2 * face : 2 * face + 1].astype(F32)
    tab[MIXED : MIXED + 1, :] = jnp.max(odd_one, axis=0, keepdims=True)
    mine_m = [PENALTY * HALVES[o].T @ np.diag(W) @ HALVES[o] for o in range(3)]
    far_m = [
        [-PENALTY * HALVES[o].T @ np.diag(W) @ HALVES[c] for c in range(3)] for o in range(3)
    ]
    for code, facing, own_ref, far_ref in (
        (inside, other, own_c, far_c),
        (edge_mine, edge_theirs, edge_own, edge_far),
    ):
        hot = [(code == o).astype(F32) for o in range(3)]
        pair = [[hot[o] * (facing == c).astype(F32) for c in range(3)] for o in range(3)]
        for a in range(6):
            for b in range(6):
                n = 6 * a + b
                total = sum(float(mine_m[o][a, b]) * hot[o] for o in range(3))
                own_ref[n] = total + pltpu.roll(total, 7, 0)
                far_ref[n] = sum(
                    float(far_m[o][c][a, b]) * pair[o][c] for o in range(3) for c in range(3)
                )


def group_rows(group):
    return pl.ds(pl.multiple_of(group * 8, 8), 8)


def row_of(ref, r):
    return jnp.broadcast_to(ref[r : r + 1, :], (8, 128))


def face_nodes(face):
    return [
        6 * i + j
        for i, j in [
            (0, b) if face == 0 else (5, b) if face == 1 else (b, 0) if face == 2 else (b, 5)
            for b in range(6)
        ]
    ]


def either(tab, loop):
    mixed = jnp.max(tab[MIXED : MIXED + 1, :]) > 0.5
    for plain in (True, False):

        @pl.when(mixed != plain)
        def _(plain=plain):
            lax.fori_loop(
                0, 4, lambda group, carry: loop(group, plain) or carry, 0, unroll=2 if plain else 1
            )


def weighted(factors, values):
    total = float(factors[0]) * values[0]
    for f, v in zip(factors[1:], values[1:]):
        total = total + float(f) * v
    return total


def plain_terms(env, v):
    idx, tab, _, _ = env

    def of_face(face):
        active = row_of(tab, 3 + face)
        local = row_of(idx, LOCAL + 2 * face)

        def term(a):
            n, m = face_nodes(face)[a], face_nodes(face ^ 1)[a]
            return (float(PENALTY * W[a]) * active) * (v(n) - take(v(m), local))

        return term

    return [of_face(face) for face in range(4)]


def general_terms(env, v):
    idx, _, own_c, far_c = env
    found = []
    for face in range(4):
        mine = [v(n) for n in face_nodes(face)]
        theirs = [
            [take(v(n), row_of(idx, LOCAL + 2 * face + t)) for n in face_nodes(face ^ 1)]
            for t in range(2)
        ]
        values = []
        for a in range(6):
            extra = jnp.zeros((8, 128), F32)
            for b in range(6):
                extra = extra + own_c[6 * a + b, 2 * face : 2 * face + 1, :] * mine[b]
                for t in range(2):
                    s = 2 * face + t
                    extra = extra + far_c[6 * a + b, s : s + 1, :] * theirs[t][b]
            values.append(extra)
        found.append(values.__getitem__)
    return found


def inner(group, env, v_ref, plain, emit):
    idx, tab, _, _ = env
    rows = group_rows(group)

    def v(n):
        return v_ref[n, rows, :]

    terms = (plain_terms if plain else general_terms)(env, v)
    q = row_of(idx, FIRST) + group * 8 + lax.broadcasted_iota(jnp.int32, (8, 128), 0)
    harmonic = lax.shift_right_logical(q + 1, 1).astype(F32) * SPANWISE
    cx, cy = row_of(tab, 0), row_of(tab, 1)
    shift = 1.0 + 0.5 * tab[2:3, :] * (harmonic * harmonic)
    plus, minus = STIFF_FOLD
    even = [[v(6 * a + j) + v(30 - 6 * a + j) for a in range(3)] for j in range(6)]
    odd = [[v(6 * a + j) - v(30 - 6 * a + j) for a in range(3)] for j in range(6)]
    for i in range(3):
        e = [weighted(plus[i], even[j]) for j in range(6)]
        o = [weighted(minus[i], odd[j]) for j in range(6)]
        for line in (i, 5 - i):
            mine = [v(6 * line + j) for j in range(6)]
            g = folded(mine, STIFF_FOLD, 1)
            for j in range(6):
                n = 6 * line + j
                gx = e[j] + o[j] if line == i else e[j] - o[j]
                value = float(W[line] * W[j]) * (shift * mine[j] + cx * gx + cy * g[j])
                for face, (at, b) in enumerate(((line == 0, j), (line == 5, j), (j == 0, line), (j == 5, line))):
                    if at:
                        value = value + terms[face](b)
                emit(n, value)


def compact(idx, v_ref, h_ref, send_w, send_e):
    part = lax.shift_right_logical(lane_ids((8, 128)), 4)
    for face, ref in ((0, send_w), (1, send_e)):
        index = row_of(idx, face)
        for b in range(6):
            n = face_nodes(face)[b]
            value = take(v_ref[n, 0:8, :], index)
            for k in range(1, 8):
                source = v_ref if k < 4 else h_ref
                other = take(source[n, 8 * (k % 4) : 8 * (k % 4) + 8, :], index)
                value = jnp.where(part == k, other, value)
            ref[8 * b : 8 * b + 8, :] = value


def outer(group, idx, edge, first):
    found = {}
    for face in range(2):
        lanes = row_of(idx, SELF + face) + (64 * face + 16 * group)
        on = row_of(idx, ANY + face) > 0
        for b in range(6):
            value = take(edge[first + 8 * b : first + 8 * b + 8, :], lanes)
            found[face_nodes(face)[b]] = jnp.where(on, value, 0.0)
    return found


def edge_blocks(ref):
    return [ref[8 * b : 8 * b + 8, :] for b in range(6)]


def merge(to_w, to_e):
    west = lane_ids((8, 128)) < 64
    plain, inner_h = [], []
    for w, e in zip(edge_blocks(to_w), edge_blocks(to_e)):
        plain.append(jnp.where(west, w, pltpu.roll(e, 64, 1)))
        inner_h.append(jnp.where(west, pltpu.roll(w, 64, 1), e))
    return plain, inner_h


def edge_term(edge_idx, edge_own, edge_far, mine, theirs, row):
    near = [[take(t, row_of(edge_idx, row + k)) for t in theirs] for k in range(2)]
    out = []
    for a in range(6):
        chains = [None] * 3
        for b in range(6):
            n = 6 * a + b
            terms = [edge_own[n, row : row + 1, :] * mine[b]]
            terms += [edge_far[n, row + k : row + k + 1, :] * near[k][b] for k in range(2)]
            chains = terms if chains[0] is None else [c + t for c, t in zip(chains, terms)]
        out.append(chains[0] + (chains[1] + chains[2]))
    return out


def store_sums(acc, pad, first, count):
    width = count * 128
    lhs = (
        lax.broadcasted_iota(jnp.int32, (8, width), 0)
        == lax.shift_right_logical(lane_ids((8, width)), 7) + first
    ).astype(F32)
    sums = lax.dot_general(
        lhs, acc[...], (((1,), (1,)), ((), ())),
        precision=lax.Precision.HIGHEST, preferred_element_type=F32,
    )
    pad[...] = jnp.ones((8, 128), F32)
    pad[:, 0:32] = sums


HALF = 10.0


def store(ref, rows):
    def emit(n, value):
        ref[n, rows, :] = value

    return emit


def guess_kernel(
    links, sides, visc, layout, u_far,
    idx, edge_idx, tab, own_c, far_c, edge_own, edge_far, out, u, sem,
):
    copy = pltpu.make_async_copy(u_far, u, sem)
    copy.start()
    build_tables(
        links, sides, visc, layout, idx, edge_idx, tab, own_c, far_c, edge_own, edge_far
    )
    copy.wait()
    env = (idx, tab, own_c, far_c)

    def loop(group, plain):
        rows = group_rows(group)

        def emit(n, value):
            out[n, rows, :] = float(W[n // 6] * W[n % 6]) * u[n, rows, :] - value

        inner(group, env, u, plain, emit)

    either(tab, loop)


def guess_edge_kernel(edge_idx, edge_own, edge_far, to_w, to_e, from_w, from_e, edge):
    mine, _ = merge(to_w, to_e)
    theirs, _ = merge(from_w, from_e)
    for b, value in enumerate(edge_term(edge_idx, edge_own, edge_far, mine, theirs, 0)):
        edge[8 * b : 8 * b + 8, :] = value


def residual_kernel(
    idx, tab, own_c, far_c, back, base, edge, out, h_out, send_w, send_e
):
    env = (idx, tab, own_c, far_c)

    def turn(g, carry):
        part = pl.ds(pl.multiple_of(16 * g, 16), 16)
        turned = back[:, part, :].reshape(128, 128).T
        for m in range(4):
            out[4 * g + m] = base[4 * g + m] + turned[32 * m : 32 * m + 32]
        return carry

    lax.fori_loop(0, 9, turn, 0, unroll=3)

    def loop(group, plain):
        rows = group_rows(group)
        for n, extra in outer(group, idx, edge, 0).items():
            out[n, rows, :] -= extra
        inner(group, env, out, plain, store(h_out, rows))

    either(tab, loop)
    compact(idx, out, h_out, send_w, send_e)


def edge_steps(tables, to_w, to_e, from_w, from_e, before, edge, keep):
    edge_idx, edge_own, edge_far = tables
    mine, mine_h = merge(to_w, to_e)
    theirs, theirs_h = merge(from_w, from_e)
    scale = (1.0 if before is None else 2.0) / HALF
    first = edge_term(edge_idx, edge_own, edge_far, mine, theirs, 0)
    facing = edge_term(edge_idx, edge_own, edge_far, theirs, mine, 2)
    mine_next, theirs_next = [], []
    for b in range(6):
        if before is None:
            mine_next.append(scale * (mine_h[b] + first[b]) - mine[b])
            theirs_next.append(scale * (theirs_h[b] + facing[b]) - theirs[b])
        else:
            old = before[8 * b : 8 * b + 8, :], before[48 + 8 * b : 56 + 8 * b, :]
            mine_next.append(scale * (mine_h[b] + first[b]) - 2.0 * mine[b] - old[0])
            theirs_next.append(scale * (theirs_h[b] + facing[b]) - 2.0 * theirs[b] - old[1])
    second = edge_term(edge_idx, edge_own, edge_far, mine_next, theirs_next, 0)
    for b in range(6):
        edge[8 * b : 8 * b + 8, :] = first[b]
        edge[48 + 8 * b : 56 + 8 * b, :] = second[b]
        if keep is not None:
            keep[8 * b : 8 * b + 8, :] = mine_next[b]
            keep[48 + 8 * b : 56 + 8 * b, :] = theirs_next[b]


def two_steps_kernel(
    idx, tab, own_c, far_c, edge_idx, edge_own, edge_far,
    t0, h0, to_w, to_e, from_w, from_e,
    t1, t2, h2, send_w, send_e, keep, edge,
):
    env = (idx, tab, own_c, far_c)
    tables = (edge_idx, edge_own, edge_far)
    edge_steps(tables, to_w, to_e, from_w, from_e, None, edge, keep)

    def loop(group, plain):
        rows = group_rows(group)
        extra = outer(group, idx, edge, 0)
        for n in range(36):
            image = h0[n, rows, :]
            if n in extra:
                image = image + extra[n]
            t1[n, rows, :] = (1.0 / HALF) * image - t0[n, rows, :]
        extra_next = outer(group, idx, edge, 48)

        def emit(n, image):
            if n in extra_next:
                image = image + extra_next[n]
            t2[n, rows, :] = (2.0 / HALF) * image - 2.0 * t1[n, rows, :] - t0[n, rows, :]

        inner(group, env, t1, plain, emit)
        inner(group, env, t2, plain, store(h2, rows))

    either(tab, loop)
    compact(idx, t2, h2, send_w, send_e)


def sums_kernel(t0, t1, t2, part, acc, pad):
    def body(group, carry):
        rows = group_rows(group)
        sums = [jnp.zeros((8, 128), F32)] * 5
        for n in range(36):
            a, b, c = t0[n, rows, :], t1[n, rows, :], t2[n, rows, :]
            for k, term in enumerate((a * a, a * b, b * b, b * c, c * c)):
                sums[k] = sums[k] + term
        for k in range(5):
            acc[rows, 128 * k : 128 * k + 128] = sums[k]
        return carry

    lax.fori_loop(0, 4, body, 0)
    store_sums(acc, pad, 0, 5)
    part[...] = pad[...]


def last_steps_kernel(
    idx, tab, own_c, far_c, edge_idx, edge_own, edge_far,
    t1, t2, h2, to_w, to_e, from_w, from_e, keep, part,
    t3, red, edge, acc, pad,
):
    env = (idx, tab, own_c, far_c)
    tables = (edge_idx, edge_own, edge_far)
    edge_steps(tables, to_w, to_e, from_w, from_e, keep, edge, None)

    def loop(group, plain):
        rows = group_rows(group)
        extra = outer(group, idx, edge, 0)
        sums = [jnp.zeros((8, 128), F32)] * 3
        for n in range(36):
            image = h2[n, rows, :]
            if n in extra:
                image = image + extra[n]
            c = t2[n, rows, :]
            d = (2.0 / HALF) * image - 2.0 * c - t1[n, rows, :]
            t3[n, rows, :] = d
            sums[0] = sums[0] + c * d
            sums[1] = sums[1] + d * d
        extra_next = outer(group, idx, edge, 48)

        def emit(n, image):
            if n in extra_next:
                image = image + extra_next[n]
            d = t3[n, rows, :]
            sums[2] = sums[2] + d * ((2.0 / HALF) * image - 2.0 * d - t2[n, rows, :])

        inner(group, env, t3, plain, emit)
        for k in range(3):
            acc[rows, 128 * k : 128 * k + 128] = sums[k]

    either(tab, loop)
    store_sums(acc, pad, 5, 3)
    row = lax.broadcasted_iota(jnp.int32, (8, 128), 0)
    mixed = jnp.where(row < 5, part[...], pad[...])
    for k in range(16):
        red[k] = mixed


def finish_kernel(red, x0, t0, t1, t2, t3, out, coef, held, sems):
    total = red[0]
    for k in range(1, 16):
        total = total + red[k]
    even = [total[2 * k : 2 * k + 1] for k in range(4)]
    odd = [total[2 * k + 1 : 2 * k + 2] for k in range(4)]
    moment = []
    for k in range(4):
        moment.append(even[0] if k == 0 else 2.0 * even[k] - even[0])
        moment.append(odd[0] if k == 0 else 2.0 * odd[k] - odd[0])

    def inner_product(i, j):
        return 0.5 * (moment[i + j] + moment[abs(i - j)])

    def energy(i, j):
        shifted = 0.5 * (inner_product(i, j + 1) + inner_product(i, abs(j - 1)))
        return HALF * (shifted + inner_product(i, j))

    low = [[None] * 4 for _ in range(4)]
    diag, inverse, half = [], [], []
    for j in range(4):
        d = energy(j, j)
        value = moment[j]
        for k in range(j):
            d = d - low[j][k] * low[j][k] * diag[k]
            value = value - low[j][k] * half[k]
        diag.append(d)
        half.append(value)
        inverse.append(1.0 / d)
        for i in range(j + 1, 4):
            e = energy(i, j)
            for k in range(j):
                e = e - low[i][k] * low[j][k] * diag[k]
            low[i][j] = e * inverse[j]
    weight = [half[k] * inverse[k] for k in range(4)]
    for i in (2, 1, 0):
        for k in range(i + 1, 4):
            weight[i] = weight[i] - low[k][i] * weight[k]
    turned = jnp.concatenate(weight + [jnp.zeros((4, 128), F32)], axis=0).T
    for k in range(4):
        coef[k] = jnp.broadcast_to(turned[0:32, k : k + 1], (32, 128))
    copies = []
    for c in range(3):
        def add(n, carry):
            terms = coef[0] * t0[n] + coef[1] * t1[n] + coef[2] * t2[n] + coef[3] * t3[n]
            held[n] = x0[n] + terms
            return carry

        lax.fori_loop(12 * c, 12 * c + 12, add, 0, unroll=3)
        part = pl.ds(12 * c, 12)
        copies.append(pltpu.make_async_copy(held.at[part], out.at[part], sems.at[c]))
        copies[c].start()
    for copy in copies:
        copy.wait()


def pack_kernel(u, links, out, send_w, send_e, held, ready, near_links, lists, sems):
    loads, stores = [], []
    first = pltpu.make_async_copy(links, near_links, sems.at[6])
    first.start()
    for c in range(3):
        part = pl.ds(12 * c, 12)
        loads.append(pltpu.make_async_copy(u.at[part], held.at[part], sems.at[c]))
        loads[c].start()
    first.wait()
    dev = lax.shift_right_logical(near_links[...], 7)
    remote = (dev != lax.axis_index("elem")).astype(jnp.int32)
    for side in range(2):
        lists[side : side + 1, :] = boundary(remote, side)[0].astype(jnp.int32)
    for c in range(3):
        loads[c].wait()
        for g in range(3 * c, 3 * c + 3):
            turned = held[4 * g : 4 * g + 4].reshape(128, 128).T
            ready[:, 16 * g : 16 * g + 16, :] = turned.reshape(8, 16, 128)
        part = pl.ds(48 * c, 48)
        stores.append(pltpu.make_async_copy(ready.at[:, part], out.at[:, part], sems.at[3 + c]))
        stores[c].start()
    compact(lists, held, held, send_w, send_e)
    for copy in stores:
        copy.wait()


def block_turn(blocks):
    part = lax.shift_right_logical(lane_ids(blocks[0].shape), 5)
    rolled = [blocks[0]] + [pltpu.roll(blocks[s], 32 * s, 1) for s in range(1, 4)]
    out = []
    for m in range(4):
        mixed = rolled[-m % 4]
        for t in range(1, 4):
            mixed = jnp.where(part == t, rolled[(t - m) % 4], mixed)
        out.append(pltpu.roll(mixed, 128 - 32 * m, 1) if m else mixed)
    return out


def product3(high, low, table, dim):
    def dot(a, b):
        return lax.dot_general(a, b, (((1,), (dim,)), ((), ())), preferred_element_type=F32)

    return dot(high, table[0]) + dot(high, table[1]) + dot(low, table[0])


def advect_kernel(idx, came, speed, synth, out, high, low, phys):
    for g in range(9):
        for h in range(2):
            pieces = block_turn([came[4 * h + s, 16 * g : 16 * g + 16, :] for s in range(4)])
            for m in range(4):
                n = 16 * (4 * g + m)
                hi, lo = split(pieces[m])
                high[n : n + 16, 128 * h : 128 * h + 128] = hi
                low[n : n + 16, 128 * h : 128 * h + 128] = lo
    for i in range(2):
        part = slice(288 * i, 288 * i + 288)
        phys[part, :] = product3(high[part, :], low[part, :], synth, 1)
    wide = jnp.broadcast_to(idx[LAYOUT : LAYOUT + 1, :], (16, 128)) == 0
    sx = jnp.where(wide, 2.0, 1.0)
    sy = jnp.where(wide, 1.0, 2.0)
    for h in range(2):
        cols = slice(128 * h, 128 * h + 128)
        u = [[phys[16 * (6 * i + j) : 16 * (6 * i + j) + 16, cols] for j in range(6)] for i in range(6)]
        acc = [[None] * 6 for _ in range(6)]
        for j in range(6):
            g = folded([u[i][j] for i in range(6)], DERIV_FOLD, -1)
            for i in range(6):
                acc[i][j] = sx * (speed[0, 6 * i + j, :, cols] * g[i])
        for i in range(6):
            g = folded(u[i], DERIV_FOLD, -1)
            for j in range(6):
                n = 16 * (6 * i + j)
                total = acc[i][j] + sy * (speed[1, 6 * i + j, :, cols] * g[j])
                hi, lo = split(float(-0.5 * W[i] * W[j]) * total)
                high[n : n + 16, cols] = hi
                low[n : n + 16, cols] = lo
    for i in range(2):
        part = slice(288 * i, 288 * i + 288)
        phys[part, :] = product3(high[part, :], low[part, :], synth, 0)
    for h in range(2):
        q = lane_ids((16, 128)) + 128 * h
        norm = jnp.where((q == 0) | (q == 255), 1.0 / 256, 1.0 / 128)
        cols = slice(128 * h, 128 * h + 128)
        for g in range(9):
            pieces = block_turn(
                [norm * phys[16 * (4 * g + m) : 16 * (4 * g + m) + 16, cols] for m in range(4)]
            )
            for s in range(4):
                out[4 * h + s, 16 * g : 16 * g + 16, :] = pieces[s]


def shift_by(array, by):
    count = lax.axis_size("elem")
    return lax.ppermute(array, "elem", [(i, (i + by) % count) for i in range(count)])


def shards(scalar_modes, velocity, viscosity, mortar_links, mortar_sides, layout):
    u = jnp.transpose(scalar_modes, (1, 2, 0, 3)).reshape(36, 32, 128)
    speed = jnp.transpose(velocity, (0, 2, 3, 4, 1)).reshape(2, 36, 16, 256)
    synth = jnp.asarray(split_table(plane_tables(256)))
    vol, edge = shape(36, 32, 128), shape(48, 128)
    both = shape(96, 128)
    blocks = shape(8, 144, 128)
    packed, *sent = call(
        pack_kernel,
        [blocks, edge, edge],
        [
            VMEM((36, 32, 128), F32),
            VMEM((8, 144, 128), F32),
            VMEM((8, 128), jnp.int32),
            VMEM((8, 128), jnp.int32),
            pltpu.SemaphoreType.DMA((7,)),
        ],
        [u, mortar_links],
        [HBM, HBM],
        [HBM, VMEM, VMEM],
    )
    came = lax.all_to_all(packed, "plane", 0, 0, tiled=True)

    table = shape(36, 8, 128)
    idx, edge_idx, tab, own_c, far_c, edge_own, edge_far, base = call(
        guess_kernel,
        [
            shape(24, 128, dtype=jnp.int32),
            shape(8, 128, dtype=jnp.int32),
            shape(8, 128),
        ]
        + [table] * 4
        + [vol],
        [VMEM((36, 32, 128), F32), pltpu.SemaphoreType.DMA],
        [mortar_links, mortar_sides, viscosity[None], layout[None], u],
        [VMEM] * 4 + [HBM],
    )
    head = [idx, tab, own_c, far_c]
    edges = [edge_idx, edge_own, edge_far]

    def run(kernel, outs, scratch, args):
        return call(kernel, outs, scratch, args, [VMEM] * len(args))

    def trade(send_w, send_e):
        return shift_by(send_e, 1), shift_by(send_w, -1)

    guess_edge = run(guess_edge_kernel, [shape(48, 128)], [], [*edges, *sent, *trade(*sent)])[0]
    came, guess_edge, base = lax.optimization_barrier((came, guess_edge, base))
    back = call(
        advect_kernel,
        [blocks],
        [
            VMEM((576, 256), BF16),
            VMEM((576, 256), BF16),
            VMEM((576, 256), F32),
        ],
        [idx, came, speed, synth],
        [VMEM] * 4,
        grant=8,
    )[0]
    back = lax.all_to_all(back, "plane", 0, 0, tiled=True)

    def work(count):
        return [
            VMEM((96, 128), F32),
            VMEM((32, 128 * count), F32),
            VMEM((8, 128), F32),
        ]

    t0, h0, *sent = run(residual_kernel, [vol, vol, edge, edge], [], head + [back, base, guess_edge])
    got = trade(*sent)
    t1, t2, h2, to_w, to_e, keep = run(
        two_steps_kernel,
        [vol, vol, vol, edge, edge, both],
        [VMEM((96, 128), F32)],
        head + edges + [t0, h0, *sent, *got],
    )
    got = trade(to_w, to_e)
    part = run(sums_kernel, [shape(8, 128)], work(5)[1:], [t0, t1, t2])[0]
    t3, red = run(
        last_steps_kernel,
        [vol, shape(16, 8, 128)],
        work(3),
        head + edges + [t1, t2, h2, to_w, to_e, *got, keep, part],
    )
    red = lax.all_to_all(red, "elem", 0, 0, tiled=True)
    out = call(
        finish_kernel,
        [vol],
        [VMEM((4, 32, 128), F32), VMEM((36, 32, 128), F32), pltpu.SemaphoreType.DMA((3,))],
        [red, u, t0, t1, t2, t3],
        [VMEM] * 6,
        [HBM],
    )[0]
    return jnp.transpose(out.reshape(6, 6, 32, 128), (2, 0, 1, 3))


def solution(mesh):
    placed = (
        P("plane", None, None, "elem"),
        P(None, None, None, None, ("elem", "plane")),
        P("elem"),
        P(None, "elem"),
        P(None, None, "elem"),
        P("elem"),
    )
    return jax.shard_map(
        shards,
        mesh=mesh,
        in_specs=placed,
        out_specs=P("plane", None, None, "elem"),
        check_vma=False,
    )
```

```python
import math

import jax
import jax.numpy as jnp
import ml_dtypes
import numpy as np
from jax import lax
from jax.experimental import pallas as pl
from jax.experimental.pallas import tpu as pltpu
from jax.sharding import PartitionSpec as P

F32 = jnp.float32
BF16 = jnp.bfloat16
PENALTY = 10.0
SPANWISE = 0.0625
VMEM = pltpu.VMEM
SMEM = pltpu.SMEM
HBM = pltpu.HBM
MIXED = 7
SELF, ANY, FIRST, LAYOUT, LOCAL = 2, 4, 6, 7, 10


def lagrange_at(points, targets):
    out = np.ones((6, 6))
    for row in range(6):
        for col in range(6):
            for other in range(6):
                if other != col:
                    out[row, col] *= (targets[row] - points[other]) / (points[col] - points[other])
    return out


def node_tables():
    root = math.sqrt(7.0)
    outer = math.sqrt(1.0 / 3.0 + 2.0 * root / 21.0)
    inner = math.sqrt(1.0 / 3.0 - 2.0 * root / 21.0)
    points = np.array([-1.0, -outer, -inner, inner, outer, 1.0])
    half = [1.0 / 15.0, (14.0 - root) / 30.0, (14.0 + root) / 30.0]
    weights = np.array(half + half[::-1])
    bary = np.array(
        [1.0 / np.prod([points[c] - points[k] for k in range(6) if k != c]) for c in range(6)]
    )
    deriv = np.zeros((6, 6))
    for i in range(6):
        for j in range(6):
            if i != j:
                deriv[i, j] = bary[j] / bary[i] / (points[i] - points[j])
        deriv[i, i] = -np.sum(deriv[i])
    lower = lagrange_at(points, (points - 1.0) / 2.0)
    upper = lagrange_at(points, (points + 1.0) / 2.0)
    stiff = deriv.T @ (weights[:, None] * deriv)
    return weights, deriv, lower, upper, stiff


W, D, QLO, QHI, K1 = node_tables()
HALVES = [np.eye(6), QLO, QHI]


def plane_tables(count):
    planes = np.arange(count)[:, None]
    coeffs = np.arange(count)[None, :]
    harmonic = (coeffs + 1) // 2
    phase = 2.0 * np.pi * (harmonic * planes % count) / count
    synth = np.where(coeffs == 0, 1.0, np.where(coeffs % 2 == 1, np.cos(phase), np.sin(phase)))
    return synth


def split_table(table):
    table = np.asarray(table, np.float32)
    high = table.astype(ml_dtypes.bfloat16)
    low = (table - high.astype(np.float32)).astype(ml_dtypes.bfloat16)
    return np.stack([high, low])


def fold(matrix):
    plus = (matrix[:3, :3] + matrix[:3, :2:-1]) / 2.0
    minus = (matrix[:3, :3] - matrix[:3, :2:-1]) / 2.0
    return plus, minus


STIFF_FOLD = fold(K1 / W[:, None])
DERIV_FOLD = fold(D)


def folded(values, tables, sign):
    plus, minus = tables
    even = [values[a] + values[5 - a] for a in range(3)]
    odd = [values[a] - values[5 - a] for a in range(3)]
    out = [None] * 6
    for i in range(3):
        e = sum(float(plus[i, a]) * even[a] for a in range(3))
        o = sum(float(minus[i, a]) * odd[a] for a in range(3))
        out[i] = e + o
        out[5 - i] = e - o if sign > 0 else o - e
    return out


def split(value):
    high = value.astype(BF16)
    return high, (value - high.astype(F32)).astype(BF16)


def lane_ids(shape):
    return lax.broadcasted_iota(jnp.int32, shape, len(shape) - 1)


def call(kernel, outs, scratch, operands, spaces, out_spaces=None, grant=3):
    total = sum(int(np.prod(o.shape)) * 4 for o in outs)
    total += sum(int(np.prod(o.shape)) * 4 for o in operands)
    return pl.pallas_call(
        kernel,
        out_shape=outs,
        in_specs=[pl.BlockSpec(memory_space=s) for s in spaces],
        out_specs=[pl.BlockSpec(memory_space=s) for s in out_spaces or [VMEM] * len(outs)],
        scratch_shapes=scratch,
        compiler_params=pltpu.CompilerParams(vmem_limit_bytes=grant * 2**20),
        cost_estimate=pl.CostEstimate(flops=4_000_000, bytes_accessed=total, transcendentals=0),
    )(*[far(a) if s == HBM else a for a, s in zip(operands, spaces)])


def far(array):
    return pltpu.with_memory_space_constraint(array, HBM)


def shape(*dims, dtype=F32):
    return jax.ShapeDtypeStruct(dims, dtype)


def take(value, index):
    return jnp.take_along_axis(value, index, axis=1)


def take_row(value, index):
    wide = jnp.broadcast_to(value, (8, 128)), jnp.broadcast_to(index, (8, 128))
    return take(*wide)[0:1]


def boundary(remote, side):
    row = lax.broadcasted_iota(jnp.int32, (128, 128), 0)
    col = lane_ids((128, 128))
    any_rem = jnp.maximum(remote[2 * side : 2 * side + 1], remote[2 * side + 1 : 2 * side + 2])
    before = jnp.sum(jnp.where(col < row, any_rem, 0).astype(F32), axis=1, keepdims=True)
    mine = jnp.sum(jnp.where(col == row, any_rem, 0).astype(F32), axis=1, keepdims=True)
    slot = jnp.bitwise_and(lane_ids((1, 128)), 15).astype(F32)
    chosen = jnp.where((before == slot) & (mine > 0.0), 1.0, 0.0)
    listed = jnp.sum(chosen * row.astype(F32), axis=0, keepdims=True)
    return listed, jnp.sum(chosen, axis=0, keepdims=True), before


def build_tables(
    links, sides, visc, layout, idx, edge_idx, tab, own_c, far_c, edge_own, edge_far
):
    me = lax.axis_index("elem")
    dev = lax.shift_right_logical(links[...], 7)
    loc = jnp.bitwise_and(links[...], 127)
    remote = (dev != me).astype(jnp.int32)
    idx[LOCAL : LOCAL + 8, :] = loc
    own, other = sides[0], sides[1]
    inside = jnp.where(remote > 0, 3, own)
    whole = (inside == 0) & (other == 0)
    second = jnp.bitwise_and(lax.broadcasted_iota(jnp.int32, (8, 128), 0), 1) == 1
    odd_one = jnp.where(inside == 3, 0.0, jnp.where(whole & ~second, 0.0, 1.0))
    idx[FIRST : FIRST + 1, :] = jnp.full((1, 128), 32 * lax.axis_index("plane"), jnp.int32)
    idx[LAYOUT : LAYOUT + 1, :] = layout[...]
    row = lax.broadcasted_iota(jnp.int32, (128, 128), 0)
    col = lane_ids((128, 128))
    lane = lane_ids((1, 128))
    slot = jnp.bitwise_and(lane, 15)
    listed, present, ranks = [], [], []
    for side in range(2):
        rem = [remote[2 * side + t : 2 * side + t + 1] for t in range(2)]
        far = [loc[2 * side + t : 2 * side + t + 1] for t in range(2)]
        any_rem = jnp.maximum(rem[0], rem[1])
        places, filled, before = boundary(remote, side)
        listed.append(places.astype(jnp.int32))
        present.append(filled.astype(jnp.int32))
        idx[side : side + 1, :] = listed[side]
        mine_at = jnp.sum(jnp.where(row == col, before, 0.0), axis=0, keepdims=True)
        mine_at = jnp.where(any_rem > 0, mine_at.astype(jnp.int32), 0)
        idx[SELF + side : SELF + side + 1, :] = mine_at
        idx[ANY + side : ANY + side + 1, :] = any_rem
        named = jnp.where(
            ((far[0] == row) & (rem[0] > 0)) | ((far[1] == row) & (rem[1] > 0)), 1.0, 0.0
        )
        named = jnp.max(named, axis=1, keepdims=True)
        for t in range(2):
            rank = jnp.sum(jnp.where(row < far[t], named, 0.0), axis=0, keepdims=True)
            ranks.append(jnp.where(rem[t] > 0, rank.astype(jnp.int32), 0))
    idx[8:10, :] = jnp.zeros((2, 128), jnp.int32)
    idx[18:24, :] = jnp.zeros((6, 128), jnp.int32)

    west = lane < 64
    base = jnp.bitwise_and(lane, 112)
    element = jnp.where(west, listed[0], listed[1])
    here = jnp.where(west, present[0], present[1]) > 0

    def pick(rows_w, rows_e):
        return jnp.where(west, take_row(rows_w, element), take_row(rows_e, element))

    rank, live, mine, theirs = [], [], [], []
    for t in range(2):
        rank.append(pick(ranks[t], ranks[2 + t]))
        live.append((pick(remote[t : t + 1], remote[2 + t : 3 + t]) > 0) & here)
        mine.append(jnp.where(live[t], pick(own[t : t + 1], own[2 + t : 3 + t]), 3))
        theirs.append(jnp.where(live[t], pick(other[t : t + 1], other[2 + t : 3 + t]), 3))
    first = jnp.full((1, 128), 99, jnp.int32)
    last = jnp.full((1, 128), -1, jnp.int32)
    for t in range(2):
        target = jnp.where(live[t], rank[t], 99)
        for r in range(16):
            hit = take_row(target, base + r) == slot
            first = jnp.where(hit, jnp.minimum(first, 16 * t + r), first)
            last = jnp.where(hit, jnp.maximum(last, 16 * t + r), last)
    exists = [last >= 0, last > first]
    key = [jnp.where(exists[0], first, 0), jnp.where(exists[1], last, 0)]
    back = [base + jnp.bitwise_and(k, 15) for k in key]

    def from_key(k, pair):
        value = jnp.where(key[k] >= 16, take_row(pair[1], back[k]), take_row(pair[0], back[k]))
        return jnp.where(exists[k], value, 3)

    near_own = [from_key(k, theirs) for k in range(2)]
    near_far = [from_key(k, mine) for k in range(2)]
    edge_idx[...] = jnp.zeros((8, 128), jnp.int32)
    for k in range(2):
        edge_idx[k : k + 1, :] = base + rank[k]
        edge_idx[2 + k : 3 + k, :] = back[k]
    none = jnp.full((4, 128), 3, jnp.int32)
    edge_mine = jnp.concatenate([mine[0], mine[1], near_own[0], near_own[1], none], axis=0)
    edge_theirs = jnp.concatenate([theirs[0], theirs[1], near_far[0], near_far[1], none], axis=0)

    nu = visc[...]
    wide = layout[...] == 0
    tab[0:1, :] = nu * jnp.where(wide, 2.0, 0.5)
    tab[1:2, :] = nu * jnp.where(wide, 0.5, 2.0)
    tab[2:3, :] = nu
    for face in range(4):
        tab[3 + face : 4 + face, :] = whole[2 * face : 2 * face + 1].astype(F32)
    tab[MIXED : MIXED + 1, :] = jnp.max(odd_one, axis=0, keepdims=True)
    mine_m = [PENALTY * HALVES[o].T @ np.diag(W) @ HALVES[o] for o in range(3)]
    far_m = [
        [-PENALTY * HALVES[o].T @ np.diag(W) @ HALVES[c] for c in range(3)] for o in range(3)
    ]
    for code, facing, own_ref, far_ref in (
        (inside, other, own_c, far_c),
        (edge_mine, edge_theirs, edge_own, edge_far),
    ):
        hot = [(code == o).astype(F32) for o in range(3)]
        pair = [[hot[o] * (facing == c).astype(F32) for c in range(3)] for o in range(3)]
        for a in range(6):
            for b in range(6):
                n = 6 * a + b
                total = sum(float(mine_m[o][a, b]) * hot[o] for o in range(3))
                own_ref[n] = total + pltpu.roll(total, 7, 0)
                far_ref[n] = sum(
                    float(far_m[o][c][a, b]) * pair[o][c] for o in range(3) for c in range(3)
                )


def group_rows(group):
    return pl.ds(pl.multiple_of(group * 8, 8), 8)


def row_of(ref, r):
    return jnp.broadcast_to(ref[r : r + 1, :], (8, 128))


def face_nodes(face):
    return [
        6 * i + j
        for i, j in [
            (0, b) if face == 0 else (5, b) if face == 1 else (b, 0) if face == 2 else (b, 5)
            for b in range(6)
        ]
    ]


def either(tab, loop):
    mixed = jnp.max(tab[MIXED : MIXED + 1, :]) > 0.5
    for plain in (True, False):

        @pl.when(mixed != plain)
        def _(plain=plain):
            lax.fori_loop(
                0, 4, lambda group, carry: loop(group, plain) or carry, 0, unroll=2 if plain else 1
            )


def weighted(factors, values):
    total = float(factors[0]) * values[0]
    for f, v in zip(factors[1:], values[1:]):
        total = total + float(f) * v
    return total


def plain_terms(env, v):
    idx, tab, _, _ = env

    def of_face(face):
        active = row_of(tab, 3 + face)
        local = row_of(idx, LOCAL + 2 * face)

        def term(a):
            n, m = face_nodes(face)[a], face_nodes(face ^ 1)[a]
            return (float(PENALTY * W[a]) * active) * (v(n) - take(v(m), local))

        return term

    return [of_face(face) for face in range(4)]


def general_terms(env, v):
    idx, _, own_c, far_c = env
    found = []
    for face in range(4):
        mine = [v(n) for n in face_nodes(face)]
        theirs = [
            [take(v(n), row_of(idx, LOCAL + 2 * face + t)) for n in face_nodes(face ^ 1)]
            for t in range(2)
        ]
        values = []
        for a in range(6):
            extra = jnp.zeros((8, 128), F32)
            for b in range(6):
                extra = extra + own_c[6 * a + b, 2 * face : 2 * face + 1, :] * mine[b]
                for t in range(2):
                    s = 2 * face + t
                    extra = extra + far_c[6 * a + b, s : s + 1, :] * theirs[t][b]
            values.append(extra)
        found.append(values.__getitem__)
    return found


FACE_LINES, INSIDE_LINES, ALL_LINES = (0,), (1, 2), (0, 1, 2)


def inner(group, env, v_ref, plain, emit, pairs=ALL_LINES):
    idx, tab, _, _ = env
    rows = group_rows(group)

    def v(n):
        return v_ref[n, rows, :]

    terms = (plain_terms if plain else general_terms)(env, v)
    q = row_of(idx, FIRST) + group * 8 + lax.broadcasted_iota(jnp.int32, (8, 128), 0)
    harmonic = lax.shift_right_logical(q + 1, 1).astype(F32) * SPANWISE
    cx, cy = row_of(tab, 0), row_of(tab, 1)
    shift = 1.0 + 0.5 * tab[2:3, :] * (harmonic * harmonic)
    plus, minus = STIFF_FOLD
    even = [[v(6 * a + j) + v(30 - 6 * a + j) for a in range(3)] for j in range(6)]
    odd = [[v(6 * a + j) - v(30 - 6 * a + j) for a in range(3)] for j in range(6)]
    for i in pairs:
        e = [weighted(plus[i], even[j]) for j in range(6)]
        o = [weighted(minus[i], odd[j]) for j in range(6)]
        for line in (i, 5 - i):
            mine = [v(6 * line + j) for j in range(6)]
            g = folded(mine, STIFF_FOLD, 1)
            for j in range(6):
                n = 6 * line + j
                gx = e[j] + o[j] if line == i else e[j] - o[j]
                value = float(W[line] * W[j]) * (shift * mine[j] + cx * gx + cy * g[j])
                for face, (at, b) in enumerate(((line == 0, j), (line == 5, j), (j == 0, line), (j == 5, line))):
                    if at:
                        value = value + terms[face](b)
                emit(n, value)


def line_at(n):
    return n if n < 6 else n - 24


def compact(idx, v_ref, h_ref, send_w, send_e, at=line_at):
    part = lax.shift_right_logical(lane_ids((8, 128)), 4)
    for face, ref in ((0, send_w), (1, send_e)):
        index = row_of(idx, face)
        for b in range(6):
            n = face_nodes(face)[b]
            value = take(v_ref[n, 0:8, :], index)
            for k in range(1, 8):
                part_rows = slice(8 * (k % 4), 8 * (k % 4) + 8)
                source = v_ref[n, part_rows, :] if k < 4 else h_ref[at(n), part_rows, :]
                other = take(source, index)
                value = jnp.where(part == k, other, value)
            ref[8 * b : 8 * b + 8, :] = value


def outer(group, idx, edge, first):
    found = {}
    for face in range(2):
        lanes = row_of(idx, SELF + face) + (64 * face + 16 * group)
        on = row_of(idx, ANY + face) > 0
        for b in range(6):
            value = take(edge[first + 8 * b : first + 8 * b + 8, :], lanes)
            found[face_nodes(face)[b]] = jnp.where(on, value, 0.0)
    return found


def edge_blocks(ref):
    return [ref[8 * b : 8 * b + 8, :] for b in range(6)]


def merge(to_w, to_e):
    west = lane_ids((8, 128)) < 64
    plain, inner_h = [], []
    for w, e in zip(edge_blocks(to_w), edge_blocks(to_e)):
        plain.append(jnp.where(west, w, pltpu.roll(e, 64, 1)))
        inner_h.append(jnp.where(west, pltpu.roll(w, 64, 1), e))
    return plain, inner_h


def edge_term(edge_idx, edge_own, edge_far, mine, theirs, row):
    near = [[take(t, row_of(edge_idx, row + k)) for t in theirs] for k in range(2)]
    out = []
    for a in range(6):
        chains = [None] * 3
        for b in range(6):
            n = 6 * a + b
            terms = [edge_own[n, row : row + 1, :] * mine[b]]
            terms += [edge_far[n, row + k : row + k + 1, :] * near[k][b] for k in range(2)]
            chains = terms if chains[0] is None else [c + t for c, t in zip(chains, terms)]
        out.append(chains[0] + (chains[1] + chains[2]))
    return out


def store_sums(acc, pad, first, count):
    width = count * 128
    lhs = (
        lax.broadcasted_iota(jnp.int32, (8, width), 0)
        == lax.shift_right_logical(lane_ids((8, width)), 7) + first
    ).astype(F32)
    sums = lax.dot_general(
        lhs, acc[...], (((1,), (1,)), ((), ())),
        precision=lax.Precision.HIGHEST, preferred_element_type=F32,
    )
    pad[...] = jnp.ones((8, 128), F32)
    pad[:, 0:32] = sums


HALF = 10.0


def store_lines(ref, rows):
    def emit(n, value):
        ref[line_at(n), rows, :] = value

    return emit


def inside_kernel(idx, tab, own_c, far_c, v, out):
    env = (idx, tab, own_c, far_c)

    def loop(group, plain):
        rows = group_rows(group)

        def emit(n, value):
            out[n - 6, rows, :] = value

        inner(group, env, v, plain, emit, INSIDE_LINES)

    either(tab, loop)


def line_image(lines, inside, n, rows):
    return inside[n - 6, rows, :] if 6 <= n < 30 else lines[line_at(n), rows, :]


def guess_kernel(
    links, sides, visc, layout, u_far,
    idx, edge_idx, tab, own_c, far_c, edge_own, edge_far, out, u, sem,
):
    copy = pltpu.make_async_copy(u_far, u, sem)
    copy.start()
    build_tables(
        links, sides, visc, layout, idx, edge_idx, tab, own_c, far_c, edge_own, edge_far
    )
    copy.wait()
    env = (idx, tab, own_c, far_c)

    def loop(group, plain):
        rows = group_rows(group)

        def emit(n, value):
            out[n, rows, :] = float(W[n // 6] * W[n % 6]) * u[n, rows, :] - value

        inner(group, env, u, plain, emit)

    either(tab, loop)


def guess_edge_kernel(edge_idx, edge_own, edge_far, to_w, to_e, from_w, from_e, edge):
    mine, _ = merge(to_w, to_e)
    theirs, _ = merge(from_w, from_e)
    for b, value in enumerate(edge_term(edge_idx, edge_own, edge_far, mine, theirs, 0)):
        edge[8 * b : 8 * b + 8, :] = value


def residual_kernel(
    idx, tab, own_c, far_c, back, base, edge, out, h_out, send_w, send_e
):
    env = (idx, tab, own_c, far_c)

    def turn(g, carry):
        part = pl.ds(pl.multiple_of(16 * g, 16), 16)
        turned = back[:, part, :].reshape(128, 128).T
        for m in range(4):
            out[4 * g + m] = base[4 * g + m] + turned[32 * m : 32 * m + 32]
        return carry

    lax.fori_loop(0, 9, turn, 0, unroll=3)

    def loop(group, plain):
        rows = group_rows(group)
        for n, extra in outer(group, idx, edge, 0).items():
            out[n, rows, :] -= extra
        inner(group, env, out, plain, store_lines(h_out, rows), FACE_LINES)

    either(tab, loop)
    compact(idx, out, h_out, send_w, send_e)


def edge_steps(tables, to_w, to_e, from_w, from_e, before, edge, keep):
    edge_idx, edge_own, edge_far = tables
    mine, mine_h = merge(to_w, to_e)
    theirs, theirs_h = merge(from_w, from_e)
    scale = (1.0 if before is None else 2.0) / HALF
    first = edge_term(edge_idx, edge_own, edge_far, mine, theirs, 0)
    facing = edge_term(edge_idx, edge_own, edge_far, theirs, mine, 2)
    mine_next, theirs_next = [], []
    for b in range(6):
        if before is None:
            mine_next.append(scale * (mine_h[b] + first[b]) - mine[b])
            theirs_next.append(scale * (theirs_h[b] + facing[b]) - theirs[b])
        else:
            old = before[8 * b : 8 * b + 8, :], before[48 + 8 * b : 56 + 8 * b, :]
            mine_next.append(scale * (mine_h[b] + first[b]) - 2.0 * mine[b] - old[0])
            theirs_next.append(scale * (theirs_h[b] + facing[b]) - 2.0 * theirs[b] - old[1])
    second = edge_term(edge_idx, edge_own, edge_far, mine_next, theirs_next, 0)
    for b in range(6):
        edge[8 * b : 8 * b + 8, :] = first[b]
        edge[48 + 8 * b : 56 + 8 * b, :] = second[b]
        if keep is not None:
            keep[8 * b : 8 * b + 8, :] = mine_next[b]
            keep[48 + 8 * b : 56 + 8 * b, :] = theirs_next[b]


def two_steps_kernel(
    idx, tab, own_c, far_c, edge_idx, edge_own, edge_far,
    t0, h0, h0_in, to_w, to_e, from_w, from_e,
    t1, t2, h2, send_w, send_e, keep, edge,
):
    env = (idx, tab, own_c, far_c)
    tables = (edge_idx, edge_own, edge_far)
    edge_steps(tables, to_w, to_e, from_w, from_e, None, edge, keep)

    def loop(group, plain):
        rows = group_rows(group)
        extra = outer(group, idx, edge, 0)
        for n in range(36):
            image = line_image(h0, h0_in, n, rows)
            if n in extra:
                image = image + extra[n]
            t1[n, rows, :] = (1.0 / HALF) * image - t0[n, rows, :]
        extra_next = outer(group, idx, edge, 48)

        def emit(n, image):
            if n in extra_next:
                image = image + extra_next[n]
            t2[n, rows, :] = (2.0 / HALF) * image - 2.0 * t1[n, rows, :] - t0[n, rows, :]

        inner(group, env, t1, plain, emit)
        inner(group, env, t2, plain, store_lines(h2, rows), FACE_LINES)

    either(tab, loop)
    compact(idx, t2, h2, send_w, send_e)


def sums_kernel(t0, t1, t2, part, acc, pad):
    def body(group, carry):
        rows = group_rows(group)
        sums = [jnp.zeros((8, 128), F32)] * 5
        for n in range(36):
            a, b, c = t0[n, rows, :], t1[n, rows, :], t2[n, rows, :]
            for k, term in enumerate((a * a, a * b, b * b, b * c, c * c)):
                sums[k] = sums[k] + term
        for k in range(5):
            acc[rows, 128 * k : 128 * k + 128] = sums[k]
        return carry

    lax.fori_loop(0, 4, body, 0)
    store_sums(acc, pad, 0, 5)
    part[...] = pad[...]


def last_steps_kernel(
    idx, tab, own_c, far_c, edge_idx, edge_own, edge_far,
    t1, t2, h2, h2_in, to_w, to_e, from_w, from_e, keep, part,
    t3, red, edge, acc, pad,
):
    env = (idx, tab, own_c, far_c)
    tables = (edge_idx, edge_own, edge_far)
    edge_steps(tables, to_w, to_e, from_w, from_e, keep, edge, None)

    def loop(group, plain):
        rows = group_rows(group)
        extra = outer(group, idx, edge, 0)
        sums = [jnp.zeros((8, 128), F32)] * 3
        for n in range(36):
            image = line_image(h2, h2_in, n, rows)
            if n in extra:
                image = image + extra[n]
            c = t2[n, rows, :]
            d = (2.0 / HALF) * image - 2.0 * c - t1[n, rows, :]
            t3[n, rows, :] = d
            sums[0] = sums[0] + c * d
            sums[1] = sums[1] + d * d
        extra_next = outer(group, idx, edge, 48)

        def emit(n, image):
            if n in extra_next:
                image = image + extra_next[n]
            d = t3[n, rows, :]
            sums[2] = sums[2] + d * ((2.0 / HALF) * image - 2.0 * d - t2[n, rows, :])

        inner(group, env, t3, plain, emit)
        for k in range(3):
            acc[rows, 128 * k : 128 * k + 128] = sums[k]

    either(tab, loop)
    store_sums(acc, pad, 5, 3)
    row = lax.broadcasted_iota(jnp.int32, (8, 128), 0)
    mixed = jnp.where(row < 5, part[...], pad[...])
    for k in range(16):
        red[k] = mixed


def finish_kernel(red, x0, t0, t1, t2, t3, out, coef, held, sems):
    total = red[0]
    for k in range(1, 16):
        total = total + red[k]
    even = [total[2 * k : 2 * k + 1] for k in range(4)]
    odd = [total[2 * k + 1 : 2 * k + 2] for k in range(4)]
    moment = []
    for k in range(4):
        moment.append(even[0] if k == 0 else 2.0 * even[k] - even[0])
        moment.append(odd[0] if k == 0 else 2.0 * odd[k] - odd[0])

    def inner_product(i, j):
        return 0.5 * (moment[i + j] + moment[abs(i - j)])

    def energy(i, j):
        shifted = 0.5 * (inner_product(i, j + 1) + inner_product(i, abs(j - 1)))
        return HALF * (shifted + inner_product(i, j))

    low = [[None] * 4 for _ in range(4)]
    diag, inverse, half = [], [], []
    for j in range(4):
        d = energy(j, j)
        value = moment[j]
        for k in range(j):
            d = d - low[j][k] * low[j][k] * diag[k]
            value = value - low[j][k] * half[k]
        diag.append(d)
        half.append(value)
        inverse.append(1.0 / d)
        for i in range(j + 1, 4):
            e = energy(i, j)
            for k in range(j):
                e = e - low[i][k] * low[j][k] * diag[k]
            low[i][j] = e * inverse[j]
    weight = [half[k] * inverse[k] for k in range(4)]
    for i in (2, 1, 0):
        for k in range(i + 1, 4):
            weight[i] = weight[i] - low[k][i] * weight[k]
    turned = jnp.concatenate(weight + [jnp.zeros((4, 128), F32)], axis=0).T
    for k in range(4):
        coef[k] = jnp.broadcast_to(turned[0:32, k : k + 1], (32, 128))
    copies = []
    for c in range(3):
        def add(n, carry):
            terms = coef[0] * t0[n] + coef[1] * t1[n] + coef[2] * t2[n] + coef[3] * t3[n]
            held[n] = x0[n] + terms
            return carry

        lax.fori_loop(12 * c, 12 * c + 12, add, 0, unroll=3)
        part = pl.ds(12 * c, 12)
        copies.append(pltpu.make_async_copy(held.at[part], out.at[part], sems.at[c]))
        copies[c].start()
    for copy in copies:
        copy.wait()


def pack_kernel(u, links, out, send_w, send_e, held, ready, near_links, lists, sems):
    loads, stores = [], []
    first = pltpu.make_async_copy(links, near_links, sems.at[6])
    first.start()
    for c in range(3):
        part = pl.ds(12 * c, 12)
        loads.append(pltpu.make_async_copy(u.at[part], held.at[part], sems.at[c]))
        loads[c].start()
    first.wait()
    dev = lax.shift_right_logical(near_links[...], 7)
    remote = (dev != lax.axis_index("elem")).astype(jnp.int32)
    for side in range(2):
        lists[side : side + 1, :] = boundary(remote, side)[0].astype(jnp.int32)
    for c in range(3):
        loads[c].wait()
        for g in range(3 * c, 3 * c + 3):
            turned = held[4 * g : 4 * g + 4].reshape(128, 128).T
            ready[:, 16 * g : 16 * g + 16, :] = turned.reshape(8, 16, 128)
        part = pl.ds(48 * c, 48)
        stores.append(pltpu.make_async_copy(ready.at[:, part], out.at[:, part], sems.at[3 + c]))
        stores[c].start()
    compact(lists, held, held, send_w, send_e, lambda n: n)
    for copy in stores:
        copy.wait()


def block_turn(blocks):
    part = lax.shift_right_logical(lane_ids(blocks[0].shape), 5)
    rolled = [blocks[0]] + [pltpu.roll(blocks[s], 32 * s, 1) for s in range(1, 4)]
    out = []
    for m in range(4):
        mixed = rolled[-m % 4]
        for t in range(1, 4):
            mixed = jnp.where(part == t, rolled[(t - m) % 4], mixed)
        out.append(pltpu.roll(mixed, 128 - 32 * m, 1) if m else mixed)
    return out


def product3(high, low, table, dim):
    def dot(a, b):
        return lax.dot_general(a, b, (((1,), (dim,)), ((), ())), preferred_element_type=F32)

    return dot(high, table[0]) + dot(high, table[1]) + dot(low, table[0])


def advect_kernel(idx, came, speed, synth, out, high, low, phys):
    for g in range(9):
        for h in range(2):
            pieces = block_turn([came[4 * h + s, 16 * g : 16 * g + 16, :] for s in range(4)])
            for m in range(4):
                n = 16 * (4 * g + m)
                hi, lo = split(pieces[m])
                high[n : n + 16, 128 * h : 128 * h + 128] = hi
                low[n : n + 16, 128 * h : 128 * h + 128] = lo
    for i in range(2):
        part = slice(288 * i, 288 * i + 288)
        phys[part, :] = product3(high[part, :], low[part, :], synth, 1)
    wide = jnp.broadcast_to(idx[LAYOUT : LAYOUT + 1, :], (16, 128)) == 0
    sx = jnp.where(wide, 2.0, 1.0)
    sy = jnp.where(wide, 1.0, 2.0)
    for h in range(2):
        cols = slice(128 * h, 128 * h + 128)
        u = [[phys[16 * (6 * i + j) : 16 * (6 * i + j) + 16, cols] for j in range(6)] for i in range(6)]
        acc = [[None] * 6 for _ in range(6)]
        for j in range(6):
            g = folded([u[i][j] for i in range(6)], DERIV_FOLD, -1)
            for i in range(6):
                acc[i][j] = sx * (speed[0, 6 * i + j, :, cols] * g[i])
        for i in range(6):
            g = folded(u[i], DERIV_FOLD, -1)
            for j in range(6):
                n = 16 * (6 * i + j)
                total = acc[i][j] + sy * (speed[1, 6 * i + j, :, cols] * g[j])
                hi, lo = split(float(-0.5 * W[i] * W[j]) * total)
                high[n : n + 16, cols] = hi
                low[n : n + 16, cols] = lo
    for i in range(2):
        part = slice(288 * i, 288 * i + 288)
        phys[part, :] = product3(high[part, :], low[part, :], synth, 0)
    for h in range(2):
        q = lane_ids((16, 128)) + 128 * h
        norm = jnp.where((q == 0) | (q == 255), 1.0 / 256, 1.0 / 128)
        cols = slice(128 * h, 128 * h + 128)
        for g in range(9):
            pieces = block_turn(
                [norm * phys[16 * (4 * g + m) : 16 * (4 * g + m) + 16, cols] for m in range(4)]
            )
            for s in range(4):
                out[4 * h + s, 16 * g : 16 * g + 16, :] = pieces[s]


def shift_by(array, by):
    count = lax.axis_size("elem")
    return lax.ppermute(array, "elem", [(i, (i + by) % count) for i in range(count)])


def shards(scalar_modes, velocity, viscosity, mortar_links, mortar_sides, layout):
    u = jnp.transpose(scalar_modes, (1, 2, 0, 3)).reshape(36, 32, 128)
    speed = jnp.transpose(velocity, (0, 2, 3, 4, 1)).reshape(2, 36, 16, 256)
    synth = jnp.asarray(split_table(plane_tables(256)))
    vol, edge = shape(36, 32, 128), shape(48, 128)
    both = shape(96, 128)
    blocks = shape(8, 144, 128)
    packed, *sent = call(
        pack_kernel,
        [blocks, edge, edge],
        [
            VMEM((36, 32, 128), F32),
            VMEM((8, 144, 128), F32),
            VMEM((8, 128), jnp.int32),
            VMEM((8, 128), jnp.int32),
            pltpu.SemaphoreType.DMA((7,)),
        ],
        [u, mortar_links],
        [HBM, HBM],
        [HBM, VMEM, VMEM],
    )
    came = lax.all_to_all(packed, "plane", 0, 0, tiled=True)

    table = shape(36, 8, 128)
    idx, edge_idx, tab, own_c, far_c, edge_own, edge_far, base = call(
        guess_kernel,
        [
            shape(24, 128, dtype=jnp.int32),
            shape(8, 128, dtype=jnp.int32),
            shape(8, 128),
        ]
        + [table] * 4
        + [vol],
        [VMEM((36, 32, 128), F32), pltpu.SemaphoreType.DMA],
        [mortar_links, mortar_sides, viscosity[None], layout[None], u],
        [VMEM] * 4 + [HBM],
    )
    head = [idx, tab, own_c, far_c]
    edges = [edge_idx, edge_own, edge_far]

    def run(kernel, outs, scratch, args):
        return call(kernel, outs, scratch, args, [VMEM] * len(args))

    def trade(send_w, send_e):
        return shift_by(send_e, 1), shift_by(send_w, -1)

    guess_edge = run(guess_edge_kernel, [shape(48, 128)], [], [*edges, *sent, *trade(*sent)])[0]
    came, guess_edge, base = lax.optimization_barrier((came, guess_edge, base))
    back = call(
        advect_kernel,
        [blocks],
        [
            VMEM((576, 256), BF16),
            VMEM((576, 256), BF16),
            VMEM((576, 256), F32),
        ],
        [idx, came, speed, synth],
        [VMEM] * 4,
        grant=8,
    )[0]
    back = lax.all_to_all(back, "plane", 0, 0, tiled=True)

    def work(count):
        return [
            VMEM((96, 128), F32),
            VMEM((32, 128 * count), F32),
            VMEM((8, 128), F32),
        ]

    lines, insides = shape(12, 32, 128), shape(24, 32, 128)
    t0, h0, *sent = run(
        residual_kernel, [vol, lines, edge, edge], [], head + [back, base, guess_edge]
    )
    got = trade(*sent)
    h0_in = run(inside_kernel, [insides], [], head + [t0])[0]
    t1, t2, h2, to_w, to_e, keep = run(
        two_steps_kernel,
        [vol, vol, lines, edge, edge, both],
        [VMEM((96, 128), F32)],
        head + edges + [t0, h0, h0_in, *sent, *got],
    )
    got = trade(to_w, to_e)
    h2_in = run(inside_kernel, [insides], [], head + [t2])[0]
    part = run(sums_kernel, [shape(8, 128)], work(5)[1:], [t0, t1, t2])[0]
    t3, red = run(
        last_steps_kernel,
        [vol, shape(16, 8, 128)],
        work(3),
        head + edges + [t1, t2, h2, h2_in, to_w, to_e, *got, keep, part],
    )
    red = lax.all_to_all(red, "elem", 0, 0, tiled=True)
    out = call(
        finish_kernel,
        [vol],
        [VMEM((4, 32, 128), F32), VMEM((36, 32, 128), F32), pltpu.SemaphoreType.DMA((3,))],
        [red, u, t0, t1, t2, t3],
        [VMEM] * 6,
        [HBM],
    )[0]
    return jnp.transpose(out.reshape(6, 6, 32, 128), (2, 0, 1, 3))


def solution(mesh):
    placed = (
        P("plane", None, None, "elem"),
        P(None, None, None, None, ("elem", "plane")),
        P("elem"),
        P(None, "elem"),
        P(None, None, "elem"),
        P("elem"),
    )
    return jax.shard_map(
        shards,
        mesh=mesh,
        in_specs=placed,
        out_specs=P("plane", None, None, "elem"),
        check_vma=False,
    )
```

```python
import math

import jax
import jax.numpy as jnp
import ml_dtypes
import numpy as np
from jax import lax
from jax.experimental import pallas as pl
from jax.experimental.pallas import tpu as pltpu
from jax.sharding import PartitionSpec as P

F32 = jnp.float32
BF16 = jnp.bfloat16
PENALTY = 10.0
SPANWISE = 0.0625
VMEM = pltpu.VMEM
SMEM = pltpu.SMEM
HBM = pltpu.HBM
MIXED = 7
SELF, ANY, FIRST, LAYOUT, LOCAL = 2, 4, 6, 7, 10


def lagrange_at(points, targets):
    out = np.ones((6, 6))
    for row in range(6):
        for col in range(6):
            for other in range(6):
                if other != col:
                    out[row, col] *= (targets[row] - points[other]) / (points[col] - points[other])
    return out


def node_tables():
    root = math.sqrt(7.0)
    outer = math.sqrt(1.0 / 3.0 + 2.0 * root / 21.0)
    inner = math.sqrt(1.0 / 3.0 - 2.0 * root / 21.0)
    points = np.array([-1.0, -outer, -inner, inner, outer, 1.0])
    half = [1.0 / 15.0, (14.0 - root) / 30.0, (14.0 + root) / 30.0]
    weights = np.array(half + half[::-1])
    bary = np.array(
        [1.0 / np.prod([points[c] - points[k] for k in range(6) if k != c]) for c in range(6)]
    )
    deriv = np.zeros((6, 6))
    for i in range(6):
        for j in range(6):
            if i != j:
                deriv[i, j] = bary[j] / bary[i] / (points[i] - points[j])
        deriv[i, i] = -np.sum(deriv[i])
    lower = lagrange_at(points, (points - 1.0) / 2.0)
    upper = lagrange_at(points, (points + 1.0) / 2.0)
    stiff = deriv.T @ (weights[:, None] * deriv)
    return weights, deriv, lower, upper, stiff


W, D, QLO, QHI, K1 = node_tables()
HALVES = [np.eye(6), QLO, QHI]


def plane_tables(count):
    planes = np.arange(count)[:, None]
    coeffs = np.arange(count)[None, :]
    harmonic = (coeffs + 1) // 2
    phase = 2.0 * np.pi * (harmonic * planes % count) / count
    synth = np.where(coeffs == 0, 1.0, np.where(coeffs % 2 == 1, np.cos(phase), np.sin(phase)))
    return synth


def split_table(table):
    table = np.asarray(table, np.float32)
    high = table.astype(ml_dtypes.bfloat16)
    low = (table - high.astype(np.float32)).astype(ml_dtypes.bfloat16)
    return np.stack([high, low])


def fold(matrix):
    plus = (matrix[:3, :3] + matrix[:3, :2:-1]) / 2.0
    minus = (matrix[:3, :3] - matrix[:3, :2:-1]) / 2.0
    return plus, minus


STIFF_FOLD = fold(K1 / W[:, None])
DERIV_FOLD = fold(D)


def folded(values, tables, sign):
    plus, minus = tables
    even = [values[a] + values[5 - a] for a in range(3)]
    odd = [values[a] - values[5 - a] for a in range(3)]
    out = [None] * 6
    for i in range(3):
        e = sum(float(plus[i, a]) * even[a] for a in range(3))
        o = sum(float(minus[i, a]) * odd[a] for a in range(3))
        out[i] = e + o
        out[5 - i] = e - o if sign > 0 else o - e
    return out


def split(value):
    high = value.astype(BF16)
    return high, (value - high.astype(F32)).astype(BF16)


def lane_ids(shape):
    return lax.broadcasted_iota(jnp.int32, shape, len(shape) - 1)


def call(kernel, outs, scratch, operands, spaces, out_spaces=None, grant=3):
    total = sum(int(np.prod(o.shape)) * 4 for o in outs)
    total += sum(int(np.prod(o.shape)) * 4 for o in operands)
    return pl.pallas_call(
        kernel,
        out_shape=outs,
        in_specs=[pl.BlockSpec(memory_space=s) for s in spaces],
        out_specs=[pl.BlockSpec(memory_space=s) for s in out_spaces or [VMEM] * len(outs)],
        scratch_shapes=scratch,
        compiler_params=pltpu.CompilerParams(vmem_limit_bytes=grant * 2**20),
        cost_estimate=pl.CostEstimate(flops=4_000_000, bytes_accessed=total, transcendentals=0),
    )(*[far(a) if s == HBM else a for a, s in zip(operands, spaces)])


def far(array):
    return pltpu.with_memory_space_constraint(array, HBM)


def shape(*dims, dtype=F32):
    return jax.ShapeDtypeStruct(dims, dtype)


def take(value, index):
    return jnp.take_along_axis(value, index, axis=1)


def take_row(value, index):
    wide = jnp.broadcast_to(value, (8, 128)), jnp.broadcast_to(index, (8, 128))
    return take(*wide)[0:1]


def boundary(remote, side):
    row = lax.broadcasted_iota(jnp.int32, (128, 128), 0)
    col = lane_ids((128, 128))
    any_rem = jnp.maximum(remote[2 * side : 2 * side + 1], remote[2 * side + 1 : 2 * side + 2])
    before = jnp.sum(jnp.where(col < row, any_rem, 0).astype(F32), axis=1, keepdims=True)
    mine = jnp.sum(jnp.where(col == row, any_rem, 0).astype(F32), axis=1, keepdims=True)
    slot = jnp.bitwise_and(lane_ids((1, 128)), 15).astype(F32)
    chosen = jnp.where((before == slot) & (mine > 0.0), 1.0, 0.0)
    listed = jnp.sum(chosen * row.astype(F32), axis=0, keepdims=True)
    return listed, jnp.sum(chosen, axis=0, keepdims=True), before


def build_tables(
    links, sides, visc, layout, idx, edge_idx, tab, own_c, far_c, edge_own, edge_far
):
    me = lax.axis_index("elem")
    dev = lax.shift_right_logical(links[...], 7)
    loc = jnp.bitwise_and(links[...], 127)
    remote = (dev != me).astype(jnp.int32)
    idx[LOCAL : LOCAL + 8, :] = loc
    own, other = sides[0], sides[1]
    inside = jnp.where(remote > 0, 3, own)
    whole = (inside == 0) & (other == 0)
    second = jnp.bitwise_and(lax.broadcasted_iota(jnp.int32, (8, 128), 0), 1) == 1
    odd_one = jnp.where(inside == 3, 0.0, jnp.where(whole & ~second, 0.0, 1.0))
    idx[FIRST : FIRST + 1, :] = jnp.full((1, 128), 32 * lax.axis_index("plane"), jnp.int32)
    idx[LAYOUT : LAYOUT + 1, :] = layout[...]
    row = lax.broadcasted_iota(jnp.int32, (128, 128), 0)
    col = lane_ids((128, 128))
    lane = lane_ids((1, 128))
    slot = jnp.bitwise_and(lane, 15)
    listed, present, ranks = [], [], []
    for side in range(2):
        rem = [remote[2 * side + t : 2 * side + t + 1] for t in range(2)]
        far = [loc[2 * side + t : 2 * side + t + 1] for t in range(2)]
        any_rem = jnp.maximum(rem[0], rem[1])
        places, filled, before = boundary(remote, side)
        listed.append(places.astype(jnp.int32))
        present.append(filled.astype(jnp.int32))
        idx[side : side + 1, :] = listed[side]
        mine_at = jnp.sum(jnp.where(row == col, before, 0.0), axis=0, keepdims=True)
        mine_at = jnp.where(any_rem > 0, mine_at.astype(jnp.int32), 0)
        idx[SELF + side : SELF + side + 1, :] = mine_at
        idx[ANY + side : ANY + side + 1, :] = any_rem
        named = jnp.where(
            ((far[0] == row) & (rem[0] > 0)) | ((far[1] == row) & (rem[1] > 0)), 1.0, 0.0
        )
        named = jnp.max(named, axis=1, keepdims=True)
        for t in range(2):
            rank = jnp.sum(jnp.where(row < far[t], named, 0.0), axis=0, keepdims=True)
            ranks.append(jnp.where(rem[t] > 0, rank.astype(jnp.int32), 0))
    idx[8:10, :] = jnp.zeros((2, 128), jnp.int32)
    idx[18:24, :] = jnp.zeros((6, 128), jnp.int32)

    west = lane < 64
    base = jnp.bitwise_and(lane, 112)
    element = jnp.where(west, listed[0], listed[1])
    here = jnp.where(west, present[0], present[1]) > 0

    def pick(rows_w, rows_e):
        return jnp.where(west, take_row(rows_w, element), take_row(rows_e, element))

    rank, live, mine, theirs = [], [], [], []
    for t in range(2):
        rank.append(pick(ranks[t], ranks[2 + t]))
        live.append((pick(remote[t : t + 1], remote[2 + t : 3 + t]) > 0) & here)
        mine.append(jnp.where(live[t], pick(own[t : t + 1], own[2 + t : 3 + t]), 3))
        theirs.append(jnp.where(live[t], pick(other[t : t + 1], other[2 + t : 3 + t]), 3))
    first = jnp.full((1, 128), 99, jnp.int32)
    last = jnp.full((1, 128), -1, jnp.int32)
    for t in range(2):
        target = jnp.where(live[t], rank[t], 99)
        for r in range(16):
            hit = take_row(target, base + r) == slot
            first = jnp.where(hit, jnp.minimum(first, 16 * t + r), first)
            last = jnp.where(hit, jnp.maximum(last, 16 * t + r), last)
    exists = [last >= 0, last > first]
    key = [jnp.where(exists[0], first, 0), jnp.where(exists[1], last, 0)]
    back = [base + jnp.bitwise_and(k, 15) for k in key]

    def from_key(k, pair):
        value = jnp.where(key[k] >= 16, take_row(pair[1], back[k]), take_row(pair[0], back[k]))
        return jnp.where(exists[k], value, 3)

    near_own = [from_key(k, theirs) for k in range(2)]
    near_far = [from_key(k, mine) for k in range(2)]
    edge_idx[...] = jnp.zeros((8, 128), jnp.int32)
    for k in range(2):
        edge_idx[k : k + 1, :] = base + rank[k]
        edge_idx[2 + k : 3 + k, :] = back[k]
    none = jnp.full((4, 128), 3, jnp.int32)
    edge_mine = jnp.concatenate([mine[0], mine[1], near_own[0], near_own[1], none], axis=0)
    edge_theirs = jnp.concatenate([theirs[0], theirs[1], near_far[0], near_far[1], none], axis=0)

    nu = visc[...]
    wide = layout[...] == 0
    tab[0:1, :] = nu * jnp.where(wide, 2.0, 0.5)
    tab[1:2, :] = nu * jnp.where(wide, 0.5, 2.0)
    tab[2:3, :] = nu
    for face in range(4):
        tab[3 + face : 4 + face, :] = whole[2 * face : 2 * face + 1].astype(F32)
    tab[MIXED : MIXED + 1, :] = jnp.max(odd_one, axis=0, keepdims=True)
    mine_m = [PENALTY * HALVES[o].T @ np.diag(W) @ HALVES[o] for o in range(3)]
    far_m = [
        [-PENALTY * HALVES[o].T @ np.diag(W) @ HALVES[c] for c in range(3)] for o in range(3)
    ]
    for code, facing, own_ref, far_ref in (
        (inside, other, own_c, far_c),
        (edge_mine, edge_theirs, edge_own, edge_far),
    ):
        hot = [(code == o).astype(F32) for o in range(3)]
        pair = [[hot[o] * (facing == c).astype(F32) for c in range(3)] for o in range(3)]
        for a in range(6):
            for b in range(6):
                n = 6 * a + b
                total = sum(float(mine_m[o][a, b]) * hot[o] for o in range(3))
                own_ref[n] = total + pltpu.roll(total, 7, 0)
                far_ref[n] = sum(
                    float(far_m[o][c][a, b]) * pair[o][c] for o in range(3) for c in range(3)
                )


def group_rows(group):
    return pl.ds(pl.multiple_of(group * 8, 8), 8)


def row_of(ref, r):
    return jnp.broadcast_to(ref[r : r + 1, :], (8, 128))


def face_nodes(face):
    return [
        6 * i + j
        for i, j in [
            (0, b) if face == 0 else (5, b) if face == 1 else (b, 0) if face == 2 else (b, 5)
            for b in range(6)
        ]
    ]


def either(tab, loop):
    mixed = jnp.max(tab[MIXED : MIXED + 1, :]) > 0.5
    for plain in (True, False):

        @pl.when(mixed != plain)
        def _(plain=plain):
            lax.fori_loop(
                0, 4, lambda group, carry: loop(group, plain) or carry, 0, unroll=2 if plain else 1
            )


def weighted(factors, values):
    total = float(factors[0]) * values[0]
    for f, v in zip(factors[1:], values[1:]):
        total = total + float(f) * v
    return total


def plain_terms(env, v):
    idx, tab, _, _ = env

    def of_face(face):
        active = row_of(tab, 3 + face)
        local = row_of(idx, LOCAL + 2 * face)

        def term(a):
            n, m = face_nodes(face)[a], face_nodes(face ^ 1)[a]
            return (float(PENALTY * W[a]) * active) * (v(n) - take(v(m), local))

        return term

    return [of_face(face) for face in range(4)]


def general_terms(env, v):
    idx, _, own_c, far_c = env
    found = []
    for face in range(4):
        mine = [v(n) for n in face_nodes(face)]
        theirs = [
            [take(v(n), row_of(idx, LOCAL + 2 * face + t)) for n in face_nodes(face ^ 1)]
            for t in range(2)
        ]
        values = []
        for a in range(6):
            extra = jnp.zeros((8, 128), F32)
            for b in range(6):
                extra = extra + own_c[6 * a + b, 2 * face : 2 * face + 1, :] * mine[b]
                for t in range(2):
                    s = 2 * face + t
                    extra = extra + far_c[6 * a + b, s : s + 1, :] * theirs[t][b]
            values.append(extra)
        found.append(values.__getitem__)
    return found


FACE_LINES, INSIDE_LINES, ALL_LINES = (0,), (1, 2), (0, 1, 2)


def inner(group, env, v_ref, plain, emit, pairs=ALL_LINES):
    idx, tab, _, _ = env
    rows = group_rows(group)

    def v(n):
        return v_ref[n, rows, :]

    terms = (plain_terms if plain else general_terms)(env, v)
    q = row_of(idx, FIRST) + group * 8 + lax.broadcasted_iota(jnp.int32, (8, 128), 0)
    harmonic = lax.shift_right_logical(q + 1, 1).astype(F32) * SPANWISE
    cx, cy = row_of(tab, 0), row_of(tab, 1)
    shift = 1.0 + 0.5 * tab[2:3, :] * (harmonic * harmonic)
    plus, minus = STIFF_FOLD
    even = [[v(6 * a + j) + v(30 - 6 * a + j) for a in range(3)] for j in range(6)]
    odd = [[v(6 * a + j) - v(30 - 6 * a + j) for a in range(3)] for j in range(6)]
    for i in pairs:
        e = [weighted(plus[i], even[j]) for j in range(6)]
        o = [weighted(minus[i], odd[j]) for j in range(6)]
        for line in (i, 5 - i):
            mine = [v(6 * line + j) for j in range(6)]
            g = folded(mine, STIFF_FOLD, 1)
            for j in range(6):
                n = 6 * line + j
                gx = e[j] + o[j] if line == i else e[j] - o[j]
                value = float(W[line] * W[j]) * (shift * mine[j] + cx * gx + cy * g[j])
                for face, (at, b) in enumerate(((line == 0, j), (line == 5, j), (j == 0, line), (j == 5, line))):
                    if at:
                        value = value + terms[face](b)
                emit(n, value)


def line_at(n):
    return n if n < 6 else n - 24


def compact(idx, v_ref, h_ref, send_e, send_w, at=line_at):
    part = lax.shift_right_logical(lane_ids((8, 128)), 4)
    for face, ref in ((0, send_w), (1, send_e)):
        index = row_of(idx, face)
        for b in range(6):
            n = face_nodes(face)[b]
            value = take(v_ref[n, 0:8, :], index)
            for k in range(1, 8):
                part_rows = slice(8 * (k % 4), 8 * (k % 4) + 8)
                source = v_ref[n, part_rows, :] if k < 4 else h_ref[at(n), part_rows, :]
                other = take(source, index)
                value = jnp.where(part == k, other, value)
            ref[8 * b : 8 * b + 8, :] = value


def outer(group, idx, edge, first):
    found = {}
    for face in range(2):
        lanes = row_of(idx, SELF + face) + (64 * face + 16 * group)
        on = row_of(idx, ANY + face) > 0
        for b in range(6):
            value = take(edge[first + 8 * b : first + 8 * b + 8, :], lanes)
            found[face_nodes(face)[b]] = jnp.where(on, value, 0.0)
    return found


def edge_blocks(ref):
    return [ref[8 * b : 8 * b + 8, :] for b in range(6)]


def merge(to_e, to_w):
    west = lane_ids((8, 128)) < 64
    plain, inner_h = [], []
    for w, e in zip(edge_blocks(to_w), edge_blocks(to_e)):
        plain.append(jnp.where(west, w, pltpu.roll(e, 64, 1)))
        inner_h.append(jnp.where(west, pltpu.roll(w, 64, 1), e))
    return plain, inner_h


def edge_term(edge_idx, edge_own, edge_far, mine, theirs, row):
    near = [[take(t, row_of(edge_idx, row + k)) for t in theirs] for k in range(2)]
    out = []
    for a in range(6):
        chains = [None] * 3
        for b in range(6):
            n = 6 * a + b
            terms = [edge_own[n, row : row + 1, :] * mine[b]]
            terms += [edge_far[n, row + k : row + k + 1, :] * near[k][b] for k in range(2)]
            chains = terms if chains[0] is None else [c + t for c, t in zip(chains, terms)]
        out.append(chains[0] + (chains[1] + chains[2]))
    return out


def store_sums(acc, pad, first, count):
    width = count * 128
    lhs = (
        lax.broadcasted_iota(jnp.int32, (8, width), 0)
        == lax.shift_right_logical(lane_ids((8, width)), 7) + first
    ).astype(F32)
    sums = lax.dot_general(
        lhs, acc[...], (((1,), (1,)), ((), ())),
        precision=lax.Precision.HIGHEST, preferred_element_type=F32,
    )
    pad[...] = jnp.ones((8, 128), F32)
    pad[:, 0:32] = sums


HALF = 10.0


def store_lines(ref, rows):
    def emit(n, value):
        ref[line_at(n), rows, :] = value

    return emit


def inside_kernel(idx, tab, own_c, far_c, v, out):
    env = (idx, tab, own_c, far_c)

    def loop(group, plain):
        rows = group_rows(group)

        def emit(n, value):
            out[n - 6, rows, :] = value

        inner(group, env, v, plain, emit, INSIDE_LINES)

    either(tab, loop)


def line_image(lines, inside, n, rows):
    return inside[n - 6, rows, :] if 6 <= n < 30 else lines[line_at(n), rows, :]


def guess_kernel(
    links, sides, visc, layout, u_far,
    idx, edge_idx, tab, own_c, far_c, edge_own, edge_far, out, u, sem,
):
    copy = pltpu.make_async_copy(u_far, u, sem)
    copy.start()
    build_tables(
        links, sides, visc, layout, idx, edge_idx, tab, own_c, far_c, edge_own, edge_far
    )
    copy.wait()
    env = (idx, tab, own_c, far_c)

    def loop(group, plain):
        rows = group_rows(group)

        def emit(n, value):
            out[n, rows, :] = float(W[n // 6] * W[n % 6]) * u[n, rows, :] - value

        inner(group, env, u, plain, emit)

    either(tab, loop)


def guess_edge_kernel(edge_idx, edge_own, edge_far, to_e, to_w, from_e, from_w, edge):
    mine, _ = merge(to_e, to_w)
    theirs, _ = merge(from_e, from_w)
    for b, value in enumerate(edge_term(edge_idx, edge_own, edge_far, mine, theirs, 0)):
        edge[8 * b : 8 * b + 8, :] = value


def residual_kernel(
    idx, tab, own_c, far_c, back, base, edge, out, h_out, send_e, send_w
):
    env = (idx, tab, own_c, far_c)

    def turn(g, carry):
        part = pl.ds(pl.multiple_of(16 * g, 16), 16)
        turned = back[:, part, :].reshape(128, 128).T
        for m in range(4):
            out[4 * g + m] = base[4 * g + m] + turned[32 * m : 32 * m + 32]
        return carry

    lax.fori_loop(0, 9, turn, 0, unroll=3)

    def loop(group, plain):
        rows = group_rows(group)
        for n, extra in outer(group, idx, edge, 0).items():
            out[n, rows, :] -= extra
        inner(group, env, out, plain, store_lines(h_out, rows), FACE_LINES)

    either(tab, loop)
    compact(idx, out, h_out, send_e, send_w)


def edge_steps(tables, to_e, to_w, from_e, from_w, before, edge, keep):
    edge_idx, edge_own, edge_far = tables
    mine, mine_h = merge(to_e, to_w)
    theirs, theirs_h = merge(from_e, from_w)
    scale = (1.0 if before is None else 2.0) / HALF
    first = edge_term(edge_idx, edge_own, edge_far, mine, theirs, 0)
    facing = edge_term(edge_idx, edge_own, edge_far, theirs, mine, 2)
    mine_next, theirs_next = [], []
    for b in range(6):
        if before is None:
            mine_next.append(scale * (mine_h[b] + first[b]) - mine[b])
            theirs_next.append(scale * (theirs_h[b] + facing[b]) - theirs[b])
        else:
            old = before[8 * b : 8 * b + 8, :], before[48 + 8 * b : 56 + 8 * b, :]
            mine_next.append(scale * (mine_h[b] + first[b]) - 2.0 * mine[b] - old[0])
            theirs_next.append(scale * (theirs_h[b] + facing[b]) - 2.0 * theirs[b] - old[1])
    second = edge_term(edge_idx, edge_own, edge_far, mine_next, theirs_next, 0)
    for b in range(6):
        edge[8 * b : 8 * b + 8, :] = first[b]
        edge[48 + 8 * b : 56 + 8 * b, :] = second[b]
        if keep is not None:
            keep[8 * b : 8 * b + 8, :] = mine_next[b]
            keep[48 + 8 * b : 56 + 8 * b, :] = theirs_next[b]


def two_steps_kernel(
    idx, tab, own_c, far_c, edge_idx, edge_own, edge_far,
    t0, h0, h0_in, to_e, to_w, from_e, from_w,
    t1, t2, h2, send_e, send_w, keep, edge,
):
    env = (idx, tab, own_c, far_c)
    tables = (edge_idx, edge_own, edge_far)
    edge_steps(tables, to_e, to_w, from_e, from_w, None, edge, keep)

    def loop(group, plain):
        rows = group_rows(group)
        extra = outer(group, idx, edge, 0)
        for n in range(36):
            image = line_image(h0, h0_in, n, rows)
            if n in extra:
                image = image + extra[n]
            t1[n, rows, :] = (1.0 / HALF) * image - t0[n, rows, :]
        extra_next = outer(group, idx, edge, 48)

        def emit(n, image):
            if n in extra_next:
                image = image + extra_next[n]
            t2[n, rows, :] = (2.0 / HALF) * image - 2.0 * t1[n, rows, :] - t0[n, rows, :]

        inner(group, env, t1, plain, emit)
        inner(group, env, t2, plain, store_lines(h2, rows), FACE_LINES)

    either(tab, loop)
    compact(idx, t2, h2, send_e, send_w)


def sums_kernel(t0, t1, t2, part, acc, pad):
    def body(group, carry):
        rows = group_rows(group)
        sums = [jnp.zeros((8, 128), F32)] * 5
        for n in range(36):
            a, b, c = t0[n, rows, :], t1[n, rows, :], t2[n, rows, :]
            for k, term in enumerate((a * a, a * b, b * b, b * c, c * c)):
                sums[k] = sums[k] + term
        for k in range(5):
            acc[rows, 128 * k : 128 * k + 128] = sums[k]
        return carry

    lax.fori_loop(0, 4, body, 0)
    store_sums(acc, pad, 0, 5)
    part[...] = pad[...]


def last_steps_kernel(
    idx, tab, own_c, far_c, edge_idx, edge_own, edge_far,
    t1, t2, h2, h2_in, to_e, to_w, from_e, from_w, keep, part,
    t3, red, edge, acc, pad,
):
    env = (idx, tab, own_c, far_c)
    tables = (edge_idx, edge_own, edge_far)
    edge_steps(tables, to_e, to_w, from_e, from_w, keep, edge, None)

    def loop(group, plain):
        rows = group_rows(group)
        extra = outer(group, idx, edge, 0)
        sums = [jnp.zeros((8, 128), F32)] * 3
        for n in range(36):
            image = line_image(h2, h2_in, n, rows)
            if n in extra:
                image = image + extra[n]
            c = t2[n, rows, :]
            d = (2.0 / HALF) * image - 2.0 * c - t1[n, rows, :]
            t3[n, rows, :] = d
            sums[0] = sums[0] + c * d
            sums[1] = sums[1] + d * d
        extra_next = outer(group, idx, edge, 48)

        def emit(n, image):
            if n in extra_next:
                image = image + extra_next[n]
            d = t3[n, rows, :]
            sums[2] = sums[2] + d * ((2.0 / HALF) * image - 2.0 * d - t2[n, rows, :])

        inner(group, env, t3, plain, emit)
        for k in range(3):
            acc[rows, 128 * k : 128 * k + 128] = sums[k]

    either(tab, loop)
    store_sums(acc, pad, 5, 3)
    row = lax.broadcasted_iota(jnp.int32, (8, 128), 0)
    mixed = jnp.where(row < 5, part[...], pad[...])
    for k in range(16):
        red[k] = mixed


def finish_kernel(red, x0, t0, t1, t2, t3, out, coef, held, sems):
    parts = [red[k] for k in range(16)]
    while len(parts) > 1:
        parts = [a + b for a, b in zip(parts[::2], parts[1::2])]
    total = parts[0]
    even = [total[2 * k : 2 * k + 1] for k in range(4)]
    odd = [total[2 * k + 1 : 2 * k + 2] for k in range(4)]
    moment = []
    for k in range(4):
        moment.append(even[0] if k == 0 else 2.0 * even[k] - even[0])
        moment.append(odd[0] if k == 0 else 2.0 * odd[k] - odd[0])

    def inner_product(i, j):
        return 0.5 * (moment[i + j] + moment[abs(i - j)])

    def energy(i, j):
        shifted = 0.5 * (inner_product(i, j + 1) + inner_product(i, abs(j - 1)))
        return HALF * (shifted + inner_product(i, j))

    low = [[None] * 4 for _ in range(4)]
    diag, inverse, half = [], [], []
    for j in range(4):
        d = energy(j, j)
        value = moment[j]
        for k in range(j):
            d = d - low[j][k] * low[j][k] * diag[k]
            value = value - low[j][k] * half[k]
        diag.append(d)
        half.append(value)
        inverse.append(1.0 / d)
        for i in range(j + 1, 4):
            e = energy(i, j)
            for k in range(j):
                e = e - low[i][k] * low[j][k] * diag[k]
            low[i][j] = e * inverse[j]
    weight = [half[k] * inverse[k] for k in range(4)]
    for i in (2, 1, 0):
        for k in range(i + 1, 4):
            weight[i] = weight[i] - low[k][i] * weight[k]
    turned = jnp.concatenate(weight + [jnp.zeros((4, 128), F32)], axis=0).T
    for k in range(4):
        coef[k] = jnp.broadcast_to(turned[0:32, k : k + 1], (32, 128))
    cuts = (0, 15, 30, 36)
    copies = []
    for c in range(3):
        def add(n, carry):
            terms = coef[0] * t0[n] + coef[1] * t1[n] + coef[2] * t2[n] + coef[3] * t3[n]
            held[n] = x0[n] + terms
            return carry

        lax.fori_loop(cuts[c], cuts[c + 1], add, 0, unroll=3)
        part = pl.ds(cuts[c], cuts[c + 1] - cuts[c])
        copies.append(pltpu.make_async_copy(held.at[part], out.at[part], sems.at[c]))
        copies[c].start()
    for copy in copies:
        copy.wait()


def pack_kernel(u, links, out, send_e, send_w, held, ready, near_links, lists, sems):
    loads, stores = [], []
    first = pltpu.make_async_copy(links, near_links, sems.at[6])
    first.start()
    cuts = (0, 4, 8, 9)
    for c in range(3):
        part = pl.ds(4 * cuts[c], 4 * (cuts[c + 1] - cuts[c]))
        loads.append(pltpu.make_async_copy(u.at[part], held.at[part], sems.at[c]))
        loads[c].start()
    first.wait()
    dev = lax.shift_right_logical(near_links[...], 7)
    remote = (dev != lax.axis_index("elem")).astype(jnp.int32)
    for side in range(2):
        lists[side : side + 1, :] = boundary(remote, side)[0].astype(jnp.int32)
    for c in range(3):
        loads[c].wait()
        for g in range(cuts[c], cuts[c + 1]):
            turned = held[4 * g : 4 * g + 4].reshape(128, 128).T
            ready[:, 16 * g : 16 * g + 16, :] = turned.reshape(8, 16, 128)
        part = pl.ds(16 * cuts[c], 16 * (cuts[c + 1] - cuts[c]))
        stores.append(pltpu.make_async_copy(ready.at[:, part], out.at[:, part], sems.at[3 + c]))
        stores[c].start()
    compact(lists, held, held, send_e, send_w, lambda n: n)
    for copy in stores:
        copy.wait()


def block_turn(blocks):
    part = lax.shift_right_logical(lane_ids(blocks[0].shape), 5)
    rolled = [blocks[0]] + [pltpu.roll(blocks[s], 32 * s, 1) for s in range(1, 4)]
    out = []
    for m in range(4):
        mixed = rolled[-m % 4]
        for t in range(1, 4):
            mixed = jnp.where(part == t, rolled[(t - m) % 4], mixed)
        out.append(pltpu.roll(mixed, 128 - 32 * m, 1) if m else mixed)
    return out


def product3(high, low, table, dim):
    def dot(a, b):
        return lax.dot_general(a, b, (((1,), (dim,)), ((), ())), preferred_element_type=F32)

    return dot(high, table[0]) + dot(high, table[1]) + dot(low, table[0])


def advect_kernel(idx, came, speed, synth, out, high, low, phys):
    for g in range(9):
        for h in range(2):
            pieces = block_turn([came[4 * h + s, 16 * g : 16 * g + 16, :] for s in range(4)])
            for m in range(4):
                n = 16 * (4 * g + m)
                hi, lo = split(pieces[m])
                high[n : n + 16, 128 * h : 128 * h + 128] = hi
                low[n : n + 16, 128 * h : 128 * h + 128] = lo
    for i in range(2):
        part = slice(288 * i, 288 * i + 288)
        phys[part, :] = product3(high[part, :], low[part, :], synth, 1)
    wide = jnp.broadcast_to(idx[LAYOUT : LAYOUT + 1, :], (16, 128)) == 0
    sx = jnp.where(wide, 2.0, 1.0)
    sy = jnp.where(wide, 1.0, 2.0)
    for h in range(2):
        cols = slice(128 * h, 128 * h + 128)
        u = [[phys[16 * (6 * i + j) : 16 * (6 * i + j) + 16, cols] for j in range(6)] for i in range(6)]
        acc = [[None] * 6 for _ in range(6)]
        for j in range(6):
            g = folded([u[i][j] for i in range(6)], DERIV_FOLD, -1)
            for i in range(6):
                acc[i][j] = sx * (speed[0, 6 * i + j, :, cols] * g[i])
        for i in range(6):
            g = folded(u[i], DERIV_FOLD, -1)
            for j in range(6):
                n = 16 * (6 * i + j)
                total = acc[i][j] + sy * (speed[1, 6 * i + j, :, cols] * g[j])
                hi, lo = split(float(-0.5 * W[i] * W[j]) * total)
                high[n : n + 16, cols] = hi
                low[n : n + 16, cols] = lo
    for i in range(2):
        part = slice(288 * i, 288 * i + 288)
        phys[part, :] = product3(high[part, :], low[part, :], synth, 0)
    for h in range(2):
        q = lane_ids((16, 128)) + 128 * h
        norm = jnp.where((q == 0) | (q == 255), 1.0 / 256, 1.0 / 128)
        cols = slice(128 * h, 128 * h + 128)
        for g in range(9):
            pieces = block_turn(
                [norm * phys[16 * (4 * g + m) : 16 * (4 * g + m) + 16, cols] for m in range(4)]
            )
            for s in range(4):
                out[4 * h + s, 16 * g : 16 * g + 16, :] = pieces[s]


def shift_by(array, by):
    count = lax.axis_size("elem")
    return lax.ppermute(array, "elem", [(i, (i + by) % count) for i in range(count)])


def shards(scalar_modes, velocity, viscosity, mortar_links, mortar_sides, layout):
    u = jnp.transpose(scalar_modes, (1, 2, 0, 3)).reshape(36, 32, 128)
    speed = jnp.transpose(velocity, (0, 2, 3, 4, 1)).reshape(2, 36, 16, 256)
    synth = jnp.asarray(split_table(plane_tables(256)))
    vol, edge = shape(36, 32, 128), shape(48, 128)
    both = shape(96, 128)
    blocks = shape(8, 144, 128)
    packed, *sent = call(
        pack_kernel,
        [blocks, edge, edge],
        [
            VMEM((36, 32, 128), F32),
            VMEM((8, 144, 128), F32),
            VMEM((8, 128), jnp.int32),
            VMEM((8, 128), jnp.int32),
            pltpu.SemaphoreType.DMA((7,)),
        ],
        [u, mortar_links],
        [HBM, HBM],
        [HBM, VMEM, VMEM],
    )
    came = lax.all_to_all(packed, "plane", 0, 0, tiled=True)

    table = shape(36, 8, 128)
    idx, edge_idx, tab, own_c, far_c, edge_own, edge_far, base = call(
        guess_kernel,
        [
            shape(24, 128, dtype=jnp.int32),
            shape(8, 128, dtype=jnp.int32),
            shape(8, 128),
        ]
        + [table] * 4
        + [vol],
        [VMEM((36, 32, 128), F32), pltpu.SemaphoreType.DMA],
        [mortar_links, mortar_sides, viscosity[None], layout[None], u],
        [VMEM] * 4 + [HBM],
    )
    head = [idx, tab, own_c, far_c]
    edges = [edge_idx, edge_own, edge_far]

    def run(kernel, outs, scratch, args):
        return call(kernel, outs, scratch, args, [VMEM] * len(args))

    def trade(send_e, send_w):
        from_w = shift_by(send_e, 1)
        return shift_by(send_w, -1), from_w

    guess_edge = run(guess_edge_kernel, [shape(48, 128)], [], [*edges, *sent, *trade(*sent)])[0]
    came, guess_edge, base = lax.optimization_barrier((came, guess_edge, base))
    back = call(
        advect_kernel,
        [blocks],
        [
            VMEM((576, 256), BF16),
            VMEM((576, 256), BF16),
            VMEM((576, 256), F32),
        ],
        [idx, came, speed, synth],
        [VMEM] * 4,
        grant=8,
    )[0]
    back = lax.all_to_all(back, "plane", 0, 0, tiled=True)

    def work(count):
        return [
            VMEM((96, 128), F32),
            VMEM((32, 128 * count), F32),
            VMEM((8, 128), F32),
        ]

    lines, insides = shape(12, 32, 128), shape(24, 32, 128)
    t0, h0, *sent = run(
        residual_kernel, [vol, lines, edge, edge], [], head + [back, base, guess_edge]
    )
    got = trade(*sent)
    h0_in = run(inside_kernel, [insides], [], head + [t0])[0]
    t1, t2, h2, to_e, to_w, keep = run(
        two_steps_kernel,
        [vol, vol, lines, edge, edge, both],
        [VMEM((96, 128), F32)],
        head + edges + [t0, h0, h0_in, *sent, *got],
    )
    got = trade(to_e, to_w)
    h2_in = run(inside_kernel, [insides], [], head + [t2])[0]
    part = run(sums_kernel, [shape(8, 128)], work(5)[1:], [t0, t1, t2])[0]
    t3, red = run(
        last_steps_kernel,
        [vol, shape(16, 8, 128)],
        work(3),
        head + edges + [t1, t2, h2, h2_in, to_e, to_w, *got, keep, part],
    )
    red = lax.all_to_all(red, "elem", 0, 0, tiled=True)
    out = call(
        finish_kernel,
        [vol],
        [VMEM((4, 32, 128), F32), VMEM((36, 32, 128), F32), pltpu.SemaphoreType.DMA((3,))],
        [red, u, t0, t1, t2, t3],
        [VMEM] * 6,
        [HBM],
    )[0]
    return jnp.transpose(out.reshape(6, 6, 32, 128), (2, 0, 1, 3))


def solution(mesh):
    placed = (
        P("plane", None, None, "elem"),
        P(None, None, None, None, ("elem", "plane")),
        P("elem"),
        P(None, "elem"),
        P(None, None, "elem"),
        P("elem"),
    )
    return jax.shard_map(
        shards,
        mesh=mesh,
        in_specs=placed,
        out_specs=P("plane", None, None, "elem"),
        check_vma=False,
    )
```

```python
import math

import jax
import jax.numpy as jnp
import ml_dtypes
import numpy as np
from jax import lax
from jax.experimental import pallas as pl
from jax.experimental.pallas import tpu as pltpu
from jax.sharding import PartitionSpec as P

F32 = jnp.float32
BF16 = jnp.bfloat16
PENALTY = 10.0
SPANWISE = 0.0625
VMEM = pltpu.VMEM
SMEM = pltpu.SMEM
HBM = pltpu.HBM
MIXED = 7
SELF, ANY, FIRST, LAYOUT, LOCAL = 2, 4, 6, 7, 10


def lagrange_at(points, targets):
    out = np.ones((6, 6))
    for row in range(6):
        for col in range(6):
            for other in range(6):
                if other != col:
                    out[row, col] *= (targets[row] - points[other]) / (points[col] - points[other])
    return out


def node_tables():
    root = math.sqrt(7.0)
    outer = math.sqrt(1.0 / 3.0 + 2.0 * root / 21.0)
    inner = math.sqrt(1.0 / 3.0 - 2.0 * root / 21.0)
    points = np.array([-1.0, -outer, -inner, inner, outer, 1.0])
    half = [1.0 / 15.0, (14.0 - root) / 30.0, (14.0 + root) / 30.0]
    weights = np.array(half + half[::-1])
    bary = np.array(
        [1.0 / np.prod([points[c] - points[k] for k in range(6) if k != c]) for c in range(6)]
    )
    deriv = np.zeros((6, 6))
    for i in range(6):
        for j in range(6):
            if i != j:
                deriv[i, j] = bary[j] / bary[i] / (points[i] - points[j])
        deriv[i, i] = -np.sum(deriv[i])
    lower = lagrange_at(points, (points - 1.0) / 2.0)
    upper = lagrange_at(points, (points + 1.0) / 2.0)
    stiff = deriv.T @ (weights[:, None] * deriv)
    return weights, deriv, lower, upper, stiff


W, D, QLO, QHI, K1 = node_tables()
HALVES = [np.eye(6), QLO, QHI]


def plane_tables(count):
    planes = np.arange(count)[:, None]
    coeffs = np.arange(count)[None, :]
    harmonic = (coeffs + 1) // 2
    phase = 2.0 * np.pi * (harmonic * planes % count) / count
    synth = np.where(coeffs == 0, 1.0, np.where(coeffs % 2 == 1, np.cos(phase), np.sin(phase)))
    return synth


def split_table(table):
    table = np.asarray(table, np.float32)
    high = table.astype(ml_dtypes.bfloat16)
    low = (table - high.astype(np.float32)).astype(ml_dtypes.bfloat16)
    return np.stack([high, low])


def fold(matrix):
    plus = (matrix[:3, :3] + matrix[:3, :2:-1]) / 2.0
    minus = (matrix[:3, :3] - matrix[:3, :2:-1]) / 2.0
    return plus, minus


STIFF_FOLD = fold(K1 / W[:, None])
DERIV_FOLD = fold(D)


def folded(values, tables, sign):
    plus, minus = tables
    even = [values[a] + values[5 - a] for a in range(3)]
    odd = [values[a] - values[5 - a] for a in range(3)]
    out = [None] * 6
    for i in range(3):
        e = sum(float(plus[i, a]) * even[a] for a in range(3))
        o = sum(float(minus[i, a]) * odd[a] for a in range(3))
        out[i] = e + o
        out[5 - i] = e - o if sign > 0 else o - e
    return out


def split(value):
    high = value.astype(BF16)
    return high, (value - high.astype(F32)).astype(BF16)


def lane_ids(shape):
    return lax.broadcasted_iota(jnp.int32, shape, len(shape) - 1)


def call(kernel, outs, scratch, operands, spaces, out_spaces=None, grant=3):
    total = sum(int(np.prod(o.shape)) * 4 for o in outs)
    total += sum(int(np.prod(o.shape)) * 4 for o in operands)
    return pl.pallas_call(
        kernel,
        out_shape=outs,
        in_specs=[pl.BlockSpec(memory_space=s) for s in spaces],
        out_specs=[pl.BlockSpec(memory_space=s) for s in out_spaces or [VMEM] * len(outs)],
        scratch_shapes=scratch,
        compiler_params=pltpu.CompilerParams(vmem_limit_bytes=grant * 2**20),
        cost_estimate=pl.CostEstimate(flops=4_000_000, bytes_accessed=total, transcendentals=0),
    )(*[far(a) if s == HBM else a for a, s in zip(operands, spaces)])


def far(array):
    return pltpu.with_memory_space_constraint(array, HBM)


def shape(*dims, dtype=F32):
    return jax.ShapeDtypeStruct(dims, dtype)


def take(value, index):
    return jnp.take_along_axis(value, index, axis=1)


def take_row(value, index):
    wide = jnp.broadcast_to(value, (8, 128)), jnp.broadcast_to(index, (8, 128))
    return take(*wide)[0:1]


def boundary(remote, side):
    row = lax.broadcasted_iota(jnp.int32, (128, 128), 0)
    col = lane_ids((128, 128))
    any_rem = jnp.maximum(remote[2 * side : 2 * side + 1], remote[2 * side + 1 : 2 * side + 2])
    before = jnp.sum(jnp.where(col < row, any_rem, 0).astype(F32), axis=1, keepdims=True)
    mine = jnp.sum(jnp.where(col == row, any_rem, 0).astype(F32), axis=1, keepdims=True)
    slot = jnp.bitwise_and(lane_ids((1, 128)), 15).astype(F32)
    chosen = jnp.where((before == slot) & (mine > 0.0), 1.0, 0.0)
    listed = jnp.sum(chosen * row.astype(F32), axis=0, keepdims=True)
    return listed, jnp.sum(chosen, axis=0, keepdims=True), before


def build_tables(
    links, sides, visc, layout, idx, edge_idx, tab, own_c, far_c, edge_own, edge_far
):
    me = lax.axis_index("elem")
    dev = lax.shift_right_logical(links[...], 7)
    loc = jnp.bitwise_and(links[...], 127)
    remote = (dev != me).astype(jnp.int32)
    idx[LOCAL : LOCAL + 8, :] = loc
    own, other = sides[0], sides[1]
    inside = jnp.where(remote > 0, 3, own)
    whole = (inside == 0) & (other == 0)
    second = jnp.bitwise_and(lax.broadcasted_iota(jnp.int32, (8, 128), 0), 1) == 1
    odd_one = jnp.where(inside == 3, 0.0, jnp.where(whole & ~second, 0.0, 1.0))
    idx[FIRST : FIRST + 1, :] = jnp.full((1, 128), 32 * lax.axis_index("plane"), jnp.int32)
    idx[LAYOUT : LAYOUT + 1, :] = layout[...]
    row = lax.broadcasted_iota(jnp.int32, (128, 128), 0)
    col = lane_ids((128, 128))
    lane = lane_ids((1, 128))
    slot = jnp.bitwise_and(lane, 15)
    listed, present, ranks = [], [], []
    for side in range(2):
        rem = [remote[2 * side + t : 2 * side + t + 1] for t in range(2)]
        far = [loc[2 * side + t : 2 * side + t + 1] for t in range(2)]
        any_rem = jnp.maximum(rem[0], rem[1])
        places, filled, before = boundary(remote, side)
        listed.append(places.astype(jnp.int32))
        present.append(filled.astype(jnp.int32))
        idx[side : side + 1, :] = listed[side]
        mine_at = jnp.sum(jnp.where(row == col, before, 0.0), axis=0, keepdims=True)
        mine_at = jnp.where(any_rem > 0, mine_at.astype(jnp.int32), 0)
        idx[SELF + side : SELF + side + 1, :] = mine_at
        idx[ANY + side : ANY + side + 1, :] = any_rem
        named = jnp.where(
            ((far[0] == row) & (rem[0] > 0)) | ((far[1] == row) & (rem[1] > 0)), 1.0, 0.0
        )
        named = jnp.max(named, axis=1, keepdims=True)
        for t in range(2):
            rank = jnp.sum(jnp.where(row < far[t], named, 0.0), axis=0, keepdims=True)
            ranks.append(jnp.where(rem[t] > 0, rank.astype(jnp.int32), 0))
    idx[8:10, :] = jnp.zeros((2, 128), jnp.int32)
    idx[18:24, :] = jnp.zeros((6, 128), jnp.int32)

    west = lane < 64
    base = jnp.bitwise_and(lane, 112)
    element = jnp.where(west, listed[0], listed[1])
    here = jnp.where(west, present[0], present[1]) > 0

    def pick(rows_w, rows_e):
        return jnp.where(west, take_row(rows_w, element), take_row(rows_e, element))

    rank, live, mine, theirs = [], [], [], []
    for t in range(2):
        rank.append(pick(ranks[t], ranks[2 + t]))
        live.append((pick(remote[t : t + 1], remote[2 + t : 3 + t]) > 0) & here)
        mine.append(jnp.where(live[t], pick(own[t : t + 1], own[2 + t : 3 + t]), 3))
        theirs.append(jnp.where(live[t], pick(other[t : t + 1], other[2 + t : 3 + t]), 3))
    first = jnp.full((1, 128), 99, jnp.int32)
    last = jnp.full((1, 128), -1, jnp.int32)
    for t in range(2):
        target = jnp.where(live[t], rank[t], 99)
        for r in range(16):
            hit = take_row(target, base + r) == slot
            first = jnp.where(hit, jnp.minimum(first, 16 * t + r), first)
            last = jnp.where(hit, jnp.maximum(last, 16 * t + r), last)
    exists = [last >= 0, last > first]
    key = [jnp.where(exists[0], first, 0), jnp.where(exists[1], last, 0)]
    back = [base + jnp.bitwise_and(k, 15) for k in key]

    def from_key(k, pair):
        value = jnp.where(key[k] >= 16, take_row(pair[1], back[k]), take_row(pair[0], back[k]))
        return jnp.where(exists[k], value, 3)

    near_own = [from_key(k, theirs) for k in range(2)]
    near_far = [from_key(k, mine) for k in range(2)]
    edge_idx[...] = jnp.zeros((8, 128), jnp.int32)
    for k in range(2):
        edge_idx[k : k + 1, :] = base + rank[k]
        edge_idx[2 + k : 3 + k, :] = back[k]
    none = jnp.full((4, 128), 3, jnp.int32)
    edge_mine = jnp.concatenate([mine[0], mine[1], near_own[0], near_own[1], none], axis=0)
    edge_theirs = jnp.concatenate([theirs[0], theirs[1], near_far[0], near_far[1], none], axis=0)

    nu = visc[...]
    wide = layout[...] == 0
    tab[0:1, :] = nu * jnp.where(wide, 2.0, 0.5)
    tab[1:2, :] = nu * jnp.where(wide, 0.5, 2.0)
    tab[2:3, :] = nu
    for face in range(4):
        tab[3 + face : 4 + face, :] = whole[2 * face : 2 * face + 1].astype(F32)
    tab[MIXED : MIXED + 1, :] = jnp.max(odd_one, axis=0, keepdims=True)
    mine_m = [PENALTY * HALVES[o].T @ np.diag(W) @ HALVES[o] for o in range(3)]
    far_m = [
        [-PENALTY * HALVES[o].T @ np.diag(W) @ HALVES[c] for c in range(3)] for o in range(3)
    ]
    for code, facing, own_ref, far_ref in (
        (inside, other, own_c, far_c),
        (edge_mine, edge_theirs, edge_own, edge_far),
    ):
        hot = [(code == o).astype(F32) for o in range(3)]
        pair = [[hot[o] * (facing == c).astype(F32) for c in range(3)] for o in range(3)]
        for a in range(6):
            for b in range(6):
                n = 6 * a + b
                total = sum(float(mine_m[o][a, b]) * hot[o] for o in range(3))
                own_ref[n] = total + pltpu.roll(total, 7, 0)
                far_ref[n] = sum(
                    float(far_m[o][c][a, b]) * pair[o][c] for o in range(3) for c in range(3)
                )


def group_rows(group):
    return pl.ds(pl.multiple_of(group * 8, 8), 8)


def row_of(ref, r):
    return jnp.broadcast_to(ref[r : r + 1, :], (8, 128))


def face_nodes(face):
    return [
        6 * i + j
        for i, j in [
            (0, b) if face == 0 else (5, b) if face == 1 else (b, 0) if face == 2 else (b, 5)
            for b in range(6)
        ]
    ]


def either(tab, loop):
    mixed = jnp.max(tab[MIXED : MIXED + 1, :]) > 0.5
    for plain in (True, False):

        @pl.when(mixed != plain)
        def _(plain=plain):
            lax.fori_loop(
                0, 4, lambda group, carry: loop(group, plain) or carry, 0, unroll=2 if plain else 1
            )


def weighted(factors, values):
    total = float(factors[0]) * values[0]
    for f, v in zip(factors[1:], values[1:]):
        total = total + float(f) * v
    return total


def plain_terms(env, v):
    idx, tab, _, _ = env

    def of_face(face):
        active = row_of(tab, 3 + face)
        local = row_of(idx, LOCAL + 2 * face)

        def term(a):
            n, m = face_nodes(face)[a], face_nodes(face ^ 1)[a]
            return (float(PENALTY * W[a]) * active) * (v(n) - take(v(m), local))

        return term

    return [of_face(face) for face in range(4)]


def general_terms(env, v):
    idx, _, own_c, far_c = env
    found = []
    for face in range(4):
        mine = [v(n) for n in face_nodes(face)]
        theirs = [
            [take(v(n), row_of(idx, LOCAL + 2 * face + t)) for n in face_nodes(face ^ 1)]
            for t in range(2)
        ]
        values = []
        for a in range(6):
            extra = jnp.zeros((8, 128), F32)
            for b in range(6):
                extra = extra + own_c[6 * a + b, 2 * face : 2 * face + 1, :] * mine[b]
                for t in range(2):
                    s = 2 * face + t
                    extra = extra + far_c[6 * a + b, s : s + 1, :] * theirs[t][b]
            values.append(extra)
        found.append(values.__getitem__)
    return found


FACE_LINES, INSIDE_LINES, ALL_LINES = (0,), (1, 2), (0, 1, 2)


def inner(group, env, v_ref, plain, emit, pairs=ALL_LINES):
    idx, tab, _, _ = env
    rows = group_rows(group)

    def v(n):
        return v_ref[n, rows, :]

    terms = (plain_terms if plain else general_terms)(env, v)
    q = row_of(idx, FIRST) + group * 8 + lax.broadcasted_iota(jnp.int32, (8, 128), 0)
    harmonic = lax.shift_right_logical(q + 1, 1).astype(F32) * SPANWISE
    cx, cy = row_of(tab, 0), row_of(tab, 1)
    shift = 1.0 + 0.5 * tab[2:3, :] * (harmonic * harmonic)
    plus, minus = STIFF_FOLD
    even = [[v(6 * a + j) + v(30 - 6 * a + j) for a in range(3)] for j in range(6)]
    odd = [[v(6 * a + j) - v(30 - 6 * a + j) for a in range(3)] for j in range(6)]
    for i in pairs:
        e = [weighted(plus[i], even[j]) for j in range(6)]
        o = [weighted(minus[i], odd[j]) for j in range(6)]
        for line in (i, 5 - i):
            mine = [v(6 * line + j) for j in range(6)]
            g = folded(mine, STIFF_FOLD, 1)
            for j in range(6):
                n = 6 * line + j
                gx = e[j] + o[j] if line == i else e[j] - o[j]
                value = float(W[line] * W[j]) * (shift * mine[j] + cx * gx + cy * g[j])
                for face, (at, b) in enumerate(((line == 0, j), (line == 5, j), (j == 0, line), (j == 5, line))):
                    if at:
                        value = value + terms[face](b)
                emit(n, value)


def line_at(n):
    return n if n < 6 else n - 24


def compact(idx, v_ref, h_ref, send_e, send_w, at=line_at):
    part = lax.shift_right_logical(lane_ids((8, 128)), 4)
    for face, ref in ((0, send_w), (1, send_e)):
        index = row_of(idx, face)
        for b in range(6):
            n = face_nodes(face)[b]
            value = take(v_ref[n, 0:8, :], index)
            for k in range(1, 8):
                part_rows = slice(8 * (k % 4), 8 * (k % 4) + 8)
                source = v_ref[n, part_rows, :] if k < 4 else h_ref[at(n), part_rows, :]
                other = take(source, index)
                value = jnp.where(part == k, other, value)
            ref[8 * b : 8 * b + 8, :] = value


def outer(group, idx, edge, first):
    found = {}
    for face in range(2):
        lanes = row_of(idx, SELF + face) + (64 * face + 16 * group)
        on = row_of(idx, ANY + face) > 0
        for b in range(6):
            value = take(edge[first + 8 * b : first + 8 * b + 8, :], lanes)
            found[face_nodes(face)[b]] = jnp.where(on, value, 0.0)
    return found


def edge_blocks(ref):
    return [ref[8 * b : 8 * b + 8, :] for b in range(6)]


def merge(to_e, to_w):
    west = lane_ids((8, 128)) < 64
    plain, inner_h = [], []
    for w, e in zip(edge_blocks(to_w), edge_blocks(to_e)):
        plain.append(jnp.where(west, w, pltpu.roll(e, 64, 1)))
        inner_h.append(jnp.where(west, pltpu.roll(w, 64, 1), e))
    return plain, inner_h


def edge_term(edge_idx, edge_own, edge_far, mine, theirs, row):
    near = [[take(t, row_of(edge_idx, row + k)) for t in theirs] for k in range(2)]
    out = []
    for a in range(6):
        chains = [None] * 3
        for b in range(6):
            n = 6 * a + b
            terms = [edge_own[n, row : row + 1, :] * mine[b]]
            terms += [edge_far[n, row + k : row + k + 1, :] * near[k][b] for k in range(2)]
            chains = terms if chains[0] is None else [c + t for c, t in zip(chains, terms)]
        out.append(chains[0] + (chains[1] + chains[2]))
    return out


def store_sums(acc, pad, first, count):
    width = count * 128
    lhs = (
        lax.broadcasted_iota(jnp.int32, (8, width), 0)
        == lax.shift_right_logical(lane_ids((8, width)), 7) + first
    ).astype(F32)
    sums = lax.dot_general(
        lhs, acc[...], (((1,), (1,)), ((), ())),
        precision=lax.Precision.HIGHEST, preferred_element_type=F32,
    )
    pad[...] = jnp.ones((8, 128), F32)
    pad[:, 0:32] = sums


HALF = 10.0


def store_lines(ref, rows):
    def emit(n, value):
        ref[line_at(n), rows, :] = value

    return emit


def inside_kernel(idx, tab, own_c, far_c, v, out):
    env = (idx, tab, own_c, far_c)

    def loop(group, plain):
        rows = group_rows(group)

        def emit(n, value):
            out[n - 6, rows, :] = value

        inner(group, env, v, plain, emit, INSIDE_LINES)

    either(tab, loop)


def line_image(lines, inside, n, rows):
    return inside[n - 6, rows, :] if 6 <= n < 30 else lines[line_at(n), rows, :]


def guess_kernel(
    links, sides, visc, layout, u_far,
    idx, edge_idx, tab, own_c, far_c, edge_own, edge_far, out, u, sem,
):
    copy = pltpu.make_async_copy(u_far, u, sem)
    copy.start()
    build_tables(
        links, sides, visc, layout, idx, edge_idx, tab, own_c, far_c, edge_own, edge_far
    )
    copy.wait()
    env = (idx, tab, own_c, far_c)

    def loop(group, plain):
        rows = group_rows(group)

        def emit(n, value):
            out[n, rows, :] = float(W[n // 6] * W[n % 6]) * u[n, rows, :] - value

        inner(group, env, u, plain, emit)

    either(tab, loop)


def guess_edge_kernel(edge_idx, edge_own, edge_far, to_e, to_w, from_e, from_w, edge):
    mine, _ = merge(to_e, to_w)
    theirs, _ = merge(from_e, from_w)
    for b, value in enumerate(edge_term(edge_idx, edge_own, edge_far, mine, theirs, 0)):
        edge[8 * b : 8 * b + 8, :] = value


def residual_kernel(
    idx, tab, own_c, far_c, back, base, edge, out, h_out, send_w, send_e
):
    env = (idx, tab, own_c, far_c)

    def turn(g, carry):
        part = pl.ds(pl.multiple_of(16 * g, 16), 16)
        turned = back[:, part, :].reshape(128, 128).T
        for m in range(4):
            out[4 * g + m] = base[4 * g + m] + turned[32 * m : 32 * m + 32]
        return carry

    lax.fori_loop(0, 9, turn, 0, unroll=3)

    def loop(group, plain):
        rows = group_rows(group)
        for n, extra in outer(group, idx, edge, 0).items():
            out[n, rows, :] -= extra
        inner(group, env, out, plain, store_lines(h_out, rows), FACE_LINES)

    either(tab, loop)
    compact(idx, out, h_out, send_e, send_w)


def edge_steps(tables, to_e, to_w, from_e, from_w, before, edge, keep):
    edge_idx, edge_own, edge_far = tables
    mine, mine_h = merge(to_e, to_w)
    theirs, theirs_h = merge(from_e, from_w)
    scale = (1.0 if before is None else 2.0) / HALF
    first = edge_term(edge_idx, edge_own, edge_far, mine, theirs, 0)
    facing = edge_term(edge_idx, edge_own, edge_far, theirs, mine, 2)
    mine_next, theirs_next = [], []
    for b in range(6):
        if before is None:
            mine_next.append(scale * (mine_h[b] + first[b]) - mine[b])
            theirs_next.append(scale * (theirs_h[b] + facing[b]) - theirs[b])
        else:
            old = before[8 * b : 8 * b + 8, :], before[48 + 8 * b : 56 + 8 * b, :]
            mine_next.append(scale * (mine_h[b] + first[b]) - 2.0 * mine[b] - old[0])
            theirs_next.append(scale * (theirs_h[b] + facing[b]) - 2.0 * theirs[b] - old[1])
    second = edge_term(edge_idx, edge_own, edge_far, mine_next, theirs_next, 0)
    for b in range(6):
        edge[8 * b : 8 * b + 8, :] = first[b]
        edge[48 + 8 * b : 56 + 8 * b, :] = second[b]
        if keep is not None:
            keep[8 * b : 8 * b + 8, :] = mine_next[b]
            keep[48 + 8 * b : 56 + 8 * b, :] = theirs_next[b]


def two_steps_kernel(
    idx, tab, own_c, far_c, edge_idx, edge_own, edge_far,
    t0, h0, h0_in, to_w, to_e, from_w, from_e,
    t1, t2, h2, send_w, send_e, keep, edge,
):
    env = (idx, tab, own_c, far_c)
    tables = (edge_idx, edge_own, edge_far)
    edge_steps(tables, to_e, to_w, from_e, from_w, None, edge, keep)

    def loop(group, plain):
        rows = group_rows(group)
        extra = outer(group, idx, edge, 0)
        for n in range(36):
            image = line_image(h0, h0_in, n, rows)
            if n in extra:
                image = image + extra[n]
            t1[n, rows, :] = (1.0 / HALF) * image - t0[n, rows, :]
        extra_next = outer(group, idx, edge, 48)

        def emit(n, image):
            if n in extra_next:
                image = image + extra_next[n]
            t2[n, rows, :] = (2.0 / HALF) * image - 2.0 * t1[n, rows, :] - t0[n, rows, :]

        inner(group, env, t1, plain, emit)
        inner(group, env, t2, plain, store_lines(h2, rows), FACE_LINES)

    either(tab, loop)
    compact(idx, t2, h2, send_e, send_w)


def sums_kernel(t0, t1, t2, part, acc, pad):
    def body(group, carry):
        rows = group_rows(group)
        sums = [jnp.zeros((8, 128), F32)] * 5
        for n in range(36):
            a, b, c = t0[n, rows, :], t1[n, rows, :], t2[n, rows, :]
            for k, term in enumerate((a * a, a * b, b * b, b * c, c * c)):
                sums[k] = sums[k] + term
        for k in range(5):
            acc[rows, 128 * k : 128 * k + 128] = sums[k]
        return carry

    lax.fori_loop(0, 4, body, 0)
    store_sums(acc, pad, 0, 5)
    part[...] = pad[...]


def last_steps_kernel(
    idx, tab, own_c, far_c, edge_idx, edge_own, edge_far,
    t1, t2, h2, h2_in, to_w, to_e, from_w, from_e, keep, part,
    t3, red, edge, acc, pad,
):
    env = (idx, tab, own_c, far_c)
    tables = (edge_idx, edge_own, edge_far)
    edge_steps(tables, to_e, to_w, from_e, from_w, keep, edge, None)

    def loop(group, plain):
        rows = group_rows(group)
        extra = outer(group, idx, edge, 0)
        sums = [jnp.zeros((8, 128), F32)] * 3
        for n in range(36):
            image = line_image(h2, h2_in, n, rows)
            if n in extra:
                image = image + extra[n]
            c = t2[n, rows, :]
            d = (2.0 / HALF) * image - 2.0 * c - t1[n, rows, :]
            t3[n, rows, :] = d
            sums[0] = sums[0] + c * d
            sums[1] = sums[1] + d * d
        extra_next = outer(group, idx, edge, 48)

        def emit(n, image):
            if n in extra_next:
                image = image + extra_next[n]
            d = t3[n, rows, :]
            sums[2] = sums[2] + d * ((2.0 / HALF) * image - 2.0 * d - t2[n, rows, :])

        inner(group, env, t3, plain, emit)
        for k in range(3):
            acc[rows, 128 * k : 128 * k + 128] = sums[k]

    either(tab, loop)
    store_sums(acc, pad, 5, 3)
    row = lax.broadcasted_iota(jnp.int32, (8, 128), 0)
    mixed = jnp.where(row < 5, part[...], pad[...])
    for k in range(16):
        red[k] = mixed


def finish_kernel(red, x0, t0, t1, t2, t3, out, coef, held, sems):
    parts = [red[k] for k in range(16)]
    while len(parts) > 1:
        parts = [a + b for a, b in zip(parts[::2], parts[1::2])]
    total = parts[0]
    even = [total[2 * k : 2 * k + 1] for k in range(4)]
    odd = [total[2 * k + 1 : 2 * k + 2] for k in range(4)]
    moment = []
    for k in range(4):
        moment.append(even[0] if k == 0 else 2.0 * even[k] - even[0])
        moment.append(odd[0] if k == 0 else 2.0 * odd[k] - odd[0])

    def inner_product(i, j):
        return 0.5 * (moment[i + j] + moment[abs(i - j)])

    def energy(i, j):
        shifted = 0.5 * (inner_product(i, j + 1) + inner_product(i, abs(j - 1)))
        return HALF * (shifted + inner_product(i, j))

    low = [[None] * 4 for _ in range(4)]
    diag, inverse, half = [], [], []
    for j in range(4):
        d = energy(j, j)
        value = moment[j]
        for k in range(j):
            d = d - low[j][k] * low[j][k] * diag[k]
            value = value - low[j][k] * half[k]
        diag.append(d)
        half.append(value)
        inverse.append(1.0 / d)
        for i in range(j + 1, 4):
            e = energy(i, j)
            for k in range(j):
                e = e - low[i][k] * low[j][k] * diag[k]
            low[i][j] = e * inverse[j]
    weight = [half[k] * inverse[k] for k in range(4)]
    for i in (2, 1, 0):
        for k in range(i + 1, 4):
            weight[i] = weight[i] - low[k][i] * weight[k]
    turned = jnp.concatenate(weight + [jnp.zeros((4, 128), F32)], axis=0).T
    for k in range(4):
        coef[k] = jnp.broadcast_to(turned[0:32, k : k + 1], (32, 128))
    cuts = (0, 15, 30, 36)
    copies = []
    for c in range(3):
        def add(n, carry):
            terms = coef[0] * t0[n] + coef[1] * t1[n] + coef[2] * t2[n] + coef[3] * t3[n]
            held[n] = x0[n] + terms
            return carry

        lax.fori_loop(cuts[c], cuts[c + 1], add, 0, unroll=3)
        part = pl.ds(cuts[c], cuts[c + 1] - cuts[c])
        copies.append(pltpu.make_async_copy(held.at[part], out.at[part], sems.at[c]))
        copies[c].start()
    for copy in copies:
        copy.wait()


def pack_kernel(u, links, out, send_e, send_w, held, ready, near_links, lists, sems):
    loads, stores = [], []
    first = pltpu.make_async_copy(links, near_links, sems.at[6])
    first.start()
    cuts = (0, 4, 8, 9)
    for c in range(3):
        part = pl.ds(4 * cuts[c], 4 * (cuts[c + 1] - cuts[c]))
        loads.append(pltpu.make_async_copy(u.at[part], held.at[part], sems.at[c]))
        loads[c].start()
    first.wait()
    dev = lax.shift_right_logical(near_links[...], 7)
    remote = (dev != lax.axis_index("elem")).astype(jnp.int32)
    for side in range(2):
        lists[side : side + 1, :] = boundary(remote, side)[0].astype(jnp.int32)
    for c in range(3):
        loads[c].wait()
        for g in range(cuts[c], cuts[c + 1]):
            turned = held[4 * g : 4 * g + 4].reshape(128, 128).T
            ready[:, 16 * g : 16 * g + 16, :] = turned.reshape(8, 16, 128)
        part = pl.ds(16 * cuts[c], 16 * (cuts[c + 1] - cuts[c]))
        stores.append(pltpu.make_async_copy(ready.at[:, part], out.at[:, part], sems.at[3 + c]))
        stores[c].start()
    compact(lists, held, held, send_e, send_w, lambda n: n)
    for copy in stores:
        copy.wait()


def block_turn(blocks):
    part = lax.shift_right_logical(lane_ids(blocks[0].shape), 5)
    rolled = [blocks[0]] + [pltpu.roll(blocks[s], 32 * s, 1) for s in range(1, 4)]
    out = []
    for m in range(4):
        mixed = rolled[-m % 4]
        for t in range(1, 4):
            mixed = jnp.where(part == t, rolled[(t - m) % 4], mixed)
        out.append(pltpu.roll(mixed, 128 - 32 * m, 1) if m else mixed)
    return out


def product3(high, low, table, dim):
    def dot(a, b):
        return lax.dot_general(a, b, (((1,), (dim,)), ((), ())), preferred_element_type=F32)

    return dot(high, table[0]) + dot(high, table[1]) + dot(low, table[0])


def advect_kernel(idx, came, speed, synth, out, high, low, phys):
    for g in range(9):
        for h in range(2):
            pieces = block_turn([came[4 * h + s, 16 * g : 16 * g + 16, :] for s in range(4)])
            for m in range(4):
                n = 16 * (4 * g + m)
                hi, lo = split(pieces[m])
                high[n : n + 16, 128 * h : 128 * h + 128] = hi
                low[n : n + 16, 128 * h : 128 * h + 128] = lo
    for i in range(2):
        part = slice(288 * i, 288 * i + 288)
        phys[part, :] = product3(high[part, :], low[part, :], synth, 1)
    wide = jnp.broadcast_to(idx[LAYOUT : LAYOUT + 1, :], (16, 128)) == 0
    sx = jnp.where(wide, 2.0, 1.0)
    sy = jnp.where(wide, 1.0, 2.0)
    for h in range(2):
        cols = slice(128 * h, 128 * h + 128)
        u = [[phys[16 * (6 * i + j) : 16 * (6 * i + j) + 16, cols] for j in range(6)] for i in range(6)]
        acc = [[None] * 6 for _ in range(6)]
        for j in range(6):
            g = folded([u[i][j] for i in range(6)], DERIV_FOLD, -1)
            for i in range(6):
                acc[i][j] = sx * (speed[0, 6 * i + j, :, cols] * g[i])
        for i in range(6):
            g = folded(u[i], DERIV_FOLD, -1)
            for j in range(6):
                n = 16 * (6 * i + j)
                total = acc[i][j] + sy * (speed[1, 6 * i + j, :, cols] * g[j])
                hi, lo = split(float(-0.5 * W[i] * W[j]) * total)
                high[n : n + 16, cols] = hi
                low[n : n + 16, cols] = lo
    for i in range(2):
        part = slice(288 * i, 288 * i + 288)
        phys[part, :] = product3(high[part, :], low[part, :], synth, 0)
    for h in range(2):
        q = lane_ids((16, 128)) + 128 * h
        norm = jnp.where((q == 0) | (q == 255), 1.0 / 256, 1.0 / 128)
        cols = slice(128 * h, 128 * h + 128)
        for g in range(9):
            pieces = block_turn(
                [norm * phys[16 * (4 * g + m) : 16 * (4 * g + m) + 16, cols] for m in range(4)]
            )
            for s in range(4):
                out[4 * h + s, 16 * g : 16 * g + 16, :] = pieces[s]


def shift_by(array, by):
    count = lax.axis_size("elem")
    return lax.ppermute(array, "elem", [(i, (i + by) % count) for i in range(count)])


def shards(scalar_modes, velocity, viscosity, mortar_links, mortar_sides, layout):
    u = jnp.transpose(scalar_modes, (1, 2, 0, 3)).reshape(36, 32, 128)
    speed = jnp.transpose(velocity, (0, 2, 3, 4, 1)).reshape(2, 36, 16, 256)
    synth = jnp.asarray(split_table(plane_tables(256)))
    vol, edge = shape(36, 32, 128), shape(48, 128)
    both = shape(96, 128)
    blocks = shape(8, 144, 128)
    packed, *sent = call(
        pack_kernel,
        [blocks, edge, edge],
        [
            VMEM((36, 32, 128), F32),
            VMEM((8, 144, 128), F32),
            VMEM((8, 128), jnp.int32),
            VMEM((8, 128), jnp.int32),
            pltpu.SemaphoreType.DMA((7,)),
        ],
        [u, mortar_links],
        [HBM, HBM],
        [HBM, VMEM, VMEM],
    )
    came = lax.all_to_all(packed, "plane", 0, 0, tiled=True)

    table = shape(36, 8, 128)
    idx, edge_idx, tab, own_c, far_c, edge_own, edge_far, base = call(
        guess_kernel,
        [
            shape(24, 128, dtype=jnp.int32),
            shape(8, 128, dtype=jnp.int32),
            shape(8, 128),
        ]
        + [table] * 4
        + [vol],
        [VMEM((36, 32, 128), F32), pltpu.SemaphoreType.DMA],
        [mortar_links, mortar_sides, viscosity[None], layout[None], u],
        [VMEM] * 4 + [HBM],
    )
    head = [idx, tab, own_c, far_c]
    edges = [edge_idx, edge_own, edge_far]

    def run(kernel, outs, scratch, args):
        return call(kernel, outs, scratch, args, [VMEM] * len(args))

    def trade_back(send_w, send_e):
        return shift_by(send_e, 1), shift_by(send_w, -1)

    def trade(send_e, send_w):
        from_w = shift_by(send_e, 1)
        return shift_by(send_w, -1), from_w

    guess_edge = run(guess_edge_kernel, [shape(48, 128)], [], [*edges, *sent, *trade(*sent)])[0]
    came, guess_edge, base = lax.optimization_barrier((came, guess_edge, base))
    back = call(
        advect_kernel,
        [blocks],
        [
            VMEM((576, 256), BF16),
            VMEM((576, 256), BF16),
            VMEM((576, 256), F32),
        ],
        [idx, came, speed, synth],
        [VMEM] * 4,
        grant=8,
    )[0]
    back = lax.all_to_all(back, "plane", 0, 0, tiled=True)

    def work(count):
        return [
            VMEM((96, 128), F32),
            VMEM((32, 128 * count), F32),
            VMEM((8, 128), F32),
        ]

    lines, insides = shape(12, 32, 128), shape(24, 32, 128)
    t0, h0, to_w, to_e = run(
        residual_kernel, [vol, lines, edge, edge], [], head + [back, base, guess_edge]
    )
    got = trade_back(to_w, to_e)
    h0_in = run(inside_kernel, [insides], [], head + [t0])[0]
    t1, t2, h2, to_w, to_e, keep = run(
        two_steps_kernel,
        [vol, vol, lines, edge, edge, both],
        [VMEM((96, 128), F32)],
        head + edges + [t0, h0, h0_in, to_w, to_e, *got],
    )
    got = trade_back(to_w, to_e)
    h2_in = run(inside_kernel, [insides], [], head + [t2])[0]
    part = run(sums_kernel, [shape(8, 128)], work(5)[1:], [t0, t1, t2])[0]
    t3, red = run(
        last_steps_kernel,
        [vol, shape(16, 8, 128)],
        work(3),
        head + edges + [t1, t2, h2, h2_in, to_w, to_e, *got, keep, part],
    )
    red = lax.all_to_all(red, "elem", 0, 0, tiled=True)
    out = call(
        finish_kernel,
        [vol],
        [VMEM((4, 32, 128), F32), VMEM((36, 32, 128), F32), pltpu.SemaphoreType.DMA((3,))],
        [red, u, t0, t1, t2, t3],
        [VMEM] * 6,
        [HBM],
    )[0]
    return jnp.transpose(out.reshape(6, 6, 32, 128), (2, 0, 1, 3))


def solution(mesh):
    placed = (
        P("plane", None, None, "elem"),
        P(None, None, None, None, ("elem", "plane")),
        P("elem"),
        P(None, "elem"),
        P(None, None, "elem"),
        P("elem"),
    )
    return jax.shard_map(
        shards,
        mesh=mesh,
        in_specs=placed,
        out_specs=P("plane", None, None, "elem"),
        check_vma=False,
    )
```

```python
import math

import jax
import jax.numpy as jnp
import ml_dtypes
import numpy as np
from jax import lax
from jax.experimental import pallas as pl
from jax.experimental.pallas import tpu as pltpu
from jax.sharding import PartitionSpec as P

F32 = jnp.float32
BF16 = jnp.bfloat16
PENALTY = 10.0
SPANWISE = 0.0625
VMEM = pltpu.VMEM
SMEM = pltpu.SMEM
HBM = pltpu.HBM
MIXED = 7
SELF, ANY, FIRST, LAYOUT, LOCAL = 2, 4, 6, 7, 10


def lagrange_at(points, targets):
    out = np.ones((6, 6))
    for row in range(6):
        for col in range(6):
            for other in range(6):
                if other != col:
                    out[row, col] *= (targets[row] - points[other]) / (points[col] - points[other])
    return out


def node_tables():
    root = math.sqrt(7.0)
    outer = math.sqrt(1.0 / 3.0 + 2.0 * root / 21.0)
    inner = math.sqrt(1.0 / 3.0 - 2.0 * root / 21.0)
    points = np.array([-1.0, -outer, -inner, inner, outer, 1.0])
    half = [1.0 / 15.0, (14.0 - root) / 30.0, (14.0 + root) / 30.0]
    weights = np.array(half + half[::-1])
    bary = np.array(
        [1.0 / np.prod([points[c] - points[k] for k in range(6) if k != c]) for c in range(6)]
    )
    deriv = np.zeros((6, 6))
    for i in range(6):
        for j in range(6):
            if i != j:
                deriv[i, j] = bary[j] / bary[i] / (points[i] - points[j])
        deriv[i, i] = -np.sum(deriv[i])
    lower = lagrange_at(points, (points - 1.0) / 2.0)
    upper = lagrange_at(points, (points + 1.0) / 2.0)
    stiff = deriv.T @ (weights[:, None] * deriv)
    return weights, deriv, lower, upper, stiff


W, D, QLO, QHI, K1 = node_tables()
HALVES = [np.eye(6), QLO, QHI]


def plane_tables(count):
    planes = np.arange(count)[:, None]
    coeffs = np.arange(count)[None, :]
    harmonic = (coeffs + 1) // 2
    phase = 2.0 * np.pi * (harmonic * planes % count) / count
    synth = np.where(coeffs == 0, 1.0, np.where(coeffs % 2 == 1, np.cos(phase), np.sin(phase)))
    return synth


def split_table(table):
    table = np.asarray(table, np.float32)
    high = table.astype(ml_dtypes.bfloat16)
    low = (table - high.astype(np.float32)).astype(ml_dtypes.bfloat16)
    return np.stack([high, low])


def fold(matrix):
    plus = (matrix[:3, :3] + matrix[:3, :2:-1]) / 2.0
    minus = (matrix[:3, :3] - matrix[:3, :2:-1]) / 2.0
    return plus, minus


STIFF_FOLD = fold(K1 / W[:, None])
DERIV_FOLD = fold(D)


def folded(values, tables, sign):
    plus, minus = tables
    even = [values[a] + values[5 - a] for a in range(3)]
    odd = [values[a] - values[5 - a] for a in range(3)]
    out = [None] * 6
    for i in range(3):
        e = sum(float(plus[i, a]) * even[a] for a in range(3))
        o = sum(float(minus[i, a]) * odd[a] for a in range(3))
        out[i] = e + o
        out[5 - i] = e - o if sign > 0 else o - e
    return out


def split(value):
    high = value.astype(BF16)
    return high, (value - high.astype(F32)).astype(BF16)


def lane_ids(shape):
    return lax.broadcasted_iota(jnp.int32, shape, len(shape) - 1)


def call(kernel, outs, scratch, operands, spaces, out_spaces=None, grant=3):
    total = sum(int(np.prod(o.shape)) * 4 for o in outs)
    total += sum(int(np.prod(o.shape)) * 4 for o in operands)
    return pl.pallas_call(
        kernel,
        out_shape=outs,
        in_specs=[pl.BlockSpec(memory_space=s) for s in spaces],
        out_specs=[pl.BlockSpec(memory_space=s) for s in out_spaces or [VMEM] * len(outs)],
        scratch_shapes=scratch,
        compiler_params=pltpu.CompilerParams(vmem_limit_bytes=grant * 2**20),
        cost_estimate=pl.CostEstimate(flops=4_000_000, bytes_accessed=total, transcendentals=0),
    )(*[far(a) if s == HBM else a for a, s in zip(operands, spaces)])


def far(array):
    return pltpu.with_memory_space_constraint(array, HBM)


def shape(*dims, dtype=F32):
    return jax.ShapeDtypeStruct(dims, dtype)


def take(value, index):
    return jnp.take_along_axis(value, index, axis=1)


def take_row(value, index):
    wide = jnp.broadcast_to(value, (8, 128)), jnp.broadcast_to(index, (8, 128))
    return take(*wide)[0:1]


def boundary(remote, side):
    row = lax.broadcasted_iota(jnp.int32, (128, 128), 0)
    col = lane_ids((128, 128))
    any_rem = jnp.maximum(remote[2 * side : 2 * side + 1], remote[2 * side + 1 : 2 * side + 2])
    before = jnp.sum(jnp.where(col < row, any_rem, 0).astype(F32), axis=1, keepdims=True)
    mine = jnp.sum(jnp.where(col == row, any_rem, 0).astype(F32), axis=1, keepdims=True)
    slot = jnp.bitwise_and(lane_ids((1, 128)), 15).astype(F32)
    chosen = jnp.where((before == slot) & (mine > 0.0), 1.0, 0.0)
    listed = jnp.sum(chosen * row.astype(F32), axis=0, keepdims=True)
    return listed, jnp.sum(chosen, axis=0, keepdims=True), before


def build_tables(
    links, sides, visc, layout, idx, edge_idx, tab, own_c, far_c, edge_own, edge_far
):
    me = lax.axis_index("elem")
    dev = lax.shift_right_logical(links[...], 7)
    loc = jnp.bitwise_and(links[...], 127)
    remote = (dev != me).astype(jnp.int32)
    idx[LOCAL : LOCAL + 8, :] = loc
    own, other = sides[0], sides[1]
    inside = jnp.where(remote > 0, 3, own)
    whole = (inside == 0) & (other == 0)
    second = jnp.bitwise_and(lax.broadcasted_iota(jnp.int32, (8, 128), 0), 1) == 1
    odd_one = jnp.where(inside == 3, 0.0, jnp.where(whole & ~second, 0.0, 1.0))
    idx[FIRST : FIRST + 1, :] = jnp.full((1, 128), 32 * lax.axis_index("plane"), jnp.int32)
    idx[LAYOUT : LAYOUT + 1, :] = layout[...]
    row = lax.broadcasted_iota(jnp.int32, (128, 128), 0)
    col = lane_ids((128, 128))
    lane = lane_ids((1, 128))
    slot = jnp.bitwise_and(lane, 15)
    listed, present, ranks = [], [], []
    for side in range(2):
        rem = [remote[2 * side + t : 2 * side + t + 1] for t in range(2)]
        far = [loc[2 * side + t : 2 * side + t + 1] for t in range(2)]
        any_rem = jnp.maximum(rem[0], rem[1])
        places, filled, before = boundary(remote, side)
        listed.append(places.astype(jnp.int32))
        present.append(filled.astype(jnp.int32))
        idx[side : side + 1, :] = listed[side]
        mine_at = jnp.sum(jnp.where(row == col, before, 0.0), axis=0, keepdims=True)
        mine_at = jnp.where(any_rem > 0, mine_at.astype(jnp.int32), 0)
        idx[SELF + side : SELF + side + 1, :] = mine_at
        idx[ANY + side : ANY + side + 1, :] = any_rem
        named = jnp.where(
            ((far[0] == row) & (rem[0] > 0)) | ((far[1] == row) & (rem[1] > 0)), 1.0, 0.0
        )
        named = jnp.max(named, axis=1, keepdims=True)
        for t in range(2):
            rank = jnp.sum(jnp.where(row < far[t], named, 0.0), axis=0, keepdims=True)
            ranks.append(jnp.where(rem[t] > 0, rank.astype(jnp.int32), 0))
    idx[8:10, :] = jnp.zeros((2, 128), jnp.int32)
    idx[18:24, :] = jnp.zeros((6, 128), jnp.int32)

    west = lane < 64
    base = jnp.bitwise_and(lane, 112)
    element = jnp.where(west, listed[0], listed[1])
    here = jnp.where(west, present[0], present[1]) > 0

    def pick(rows_w, rows_e):
        return jnp.where(west, take_row(rows_w, element), take_row(rows_e, element))

    rank, live, mine, theirs = [], [], [], []
    for t in range(2):
        rank.append(pick(ranks[t], ranks[2 + t]))
        live.append((pick(remote[t : t + 1], remote[2 + t : 3 + t]) > 0) & here)
        mine.append(jnp.where(live[t], pick(own[t : t + 1], own[2 + t : 3 + t]), 3))
        theirs.append(jnp.where(live[t], pick(other[t : t + 1], other[2 + t : 3 + t]), 3))
    first = jnp.full((1, 128), 99, jnp.int32)
    last = jnp.full((1, 128), -1, jnp.int32)
    for t in range(2):
        target = jnp.where(live[t], rank[t], 99)
        for r in range(16):
            hit = take_row(target, base + r) == slot
            first = jnp.where(hit, jnp.minimum(first, 16 * t + r), first)
            last = jnp.where(hit, jnp.maximum(last, 16 * t + r), last)
    exists = [last >= 0, last > first]
    key = [jnp.where(exists[0], first, 0), jnp.where(exists[1], last, 0)]
    back = [base + jnp.bitwise_and(k, 15) for k in key]

    def from_key(k, pair):
        value = jnp.where(key[k] >= 16, take_row(pair[1], back[k]), take_row(pair[0], back[k]))
        return jnp.where(exists[k], value, 3)

    near_own = [from_key(k, theirs) for k in range(2)]
    near_far = [from_key(k, mine) for k in range(2)]
    edge_idx[...] = jnp.zeros((8, 128), jnp.int32)
    for k in range(2):
        edge_idx[k : k + 1, :] = base + rank[k]
        edge_idx[2 + k : 3 + k, :] = back[k]
    none = jnp.full((4, 128), 3, jnp.int32)
    edge_mine = jnp.concatenate([mine[0], mine[1], near_own[0], near_own[1], none], axis=0)
    edge_theirs = jnp.concatenate([theirs[0], theirs[1], near_far[0], near_far[1], none], axis=0)

    nu = visc[...]
    wide = layout[...] == 0
    tab[0:1, :] = nu * jnp.where(wide, 2.0, 0.5)
    tab[1:2, :] = nu * jnp.where(wide, 0.5, 2.0)
    tab[2:3, :] = nu
    for face in range(4):
        tab[3 + face : 4 + face, :] = whole[2 * face : 2 * face + 1].astype(F32)
    tab[MIXED : MIXED + 1, :] = jnp.max(odd_one, axis=0, keepdims=True)
    mine_m = [PENALTY * HALVES[o].T @ np.diag(W) @ HALVES[o] for o in range(3)]
    far_m = [
        [-PENALTY * HALVES[o].T @ np.diag(W) @ HALVES[c] for c in range(3)] for o in range(3)
    ]
    for code, facing, own_ref, far_ref in (
        (inside, other, own_c, far_c),
        (edge_mine, edge_theirs, edge_own, edge_far),
    ):
        hot = [(code == o).astype(F32) for o in range(3)]
        pair = [[hot[o] * (facing == c).astype(F32) for c in range(3)] for o in range(3)]
        for a in range(6):
            for b in range(6):
                n = 6 * a + b
                total = sum(float(mine_m[o][a, b]) * hot[o] for o in range(3))
                own_ref[n] = total + pltpu.roll(total, 7, 0)
                far_ref[n] = sum(
                    float(far_m[o][c][a, b]) * pair[o][c] for o in range(3) for c in range(3)
                )


def group_rows(group):
    return pl.ds(pl.multiple_of(group * 8, 8), 8)


def row_of(ref, r):
    return jnp.broadcast_to(ref[r : r + 1, :], (8, 128))


def face_nodes(face):
    return [
        6 * i + j
        for i, j in [
            (0, b) if face == 0 else (5, b) if face == 1 else (b, 0) if face == 2 else (b, 5)
            for b in range(6)
        ]
    ]


def either(tab, loop):
    mixed = jnp.max(tab[MIXED : MIXED + 1, :]) > 0.5
    for plain in (True, False):

        @pl.when(mixed != plain)
        def _(plain=plain):
            lax.fori_loop(
                0, 4, lambda group, carry: loop(group, plain) or carry, 0, unroll=4 if plain else 1
            )


def weighted(factors, values):
    total = float(factors[0]) * values[0]
    for f, v in zip(factors[1:], values[1:]):
        total = total + float(f) * v
    return total


def plain_terms(env, v):
    idx, tab, _, _ = env

    def of_face(face):
        active = row_of(tab, 3 + face)
        local = row_of(idx, LOCAL + 2 * face)

        def term(a):
            n, m = face_nodes(face)[a], face_nodes(face ^ 1)[a]
            return (float(PENALTY * W[a]) * active) * (v(n) - take(v(m), local))

        return term

    return [of_face(face) for face in range(4)]


def general_terms(env, v):
    idx, _, own_c, far_c = env
    found = []
    for face in range(4):
        mine = [v(n) for n in face_nodes(face)]
        theirs = [
            [take(v(n), row_of(idx, LOCAL + 2 * face + t)) for n in face_nodes(face ^ 1)]
            for t in range(2)
        ]
        values = []
        for a in range(6):
            extra = jnp.zeros((8, 128), F32)
            for b in range(6):
                extra = extra + own_c[6 * a + b, 2 * face : 2 * face + 1, :] * mine[b]
                for t in range(2):
                    s = 2 * face + t
                    extra = extra + far_c[6 * a + b, s : s + 1, :] * theirs[t][b]
            values.append(extra)
        found.append(values.__getitem__)
    return found


FACE_LINES, INSIDE_LINES, ALL_LINES = (0,), (1, 2), (0, 1, 2)


def inner(group, env, v_ref, plain, emit, pairs=ALL_LINES):
    idx, tab, _, _ = env
    rows = group_rows(group)

    def v(n):
        return v_ref[n, rows, :]

    terms = (plain_terms if plain else general_terms)(env, v)
    q = row_of(idx, FIRST) + group * 8 + lax.broadcasted_iota(jnp.int32, (8, 128), 0)
    harmonic = lax.shift_right_logical(q + 1, 1).astype(F32) * SPANWISE
    cx, cy = row_of(tab, 0), row_of(tab, 1)
    shift = 1.0 + 0.5 * tab[2:3, :] * (harmonic * harmonic)
    plus, minus = STIFF_FOLD
    even = [[v(6 * a + j) + v(30 - 6 * a + j) for a in range(3)] for j in range(6)]
    odd = [[v(6 * a + j) - v(30 - 6 * a + j) for a in range(3)] for j in range(6)]
    for i in pairs:
        e = [weighted(plus[i], even[j]) for j in range(6)]
        o = [weighted(minus[i], odd[j]) for j in range(6)]
        for line in (i, 5 - i):
            mine = [v(6 * line + j) for j in range(6)]
            g = folded(mine, STIFF_FOLD, 1)
            for j in range(6):
                n = 6 * line + j
                gx = e[j] + o[j] if line == i else e[j] - o[j]
                value = float(W[line] * W[j]) * (shift * mine[j] + cx * gx + cy * g[j])
                for face, (at, b) in enumerate(((line == 0, j), (line == 5, j), (j == 0, line), (j == 5, line))):
                    if at:
                        value = value + terms[face](b)
                emit(n, value)


def line_at(n):
    return n if n < 6 else n - 24


def compact(idx, v_ref, h_ref, send_e, send_w, at=line_at):
    part = lax.shift_right_logical(lane_ids((8, 128)), 4)
    for face, ref in ((0, send_w), (1, send_e)):
        index = row_of(idx, face)
        for b in range(6):
            n = face_nodes(face)[b]
            value = take(v_ref[n, 0:8, :], index)
            for k in range(1, 8):
                part_rows = slice(8 * (k % 4), 8 * (k % 4) + 8)
                source = v_ref[n, part_rows, :] if k < 4 else h_ref[at(n), part_rows, :]
                other = take(source, index)
                value = jnp.where(part == k, other, value)
            ref[8 * b : 8 * b + 8, :] = value


def outer(group, idx, edge, first):
    found = {}
    for face in range(2):
        lanes = row_of(idx, SELF + face) + (64 * face + 16 * group)
        on = row_of(idx, ANY + face) > 0
        for b in range(6):
            value = take(edge[first + 8 * b : first + 8 * b + 8, :], lanes)
            found[face_nodes(face)[b]] = jnp.where(on, value, 0.0)
    return found


def edge_blocks(ref):
    return [ref[8 * b : 8 * b + 8, :] for b in range(6)]


def merge(to_e, to_w):
    west = lane_ids((8, 128)) < 64
    plain, inner_h = [], []
    for w, e in zip(edge_blocks(to_w), edge_blocks(to_e)):
        plain.append(jnp.where(west, w, pltpu.roll(e, 64, 1)))
        inner_h.append(jnp.where(west, pltpu.roll(w, 64, 1), e))
    return plain, inner_h


def edge_term(edge_idx, edge_own, edge_far, mine, theirs, row):
    near = [[take(t, row_of(edge_idx, row + k)) for t in theirs] for k in range(2)]
    out = []
    for a in range(6):
        chains = [None] * 3
        for b in range(6):
            n = 6 * a + b
            terms = [edge_own[n, row : row + 1, :] * mine[b]]
            terms += [edge_far[n, row + k : row + k + 1, :] * near[k][b] for k in range(2)]
            chains = terms if chains[0] is None else [c + t for c, t in zip(chains, terms)]
        out.append(chains[0] + (chains[1] + chains[2]))
    return out


def store_sums(acc, pad, first, count):
    width = count * 128
    lhs = (
        lax.broadcasted_iota(jnp.int32, (8, width), 0)
        == lax.shift_right_logical(lane_ids((8, width)), 7) + first
    ).astype(F32)
    sums = lax.dot_general(
        lhs, acc[...], (((1,), (1,)), ((), ())),
        precision=lax.Precision.HIGHEST, preferred_element_type=F32,
    )
    pad[...] = jnp.ones((8, 128), F32)
    pad[:, 0:32] = sums


HALF = 10.0


def store_lines(ref, rows):
    def emit(n, value):
        ref[line_at(n), rows, :] = value

    return emit


def inside_kernel(idx, tab, own_c, far_c, v, out):
    env = (idx, tab, own_c, far_c)

    def loop(group, plain):
        rows = group_rows(group)

        def emit(n, value):
            out[n - 6, rows, :] = value

        inner(group, env, v, plain, emit, INSIDE_LINES)

    either(tab, loop)


def line_image(lines, inside, n, rows):
    return inside[n - 6, rows, :] if 6 <= n < 30 else lines[line_at(n), rows, :]


def guess_kernel(
    links, sides, visc, layout, u_far,
    idx, edge_idx, tab, own_c, far_c, edge_own, edge_far, out, u, sem,
):
    copy = pltpu.make_async_copy(u_far, u, sem)
    copy.start()
    build_tables(
        links, sides, visc, layout, idx, edge_idx, tab, own_c, far_c, edge_own, edge_far
    )
    copy.wait()
    env = (idx, tab, own_c, far_c)

    def loop(group, plain):
        rows = group_rows(group)

        def emit(n, value):
            out[n, rows, :] = float(W[n // 6] * W[n % 6]) * u[n, rows, :] - value

        inner(group, env, u, plain, emit)

    either(tab, loop)


def guess_edge_kernel(edge_idx, edge_own, edge_far, to_e, to_w, from_e, from_w, edge):
    mine, _ = merge(to_e, to_w)
    theirs, _ = merge(from_e, from_w)
    for b, value in enumerate(edge_term(edge_idx, edge_own, edge_far, mine, theirs, 0)):
        edge[8 * b : 8 * b + 8, :] = value


def residual_kernel(
    idx, tab, own_c, far_c, back, base, edge, out, h_out, send_e, send_w
):
    env = (idx, tab, own_c, far_c)

    def turn(g, carry):
        part = pl.ds(pl.multiple_of(16 * g, 16), 16)
        turned = back[:, part, :].reshape(128, 128).T
        for m in range(4):
            out[4 * g + m] = base[4 * g + m] + turned[32 * m : 32 * m + 32]
        return carry

    lax.fori_loop(0, 9, turn, 0, unroll=3)

    def loop(group, plain):
        rows = group_rows(group)
        for n, extra in outer(group, idx, edge, 0).items():
            out[n, rows, :] -= extra
        inner(group, env, out, plain, store_lines(h_out, rows), FACE_LINES)

    either(tab, loop)
    compact(idx, out, h_out, send_e, send_w)


def edge_steps(tables, to_e, to_w, from_e, from_w, before, edge, keep):
    edge_idx, edge_own, edge_far = tables
    mine, mine_h = merge(to_e, to_w)
    theirs, theirs_h = merge(from_e, from_w)
    scale = (1.0 if before is None else 2.0) / HALF
    first = edge_term(edge_idx, edge_own, edge_far, mine, theirs, 0)
    facing = edge_term(edge_idx, edge_own, edge_far, theirs, mine, 2)
    mine_next, theirs_next = [], []
    for b in range(6):
        if before is None:
            mine_next.append(scale * (mine_h[b] + first[b]) - mine[b])
            theirs_next.append(scale * (theirs_h[b] + facing[b]) - theirs[b])
        else:
            old = before[8 * b : 8 * b + 8, :], before[48 + 8 * b : 56 + 8 * b, :]
            mine_next.append(scale * (mine_h[b] + first[b]) - 2.0 * mine[b] - old[0])
            theirs_next.append(scale * (theirs_h[b] + facing[b]) - 2.0 * theirs[b] - old[1])
    second = edge_term(edge_idx, edge_own, edge_far, mine_next, theirs_next, 0)
    for b in range(6):
        edge[8 * b : 8 * b + 8, :] = first[b]
        edge[48 + 8 * b : 56 + 8 * b, :] = second[b]
        if keep is not None:
            keep[8 * b : 8 * b + 8, :] = mine_next[b]
            keep[48 + 8 * b : 56 + 8 * b, :] = theirs_next[b]


def two_steps_kernel(
    idx, tab, own_c, far_c, edge_idx, edge_own, edge_far,
    t0, h0, h0_in, to_e, to_w, from_e, from_w,
    t1, t2, h2, send_e, send_w, keep, edge,
):
    env = (idx, tab, own_c, far_c)
    tables = (edge_idx, edge_own, edge_far)
    edge_steps(tables, to_e, to_w, from_e, from_w, None, edge, keep)

    def loop(group, plain):
        rows = group_rows(group)
        extra = outer(group, idx, edge, 0)
        for n in range(36):
            image = line_image(h0, h0_in, n, rows)
            if n in extra:
                image = image + extra[n]
            t1[n, rows, :] = (1.0 / HALF) * image - t0[n, rows, :]
        extra_next = outer(group, idx, edge, 48)

        def emit(n, image):
            if n in extra_next:
                image = image + extra_next[n]
            t2[n, rows, :] = (2.0 / HALF) * image - 2.0 * t1[n, rows, :] - t0[n, rows, :]

        inner(group, env, t1, plain, emit)
        inner(group, env, t2, plain, store_lines(h2, rows), FACE_LINES)

    either(tab, loop)
    compact(idx, t2, h2, send_e, send_w)


def sums_kernel(t0, t1, t2, part, acc, pad):
    def body(group, carry):
        rows = group_rows(group)
        sums = [jnp.zeros((8, 128), F32)] * 5
        for n in range(36):
            a, b, c = t0[n, rows, :], t1[n, rows, :], t2[n, rows, :]
            for k, term in enumerate((a * a, a * b, b * b, b * c, c * c)):
                sums[k] = sums[k] + term
        for k in range(5):
            acc[rows, 128 * k : 128 * k + 128] = sums[k]
        return carry

    lax.fori_loop(0, 4, body, 0)
    store_sums(acc, pad, 0, 5)
    part[...] = pad[...]


def last_steps_kernel(
    idx, tab, own_c, far_c, edge_idx, edge_own, edge_far,
    t1, t2, h2, h2_in, to_e, to_w, from_e, from_w, keep, part,
    t3, red, edge, acc, pad,
):
    env = (idx, tab, own_c, far_c)
    tables = (edge_idx, edge_own, edge_far)
    edge_steps(tables, to_e, to_w, from_e, from_w, keep, edge, None)

    def loop(group, plain):
        rows = group_rows(group)
        extra = outer(group, idx, edge, 0)
        sums = [jnp.zeros((8, 128), F32)] * 3
        for n in range(36):
            image = line_image(h2, h2_in, n, rows)
            if n in extra:
                image = image + extra[n]
            c = t2[n, rows, :]
            d = (2.0 / HALF) * image - 2.0 * c - t1[n, rows, :]
            t3[n, rows, :] = d
            sums[0] = sums[0] + c * d
            sums[1] = sums[1] + d * d
        extra_next = outer(group, idx, edge, 48)

        def emit(n, image):
            if n in extra_next:
                image = image + extra_next[n]
            d = t3[n, rows, :]
            sums[2] = sums[2] + d * ((2.0 / HALF) * image - 2.0 * d - t2[n, rows, :])

        inner(group, env, t3, plain, emit)
        for k in range(3):
            acc[rows, 128 * k : 128 * k + 128] = sums[k]

    either(tab, loop)
    store_sums(acc, pad, 5, 3)
    row = lax.broadcasted_iota(jnp.int32, (8, 128), 0)
    mixed = jnp.where(row < 5, part[...], pad[...])
    for k in range(16):
        red[k] = mixed


def finish_kernel(red, x0, t0, t1, t2, t3, out, coef, held, sems):
    parts = [red[k] for k in range(16)]
    while len(parts) > 1:
        parts = [a + b for a, b in zip(parts[::2], parts[1::2])]
    total = parts[0]
    even = [total[2 * k : 2 * k + 1] for k in range(4)]
    odd = [total[2 * k + 1 : 2 * k + 2] for k in range(4)]
    moment = []
    for k in range(4):
        moment.append(even[0] if k == 0 else 2.0 * even[k] - even[0])
        moment.append(odd[0] if k == 0 else 2.0 * odd[k] - odd[0])

    def inner_product(i, j):
        return 0.5 * (moment[i + j] + moment[abs(i - j)])

    def energy(i, j):
        shifted = 0.5 * (inner_product(i, j + 1) + inner_product(i, abs(j - 1)))
        return HALF * (shifted + inner_product(i, j))

    low = [[None] * 4 for _ in range(4)]
    diag, inverse, half = [], [], []
    for j in range(4):
        d = energy(j, j)
        value = moment[j]
        for k in range(j):
            d = d - low[j][k] * low[j][k] * diag[k]
            value = value - low[j][k] * half[k]
        diag.append(d)
        half.append(value)
        inverse.append(1.0 / d)
        for i in range(j + 1, 4):
            e = energy(i, j)
            for k in range(j):
                e = e - low[i][k] * low[j][k] * diag[k]
            low[i][j] = e * inverse[j]
    weight = [half[k] * inverse[k] for k in range(4)]
    for i in (2, 1, 0):
        for k in range(i + 1, 4):
            weight[i] = weight[i] - low[k][i] * weight[k]
    turned = jnp.concatenate(weight + [jnp.zeros((4, 128), F32)], axis=0).T
    for k in range(4):
        coef[k] = jnp.broadcast_to(turned[0:32, k : k + 1], (32, 128))
    cuts = (0, 15, 30, 36)
    copies = []
    for c in range(3):
        def add(n, carry):
            terms = coef[0] * t0[n] + coef[1] * t1[n] + coef[2] * t2[n] + coef[3] * t3[n]
            held[n] = x0[n] + terms
            return carry

        lax.fori_loop(cuts[c], cuts[c + 1], add, 0, unroll=3)
        part = pl.ds(cuts[c], cuts[c + 1] - cuts[c])
        copies.append(pltpu.make_async_copy(held.at[part], out.at[part], sems.at[c]))
        copies[c].start()
    for copy in copies:
        copy.wait()


def pack_kernel(u, links, out, send_e, send_w, held, ready, near_links, lists, sems):
    loads, stores = [], []
    first = pltpu.make_async_copy(links, near_links, sems.at[6])
    first.start()
    cuts = (0, 4, 8, 9)
    for c in range(3):
        part = pl.ds(4 * cuts[c], 4 * (cuts[c + 1] - cuts[c]))
        loads.append(pltpu.make_async_copy(u.at[part], held.at[part], sems.at[c]))
        loads[c].start()
    first.wait()
    dev = lax.shift_right_logical(near_links[...], 7)
    remote = (dev != lax.axis_index("elem")).astype(jnp.int32)
    for side in range(2):
        lists[side : side + 1, :] = boundary(remote, side)[0].astype(jnp.int32)
    for c in range(3):
        loads[c].wait()
        for g in range(cuts[c], cuts[c + 1]):
            turned = held[4 * g : 4 * g + 4].reshape(128, 128).T
            ready[:, 16 * g : 16 * g + 16, :] = turned.reshape(8, 16, 128)
        part = pl.ds(16 * cuts[c], 16 * (cuts[c + 1] - cuts[c]))
        stores.append(pltpu.make_async_copy(ready.at[:, part], out.at[:, part], sems.at[3 + c]))
        stores[c].start()
    compact(lists, held, held, send_e, send_w, lambda n: n)
    for copy in stores:
        copy.wait()


def block_turn(blocks):
    part = lax.shift_right_logical(lane_ids(blocks[0].shape), 5)
    rolled = [blocks[0]] + [pltpu.roll(blocks[s], 32 * s, 1) for s in range(1, 4)]
    out = []
    for m in range(4):
        mixed = rolled[-m % 4]
        for t in range(1, 4):
            mixed = jnp.where(part == t, rolled[(t - m) % 4], mixed)
        out.append(pltpu.roll(mixed, 128 - 32 * m, 1) if m else mixed)
    return out


def product3(high, low, table, dim):
    def dot(a, b):
        return lax.dot_general(a, b, (((1,), (dim,)), ((), ())), preferred_element_type=F32)

    return dot(high, table[0]) + dot(high, table[1]) + dot(low, table[0])


def advect_kernel(idx, came, speed, synth, out, high, low, phys):
    for g in range(9):
        for h in range(2):
            pieces = block_turn([came[4 * h + s, 16 * g : 16 * g + 16, :] for s in range(4)])
            for m in range(4):
                n = 16 * (4 * g + m)
                hi, lo = split(pieces[m])
                high[n : n + 16, 128 * h : 128 * h + 128] = hi
                low[n : n + 16, 128 * h : 128 * h + 128] = lo
    for i in range(2):
        part = slice(288 * i, 288 * i + 288)
        phys[part, :] = product3(high[part, :], low[part, :], synth, 1)
    wide = jnp.broadcast_to(idx[LAYOUT : LAYOUT + 1, :], (16, 128)) == 0
    sx = jnp.where(wide, 2.0, 1.0)
    sy = jnp.where(wide, 1.0, 2.0)
    for h in range(2):
        cols = slice(128 * h, 128 * h + 128)
        u = [[phys[16 * (6 * i + j) : 16 * (6 * i + j) + 16, cols] for j in range(6)] for i in range(6)]
        acc = [[None] * 6 for _ in range(6)]
        for j in range(6):
            g = folded([u[i][j] for i in range(6)], DERIV_FOLD, -1)
            for i in range(6):
                acc[i][j] = sx * (speed[0, 6 * i + j, :, cols] * g[i])
        for i in range(6):
            g = folded(u[i], DERIV_FOLD, -1)
            for j in range(6):
                n = 16 * (6 * i + j)
                total = acc[i][j] + sy * (speed[1, 6 * i + j, :, cols] * g[j])
                hi, lo = split(float(-0.5 * W[i] * W[j]) * total)
                high[n : n + 16, cols] = hi
                low[n : n + 16, cols] = lo
    for i in range(2):
        part = slice(288 * i, 288 * i + 288)
        phys[part, :] = product3(high[part, :], low[part, :], synth, 0)
    for h in range(2):
        q = lane_ids((16, 128)) + 128 * h
        norm = jnp.where((q == 0) | (q == 255), 1.0 / 256, 1.0 / 128)
        cols = slice(128 * h, 128 * h + 128)
        for g in range(9):
            pieces = block_turn(
                [norm * phys[16 * (4 * g + m) : 16 * (4 * g + m) + 16, cols] for m in range(4)]
            )
            for s in range(4):
                out[4 * h + s, 16 * g : 16 * g + 16, :] = pieces[s]


def shift_by(array, by):
    count = lax.axis_size("elem")
    return lax.ppermute(array, "elem", [(i, (i + by) % count) for i in range(count)])


def shards(scalar_modes, velocity, viscosity, mortar_links, mortar_sides, layout):
    u = jnp.transpose(scalar_modes, (1, 2, 0, 3)).reshape(36, 32, 128)
    speed = jnp.transpose(velocity, (0, 2, 3, 4, 1)).reshape(2, 36, 16, 256)
    synth = jnp.asarray(split_table(plane_tables(256)))
    vol, edge = shape(36, 32, 128), shape(48, 128)
    both = shape(96, 128)
    blocks = shape(8, 144, 128)
    packed, *sent = call(
        pack_kernel,
        [blocks, edge, edge],
        [
            VMEM((36, 32, 128), F32),
            VMEM((8, 144, 128), F32),
            VMEM((8, 128), jnp.int32),
            VMEM((8, 128), jnp.int32),
            pltpu.SemaphoreType.DMA((7,)),
        ],
        [u, mortar_links],
        [HBM, HBM],
        [HBM, VMEM, VMEM],
    )
    came = lax.all_to_all(packed, "plane", 0, 0, tiled=True)

    table = shape(36, 8, 128)
    idx, edge_idx, tab, own_c, far_c, edge_own, edge_far, base = call(
        guess_kernel,
        [
            shape(24, 128, dtype=jnp.int32),
            shape(8, 128, dtype=jnp.int32),
            shape(8, 128),
        ]
        + [table] * 4
        + [vol],
        [VMEM((36, 32, 128), F32), pltpu.SemaphoreType.DMA],
        [mortar_links, mortar_sides, viscosity[None], layout[None], u],
        [VMEM] * 4 + [HBM],
    )
    head = [idx, tab, own_c, far_c]
    edges = [edge_idx, edge_own, edge_far]

    def run(kernel, outs, scratch, args):
        return call(kernel, outs, scratch, args, [VMEM] * len(args))

    def trade(send_e, send_w):
        from_w = shift_by(send_e, 1)
        return shift_by(send_w, -1), from_w

    guess_edge = run(guess_edge_kernel, [shape(48, 128)], [], [*edges, *sent, *trade(*sent)])[0]
    came, guess_edge, base = lax.optimization_barrier((came, guess_edge, base))
    back = call(
        advect_kernel,
        [blocks],
        [
            VMEM((576, 256), BF16),
            VMEM((576, 256), BF16),
            VMEM((576, 256), F32),
        ],
        [idx, came, speed, synth],
        [VMEM] * 4,
        grant=8,
    )[0]
    back = lax.all_to_all(back, "plane", 0, 0, tiled=True)

    def work(count):
        return [
            VMEM((96, 128), F32),
            VMEM((32, 128 * count), F32),
            VMEM((8, 128), F32),
        ]

    lines, insides = shape(12, 32, 128), shape(24, 32, 128)
    t0, h0, *sent = run(
        residual_kernel, [vol, lines, edge, edge], [], head + [back, base, guess_edge]
    )
    got = trade(*sent)
    h0_in = run(inside_kernel, [insides], [], head + [t0])[0]
    t1, t2, h2, to_e, to_w, keep = run(
        two_steps_kernel,
        [vol, vol, lines, edge, edge, both],
        [VMEM((96, 128), F32)],
        head + edges + [t0, h0, h0_in, *sent, *got],
    )
    got = trade(to_e, to_w)
    h2_in = run(inside_kernel, [insides], [], head + [t2])[0]
    part = run(sums_kernel, [shape(8, 128)], work(5)[1:], [t0, t1, t2])[0]
    t3, red = run(
        last_steps_kernel,
        [vol, shape(16, 8, 128)],
        work(3),
        head + edges + [t1, t2, h2, h2_in, to_e, to_w, *got, keep, part],
    )
    red = lax.all_to_all(red, "elem", 0, 0, tiled=True)
    out = call(
        finish_kernel,
        [vol],
        [VMEM((4, 32, 128), F32), VMEM((36, 32, 128), F32), pltpu.SemaphoreType.DMA((3,))],
        [red, u, t0, t1, t2, t3],
        [VMEM] * 6,
        [HBM],
    )[0]
    return jnp.transpose(out.reshape(6, 6, 32, 128), (2, 0, 1, 3))


def solution(mesh):
    placed = (
        P("plane", None, None, "elem"),
        P(None, None, None, None, ("elem", "plane")),
        P("elem"),
        P(None, "elem"),
        P(None, None, "elem"),
        P("elem"),
    )
    return jax.shard_map(
        shards,
        mesh=mesh,
        in_specs=placed,
        out_specs=P("plane", None, None, "elem"),
        check_vma=False,
    )
```
